32 devices in a mesh: grp: 4 (over x, core), seq: 8 (over z, y).
Axes of the slice: x: 2, y: 2, z: 4, core: 2. Of those that a mesh axis runs over, the one named last changes fastest.
Arguments:
- prompt: bfloat16 [4, 2048, 2048], P('grp', 'seq'), may hold values from -6 to 6
- conts: bfloat16 [4, 8, 256, 2048], P('grp', 'seq'), may hold values from -6 to 6
- assignment: int32 [4, 8], P('grp', 'seq'), may hold values from 0 to 7, each once within a row
- offsets: int32 [4, 8], P('grp'), may hold values from 0 to 2047
- ln1_gain: float32 [2048], replicated, may hold values from 0.5 to 1.5
- ln1_bias: float32 [2048], replicated, may hold values from -1.75 to 1.75
- ln2_gain: float32 [2048], replicated, may hold values from 0.5 to 1.5
- ln2_bias: float32 [2048], replicated, may hold values from -1.75 to 1.75
- qkv_weight: bfloat16 [2048, 6144], P(('grp', 'seq')), may hold values from -0.125 to 0.125
- qkv_bias: float32 [6144], replicated, may hold values from -1.75 to 1.75
- out_weight: bfloat16 [2048, 2048], P(None, ('grp', 'seq')), may hold values from -2 to 2
- out_bias: float32 [2048], replicated, may hold values from -1.75 to 1.75
- up_weight: bfloat16 [2048, 8192], P(('grp', 'seq')), may hold values from -0.125 to 0.125
- up_bias: float32 [8192], replicated, may hold values from -3 to 3
- down_weight: bfloat16 [8192, 2048], P(None, ('grp', 'seq')), may hold values from -0.09375 to 0.09375
- down_bias: float32 [2048], replicated, may hold values from -1.75 to 1.75
- prompt_cot: bfloat16 [4, 2048, 2048], P('grp', 'seq'), may hold values from -6 to 6
- cont_cot: bfloat16 [4, 8, 256, 2048], P('grp', 'seq'), may hold values from -6 to 6
Outputs:
- prompt_out: float32 [4, 2048, 2048], P('grp', 'seq')
- cont_out: float32 [4, 8, 256, 2048], P('grp', 'seq')
- prompt_grad: float32 [4, 2048, 2048], P('grp', 'seq')
- cont_grad: float32 [4, 8, 256, 2048], P('grp', 'seq')
- ln1_gain_grad: float32 [2048], replicated
- ln1_bias_grad: float32 [2048], replicated
- ln2_gain_grad: float32 [2048], replicated
- ln2_bias_grad: float32 [2048], replicated
- qkv_weight_grad: float32 [2048, 6144], P(('grp', 'seq'))
- qkv_bias_grad: float32 [6144], replicated
- out_weight_grad: float32 [2048, 2048], P(None, ('grp', 'seq'))
- out_bias_grad: float32 [2048], replicated
- up_weight_grad: float32 [2048, 8192], P(('grp', 'seq'))
- up_bias_grad: float32 [8192], replicated
- down_weight_grad: float32 [8192, 2048], P(None, ('grp', 'seq'))
- down_bias_grad: float32 [2048], replicated
The draws below stay inside these ranges and needn't reach their ends.
Inputs may be any that keep to these rules, and one draw needn't show every extreme that they name: `assignment`: each group's row is a permutation of 0 to 7.
All inputs are finite; a program needn't handle non-finite values.
Results may differ from the reference program's by a relative error of at most 0.015.
Values may be sent and summed in bfloat16 or wider, within the bound.
No kernel may reach another device: no remote copies, remote signals or barrier semaphores. Data moves between devices by JAX's collectives and lax.ppermute only.
A program may use at most 704 MiB of HBM per device.

```python
import math
import jax
import jax.numpy as jnp
from jax import lax

D = 2048
HEADS = 8
HEAD = 256
ROT = 64
FF = 8192
PROMPT = 2048
CONT = 256
GROUPS = 4
BRANCH = 8


def with_ends(array, stream_key, least, high):
    place = [jax.random.randint(jax.random.fold_in(stream_key, axis), (), 0, length) for axis, length in enumerate(array.shape)]
    widest = array.shape.index(max(array.shape))
    beside = place[:widest] + [(place[widest] + 1) % array.shape[widest]] + place[widest + 1:]
    return array.at[tuple(place)].set(least).at[tuple(beside)].set(high)


def steps_of(rng, dims, pieces, smallest, largest):
    def one(axis_at, parts):
        steps = jax.random.uniform(jax.random.fold_in(jax.random.fold_in(rng, 6), axis_at), (parts,), jnp.float32, smallest / len(pieces), largest / len(pieces))
        return jnp.repeat(jnp.exp(steps), dims[axis_at] // parts).reshape((-1,) + (1,) * (len(dims) - axis_at - 1))

    loudness = one(*pieces[0])
    for cut in pieces[1:]:
        loudness = loudness * one(*cut)
    return loudness


def bell_draw(rng, extent, spread, limit, split=(), held_as=jnp.bfloat16):
    result = jax.random.normal(rng, extent, jnp.float32) * spread
    if len(split) > 0:
        result = steps_of(rng, extent, split, -0.22, 0.18) * result
    return jnp.clip(result, min=-limit, max=limit).astype(held_as)


def setup_inputs(seed: int = 0) -> dict:
    arg_keys = jax.random.split(jax.random.key(seed), 19)
    return {
        "prompt": bell_draw(arg_keys[0], (GROUPS, PROMPT, D), 1.0, 6.0, ((0, 4), (1, 8))),
        "conts": bell_draw(arg_keys[1], (GROUPS, BRANCH, CONT, D), 1.0, 6.0, ((0, 4), (1, 8))),
        "assignment": jax.vmap(lambda own: jax.random.permutation(own, BRANCH))(jax.random.split(arg_keys[2], GROUPS)).reshape((GROUPS, BRANCH)).astype(jnp.int32),
        "offsets": with_ends(jax.random.randint(arg_keys[3], (GROUPS, BRANCH), 0, PROMPT), jax.random.fold_in(arg_keys[3], 1), 0, PROMPT - 1).astype(jnp.int32),
        "ln1_gain": jnp.clip(1.0 + 0.1 * jax.random.normal(arg_keys[4], (D,), jnp.float32), 0.5, 1.5),
        "ln1_bias": bell_draw(arg_keys[5], (D,), 0.3, 1.75, (), jnp.float32),
        "ln2_gain": jnp.clip(1.0 + 0.1 * jax.random.normal(arg_keys[6], (D,), jnp.float32), 0.5, 1.5),
        "ln2_bias": bell_draw(arg_keys[7], (D,), 0.3, 1.75, (), jnp.float32),
        "qkv_weight": bell_draw(arg_keys[8], (D, 3 * D), D ** -0.5, 0.125, ((0, 32),)),
        "qkv_bias": bell_draw(arg_keys[9], (3 * D,), 0.3, 1.75, (), jnp.float32),
        "out_weight": bell_draw(arg_keys[10], (D, D), 8 ** -0.5, 2.0, ((1, 32),)),
        "out_bias": bell_draw(arg_keys[11], (D,), 0.3, 1.75, (), jnp.float32),
        "up_weight": bell_draw(arg_keys[12], (D, FF), D ** -0.5, 0.125, ((0, 32),)),
        "up_bias": bell_draw(arg_keys[13], (FF,), 0.5, 3.0, (), jnp.float32),
        "down_weight": bell_draw(arg_keys[14], (FF, D), (FF // 2) ** -0.5, 0.09375, ((1, 32),)),
        "down_bias": bell_draw(arg_keys[15], (D,), 0.3, 1.75, (), jnp.float32),
        "prompt_cot": bell_draw(arg_keys[16], (GROUPS, PROMPT, D), 1.0, 6.0, ((0, 4), (1, 8))),
        "cont_cot": bell_draw(arg_keys[17], (GROUPS, BRANCH, CONT, D), 1.0, 6.0, ((0, 4), (1, 8))),
    }


EPSILON = 1e-05
NEG_FILL = -1e+30
ROPE_BASE = 10000.0

@jax.custom_vjp
def low(v):
    return lax.optimization_barrier(v.astype(jnp.bfloat16)).astype(jnp.float32)

@jax.custom_vjp
def low_back(v):
    return v

def low_keep(v):
    return (low(v), None)

def low_pass(kept, grad):
    return (grad,)

def back_keep(v):
    return (v, None)

def back_low(kept, grad):
    return (low(grad),)
low.defvjp(low_keep, low_pass)
low_back.defvjp(back_keep, back_low)

def matmul(left, right):
    return jnp.dot(left, right, precision=lax.Precision.HIGHEST, preferred_element_type=jnp.float32)

def layer_norm(values, ln_gain, ln_shift):
    center = values - lax.optimization_barrier(jnp.mean(values, axis=-1, keepdims=True))
    normed = center * lax.rsqrt(lax.optimization_barrier(jnp.mean(center * center, axis=-1, keepdims=True)) + EPSILON)
    return normed * ln_gain + ln_shift

def rotate(head_data, positions):
    half_rot = ROT // 2
    inv_freq = ROPE_BASE ** (-(2.0 * jnp.arange(half_rot, dtype=jnp.float32)) / ROT)
    angles = positions[:, None] * inv_freq[None, :]
    cos_table = jnp.cos(angles)[:, None, :]
    sin_table = jnp.sin(angles)[:, None, :]
    first_half = head_data[..., :half_rot]
    second = head_data[..., half_rot:ROT]
    return jnp.concatenate([first_half * cos_table - second * sin_table, second * cos_table + first_half * sin_table, head_data[..., ROT:]], axis=-1)

def project(params, tokens, positions):
    ln1_gain, ln1_bias, ln2_gain, ln2_bias, qkv_weight, qkv_bias, out_weight, out_bias, up_weight, up_bias, down_weight, down_bias = params
    first_norm = low(layer_norm(tokens, ln1_gain, ln1_bias))
    second_norm = low(layer_norm(tokens, ln2_gain, ln2_bias))
    qkv_all = low_back(matmul(first_norm, qkv_weight) + qkv_bias)
    row_count = tokens.shape[0]
    split_qkv = qkv_all.reshape(row_count, 3, HEADS, HEAD)
    queries = low(rotate(split_qkv[:, 0], positions))
    keys_rot = low(rotate(split_qkv[:, 1], positions))
    values_low = low(split_qkv[:, 2])
    hidden_pre = low_back(matmul(second_norm, up_weight) + up_bias)
    activated = low(jax.nn.gelu(hidden_pre, approximate=False))
    mlp_out = matmul(activated, down_weight) + down_bias
    return (queries, keys_rot, values_low, mlp_out)

def attend(queries, keys_rot, values_low, allowed):
    score_scale = 1.0 / math.sqrt(HEAD)
    scores = low_back(jnp.einsum('qhd,khd->hqk', queries, keys_rot, precision=lax.Precision.HIGHEST) * score_scale)
    masked = jnp.where(allowed[None], scores, NEG_FILL)
    weights = low(jax.nn.softmax(masked, axis=-1))
    mixed_heads = jnp.einsum('hqk,khd->qhd', weights, values_low, precision=lax.Precision.HIGHEST)
    return mixed_heads.reshape(mixed_heads.shape[0], D)

def finish(params, tokens, attention, mlp_out):
    attention_low = low_back(low(attention))
    return tokens + matmul(attention_low, params[6]) + params[7] + mlp_out

def group_forward(params, prompt_rows, cont_rows, starts):
    branch_count = cont_rows.shape[0]
    prompt_pos = jnp.arange(PROMPT, dtype=jnp.int32).astype(jnp.float32)
    cont_pos = (PROMPT + starts[:, None] + jnp.arange(CONT, dtype=jnp.int32)[None, :]).astype(jnp.float32).reshape(-1)
    prompt_q, prompt_k, prompt_v, prompt_mlp = project(params, prompt_rows, prompt_pos)
    flat_conts = cont_rows.reshape(branch_count * CONT, D)
    cont_q, cont_k, cont_v, cont_mlp = project(params, flat_conts, cont_pos)
    q_block = min(512, PROMPT)
    block_count = PROMPT // q_block
    key_index = jnp.arange(PROMPT, dtype=jnp.int32)

    def prompt_block(inputs):
        block_queries, block_start = inputs
        query_index = block_start + jnp.arange(q_block, dtype=jnp.int32)
        allowed = key_index[None, :] <= query_index[:, None]
        return attend(block_queries, prompt_k, prompt_v, allowed)
    prompt_attn = lax.map(jax.checkpoint(prompt_block), (prompt_q.reshape(block_count, q_block, HEADS, HEAD), jnp.arange(block_count, dtype=jnp.int32) * q_block)).reshape(PROMPT, D)
    key_mark = jnp.concatenate([key_index, PROMPT + jnp.arange(CONT, dtype=jnp.int32)])
    query_mark = PROMPT + jnp.arange(CONT, dtype=jnp.int32)
    allowed_cont = key_mark[None, :] <= query_mark[:, None]

    def cont_block(inputs):
        branch_q, branch_k, branch_v = inputs
        all_keys = jnp.concatenate([prompt_k, branch_k], axis=0)
        all_values = jnp.concatenate([prompt_v, branch_v], axis=0)
        return attend(branch_q, all_keys, all_values, allowed_cont)
    shaped = (branch_count, CONT, HEADS, HEAD)
    cont_attn = lax.map(jax.checkpoint(cont_block), (cont_q.reshape(shaped), cont_k.reshape(shaped), cont_v.reshape(shaped))).reshape(branch_count * CONT, D)
    prompt_result = finish(params, prompt_rows, prompt_attn, prompt_mlp)
    cont_result = finish(params, flat_conts, cont_attn, cont_mlp).reshape(cont_rows.shape)
    return (prompt_result, cont_result)

def forward_all(params, prompt_all, conts_all, starts_all):

    def one_group(inputs):
        return group_forward(params, inputs[0], inputs[1], inputs[2])
    return lax.map(jax.checkpoint(one_group), (prompt_all, conts_all, starts_all))

def reference(prompt, conts, assignment, offsets, ln1_gain, ln1_bias, ln2_gain, ln2_bias, qkv_weight, qkv_bias, out_weight, out_bias, up_weight, up_bias, down_weight, down_bias, prompt_cot, cont_cot):
    starts = jnp.take_along_axis(offsets, assignment, axis=1).astype(jnp.int32)
    params = tuple((weight_arg.astype(jnp.float32) for weight_arg in (ln1_gain, ln1_bias, ln2_gain, ln2_bias, qkv_weight, qkv_bias, out_weight, out_bias, up_weight, up_bias, down_weight, down_bias)))

    def wrapped(weights, prompt_in, conts_in):
        return forward_all(weights, prompt_in, conts_in, starts)
    outputs, pullback = jax.vjp(wrapped, params, prompt.astype(jnp.float32), conts.astype(jnp.float32))
    grads, prompt_grad, cont_grad = pullback((prompt_cot.astype(jnp.float32), cont_cot.astype(jnp.float32)))
    return (outputs[0], outputs[1], prompt_grad, cont_grad, grads[0], grads[1], grads[2], grads[3], grads[4], grads[5], grads[6], grads[7], grads[8], grads[9], grads[10], grads[11])
```

```python
from functools import partial
import math

import jax
import jax.numpy as jnp
import numpy as np
from jax import lax
from jax.experimental import pallas as pl
from jax.experimental.pallas import tpu as pltpu
from jax.sharding import PartitionSpec as P

D = 2048
HEADS = 8
HEAD = 256
ROT = 64
PROMPT = 2048


EPSILON = 1e-05
NEG_FILL = -1e30
ROPE_BASE = 10000.0


def layer_norm(values, ln_gain, ln_shift):
    center = values - jnp.mean(values, axis=-1, keepdims=True)
    normed = center * lax.rsqrt(jnp.mean(center * center, axis=-1, keepdims=True) + EPSILON)
    return normed * ln_gain + ln_shift


def both_norms(values, gain_one, shift_one, gain_two, shift_two):
    return (layer_norm(values, gain_one, shift_one), layer_norm(values, gain_two, shift_two))


def rotate(head_data, positions, sign_flip):
    half_rot = ROT // 2
    inv_freq = ROPE_BASE ** (-(2.0 * jnp.arange(half_rot, dtype=jnp.float32)) / ROT)
    angles = positions[:, None] * inv_freq[None, :]
    cos_table = jnp.cos(angles)[:, None, :]
    sin_table = sign_flip * jnp.sin(angles)[:, None, :]
    first_half = head_data[..., :half_rot]
    second = head_data[..., half_rot:ROT]
    return jnp.concatenate(
        [
            first_half * cos_table - second * sin_table,
            second * cos_table + first_half * sin_table,
            head_data[..., ROT:],
        ],
        axis=-1,
    )


def contract_rows(left, right):
    return lax.dot_general(
        left, right, (((1,), (1,)), ((), ())), preferred_element_type=jnp.float32
    )


def contract_cols(left, right):
    return lax.dot_general(
        left, right, (((0,), (0,)), ((), ())), preferred_element_type=jnp.float32
    )


def local(
    prompt,
    conts,
    assignment,
    offsets,
    ln1_gain,
    ln1_bias,
    ln2_gain,
    ln2_bias,
    qkv_weight,
    qkv_bias,
    out_weight,
    out_bias,
    up_weight,
    up_bias,
    down_weight,
    down_bias,
    prompt_cot,
    cont_cot,
):
    prompt_rows = prompt.shape[1]
    cont_rows = conts.shape[2]
    row_total = prompt_rows + cont_rows
    score_scale = 1.0 / math.sqrt(HEAD)
    shard_index = lax.axis_index("seq")
    tokens = jnp.concatenate([prompt[0], conts[0, 0]], axis=0).astype(jnp.float32)
    branch_ids = jnp.arange(offsets.shape[1], dtype=jnp.int32)
    my_offset = jnp.sum(jnp.where(branch_ids == assignment[0, 0], offsets[0], 0))
    prompt_mark = shard_index * prompt_rows + jnp.arange(prompt_rows, dtype=jnp.int32)
    cont_mark = PROMPT + jnp.arange(cont_rows, dtype=jnp.int32)
    query_mark = jnp.concatenate([prompt_mark, cont_mark])
    positions = jnp.concatenate([prompt_mark, cont_mark + my_offset]).astype(jnp.float32)
    (first_norm, second_norm), norm_pullback = jax.vjp(
        both_norms, tokens, ln1_gain, ln1_bias, ln2_gain, ln2_bias
    )
    first_low = first_norm.astype(jnp.bfloat16)
    second_low = second_norm.astype(jnp.bfloat16)
    qkv_full, up_full = (
        lax.all_gather(qkv_weight, ("grp", "seq"), axis=0, tiled=True),
        lax.all_gather(up_weight, ("grp", "seq"), axis=0, tiled=True),
    )
    qkv_acc = jnp.dot(first_low, qkv_full, preferred_element_type=jnp.float32)
    up_acc = jnp.dot(second_low, up_full, preferred_element_type=jnp.float32)
    split_qkv = (qkv_acc + qkv_bias).reshape(row_total, 3, HEADS, HEAD)
    queries = rotate(split_qkv[:, 0], positions, 1.0).astype(jnp.bfloat16)
    keys_rot = rotate(split_qkv[:, 1], positions, 1.0).astype(jnp.bfloat16)
    values_low = split_qkv[:, 2].astype(jnp.bfloat16)
    hidden_pre = up_acc + up_bias
    activated, gelu_pullback = jax.vjp(partial(jax.nn.gelu, approximate=False), hidden_pre)
    act_low = activated.astype(jnp.bfloat16)

    def score_block(key_block, key_mark):
        raw_scores = (
            jnp.einsum("qhd,khd->hqk", queries, key_block, preferred_element_type=jnp.float32)
            * score_scale
        )
        allowed = key_mark[None, :] <= query_mark[:, None]
        return (raw_scores, allowed)

    def absorb(soft_state, key_block, value_block, key_mark):
        run_max, run_sum, run_acc = soft_state
        raw_scores, allowed = score_block(key_block, key_mark)
        masked = jnp.where(allowed[None], raw_scores, NEG_FILL)
        new_max = jnp.maximum(run_max, jnp.max(masked, axis=-1))
        exp_scores = jnp.where(allowed[None], jnp.exp(masked - new_max[..., None]), 0.0)
        factor = jnp.exp(run_max - new_max)
        mixed_heads = jnp.einsum(
            "hqk,khd->qhd",
            exp_scores.astype(jnp.bfloat16),
            value_block,
            preferred_element_type=jnp.float32,
        )
        return (
            new_max,
            run_sum * factor + jnp.sum(exp_scores, axis=-1),
            run_acc * factor.T[:, :, None] + mixed_heads,
        )

    cont_keys = keys_rot[prompt_rows:]
    cont_values = values_low[prompt_rows:]
    start_state = (
        jnp.full((HEADS, row_total), NEG_FILL, jnp.float32),
        jnp.zeros((HEADS, row_total), jnp.float32),
        jnp.zeros((row_total, HEADS, HEAD), jnp.float32),
    )
    start_state = absorb(start_state, cont_keys, cont_values, cont_mark)
    prompt_keys_send = keys_rot[:prompt_rows].reshape(prompt_rows, D)
    prompt_values_send = values_low[:prompt_rows].reshape(prompt_rows, D)
    key_piece = lax.all_gather(prompt_keys_send, "seq", axis=0, tiled=True)
    value_piece = lax.all_gather(prompt_values_send, "seq", axis=0, tiled=True)
    piece_width = key_piece.shape[0]
    key_mark = jnp.arange(piece_width, dtype=jnp.int32)
    run_max, run_sum, run_acc = absorb(
        start_state,
        key_piece.reshape(piece_width, HEADS, HEAD),
        value_piece.reshape(piece_width, HEADS, HEAD),
        key_mark,
    )
    attention = run_acc / run_sum.T[:, :, None]
    log_total = run_max + jnp.log(run_sum)
    attention_low = attention.reshape(row_total, D).astype(jnp.bfloat16)
    out_full, down_full = (
        lax.all_gather(out_weight, ("grp", "seq"), axis=1, tiled=True),
        lax.all_gather(down_weight, ("grp", "seq"), axis=1, tiled=True),
    )
    branch_sum = jnp.dot(attention_low, out_full, preferred_element_type=jnp.float32) + jnp.dot(
        act_low, down_full, preferred_element_type=jnp.float32
    )
    layer_out = tokens + branch_sum + out_bias + down_bias
    grad_out = jnp.concatenate([prompt_cot[0], cont_cot[0, 0]], axis=0)
    grad_f32 = grad_out.astype(jnp.float32)
    bias_out_term = jnp.sum(grad_f32, axis=0)
    out_again, down_again = (
        lax.all_gather(out_weight, ("grp", "seq"), axis=1, tiled=True),
        lax.all_gather(down_weight, ("grp", "seq"), axis=1, tiled=True),
    )
    attn_grad = contract_rows(grad_out, out_again)
    act_grad = contract_rows(grad_out, down_again)
    attn_grad_low = attn_grad.astype(jnp.bfloat16)
    (hidden_grad,) = gelu_pullback(act_grad)
    hidden_grad_low = hidden_grad.astype(jnp.bfloat16)
    up_bias_term = jnp.sum(hidden_grad_low.astype(jnp.float32), axis=0)
    grad_heads = attn_grad_low.reshape(row_total, HEADS, HEAD)
    row_delta = jnp.sum(grad_heads.astype(jnp.float32) * attention, axis=-1).T

    def back_block(key_block, value_block, key_mark):
        raw_scores, allowed = score_block(key_block, key_mark)
        probabilities = jnp.exp(
            jnp.where(allowed[None], raw_scores - log_total[..., None], NEG_FILL)
        )
        prob_grad = jnp.einsum(
            "qhd,khd->hqk", grad_heads, value_block, preferred_element_type=jnp.float32
        )
        score_grad = (probabilities * (prob_grad - row_delta[..., None])).astype(jnp.bfloat16)
        query_term = (
            jnp.einsum("hqk,khd->qhd", score_grad, key_block, preferred_element_type=jnp.float32)
            * score_scale
        )
        key_term = (
            jnp.einsum("hqk,qhd->khd", score_grad, queries, preferred_element_type=jnp.float32)
            * score_scale
        )
        value_term = jnp.einsum(
            "hqk,qhd->khd",
            probabilities.astype(jnp.bfloat16),
            grad_heads,
            preferred_element_type=jnp.float32,
        )
        return (query_term, key_term, value_term)

    query_local, key_local, value_local = back_block(cont_keys, cont_values, cont_mark)
    gathered_keys, gathered_values = (
        lax.all_gather(prompt_keys_send, "seq", axis=0, tiled=True),
        lax.all_gather(prompt_values_send, "seq", axis=0, tiled=True),
    )
    key_block_size = min(512, PROMPT)
    block_count = PROMPT // key_block_size

    def scan_step(query_total, inputs):
        key_block, value_block, block_start = inputs
        key_mark = block_start + jnp.arange(key_block_size, dtype=jnp.int32)
        query_term, key_term, value_term = back_block(
            key_block.reshape(key_block_size, HEADS, HEAD),
            value_block.reshape(key_block_size, HEADS, HEAD),
            key_mark,
        )
        return (
            query_total + query_term,
            (key_term.reshape(key_block_size, D), value_term.reshape(key_block_size, D)),
        )

    query_grad, (key_terms, value_terms) = lax.scan(
        scan_step,
        query_local,
        (
            gathered_keys.reshape(block_count, key_block_size, D),
            gathered_values.reshape(block_count, key_block_size, D),
            jnp.arange(block_count, dtype=jnp.int32) * key_block_size,
        ),
    )
    key_prompt_grad, value_prompt_grad = (
        lax.psum_scatter(
            key_terms.reshape(PROMPT, D).astype(jnp.bfloat16),
            "seq",
            scatter_dimension=0,
            tiled=True,
        ).astype(jnp.float32),
        lax.psum_scatter(
            value_terms.reshape(PROMPT, D).astype(jnp.bfloat16),
            "seq",
            scatter_dimension=0,
            tiled=True,
        ).astype(jnp.float32),
    )
    key_grad = jnp.concatenate([key_prompt_grad, key_local.reshape(cont_rows, D)], axis=0).reshape(
        row_total, HEADS, HEAD
    )
    value_grad = jnp.concatenate(
        [value_prompt_grad, value_local.reshape(cont_rows, D)], axis=0
    ).reshape(row_total, HEADS, HEAD)
    qkv_grad = (
        jnp.stack(
            [rotate(query_grad, positions, -1.0), rotate(key_grad, positions, -1.0), value_grad],
            axis=1,
        )
        .reshape(row_total, 3 * D)
        .astype(jnp.bfloat16)
    )
    qkv_bias_term = jnp.sum(qkv_grad.astype(jnp.float32), axis=0)
    qkv_again, up_again = (
        lax.all_gather(qkv_weight, ("grp", "seq"), axis=0, tiled=True),
        lax.all_gather(up_weight, ("grp", "seq"), axis=0, tiled=True),
    )
    first_grad = contract_rows(qkv_grad, qkv_again)
    second_grad = contract_rows(hidden_grad_low, up_again)
    token_grad, gain_one, shift_one, gain_two, shift_two = norm_pullback((first_grad, second_grad))
    token_grad = token_grad + grad_f32
    small_sums = lax.psum(
        (gain_one, shift_one, gain_two, shift_two, qkv_bias_term, bias_out_term, up_bias_term),
        ("grp", "seq"),
    )
    out_sources = jnp.concatenate([attention_low, act_low], axis=1)
    in_group = lax.psum_scatter(
        jnp.concatenate(
            [contract_cols(first_low, qkv_grad), contract_cols(second_low, hidden_grad_low)], axis=1
        ).astype(jnp.bfloat16),
        "grp",
        scatter_dimension=0,
        tiled=True,
    )
    in_share = lax.psum_scatter(in_group, "seq", scatter_dimension=0, tiled=True).astype(
        jnp.float32
    )
    out_group = lax.psum_scatter(
        contract_cols(grad_out, out_sources).astype(jnp.bfloat16),
        "grp",
        scatter_dimension=0,
        tiled=True,
    )
    out_share = lax.psum_scatter(out_group, "seq", scatter_dimension=0, tiled=True).astype(
        jnp.float32
    )
    qkv_weight_grad = in_share[:, : 3 * D]
    up_weight_grad = in_share[:, 3 * D :]
    out_weight_grad = out_share[:, :D].T
    down_weight_grad = out_share[:, D:].T
    prompt_result = layer_out[:prompt_rows][None]
    cont_result = layer_out[prompt_rows:][None, None]
    prompt_grad = token_grad[:prompt_rows][None]
    cont_grad = token_grad[prompt_rows:][None, None]
    return (
        prompt_result,
        cont_result,
        prompt_grad,
        cont_grad,
        small_sums[0],
        small_sums[1],
        small_sums[2],
        small_sums[3],
        qkv_weight_grad,
        small_sums[4],
        out_weight_grad,
        small_sums[5],
        up_weight_grad,
        small_sums[6],
        down_weight_grad,
        small_sums[5],
    )


ORDER = (0, 2, 1, 3)
TP = 4
HEADS_HERE = HEADS // TP
HCOLS = HEADS_HERE * HEAD
LANES = 128
BF = jnp.bfloat16
F32 = jnp.float32


def swap_grp(array, bits):
    return lax.ppermute(array, "grp", [(i, i ^ bits) for i in range(4)])


def swap_seq(array, bits):
    return lax.ppermute(array, "seq", [(i, i ^ bits) for i in range(8)])


def matmul_nn(left, right):
    return jnp.dot(left, right, preferred_element_type=F32)


def pick(array, index, axis):
    return lax.dynamic_index_in_dim(array, index, axis, keepdims=False)


def place(buffer, piece, index):
    return lax.dynamic_update_index_in_dim(buffer, piece, index, 0)


def tie(*arrays):
    return lax.optimization_barrier(arrays)


def whole(shape):
    return pl.BlockSpec(shape, lambda i, rank: (0,) * len(shape))


def ranked_call(body, rank, ins, shapes, name):
    return pl.pallas_call(
        body,
        grid_spec=pltpu.PrefetchScalarGridSpec(
            num_scalar_prefetch=1,
            grid=(1,),
            in_specs=[whole(a.shape) for a in ins],
            out_specs=[whole(s.shape) for s in shapes],
        ),
        out_shape=shapes,
        compiler_params=pltpu.CompilerParams(vmem_limit_bytes=56 << 20),
        name=name,
    )(rank.reshape(1), *ins)


def split_columns(shards, groups, tp_rank):
    rows = shards[0].shape[0]
    widths = [shard.shape[1] // (TP * count) for shard, count in zip(shards, groups)]
    cols = sum(width * count for width, count in zip(widths, groups))

    def body(rank_ref, *refs):
        ins, (own_ref, side_ref, far_ref) = refs[: len(shards)], refs[len(shards) :]
        at = 0
        for ref, count, width in zip(ins, groups, widths):
            for part in range(count):
                for bits in range(TP):
                    start = pl.multiple_of((part * TP + (rank_ref[0] ^ bits)) * width, width)
                    run = ref[:, pl.ds(start, width)]
                    here = slice(at, at + width)
                    if bits == 0:
                        own_ref[:, here] = run
                    elif bits == 2:
                        far_ref[:, here] = run
                    else:
                        side_ref[bits // 2, :, here] = run
                at += width

    shapes = [
        jax.ShapeDtypeStruct((rows, cols), BF),
        jax.ShapeDtypeStruct((2, rows, cols), BF),
        jax.ShapeDtypeStruct((rows, cols), BF),
    ]
    return ranked_call(body, tp_rank, list(shards), shapes, "split_columns")


def exchange(own, side, far):
    over_y = swap_seq(side, 1)
    over_z = swap_seq(jnp.stack([far, over_y[1]]), 2)
    return own, over_y, over_z


def stack_ranks(own, over_y, over_z, cuts, tp_rank):
    rows = own.shape[0]

    def body(rank_ref, own_ref, y_ref, z_ref, *outs):
        at = 0
        for out, width in zip(outs, cuts):
            here = slice(at, at + width)
            pieces = (own_ref[:, here], y_ref[0, :, here], z_ref[0, :, here], z_ref[1, :, here])
            for bits, piece in enumerate(pieces):
                start = pl.multiple_of((rank_ref[0] ^ bits) * rows, rows)
                out[pl.ds(start, rows), :] = piece
            at += width

    shapes = [jax.ShapeDtypeStruct((TP * rows, width), BF) for width in cuts]
    return ranked_call(body, tp_rank, [own, over_y, over_z], shapes, "stack_ranks")


def split_rows(stacked, tp_rank):
    rows, cols = stacked.shape[0] // TP, stacked.shape[1]

    def body(rank_ref, in_ref, own_ref, side_ref, far_ref):
        for bits in range(TP):
            start = pl.multiple_of((rank_ref[0] ^ bits) * rows, rows)
            run = in_ref[pl.ds(start, rows), :]
            if bits == 0:
                own_ref[...] = run
            elif bits == 2:
                far_ref[...] = run
            else:
                side_ref[bits // 2] = run

    shapes = [
        jax.ShapeDtypeStruct((rows, cols), BF),
        jax.ShapeDtypeStruct((2, rows, cols), BF),
        jax.ShapeDtypeStruct((rows, cols), BF),
    ]
    return ranked_call(body, tp_rank, [stacked], shapes, "split_rows")


def join_columns(own, over_y, over_z, parts, tp_rank):
    rows = own.shape[0]

    def body(rank_ref, own_ref, y_ref, z_ref, *outs):
        at = 0
        for out, (count, width) in zip(outs, parts):
            for part in range(count):
                here = slice(at, at + width)
                pieces = (own_ref[:, here], y_ref[0, :, here], z_ref[0, :, here], z_ref[1, :, here])
                for bits, piece in enumerate(pieces):
                    start = pl.multiple_of((part * TP + (rank_ref[0] ^ bits)) * width, width)
                    out[:, pl.ds(start, width)] = piece.astype(F32)
                at += width

    shapes = [jax.ShapeDtypeStruct((rows, TP * count * width), F32) for count, width in parts]
    return ranked_call(body, tp_rank, [own, over_y, over_z], shapes, "join_columns")


def unwritten(shape):
    return pl.pallas_call(
        lambda out_ref: None,
        out_specs=pl.BlockSpec(memory_space=pl.ANY),
        out_shape=jax.ShapeDtypeStruct(shape, BF),
        name="buffer",
    )()


def put_pieces(full, pieces, piece_index):
    for piece, bits in pieces:
        full = place(full, piece, piece_index ^ bits)
        full = place(full, swap_grp(piece, 1), piece_index ^ bits ^ 2)
    return full


def core_step(partial, core):
    view = partial.reshape(2, 2, 2, partial.shape[0] // 8, partial.shape[1])
    got = swap_grp(pick(view, core ^ 1, 1), 1)
    return (pick(view, core, 1).astype(F32) + got.astype(F32)).astype(BF)


def side_step(step, side):
    got = swap_grp(pick(step, side ^ 1, 0), 2)
    return (pick(step, side, 0).astype(F32) + got.astype(F32)).astype(BF)


def half_step(step, z_half):
    got = swap_seq(pick(step, z_half ^ 1, 0), 4)
    return (pick(step, z_half, 0).astype(F32) + got.astype(F32)).astype(BF)


def scatter_rows(partial):
    half = partial.shape[0] // 2
    quarter = half // 2
    got = swap_seq(partial[half:], 1)
    away = (partial[quarter:half].astype(F32) + got[quarter:].astype(F32)).astype(BF)
    got_away = swap_seq(away, 2)
    return partial[:quarter].astype(F32) + got[:quarter].astype(F32) + got_away.astype(F32)


def rotary_tables(positions):
    lane = jnp.arange(LANES, dtype=jnp.int32)
    half_rot = ROT // 2
    exponent = -(2.0 * (lane % half_rot).astype(F32)) / ROT
    angles = positions[:, None] * (ROPE_BASE**exponent)[None, :]
    turning = (lane < ROT)[None, :]
    cos_table = jnp.where(turning, jnp.cos(angles), 1.0)
    sin_part = jnp.sin(angles)
    sin_table = jnp.where((lane < half_rot)[None, :], -sin_part, sin_part)
    return cos_table, jnp.where(turning, sin_table, 0.0)


def swapped_halves(values):
    half_rot = ROT // 2
    lane = lax.broadcasted_iota(jnp.int32, values.shape, 1)
    return jnp.where(
        lane < half_rot,
        pltpu.roll(values, LANES - half_rot, 1),
        pltpu.roll(values, half_rot, 1),
    )


def turned(values, cos_table, sin_table):
    first = values[:, :LANES]
    return jnp.concatenate(
        [first * cos_table + swapped_halves(first) * sin_table, values[:, LANES:]], axis=1
    )


def qkv_body(rows_ref, weight_ref, bias_ref, cos_ref, sin_ref, q_ref, *outs):
    near_refs, own_refs = outs[:HEADS_HERE], outs[HEADS_HERE:]
    prompt_rows = near_refs[0].shape[0]
    acc = matmul_nn(rows_ref[...], weight_ref[...]) + bias_ref[...]
    cos_table, sin_table = cos_ref[...], sin_ref[...]
    for head, (near_ref, own_ref) in enumerate(zip(near_refs, own_refs)):
        at = head * HEAD
        query = turned(acc[:, at : at + HEAD], cos_table, sin_table)
        q_ref[:, at : at + HEAD] = (query * (1.0 / math.sqrt(HEAD))).astype(BF)
        key = turned(acc[:, HCOLS + at : HCOLS + at + HEAD], cos_table, sin_table).astype(BF)
        value = acc[:, 2 * HCOLS + at : 2 * HCOLS + at + HEAD].astype(BF)
        near_ref[:, :HEAD] = key[:prompt_rows]
        near_ref[:, HEAD:] = value[:prompt_rows]
        own_ref[:, :HEAD] = key[prompt_rows:]
        own_ref[:, HEAD:] = value[prompt_rows:]


def project_qkv(rows, weight, bias, cos_table, sin_table, block, prompt_rows):
    total = rows.shape[0]
    cont_rows = block - prompt_rows
    blocks = total // block
    outs = pl.pallas_call(
        qkv_body,
        grid=(blocks,),
        in_specs=[
            pl.BlockSpec((block, D), lambda i: (i, 0)),
            pl.BlockSpec((D, 3 * HCOLS), lambda i: (0, 0)),
            pl.BlockSpec((1, 3 * HCOLS), lambda i: (0, 0)),
            pl.BlockSpec((block, LANES), lambda i: (i, 0)),
            pl.BlockSpec((block, LANES), lambda i: (i, 0)),
        ],
        out_specs=[
            pl.BlockSpec((block, HCOLS), lambda i: (i, 0)),
            *([pl.BlockSpec((prompt_rows, 2 * HEAD), lambda i: (i, 0))] * HEADS_HERE),
            *([pl.BlockSpec((cont_rows, 2 * HEAD), lambda i: (i, 0))] * HEADS_HERE),
        ],
        out_shape=[
            jax.ShapeDtypeStruct((total, HCOLS), BF),
            *([jax.ShapeDtypeStruct((blocks * prompt_rows, 2 * HEAD), BF)] * HEADS_HERE),
            *([jax.ShapeDtypeStruct((blocks * cont_rows, 2 * HEAD), BF)] * HEADS_HERE),
        ],
        compiler_params=pltpu.CompilerParams(vmem_limit_bytes=56 << 20),
        name="qkv_rotary",
    )(rows, weight, bias, cos_table, sin_table)
    return outs[0], outs[1 : 1 + HEADS_HERE], outs[1 + HEADS_HERE :]


def attention_body(
    q_ref,
    do_ref,
    kl_ref,
    vl_ref,
    kr_ref,
    vr_ref,
    kc_ref,
    vc_ref,
    cos_ref,
    sin_ref,
    cosl_ref,
    sinl_ref,
    cosr_ref,
    sinr_ref,
    qmark_ref,
    kmark_ref,
    o_ref,
    dq_ref,
    down_ref,
    dnear_ref,
    dfar_ref,
    akl,
    avl,
    akr,
    avr,
):
    step = pl.program_id(0)
    last = pl.num_programs(0) - 1
    near = kl_ref.shape[0]

    @pl.when(step == 0)
    def _():
        for acc in (akl, avl, akr, avr):
            acc[...] = jnp.zeros_like(acc)

    query, grad = q_ref[...], do_ref[...]

    def work(own):
        scores = [contract_rows(query, kl_ref[...]), contract_rows(query, kr_ref[...])]
        if own:
            mine = contract_rows(query, kc_ref[...])
            at_row = lax.broadcasted_iota(jnp.int32, mine.shape, 0)
            at_col = lax.broadcasted_iota(jnp.int32, mine.shape, 1)
            scores.append(jnp.where(at_col <= at_row, mine, NEG_FILL))
        else:
            marks = kmark_ref[...]
            own_mark = qmark_ref[...]
            scores[0] = jnp.where(marks[:, :near] <= own_mark, scores[0], NEG_FILL)
            scores[1] = jnp.where(marks[:, near:] <= own_mark, scores[1], NEG_FILL)
        top = scores[0].max(axis=1, keepdims=True)
        for part in scores[1:]:
            top = jnp.maximum(top, part.max(axis=1, keepdims=True))
        probs = [jnp.exp(part - top) for part in scores]
        total = probs[0].sum(axis=1, keepdims=True)
        for part in probs[1:]:
            total = total + part.sum(axis=1, keepdims=True)
        share = 1.0 / total
        probs = [part * share for part in probs]
        low = [part.astype(BF) for part in probs]
        values = [vl_ref, vr_ref] + ([vc_ref] if own else [])
        keys = [kl_ref, kr_ref] + ([kc_ref] if own else [])
        mixed = matmul_nn(low[0], values[0][...])
        for part, ref in zip(low[1:], values[1:]):
            mixed = mixed + matmul_nn(part, ref[...])
        o_ref[...] = mixed.astype(BF)
        prob_grad = [contract_rows(grad, ref[...]) for ref in values]
        delta = (probs[0] * prob_grad[0]).sum(axis=1, keepdims=True)
        for part, grad_part in zip(probs[1:], prob_grad[1:]):
            delta = delta + (part * grad_part).sum(axis=1, keepdims=True)
        slopes = [
            (part * (grad_part - delta)).astype(BF) for part, grad_part in zip(probs, prob_grad)
        ]
        query_grad = matmul_nn(slopes[0], keys[0][...])
        for part, ref in zip(slopes[1:], keys[1:]):
            query_grad = query_grad + matmul_nn(part, ref[...])
        query_grad = query_grad * (1.0 / math.sqrt(HEAD))
        dq_ref[...] = turned(query_grad, cos_ref[...], -sin_ref[...]).astype(BF)
        akl[...] += contract_cols(slopes[0], query)
        akr[...] += contract_cols(slopes[1], query)
        avl[...] += contract_cols(low[0], grad)
        avr[...] += contract_cols(low[1], grad)
        if own:
            key_grad = contract_cols(slopes[2], query)
            down_ref[:, :HEAD] = turned(key_grad, cos_ref[...], -sin_ref[...]).astype(BF)
            down_ref[:, HEAD:] = contract_cols(low[2], grad).astype(BF)

    @pl.when(step < TP)
    def _():
        work(False)

    @pl.when(step >= TP)
    def _():
        work(True)

    @pl.when(step == last)
    def _():
        dnear_ref[:, :HEAD] = turned(akl[...], cosl_ref[...], -sinl_ref[...])
        dnear_ref[:, HEAD:] = avl[...]
        dfar_ref[:, :HEAD] = turned(akr[...], cosr_ref[...], -sinr_ref[...]).astype(BF)
        dfar_ref[:, HEAD:] = avr[...].astype(BF)


def attend(
    head, queries, grads, near, far, own, tables, near_tables, far_tables, query_mark, key_mark
):
    total = queries.shape[0]
    tile = total // (2 * TP)
    keys = near.shape[0]

    def row_tile(j):
        return (j % TP) * 2 + j // TP

    def cont_tile(j):
        return jnp.maximum(j - TP, 0)

    row_spec = pl.BlockSpec((tile, HEAD), lambda j: (row_tile(j), head))
    out_spec = pl.BlockSpec((tile, HEAD), lambda j: (row_tile(j), 0))
    key_spec = pl.BlockSpec((keys, HEAD), lambda j: (0, 0))
    value_spec = pl.BlockSpec((keys, HEAD), lambda j: (0, 1))
    own_key = pl.BlockSpec((tile, HEAD), lambda j: (cont_tile(j), 0))
    own_value = pl.BlockSpec((tile, HEAD), lambda j: (cont_tile(j), 1))
    own_both = pl.BlockSpec((tile, 2 * HEAD), lambda j: (cont_tile(j), 0))
    both = pl.BlockSpec((keys, 2 * HEAD), lambda j: (0, 0))
    table_spec = pl.BlockSpec((tile, LANES), lambda j: (row_tile(j), 0))
    key_table = pl.BlockSpec((keys, LANES), lambda j: (0, 0))
    mark_spec = pl.BlockSpec((tile, 1), lambda j: (row_tile(j), 0))
    key_mark_spec = pl.BlockSpec((1, 2 * keys), lambda j: (0, 0))
    wide = jax.ShapeDtypeStruct((total, HEAD), BF)
    return pl.pallas_call(
        attention_body,
        grid=(2 * TP,),
        in_specs=[
            row_spec,
            row_spec,
            key_spec,
            value_spec,
            key_spec,
            value_spec,
            own_key,
            own_value,
            table_spec,
            table_spec,
            key_table,
            key_table,
            key_table,
            key_table,
            mark_spec,
            key_mark_spec,
        ],
        out_specs=[out_spec, out_spec, own_both, both, both],
        out_shape=[
            wide,
            wide,
            jax.ShapeDtypeStruct((keys, 2 * HEAD), BF),
            jax.ShapeDtypeStruct((keys, 2 * HEAD), F32),
            jax.ShapeDtypeStruct((keys, 2 * HEAD), BF),
        ],
        scratch_shapes=[pltpu.VMEM((keys, HEAD), F32)] * 4,
        compiler_params=pltpu.CompilerParams(vmem_limit_bytes=56 << 20),
        name="attention_both_ways",
    )(
        queries,
        grads,
        near,
        near,
        far,
        far,
        own,
        own,
        *tables,
        *near_tables,
        *far_tables,
        query_mark,
        key_mark,
    )


def join_grads(query_grads, own_grads, near_grads, far_grads, prompt_rows):
    total = query_grads[0].shape[0]
    block = total // TP
    cont_rows = block - prompt_rows

    def body(*refs):
        out_ref, sum_ref = refs[-2:]
        dq, down, dnear, dfar = (
            refs[i * HEADS_HERE : (i + 1) * HEADS_HERE] for i in range(4)
        )

        @pl.when(pl.program_id(0) == 0)
        def _():
            sum_ref[...] = jnp.zeros_like(sum_ref)

        for head in range(HEADS_HERE):
            at = head * HEAD
            out_ref[:, at : at + HEAD] = dq[head][...]
            prompt = (dnear[head][...] + dfar[head][...].astype(F32)).astype(BF)
            for kind in (0, 1):
                here = slice((kind + 1) * HCOLS + at, (kind + 1) * HCOLS + at + HEAD)
                cut = slice(kind * HEAD, (kind + 1) * HEAD)
                out_ref[:prompt_rows, here] = prompt[:, cut]
                out_ref[prompt_rows:, here] = down[head][:, cut]
        sum_ref[...] += out_ref[...].astype(F32).sum(axis=0, keepdims=True)

    def rows_of(height, width):
        return [pl.BlockSpec((height, width), lambda i: (i, 0))] * HEADS_HERE

    return pl.pallas_call(
        body,
        grid=(TP,),
        in_specs=[
            *rows_of(block, HEAD),
            *rows_of(cont_rows, 2 * HEAD),
            *rows_of(prompt_rows, 2 * HEAD),
            *rows_of(prompt_rows, 2 * HEAD),
        ],
        out_specs=[
            pl.BlockSpec((block, 3 * HCOLS), lambda i: (i, 0)),
            pl.BlockSpec((1, 3 * HCOLS), lambda i: (0, 0)),
        ],
        out_shape=[
            jax.ShapeDtypeStruct((total, 3 * HCOLS), BF),
            jax.ShapeDtypeStruct((1, 3 * HCOLS), F32),
        ],
        compiler_params=pltpu.CompilerParams(vmem_limit_bytes=56 << 20),
        name="join_grads",
    )(*query_grads, *own_grads, *near_grads, *far_grads)


def square_plan(
    prompt,
    conts,
    assignment,
    offsets,
    ln1_gain,
    ln1_bias,
    ln2_gain,
    ln2_bias,
    qkv_weight,
    qkv_bias,
    out_weight,
    out_bias,
    up_weight,
    up_bias,
    down_weight,
    down_bias,
    prompt_cot,
    cont_cot,
):
    prompt_rows, cont_rows = prompt.shape[1], conts.shape[2]
    block = prompt_rows + cont_rows
    shard = qkv_weight.shape[0]
    ff = up_weight.shape[1]
    grp_index, seq_index = lax.axis_index("grp"), lax.axis_index("seq")
    tp_rank, z_half = seq_index & 3, seq_index >> 2
    piece_index = grp_index * 2 + z_half

    core, side = grp_index & 1, grp_index >> 1
    ff_here = ff // TP
    quarter = prompt_rows

    own_rows = jnp.concatenate([prompt[0], conts[0, 0]], axis=0)
    qkv_split = split_columns([qkv_weight], [3], tp_rank)
    rows_z = swap_seq(own_rows, 2)
    rows_y = swap_seq(own_rows, 1)
    qkv_got = exchange(*qkv_split)
    (qkv_base,) = stack_ranks(*qkv_got, (3 * HCOLS,), tp_rank)
    qkv_z = swap_seq(qkv_base, 4)
    qkv_x = swap_grp(qkv_base, 2)
    rest_split = split_columns([up_weight, out_weight.T, down_weight.T], [1, 1, 1], tp_rank)
    rest_own, rest_side, rest_far = rest_split
    rest_side, qkv_base = tie(rest_side, qkv_base)
    rest_got = exchange(rest_own, rest_side, rest_far)
    up_base, out_base, down_base = stack_ranks(*rest_got, (ff_here, HCOLS, ff_here), tp_rank)
    rows_a, rows_b = rows_z[:quarter], rows_y[quarter:]
    rows_a, rows_b, up_base = tie(rows_a, rows_b, up_base)
    rows_zy = jnp.concatenate([swap_seq(rows_a, 1), swap_seq(rows_b, 2)], axis=0)

    up_base, qkv_z, qkv_x = tie(up_base, qkv_z, qkv_x)
    up_z = swap_seq(up_base, 4)
    qkv_zx = swap_grp(qkv_z, 2)
    qkv_here = put_pieces(
        unwritten((8, TP * shard, 3 * HCOLS)),
        ((qkv_base, 0), (qkv_x, 4), (qkv_z, 1), (qkv_zx, 5)),
        piece_index,
    ).reshape(D, 3 * HCOLS)
    up_base, qkv_zx = tie(up_base, qkv_zx)
    up_x = swap_grp(up_base, 2)
    out_base, up_z, up_x = tie(out_base, up_z, up_x)
    out_z = swap_seq(out_base, 4)
    up_zx = swap_grp(up_z, 2)
    up_here = put_pieces(
        unwritten((8, TP * shard, ff_here)),
        ((up_base, 0), (up_x, 4), (up_z, 1), (up_zx, 5)),
        piece_index,
    ).reshape(D, ff_here)
    out_base, up_zx = tie(out_base, up_zx)
    out_x = swap_grp(out_base, 2)
    down_base, out_z, out_x = tie(down_base, out_z, out_x)
    down_z = swap_seq(down_base, 4)
    out_zx = swap_grp(out_z, 2)
    out_here = put_pieces(
        unwritten((8, TP * shard, HCOLS)),
        ((out_base, 0), (out_x, 4), (out_z, 1), (out_zx, 5)),
        piece_index,
    ).reshape(D, HCOLS)
    down_base, out_zx = tie(down_base, out_zx)
    down_x = swap_grp(down_base, 2)
    own_cot = jnp.concatenate([prompt_cot[0], cont_cot[0, 0]], axis=0)
    own_cot, rows_zy = tie(own_cot, rows_zy)
    cots_z = swap_seq(own_cot, 2)
    cots_y = swap_seq(own_cot, 1)
    qkv_bias_here = pick(qkv_bias.reshape(3, TP, HCOLS), tp_rank, 1).reshape(1, 3 * HCOLS)
    up_bias_here = pick(up_bias.reshape(TP, ff_here), tp_rank, 0)

    branch_ids = jnp.arange(offsets.shape[1], dtype=jnp.int32)
    my_offset = jnp.sum(jnp.where(branch_ids == assignment[0, 0], offsets[0], 0)).reshape(1, 1)
    offset_pair = jnp.concatenate([my_offset, swap_seq(my_offset, 2)], axis=0)
    block_offsets = jnp.concatenate([offset_pair, swap_seq(offset_pair, 1)], axis=0)
    ranks = tp_rank ^ jnp.array(ORDER, dtype=jnp.int32)
    prompt_iota = jnp.arange(prompt_rows, dtype=jnp.int32)[None, :]
    cont_iota = jnp.arange(cont_rows, dtype=jnp.int32)[None, :]
    near_mark = (z_half * TP + ranks)[:, None] * prompt_rows + prompt_iota
    far_mark = ((z_half ^ 1) * TP + ranks)[:, None] * prompt_rows + prompt_iota
    cont_mark = jnp.broadcast_to(PROMPT + cont_iota, (TP, cont_rows))
    query_mark = jnp.concatenate([near_mark, cont_mark], axis=1).reshape(-1, 1)
    positions = jnp.concatenate([near_mark, cont_mark + block_offsets], axis=1).astype(F32)
    tables = rotary_tables(positions.reshape(-1))
    near_tables = tuple(
        t.reshape(TP, block, LANES)[:, :prompt_rows].reshape(-1, LANES) for t in tables
    )
    far_tables = rotary_tables(far_mark.reshape(-1).astype(F32))
    key_mark = jnp.concatenate([near_mark.reshape(1, -1), far_mark.reshape(1, -1)], axis=1)

    rows = jnp.concatenate([own_rows, rows_z, rows_y, rows_zy], axis=0)
    rows_f32 = rows.astype(F32)
    center = rows_f32 - jnp.mean(rows_f32, axis=-1, keepdims=True)
    spread = lax.rsqrt(jnp.mean(center * center, axis=-1, keepdims=True) + EPSILON)
    normed = center * spread
    first_low = (normed * ln1_gain + ln1_bias).astype(BF)
    second_low = (normed * ln2_gain + ln2_bias).astype(BF)

    first_low, second_low, qkv_here = tie(first_low, second_low, qkv_here)
    queries, near, own = project_qkv(
        first_low, qkv_here, qkv_bias_here, *tables, block, prompt_rows
    )
    near0, down_z = tie(near[0], down_z)
    far0 = swap_seq(near0, 4)
    down_zx = swap_grp(down_z, 2)
    down_here = put_pieces(
        unwritten((8, TP * shard, ff_here)),
        ((down_base, 0), (down_x, 4), (down_z, 1), (down_zx, 5)),
        piece_index,
    ).reshape(D, ff_here)
    near1, far0 = tie(near[1], far0)
    far1 = swap_seq(near1, 4)
    second_low, up_here, queries, near0 = tie(second_low, up_here, queries, near0)
    hidden_pre = matmul_nn(second_low, up_here) + up_bias_here
    cdf = 0.5 * (1.0 + lax.erf(hidden_pre * math.sqrt(0.5)))
    act_low = (hidden_pre * cdf).astype(BF)
    density = jnp.exp(-0.5 * hidden_pre * hidden_pre) * (1.0 / math.sqrt(2.0 * math.pi))
    slope = (cdf + hidden_pre * density).astype(BF)
    cots_y, act_low = tie(cots_y, act_low)
    cots_a, cots_b = cots_z[:quarter], cots_y[quarter:]
    cots_zy = jnp.concatenate([swap_seq(cots_a, 1), swap_seq(cots_b, 2)], axis=0)

    cots = jnp.concatenate([own_cot, cots_z, cots_y, cots_zy], axis=0)
    cots, out_here, act_low, slope = tie(cots, out_here, act_low, slope)
    attn_grad = matmul_nn(cots, out_here).astype(BF)
    shared = (tables, near_tables, far_tables, query_mark, key_mark)
    attn0, dq0, down0, dnear0, dfar0 = attend(
        0, queries, attn_grad, near0, far0, own[0], *shared
    )
    back0 = swap_seq(dfar0, 4)
    attn_grad, far1, down_here, attn0 = tie(attn_grad, far1, down_here, attn0)
    attn1, dq1, down1, dnear1, dfar1 = attend(
        1, queries, attn_grad, near1, far1, own[1], *shared
    )
    dfar1, back0 = tie(dfar1, back0)
    back1 = swap_seq(dfar1, 4)

    act_low, cots, attn1, slope = tie(act_low, cots, attn1, slope)
    down_term = contract_cols(cots, act_low).astype(BF)
    down_step = core_step(down_term, core)
    slope, down_here, down_term = tie(slope, down_here, down_term)
    hidden_grad = (matmul_nn(cots, down_here) * slope.astype(F32)).astype(BF)
    up_bias_term = jnp.sum(hidden_grad.astype(F32), axis=0)
    hidden_grad, second_low, down_step = tie(hidden_grad, second_low, down_step)
    down_step = side_step(down_step, side)
    up_term = contract_cols(second_low, hidden_grad).astype(BF)
    up_step = core_step(up_term, core)

    attn_low = jnp.concatenate([attn0, attn1], axis=1)
    attn_low, act_low, up_term = tie(attn_low, act_low, up_term)
    branch = (contract_rows(attn_low, out_here) + contract_rows(act_low, down_here)).astype(BF)
    own_f32 = own_rows.astype(F32)
    layer_out = own_f32 + scatter_rows(branch) + out_bias + down_bias
    out_cots, branch, up_step = tie(cots, branch, up_step)
    out_term = contract_cols(out_cots, attn_low).astype(BF)
    out_step = core_step(out_term, core)
    up_step, down_step = tie(up_step, down_step)
    up_step = side_step(up_step, side)
    hidden_grad, up_here, out_term = tie(hidden_grad, up_here, out_term)
    second_grad = contract_rows(hidden_grad, up_here)

    second_grad, dnear1, back1, out_step = tie(second_grad, dnear1, back1, out_step)
    qkv_grad, qkv_bias_term = join_grads(
        (dq0, dq1), (down0, down1), (dnear0, dnear1), (back0, back1), prompt_rows
    )
    down_step, back1 = tie(down_step, back1)
    down_step = half_step(down_step, z_half)
    out_step, up_step = tie(out_step, up_step)
    out_step = side_step(out_step, side)
    qkv_term = contract_cols(first_low, qkv_grad).astype(BF)
    qkv_step = core_step(qkv_term, core)
    qkv_grad, qkv_term = tie(qkv_grad, qkv_term)
    first_grad = contract_rows(qkv_grad, qkv_here)
    entry_part = (first_grad * ln1_gain + second_grad * ln2_gain).astype(BF)
    entry = scatter_rows(entry_part)
    qkv_step, out_step = tie(qkv_step, out_step)
    qkv_step = side_step(qkv_step, side)
    up_step, down_step = tie(up_step, down_step)
    up_step = half_step(up_step, z_half)
    out_step, up_step = tie(out_step, up_step)
    out_step = half_step(out_step, z_half)
    qkv_step, out_step = tie(qkv_step, out_step)
    qkv_step = half_step(qkv_step, z_half)
    early = jnp.concatenate([x.reshape(TP * shard, -1) for x in (up_step, down_step)], axis=1)
    late = jnp.concatenate([x.reshape(TP * shard, -1) for x in (qkv_step, out_step)], axis=1)
    early_got = exchange(*split_rows(early, tp_rank))
    late_got = exchange(*split_rows(late, tp_rank))
    up_weight_grad, down_grad = join_columns(
        *early_got, [(1, ff_here), (1, ff_here)], tp_rank
    )
    qkv_weight_grad, out_grad = join_columns(*late_got, [(3, HCOLS), (1, HCOLS)], tp_rank)
    down_weight_grad, out_weight_grad = down_grad.T, out_grad.T

    own_normed, own_spread = normed[:block], spread[:block]
    entry_mean = jnp.mean(entry, axis=-1, keepdims=True)
    entry_dot = jnp.mean(entry * own_normed, axis=-1, keepdims=True)
    cot_f32 = own_cot.astype(F32)
    token_grad = cot_f32 + own_spread * (entry - entry_mean - own_normed * entry_dot)

    rank_ids = jnp.arange(TP, dtype=jnp.int32)
    qkv_bias_term = qkv_bias_term.reshape(3, 1, HCOLS)
    sums = jnp.concatenate(
        [
            jnp.sum(first_grad * normed, axis=0),
            jnp.sum(first_grad, axis=0),
            jnp.sum(second_grad * normed, axis=0),
            jnp.sum(second_grad, axis=0),
            jnp.where((rank_ids == tp_rank)[None, :, None], qkv_bias_term, 0.0).reshape(-1),
            jnp.sum(cot_f32, axis=0),
            jnp.where((rank_ids == tp_rank)[:, None], up_bias_term[None], 0.0).reshape(-1),
        ]
    ).reshape(-1, LANES)
    for bits in (1, 2):
        sums = sums + swap_grp(sums, bits)
    for bits in (1, 2, 4):
        sums = sums + swap_seq(sums, bits)
    sums = sums.reshape(-1)
    cuts = np.cumsum([D, D, D, D, 3 * D, D])
    gain_one, shift_one, gain_two, shift_two, qkv_sum, out_sum, up_sum = jnp.split(sums, cuts)

    return (
        layer_out[:prompt_rows][None],
        layer_out[prompt_rows:][None, None],
        token_grad[:prompt_rows][None],
        token_grad[prompt_rows:][None, None],
        gain_one,
        shift_one,
        gain_two,
        shift_two,
        qkv_weight_grad,
        qkv_sum,
        out_weight_grad,
        out_sum,
        up_weight_grad,
        up_sum,
        down_weight_grad,
        out_sum,
    )


def solution(mesh):
    in_specs = (
        P("grp", "seq", None),
        P("grp", "seq", None, None),
        P("grp", "seq"),
        P("grp", None),
        P(),
        P(),
        P(),
        P(),
        P(("grp", "seq"), None),
        P(),
        P(None, ("grp", "seq")),
        P(),
        P(("grp", "seq"), None),
        P(),
        P(None, ("grp", "seq")),
        P(),
        P("grp", "seq", None),
        P("grp", "seq", None, None),
    )
    out_specs = (
        P("grp", "seq", None),
        P("grp", "seq", None, None),
        P("grp", "seq", None),
        P("grp", "seq", None, None),
        P(),
        P(),
        P(),
        P(),
        P(("grp", "seq"), None),
        P(),
        P(None, ("grp", "seq")),
        P(),
        P(("grp", "seq"), None),
        P(),
        P(None, ("grp", "seq")),
        P(),
    )
    plan = square_plan if (mesh.shape["grp"], mesh.shape["seq"]) == (4, 8) else local
    return jax.shard_map(plan, mesh=mesh, in_specs=in_specs, out_specs=out_specs, check_vma=False)
```

```python
from functools import partial
import math

import jax
import jax.numpy as jnp
import numpy as np
from jax import lax
from jax.experimental import pallas as pl
from jax.experimental.pallas import tpu as pltpu
from jax.sharding import PartitionSpec as P

D = 2048
HEADS = 8
HEAD = 256
ROT = 64
PROMPT = 2048


EPSILON = 1e-05
NEG_FILL = -1e30
ROPE_BASE = 10000.0


def layer_norm(values, ln_gain, ln_shift):
    center = values - jnp.mean(values, axis=-1, keepdims=True)
    normed = center * lax.rsqrt(jnp.mean(center * center, axis=-1, keepdims=True) + EPSILON)
    return normed * ln_gain + ln_shift


def both_norms(values, gain_one, shift_one, gain_two, shift_two):
    return (layer_norm(values, gain_one, shift_one), layer_norm(values, gain_two, shift_two))


def rotate(head_data, positions, sign_flip):
    half_rot = ROT // 2
    inv_freq = ROPE_BASE ** (-(2.0 * jnp.arange(half_rot, dtype=jnp.float32)) / ROT)
    angles = positions[:, None] * inv_freq[None, :]
    cos_table = jnp.cos(angles)[:, None, :]
    sin_table = sign_flip * jnp.sin(angles)[:, None, :]
    first_half = head_data[..., :half_rot]
    second = head_data[..., half_rot:ROT]
    return jnp.concatenate(
        [
            first_half * cos_table - second * sin_table,
            second * cos_table + first_half * sin_table,
            head_data[..., ROT:],
        ],
        axis=-1,
    )


def contract_rows(left, right):
    return lax.dot_general(
        left, right, (((1,), (1,)), ((), ())), preferred_element_type=jnp.float32
    )


def contract_cols(left, right):
    return lax.dot_general(
        left, right, (((0,), (0,)), ((), ())), preferred_element_type=jnp.float32
    )


def local(
    prompt,
    conts,
    assignment,
    offsets,
    ln1_gain,
    ln1_bias,
    ln2_gain,
    ln2_bias,
    qkv_weight,
    qkv_bias,
    out_weight,
    out_bias,
    up_weight,
    up_bias,
    down_weight,
    down_bias,
    prompt_cot,
    cont_cot,
):
    prompt_rows = prompt.shape[1]
    cont_rows = conts.shape[2]
    row_total = prompt_rows + cont_rows
    score_scale = 1.0 / math.sqrt(HEAD)
    shard_index = lax.axis_index("seq")
    tokens = jnp.concatenate([prompt[0], conts[0, 0]], axis=0).astype(jnp.float32)
    branch_ids = jnp.arange(offsets.shape[1], dtype=jnp.int32)
    my_offset = jnp.sum(jnp.where(branch_ids == assignment[0, 0], offsets[0], 0))
    prompt_mark = shard_index * prompt_rows + jnp.arange(prompt_rows, dtype=jnp.int32)
    cont_mark = PROMPT + jnp.arange(cont_rows, dtype=jnp.int32)
    query_mark = jnp.concatenate([prompt_mark, cont_mark])
    positions = jnp.concatenate([prompt_mark, cont_mark + my_offset]).astype(jnp.float32)
    (first_norm, second_norm), norm_pullback = jax.vjp(
        both_norms, tokens, ln1_gain, ln1_bias, ln2_gain, ln2_bias
    )
    first_low = first_norm.astype(jnp.bfloat16)
    second_low = second_norm.astype(jnp.bfloat16)
    qkv_full, up_full = (
        lax.all_gather(qkv_weight, ("grp", "seq"), axis=0, tiled=True),
        lax.all_gather(up_weight, ("grp", "seq"), axis=0, tiled=True),
    )
    qkv_acc = jnp.dot(first_low, qkv_full, preferred_element_type=jnp.float32)
    up_acc = jnp.dot(second_low, up_full, preferred_element_type=jnp.float32)
    split_qkv = (qkv_acc + qkv_bias).reshape(row_total, 3, HEADS, HEAD)
    queries = rotate(split_qkv[:, 0], positions, 1.0).astype(jnp.bfloat16)
    keys_rot = rotate(split_qkv[:, 1], positions, 1.0).astype(jnp.bfloat16)
    values_low = split_qkv[:, 2].astype(jnp.bfloat16)
    hidden_pre = up_acc + up_bias
    activated, gelu_pullback = jax.vjp(partial(jax.nn.gelu, approximate=False), hidden_pre)
    act_low = activated.astype(jnp.bfloat16)

    def score_block(key_block, key_mark):
        raw_scores = (
            jnp.einsum("qhd,khd->hqk", queries, key_block, preferred_element_type=jnp.float32)
            * score_scale
        )
        allowed = key_mark[None, :] <= query_mark[:, None]
        return (raw_scores, allowed)

    def absorb(soft_state, key_block, value_block, key_mark):
        run_max, run_sum, run_acc = soft_state
        raw_scores, allowed = score_block(key_block, key_mark)
        masked = jnp.where(allowed[None], raw_scores, NEG_FILL)
        new_max = jnp.maximum(run_max, jnp.max(masked, axis=-1))
        exp_scores = jnp.where(allowed[None], jnp.exp(masked - new_max[..., None]), 0.0)
        factor = jnp.exp(run_max - new_max)
        mixed_heads = jnp.einsum(
            "hqk,khd->qhd",
            exp_scores.astype(jnp.bfloat16),
            value_block,
            preferred_element_type=jnp.float32,
        )
        return (
            new_max,
            run_sum * factor + jnp.sum(exp_scores, axis=-1),
            run_acc * factor.T[:, :, None] + mixed_heads,
        )

    cont_keys = keys_rot[prompt_rows:]
    cont_values = values_low[prompt_rows:]
    start_state = (
        jnp.full((HEADS, row_total), NEG_FILL, jnp.float32),
        jnp.zeros((HEADS, row_total), jnp.float32),
        jnp.zeros((row_total, HEADS, HEAD), jnp.float32),
    )
    start_state = absorb(start_state, cont_keys, cont_values, cont_mark)
    prompt_keys_send = keys_rot[:prompt_rows].reshape(prompt_rows, D)
    prompt_values_send = values_low[:prompt_rows].reshape(prompt_rows, D)
    key_piece = lax.all_gather(prompt_keys_send, "seq", axis=0, tiled=True)
    value_piece = lax.all_gather(prompt_values_send, "seq", axis=0, tiled=True)
    piece_width = key_piece.shape[0]
    key_mark = jnp.arange(piece_width, dtype=jnp.int32)
    run_max, run_sum, run_acc = absorb(
        start_state,
        key_piece.reshape(piece_width, HEADS, HEAD),
        value_piece.reshape(piece_width, HEADS, HEAD),
        key_mark,
    )
    attention = run_acc / run_sum.T[:, :, None]
    log_total = run_max + jnp.log(run_sum)
    attention_low = attention.reshape(row_total, D).astype(jnp.bfloat16)
    out_full, down_full = (
        lax.all_gather(out_weight, ("grp", "seq"), axis=1, tiled=True),
        lax.all_gather(down_weight, ("grp", "seq"), axis=1, tiled=True),
    )
    branch_sum = jnp.dot(attention_low, out_full, preferred_element_type=jnp.float32) + jnp.dot(
        act_low, down_full, preferred_element_type=jnp.float32
    )
    layer_out = tokens + branch_sum + out_bias + down_bias
    grad_out = jnp.concatenate([prompt_cot[0], cont_cot[0, 0]], axis=0)
    grad_f32 = grad_out.astype(jnp.float32)
    bias_out_term = jnp.sum(grad_f32, axis=0)
    out_again, down_again = (
        lax.all_gather(out_weight, ("grp", "seq"), axis=1, tiled=True),
        lax.all_gather(down_weight, ("grp", "seq"), axis=1, tiled=True),
    )
    attn_grad = contract_rows(grad_out, out_again)
    act_grad = contract_rows(grad_out, down_again)
    attn_grad_low = attn_grad.astype(jnp.bfloat16)
    (hidden_grad,) = gelu_pullback(act_grad)
    hidden_grad_low = hidden_grad.astype(jnp.bfloat16)
    up_bias_term = jnp.sum(hidden_grad_low.astype(jnp.float32), axis=0)
    grad_heads = attn_grad_low.reshape(row_total, HEADS, HEAD)
    row_delta = jnp.sum(grad_heads.astype(jnp.float32) * attention, axis=-1).T

    def back_block(key_block, value_block, key_mark):
        raw_scores, allowed = score_block(key_block, key_mark)
        probabilities = jnp.exp(
            jnp.where(allowed[None], raw_scores - log_total[..., None], NEG_FILL)
        )
        prob_grad = jnp.einsum(
            "qhd,khd->hqk", grad_heads, value_block, preferred_element_type=jnp.float32
        )
        score_grad = (probabilities * (prob_grad - row_delta[..., None])).astype(jnp.bfloat16)
        query_term = (
            jnp.einsum("hqk,khd->qhd", score_grad, key_block, preferred_element_type=jnp.float32)
            * score_scale
        )
        key_term = (
            jnp.einsum("hqk,qhd->khd", score_grad, queries, preferred_element_type=jnp.float32)
            * score_scale
        )
        value_term = jnp.einsum(
            "hqk,qhd->khd",
            probabilities.astype(jnp.bfloat16),
            grad_heads,
            preferred_element_type=jnp.float32,
        )
        return (query_term, key_term, value_term)

    query_local, key_local, value_local = back_block(cont_keys, cont_values, cont_mark)
    gathered_keys, gathered_values = (
        lax.all_gather(prompt_keys_send, "seq", axis=0, tiled=True),
        lax.all_gather(prompt_values_send, "seq", axis=0, tiled=True),
    )
    key_block_size = min(512, PROMPT)
    block_count = PROMPT // key_block_size

    def scan_step(query_total, inputs):
        key_block, value_block, block_start = inputs
        key_mark = block_start + jnp.arange(key_block_size, dtype=jnp.int32)
        query_term, key_term, value_term = back_block(
            key_block.reshape(key_block_size, HEADS, HEAD),
            value_block.reshape(key_block_size, HEADS, HEAD),
            key_mark,
        )
        return (
            query_total + query_term,
            (key_term.reshape(key_block_size, D), value_term.reshape(key_block_size, D)),
        )

    query_grad, (key_terms, value_terms) = lax.scan(
        scan_step,
        query_local,
        (
            gathered_keys.reshape(block_count, key_block_size, D),
            gathered_values.reshape(block_count, key_block_size, D),
            jnp.arange(block_count, dtype=jnp.int32) * key_block_size,
        ),
    )
    key_prompt_grad, value_prompt_grad = (
        lax.psum_scatter(
            key_terms.reshape(PROMPT, D).astype(jnp.bfloat16),
            "seq",
            scatter_dimension=0,
            tiled=True,
        ).astype(jnp.float32),
        lax.psum_scatter(
            value_terms.reshape(PROMPT, D).astype(jnp.bfloat16),
            "seq",
            scatter_dimension=0,
            tiled=True,
        ).astype(jnp.float32),
    )
    key_grad = jnp.concatenate([key_prompt_grad, key_local.reshape(cont_rows, D)], axis=0).reshape(
        row_total, HEADS, HEAD
    )
    value_grad = jnp.concatenate(
        [value_prompt_grad, value_local.reshape(cont_rows, D)], axis=0
    ).reshape(row_total, HEADS, HEAD)
    qkv_grad = (
        jnp.stack(
            [rotate(query_grad, positions, -1.0), rotate(key_grad, positions, -1.0), value_grad],
            axis=1,
        )
        .reshape(row_total, 3 * D)
        .astype(jnp.bfloat16)
    )
    qkv_bias_term = jnp.sum(qkv_grad.astype(jnp.float32), axis=0)
    qkv_again, up_again = (
        lax.all_gather(qkv_weight, ("grp", "seq"), axis=0, tiled=True),
        lax.all_gather(up_weight, ("grp", "seq"), axis=0, tiled=True),
    )
    first_grad = contract_rows(qkv_grad, qkv_again)
    second_grad = contract_rows(hidden_grad_low, up_again)
    token_grad, gain_one, shift_one, gain_two, shift_two = norm_pullback((first_grad, second_grad))
    token_grad = token_grad + grad_f32
    small_sums = lax.psum(
        (gain_one, shift_one, gain_two, shift_two, qkv_bias_term, bias_out_term, up_bias_term),
        ("grp", "seq"),
    )
    out_sources = jnp.concatenate([attention_low, act_low], axis=1)
    in_group = lax.psum_scatter(
        jnp.concatenate(
            [contract_cols(first_low, qkv_grad), contract_cols(second_low, hidden_grad_low)], axis=1
        ).astype(jnp.bfloat16),
        "grp",
        scatter_dimension=0,
        tiled=True,
    )
    in_share = lax.psum_scatter(in_group, "seq", scatter_dimension=0, tiled=True).astype(
        jnp.float32
    )
    out_group = lax.psum_scatter(
        contract_cols(grad_out, out_sources).astype(jnp.bfloat16),
        "grp",
        scatter_dimension=0,
        tiled=True,
    )
    out_share = lax.psum_scatter(out_group, "seq", scatter_dimension=0, tiled=True).astype(
        jnp.float32
    )
    qkv_weight_grad = in_share[:, : 3 * D]
    up_weight_grad = in_share[:, 3 * D :]
    out_weight_grad = out_share[:, :D].T
    down_weight_grad = out_share[:, D:].T
    prompt_result = layer_out[:prompt_rows][None]
    cont_result = layer_out[prompt_rows:][None, None]
    prompt_grad = token_grad[:prompt_rows][None]
    cont_grad = token_grad[prompt_rows:][None, None]
    return (
        prompt_result,
        cont_result,
        prompt_grad,
        cont_grad,
        small_sums[0],
        small_sums[1],
        small_sums[2],
        small_sums[3],
        qkv_weight_grad,
        small_sums[4],
        out_weight_grad,
        small_sums[5],
        up_weight_grad,
        small_sums[6],
        down_weight_grad,
        small_sums[5],
    )


PROMPT_ORDER = (0, 2, 1, 3)
CONT_ORDER = (0, 1, 2, 3)
WIDTH_ORDER = (0, 1, 4, 5, 2, 3, 6, 7)
TP = 4
HEADS_HERE = HEADS // TP
HCOLS = HEADS_HERE * HEAD
LANES = 128
COST_UNIT = 1.0e6
COSTS = {
    "norms": 15,
    "qkv_rotary": 12,
    "feed_forward_up": 30,
    "attention_grad": 11,
    "weight_grad": 14,
    "attention_both_ways": 28,
    "feed_forward_back": 25,
    "branch_outputs": 34,
    "norm_grad": 25,
    "join_grads": 8,
    "finish_outputs": 7,
    "finish_grads": 9,
}
FLAG_B = False
BF = jnp.bfloat16
F32 = jnp.float32


def swap_grp(array, bits):
    return lax.ppermute(array, "grp", [(i, i ^ bits) for i in range(4)])


def swap_seq(array, bits):
    return lax.ppermute(array, "seq", [(i, i ^ bits) for i in range(8)])


def matmul_nn(left, right):
    return jnp.dot(left, right, preferred_element_type=F32)


def pick(array, index, axis):
    return lax.dynamic_index_in_dim(array, index, axis, keepdims=False)


def place(buffer, piece, index):
    return lax.dynamic_update_index_in_dim(buffer, piece, index, 0)


def tie(*arrays):
    return lax.optimization_barrier(arrays)


def whole(shape):
    return pl.BlockSpec(shape, lambda i, rank: (0,) * len(shape))


def cost(name):
    flops = int(COSTS.get(name, 2) * COST_UNIT)
    return pl.CostEstimate(flops=flops, transcendentals=0, bytes_accessed=0)


def ranked_call(body, rank, ins, shapes, name, blocks=None):
    return pl.pallas_call(
        body,
        grid_spec=pltpu.PrefetchScalarGridSpec(
            num_scalar_prefetch=1,
            grid=(1,),
            in_specs=[whole(shape) for shape in blocks or [a.shape for a in ins]],
            out_specs=[whole(s.shape) for s in shapes],
        ),
        out_shape=shapes,
        compiler_params=pltpu.CompilerParams(vmem_limit_bytes=56 << 20),
        cost_estimate=cost(name),
        name=name,
    )(rank.reshape(1), *ins)


def split_columns(shards, groups, tp_rank):
    rows = shards[0].shape[0]
    widths = [shard.shape[1] // (TP * count) for shard, count in zip(shards, groups)]
    cols = sum(width * count for width, count in zip(widths, groups))

    def body(rank_ref, *refs):
        ins, (own_ref, side_ref, far_ref) = refs[: len(shards)], refs[len(shards) :]
        at = 0
        for ref, count, width in zip(ins, groups, widths):
            for part in range(count):
                for bits in range(TP):
                    start = pl.multiple_of((part * TP + (rank_ref[0] ^ bits)) * width, width)
                    run = ref[:, pl.ds(start, width)]
                    here = slice(at, at + width)
                    if bits == 0:
                        own_ref[:, here] = run
                    elif bits == 2:
                        far_ref[:, here] = run
                    else:
                        side_ref[bits // 2, :, here] = run
                at += width

    shapes = [
        jax.ShapeDtypeStruct((rows, cols), BF),
        jax.ShapeDtypeStruct((2, rows, cols), BF),
        jax.ShapeDtypeStruct((rows, cols), BF),
    ]
    return ranked_call(body, tp_rank, list(shards), shapes, "split_columns")


def stack_ranks(own, over_y, over_z, cuts, tp_rank):
    rows = own.shape[0]

    def body(rank_ref, own_ref, y_ref, z_ref, *outs):
        at = 0
        for out, width in zip(outs, cuts):
            here = slice(at, at + width)
            pieces = (own_ref[:, here], y_ref[0, :, here], z_ref[0, :, here], z_ref[1, :, here])
            for bits, piece in enumerate(pieces):
                start = pl.multiple_of((rank_ref[0] ^ bits) * rows, rows)
                out[pl.ds(start, rows), :] = piece
            at += width

    shapes = [jax.ShapeDtypeStruct((TP * rows, width), BF) for width in cuts]
    return ranked_call(body, tp_rank, [own, over_y, over_z], shapes, "stack_ranks")


def split_rows(groups, tp_rank, first=1):
    rows = groups[0][2].shape[0] // TP
    cols = sum(terms[0].shape[1] for terms in groups)
    flat = [term for terms in groups for term in terms]

    def body(rank_ref, *refs):
        ins, (own_ref, side_ref, far_ref) = refs[: len(flat)], refs[len(flat) :]
        at = 0
        for g in range(len(groups)):
            kept, got_x, got_z = ins[3 * g : 3 * g + 3]
            here = slice(at, at + kept.shape[1])
            at += kept.shape[1]
            for bits in range(TP):
                start = pl.multiple_of((rank_ref[0] ^ bits) * rows, rows)
                cut = (pl.ds(start, rows), slice(None))
                total = kept[cut].astype(F32) + got_x[cut].astype(F32) + got_z[cut].astype(F32)
                run = total.astype(BF)
                if bits == 0:
                    own_ref[:, here] = run
                elif bits == 3 - first:
                    far_ref[:, here] = run
                else:
                    side_ref[int(bits == 3), :, here] = run

    shapes = [
        jax.ShapeDtypeStruct((rows, cols), BF),
        jax.ShapeDtypeStruct((2, rows, cols), BF),
        jax.ShapeDtypeStruct((rows, cols), BF),
    ]
    blocks = [(TP * rows, term.shape[1]) for term in flat]
    return ranked_call(body, tp_rank, flat, shapes, "split_rows", blocks)


def join_columns(own, got_first, got_second, parts, tp_rank, first=1):
    rows = own.shape[0]

    def body(rank_ref, own_ref, first_ref, second_ref, *outs):
        at = 0
        for out, (count, width) in zip(outs, parts):
            for part in range(count):
                here = slice(at, at + width)
                pieces = {
                    0: own_ref[:, here],
                    first: first_ref[0, :, here],
                    3 - first: second_ref[0, :, here],
                    3: second_ref[1, :, here],
                }
                for bits, piece in pieces.items():
                    start = pl.multiple_of((part * TP + (rank_ref[0] ^ bits)) * width, width)
                    out[:, pl.ds(start, width)] = piece.astype(F32)
                at += width

    shapes = [jax.ShapeDtypeStruct((rows, TP * count * width), F32) for count, width in parts]
    return ranked_call(body, tp_rank, [own, got_first, got_second], shapes, "join_columns")


def reorder_runs(arrays, place_index, sums=False):
    run = D // 8
    shapes = [jax.ShapeDtypeStruct(a.shape, a.dtype) for a in arrays]
    if sums:
        shapes.append(jax.ShapeDtypeStruct((1, D), F32))

    def body(index_ref, *refs):
        ins, outs = refs[: len(arrays)], refs[len(arrays) :]
        for j, bits in enumerate(WIDTH_ORDER):
            start = pl.multiple_of((index_ref[0] ^ bits) * run, run)
            here = slice(j * run, (j + 1) * run)
            for in_ref, out_ref in zip(ins, outs):
                out_ref[:, here] = in_ref[:, pl.ds(start, run)]
        if sums:
            total = outs[0][...].astype(F32).sum(axis=0, keepdims=True)
            for out_ref in outs[1 : len(arrays)]:
                total = total + out_ref[...].astype(F32).sum(axis=0, keepdims=True)
            outs[-1][...] = total

    return ranked_call(body, place_index, list(arrays), shapes, "reorder_runs")


def restore_runs(array, place_index):
    run = D // 8

    def body(index_ref, in_ref, out_ref):
        for j, bits in enumerate(WIDTH_ORDER):
            start = pl.multiple_of((index_ref[0] ^ bits) * run, run)
            out_ref[:, pl.ds(start, run)] = in_ref[:, j * run : (j + 1) * run]

    shapes = [jax.ShapeDtypeStruct(array.shape, array.dtype)]
    return ranked_call(body, place_index, [array], shapes, "restore_runs")[0]


def finish_outputs(parts, tokens, bias, place_index):
    run = D // 8
    rows = tokens[0].shape[0]
    flat = [term for terms in parts for term in terms]

    def body(index_ref, *refs):
        ins, outs = refs[: len(flat) + len(tokens) + 1], refs[len(flat) + len(tokens) + 1 :]
        bias_ref = ins[-1]
        for i, out_ref in enumerate(outs):
            own, got, got_far = ins[3 * i : 3 * i + 3]
            token_ref = ins[len(flat) + i]
            value = token_ref[...].astype(F32) + own[...].astype(F32) + got[...].astype(F32)
            value = value + got_far[...].astype(F32) + bias_ref[...]
            for j, bits in enumerate(WIDTH_ORDER):
                start = pl.multiple_of((index_ref[0] ^ bits) * run, run)
                out_ref[:, pl.ds(start, run)] = value[:, j * run : (j + 1) * run]

    shapes = [jax.ShapeDtypeStruct((rows, D), F32) for _ in tokens]
    blocks = [(rows, D)] * (len(flat) + len(tokens)) + [bias.shape]
    return ranked_call(
        body, place_index, flat + list(tokens) + [bias], shapes, "finish_outputs", blocks
    )


def finish_grads(parts, tokens, cots, place_index):
    run = D // 8
    rows = tokens[0].shape[0]
    count = len(tokens)
    flat = [term for terms in parts for term in terms]

    def body(index_ref, *refs):
        ins, outs = refs[: 5 * count], refs[5 * count :]
        for i, out_ref in enumerate(outs):
            own, got, got_far = ins[3 * i : 3 * i + 3]
            token = ins[3 * count + i][...].astype(F32)
            cot = ins[4 * count + i][...].astype(F32)
            entry = own[...].astype(F32) + got[...].astype(F32) + got_far[...].astype(F32)
            center = token - jnp.mean(token, axis=1, keepdims=True)
            spread = lax.rsqrt(jnp.mean(center * center, axis=1, keepdims=True) + EPSILON)
            normed = center * spread
            entry_mean = jnp.mean(entry, axis=1, keepdims=True)
            entry_dot = jnp.mean(entry * normed, axis=1, keepdims=True)
            value = cot + spread * (entry - entry_mean - normed * entry_dot)
            for j, bits in enumerate(WIDTH_ORDER):
                start = pl.multiple_of((index_ref[0] ^ bits) * run, run)
                out_ref[:, pl.ds(start, run)] = value[:, j * run : (j + 1) * run]

    shapes = [jax.ShapeDtypeStruct((rows, D), F32) for _ in tokens]
    return ranked_call(
        body,
        place_index,
        flat + list(tokens) + list(cots),
        shapes,
        "finish_grads",
        [(rows, D)] * (5 * count),
    )


def part_specs(rows, tile, width, parts):
    per_part = rows // tile

    def spec(k):
        return pl.BlockSpec((tile, width), lambda i: (jnp.clip(i - k * per_part, 0, per_part - 1), 0))

    return [spec(k) for k in range(parts)]


def norms_body(gain1, bias1, gain2, bias2, *refs):
    *parts, rows_ref, first_ref, second_ref, mean_ref, spread_ref = refs
    step = pl.program_id(0)
    per_part = pl.num_programs(0) // len(parts)
    for k, part in enumerate(parts):

        @pl.when(step // per_part == k)
        def _(part=part):
            rows_ref[...] = part[...]
            values = part[...].astype(F32)
            mean = jnp.mean(values, axis=1, keepdims=True)
            center = values - mean
            spread = lax.rsqrt(jnp.mean(center * center, axis=1, keepdims=True) + EPSILON)
            normed = center * spread
            first_ref[...] = (normed * gain1[...] + bias1[...]).astype(BF)
            second_ref[...] = (normed * gain2[...] + bias2[...]).astype(BF)
            mean_ref[...] = mean
            spread_ref[...] = spread


def both_low_norms(parts, gain1, bias1, gain2, bias2):
    tile = parts[0].shape[0]
    total = tile * len(parts)
    vector = pl.BlockSpec((1, D), lambda i: (0, 0))
    wide = pl.BlockSpec((tile, D), lambda i: (i, 0))
    thin = pl.BlockSpec((tile, 1), lambda i: (i, 0))
    return pl.pallas_call(
        norms_body,
        grid=(total // tile,),
        in_specs=[vector] * 4 + part_specs(tile, tile, D, len(parts)),
        out_specs=[wide, wide, wide, thin, thin],
        out_shape=[
            jax.ShapeDtypeStruct((total, D), BF),
            jax.ShapeDtypeStruct((total, D), BF),
            jax.ShapeDtypeStruct((total, D), BF),
            jax.ShapeDtypeStruct((total, 1), F32),
            jax.ShapeDtypeStruct((total, 1), F32),
        ],
        compiler_params=pltpu.CompilerParams(vmem_limit_bytes=56 << 20),
        cost_estimate=cost("norms"),
        name="norms",
    )(gain1, bias1, gain2, bias2, *parts)


def resident(array, block=None, at=(0, 0)):
    return pl.BlockSpec(block or array.shape, lambda i: at, pipeline_mode=pl.Buffered(1))


def times(rows, halves, columns):
    upper, lower = halves
    half = upper.shape[0]
    return matmul_nn(rows[:, :half], upper[:, columns]) + matmul_nn(rows[:, half:], lower[:, columns])


def runs_of(width, run):
    return [slice(at, at + run) for at in range(0, width, run)]


def kernel(body, steps, in_specs, out_specs, out_shape, name, scratch=()):
    return pl.pallas_call(
        body,
        grid=(steps,),
        in_specs=in_specs,
        out_specs=out_specs,
        out_shape=out_shape,
        scratch_shapes=scratch,
        compiler_params=pltpu.CompilerParams(vmem_limit_bytes=58 << 20),
        cost_estimate=cost(name),
        name=name,
    )


def stacked(parts):
    tile, width = parts[0].shape

    def body(*refs):
        *ins, out_ref = refs
        for k, part in enumerate(ins):

            @pl.when(pl.program_id(0) == k)
            def _(part=part):
                out_ref[...] = part[...]

    return kernel(
        body,
        len(parts),
        part_specs(tile, tile, width, len(parts)),
        by_rows(tile, width),
        jax.ShapeDtypeStruct((tile * len(parts), width), BF),
        "stacked",
    )(*parts)


def beside(pairs, last=None):
    tile, width = pairs[0][0].shape
    count = len(pairs) + (last is not None)

    def body(*refs):
        *ins, out_ref = refs
        for k in range(count):

            @pl.when(pl.program_id(0) == k)
            def _(k=k):
                out_ref[:, :width] = ins[2 * k][...]
                out_ref[:, width:] = ins[2 * k + 1][...]

    once = pl.BlockSpec((tile, width), lambda i: (0, 0))
    below = pl.BlockSpec((tile, width), lambda i: (1, 0))
    return kernel(
        body,
        count,
        [once] * (2 * len(pairs)) + ([] if last is None else [once, below]),
        by_rows(tile, 2 * width),
        jax.ShapeDtypeStruct((tile * count, 2 * width), BF),
        "beside",
    )(*[part for pair in pairs for part in pair], *([] if last is None else [last, last]))


def second_sum(left, right):
    rows, width = left.shape[0] // 2, left.shape[1]
    wide = min(width, 512)

    def body(left_ref, right_ref, out_ref):
        out_ref[...] = (left_ref[...].astype(F32) + right_ref[...].astype(F32)).astype(BF)

    lower = pl.BlockSpec((rows, wide), lambda i: (1, i))
    return kernel(
        body,
        width // wide,
        [lower, lower],
        pl.BlockSpec((rows, wide), lambda i: (0, i)),
        jax.ShapeDtypeStruct((rows, width), BF),
        "second_sum",
    )(left, right)


def onward(far, over_y):
    rows, width = far.shape

    def body(far_ref, y_ref, out_ref):
        out_ref[0] = far_ref[...]
        out_ref[1] = y_ref[0]

    return kernel(
        body,
        1,
        [
            pl.BlockSpec((rows, width), lambda i: (0, 0)),
            pl.BlockSpec((1, rows, width), lambda i: (1, 0, 0)),
        ],
        pl.BlockSpec((2, rows, width), lambda i: (0, 0, 0)),
        jax.ShapeDtypeStruct((2, rows, width), BF),
        "onward",
    )(far, over_y)


def by_rows(tile, width, tiles=lambda i: i):
    return pl.BlockSpec((tile, width), lambda i: (tiles(i), 0))


def attention_grad(first, parts, halves, column_block):
    tile = parts[0].shape[0]
    count = 2 * len(parts)

    def body(upper, lower, first_ref, *refs):
        *ins, out_ref, rows_ref = refs
        step = pl.program_id(0)

        def work(part):
            rows = part[...]
            rows_ref[...] = rows
            out_ref[...] = times(rows, (upper, lower), slice(0, HCOLS)).astype(BF)

        @pl.when(step < len(parts))
        def _():
            work(first_ref)

        for k, part in enumerate(ins):

            @pl.when(step == len(parts) + k)
            def _(part=part):
                work(part)

    weight_spec = resident(halves[0], (D // 2, HCOLS), (0, column_block))
    once = pl.BlockSpec((tile, D), lambda i: (0, 0))
    return kernel(
        body,
        count,
        [weight_spec, weight_spec, by_rows(tile, D, lambda i: jnp.minimum(i, len(parts) - 1))]
        + [once] * len(parts),
        [by_rows(tile, HCOLS), by_rows(tile, D)],
        [
            jax.ShapeDtypeStruct((tile * count, HCOLS), BF),
            jax.ShapeDtypeStruct((tile * count, D), BF),
        ],
        "attention_grad",
    )(*halves, first, *parts)


def feed_forward_up(rows, halves, bias):
    total, ff_here = rows.shape[0], bias.shape[1]
    tile, wide = total // 4, ff_here // 2
    half = D // 2

    def body(rows_ref, upper, lower, bias_ref, act_ref, slope_ref):
        values = rows_ref[...]
        for run in runs_of(wide, 256):
            pre = times(values, (upper, lower), run) + bias_ref[:, run]
            cdf = 0.5 * (1.0 + lax.erf(pre * math.sqrt(0.5)))
            density = jnp.exp(-0.5 * pre * pre) * (1.0 / math.sqrt(2.0 * math.pi))
            act_ref[:, run] = (pre * cdf).astype(BF)
            slope_ref[:, run] = (cdf + pre * density).astype(BF)

    weight_spec = pl.BlockSpec((half, wide), lambda i: (0, i // 4))
    out_spec = pl.BlockSpec((tile, wide), lambda i: (i % 4, i // 4))
    return kernel(
        body,
        8,
        [
            by_rows(tile, D, lambda i: i % 4),
            weight_spec,
            weight_spec,
            pl.BlockSpec((1, wide), lambda i: (0, i // 4)),
        ],
        [out_spec] * 2,
        [jax.ShapeDtypeStruct((total, ff_here), BF)] * 2,
        "feed_forward_up",
    )(rows, *halves, bias)


def feed_forward_back(cots, halves, slope):
    total, ff_here = slope.shape
    tile, wide = total // 2, ff_here // 2
    half = D // 2

    def body(cot_ref, upper, lower, slope_ref, out_ref, sum_ref):
        @pl.when(pl.program_id(0) % 2 == 0)
        def _():
            sum_ref[...] = jnp.zeros_like(sum_ref)

        values = cot_ref[...]
        for run in runs_of(wide, 512):
            grad = times(values, (upper, lower), run) * slope_ref[:, run].astype(F32)
            low = grad.astype(BF)
            out_ref[:, run] = low
            sum_ref[:, run] += low.astype(F32).sum(axis=0, keepdims=True)

    weight_spec = pl.BlockSpec((half, wide), lambda i: (0, i // 2))
    both = pl.BlockSpec((tile, wide), lambda i: (i % 2, i // 2))
    return kernel(
        body,
        4,
        [by_rows(tile, D, lambda i: i % 2), weight_spec, weight_spec, both],
        [both, pl.BlockSpec((1, wide), lambda i: (0, i // 2))],
        [jax.ShapeDtypeStruct((total, ff_here), BF), jax.ShapeDtypeStruct((1, ff_here), F32)],
        "feed_forward_back",
    )(cots, *halves, slope)


def weight_grad(left, rights, core_got=None):
    total = left.shape[0]
    width = sum(right.shape[1] for right in rights)
    half = D // 2
    wide = 512
    steps = width // wide if len(rights) == 1 else 1
    keep = core_got is not None

    def body(left_ref, *refs):
        ins, rest = refs[: len(rights)], refs[len(rights) :]
        values = left_ref[...]
        at = 0
        for right in ins:
            here = slice(at, at + right.shape[1])
            at += right.shape[1]
            product = contract_cols(values, right[...])
            if keep:
                got_ref, mine_ref, side_ref = rest
                product = product + got_ref[:, here].astype(F32)
                mine_ref[:, here] = product[: half // 2].astype(BF)
                side_ref[:, here] = product[half // 2 :].astype(BF)
            else:
                rest[0][:, here] = product.astype(BF)

    if len(rights) == 1:
        right_specs = [pl.BlockSpec((total, wide), lambda i: (0, i))]
    else:
        right_specs = [resident(right) for right in rights]
    rows = half // 2 if keep else half
    count = 2 if keep else 1
    outs = kernel(
        body,
        steps,
        [resident(left, (total, half), (0, 0 if keep else 1))]
        + right_specs
        + ([pl.BlockSpec((half, wide), lambda i: (0, i))] if keep else []),
        [pl.BlockSpec((rows, wide), lambda i: (0, i))] * count,
        [jax.ShapeDtypeStruct((rows, width), BF)] * count,
        "weight_grad",
    )(left, *rights, *([core_got] if keep else []))
    return outs if keep else outs[0]


def width_tile(halves, height, columns, block=0):
    per_half = halves[0].shape[0] // height
    return [
        pl.BlockSpec((height, columns), lambda i: (jnp.minimum(i, per_half - 1), block)),
        pl.BlockSpec((height, columns), lambda i: (jnp.maximum(i - per_half, 0), block)),
    ]


def chosen(upper, lower):
    in_upper = pl.program_id(0) < pl.num_programs(0) // 2
    return jnp.where(in_upper, upper[...], lower[...])


def branch_outputs(heads_low, act_low, attn_halves, column_block, down_halves):
    total, ff_here = act_low.shape
    tile = total // 4
    wide = 512

    def body(*refs):
        heads = [refs[h * 4 : h * 4 + 4] for h in range(HEADS_HERE)]
        refs = refs[4 * HEADS_HERE :]
        acts, attn, down, outs = refs[:4], refs[4:6], refs[6:8], refs[8:]
        attn_tile, down_tile = chosen(*attn), chosen(*down)
        for k in range(4):
            value = contract_rows(acts[k][...], down_tile)
            for head in range(HEADS_HERE):
                cut = slice(head * HEAD, (head + 1) * HEAD)
                value = value + contract_rows(heads[head][k][...], attn_tile[:, cut])
            outs[k][...] = value.astype(BF)

    return kernel(
        body,
        D // wide,
        [resident(h, (tile, HEAD), (k, 0)) for h in heads_low for k in range(4)]
        + [resident(act_low, (tile, ff_here), (k, 0)) for k in range(4)]
        + width_tile(attn_halves, wide, HCOLS, column_block)
        + width_tile(down_halves, wide, ff_here),
        [pl.BlockSpec((tile, wide), lambda i: (0, i))] * 4,
        [jax.ShapeDtypeStruct((tile, D), BF)] * 4,
        "branch_outputs",
    )(*[h for h in heads_low for _ in range(4)], *([act_low] * 4), *attn_halves, *down_halves)


def norm_grad(grads, halves, gain, tokens, mean, spread, row_blocks, addends=()):
    tile = grads.shape[0] // 4
    count = len(row_blocks)
    width = grads.shape[1]
    wide = 512

    def body(upper, lower, gain_ref, *refs):
        cut = iter(range(0, 6 * count, count))
        rows, means, spreads, token_refs = (refs[at : at + count] for at in (next(cut) for _ in range(4)))
        rest = refs[4 * count :]
        adds, outs, sum_ref = rest[: len(addends)], rest[len(addends) : -1], rest[-1]
        weight = chosen(upper, lower)
        dots = jnp.zeros((1, wide), F32)
        totals = jnp.zeros((1, wide), F32)
        for k in range(count):
            value = contract_rows(rows[k][...], weight)
            scaled = value * gain_ref[...]
            if adds:
                scaled = scaled + adds[k][...].astype(F32)
            outs[k][...] = scaled.astype(BF)
            normed = (token_refs[k][...].astype(F32) - means[k][...]) * spreads[k][...]
            dots = dots + (value * normed).sum(axis=0, keepdims=True)
            totals = totals + value.sum(axis=0, keepdims=True)
        sum_ref[0:1, :] = dots
        sum_ref[1:2, :] = totals

    column = pl.BlockSpec((tile, wide), lambda i: (0, i))
    outs = kernel(
        body,
        D // wide,
        [
            *width_tile(halves, wide, width),
            pl.BlockSpec((1, wide), lambda i: (0, i)),
            *[resident(grads, (tile, width), (k, 0)) for k in row_blocks],
            *[resident(mean, (tile, 1), (k, 0)) for k in row_blocks],
            *[resident(spread, (tile, 1), (k, 0)) for k in row_blocks],
            *[pl.BlockSpec((tile, wide), lambda i, k=k: (k, i)) for k in row_blocks],
            *([column] * len(addends)),
        ],
        [column] * count + [pl.BlockSpec((8, wide), lambda i: (0, i))],
        [jax.ShapeDtypeStruct((tile, D), BF)] * count + [jax.ShapeDtypeStruct((8, D), F32)],
        "norm_grad",
    )(
        *halves,
        gain,
        *([grads] * count),
        *([mean] * count),
        *([spread] * count),
        *([tokens] * count),
        *addends,
    )
    return outs[:count], outs[count]


def rotary_tables(positions):
    lane = jnp.arange(LANES, dtype=jnp.int32)
    half_rot = ROT // 2
    exponent = -(2.0 * (lane % half_rot).astype(F32)) / ROT
    angles = positions[:, None] * (ROPE_BASE**exponent)[None, :]
    turning = (lane < ROT)[None, :]
    cos_table = jnp.where(turning, jnp.cos(angles), 1.0)
    sin_part = jnp.sin(angles)
    sin_table = jnp.where((lane < half_rot)[None, :], -sin_part, sin_part)
    return cos_table, jnp.where(turning, sin_table, 0.0)


def swapped_halves(values):
    half_rot = ROT // 2
    lane = lax.broadcasted_iota(jnp.int32, values.shape, 1)
    return jnp.where(
        lane < half_rot,
        pltpu.roll(values, LANES - half_rot, 1),
        pltpu.roll(values, half_rot, 1),
    )


def turned(values, cos_table, sin_table):
    first = values[:, :LANES]
    return jnp.concatenate(
        [first * cos_table + swapped_halves(first) * sin_table, values[:, LANES:]], axis=1
    )


def project_qkv(head, rows, halves, bias, cos_table, sin_table):
    total = rows.shape[0]
    tile = total // 2
    half = D // 2

    def body(rows_ref, *refs):
        weights, biases = refs[:6], refs[6:9]
        cos_ref, sin_ref, q_ref, near_key_ref, near_value_ref, own_ref = refs[9:]
        values = rows_ref[...]
        cos_here, sin_here = cos_ref[...], sin_ref[...]

        def product(kind):
            whole_run = slice(0, HEAD)
            return times(values, weights[2 * kind : 2 * kind + 2], whole_run) + biases[kind][...]

        query = turned(product(0), cos_here, sin_here)
        q_ref[...] = (query * (1.0 / math.sqrt(HEAD))).astype(BF)
        key = turned(product(1), cos_here, sin_here).astype(BF)
        value = product(2).astype(BF)

        @pl.when(pl.program_id(0) == 0)
        def _():
            near_key_ref[...] = key
            near_value_ref[...] = value

        @pl.when(pl.program_id(0) == 1)
        def _():
            own_ref[:, :HEAD] = key
            own_ref[:, HEAD:] = value

    columns = [kind * HEADS_HERE + head for kind in range(3)]
    both = jax.ShapeDtypeStruct((tile, 2 * HEAD), BF)
    one = jax.ShapeDtypeStruct((tile, HEAD), BF)
    kept_both = pl.BlockSpec((tile, 2 * HEAD), lambda i: (0, 0))
    kept = pl.BlockSpec((tile, HEAD), lambda i: (0, 0))
    return kernel(
        body,
        2,
        [
            by_rows(tile, D),
            *[resident(h, (half, HEAD), (0, c)) for c in columns for h in halves],
            *[resident(bias, (1, HEAD), (0, c)) for c in columns],
            by_rows(tile, LANES),
            by_rows(tile, LANES),
        ],
        [by_rows(tile, HEAD), kept, kept, kept_both],
        [jax.ShapeDtypeStruct((total, HEAD), BF), one, one, both],
        "qkv_rotary",
    )(rows, *[h for _ in columns for h in halves], *([bias] * 3), cos_table, sin_table)


def attention_body(
    q_ref,
    do_ref,
    kl_ref,
    vl_ref,
    kr_ref,
    vr_ref,
    kc_ref,
    vc_ref,
    cos_ref,
    sin_ref,
    cosl_ref,
    sinl_ref,
    cosr_ref,
    sinr_ref,
    qmark_ref,
    kmark_ref,
    o_ref,
    dq_ref,
    down_ref,
    dnear_ref,
    dfar_key_ref,
    dfar_value_ref,
    akl,
    avl,
    akr,
    avr,
):
    step = pl.program_id(0)
    last = pl.num_programs(0) - 1
    near = kl_ref.shape[0]

    @pl.when(step == 0)
    def _():
        for acc in (akl, avl, akr, avr):
            acc[...] = jnp.zeros_like(acc)

    query, grad = q_ref[...], do_ref[...]

    def work(own):
        scores = [contract_rows(query, kl_ref[...]), contract_rows(query, kr_ref[...])]
        if own:
            mine = contract_rows(query, kc_ref[...])
            at_row = lax.broadcasted_iota(jnp.int32, mine.shape, 0)
            at_col = lax.broadcasted_iota(jnp.int32, mine.shape, 1)
            scores.append(jnp.where(at_col <= at_row, mine, NEG_FILL))
        else:
            marks = kmark_ref[...]
            own_mark = qmark_ref[...]
            scores[0] = jnp.where(marks[:, :near] <= own_mark, scores[0], NEG_FILL)
            scores[1] = jnp.where(marks[:, near:] <= own_mark, scores[1], NEG_FILL)
        top = scores[0].max(axis=1, keepdims=True)
        for part in scores[1:]:
            top = jnp.maximum(top, part.max(axis=1, keepdims=True))
        probs = [jnp.exp(part - top) for part in scores]
        total = probs[0].sum(axis=1, keepdims=True)
        for part in probs[1:]:
            total = total + part.sum(axis=1, keepdims=True)
        share = 1.0 / total
        probs = [part * share for part in probs]
        low = [part.astype(BF) for part in probs]
        values = [vl_ref, vr_ref] + ([vc_ref] if own else [])
        keys = [kl_ref, kr_ref] + ([kc_ref] if own else [])
        mixed = matmul_nn(low[0], values[0][...])
        for part, ref in zip(low[1:], values[1:]):
            mixed = mixed + matmul_nn(part, ref[...])
        o_ref[...] = mixed.astype(BF)
        prob_grad = [contract_rows(grad, ref[...]) for ref in values]
        delta = (probs[0] * prob_grad[0]).sum(axis=1, keepdims=True)
        for part, grad_part in zip(probs[1:], prob_grad[1:]):
            delta = delta + (part * grad_part).sum(axis=1, keepdims=True)
        slopes = [
            (part * (grad_part - delta)).astype(BF) for part, grad_part in zip(probs, prob_grad)
        ]
        query_grad = matmul_nn(slopes[0], keys[0][...])
        for part, ref in zip(slopes[1:], keys[1:]):
            query_grad = query_grad + matmul_nn(part, ref[...])
        query_grad = query_grad * (1.0 / math.sqrt(HEAD))
        dq_ref[...] = turned(query_grad, cos_ref[...], -sin_ref[...]).astype(BF)
        akl[...] += contract_cols(slopes[0], query)
        akr[...] += contract_cols(slopes[1], query)
        avl[...] += contract_cols(low[0], grad)
        avr[...] += contract_cols(low[1], grad)
        if own:
            key_grad = contract_cols(slopes[2], query)
            down_ref[:, :HEAD] = turned(key_grad, cos_ref[...], -sin_ref[...]).astype(BF)
            down_ref[:, HEAD:] = contract_cols(low[2], grad).astype(BF)

    @pl.when(step < TP)
    def _():
        work(False)

    @pl.when(step >= TP)
    def _():
        work(True)

    @pl.when(step == last)
    def _():
        dnear_ref[:, :HEAD] = turned(akl[...], cosl_ref[...], -sinl_ref[...])
        dnear_ref[:, HEAD:] = avl[...]
        dfar_key_ref[...] = turned(akr[...], cosr_ref[...], -sinr_ref[...]).astype(BF)
        dfar_value_ref[...] = avr[...].astype(BF)


def attend(
    head, queries, grads, near, far, own, tables, near_tables, far_tables, query_mark, key_mark
):
    total = queries.shape[0]
    tile = total // (2 * TP)
    keys = near[0].shape[0]

    def row_tile(j):
        return j

    def cont_tile(j):
        return jnp.maximum(j - TP, 0)

    query_spec = pl.BlockSpec((tile, HEAD), lambda j: (row_tile(j), 0))
    row_spec = pl.BlockSpec((tile, HEAD), lambda j: (row_tile(j), head))
    out_spec = pl.BlockSpec((tile, HEAD), lambda j: (row_tile(j), 0))
    key_spec = pl.BlockSpec((keys, HEAD), lambda j: (0, 0))
    own_key = pl.BlockSpec((tile, HEAD), lambda j: (cont_tile(j), 0))
    own_value = pl.BlockSpec((tile, HEAD), lambda j: (cont_tile(j), 1))
    own_both = pl.BlockSpec((tile, 2 * HEAD), lambda j: (cont_tile(j), 0))
    both = pl.BlockSpec((keys, 2 * HEAD), lambda j: (0, 0))
    table_spec = pl.BlockSpec((tile, LANES), lambda j: (row_tile(j), 0))
    key_table = pl.BlockSpec((keys, LANES), lambda j: (0, 0))
    mark_spec = pl.BlockSpec((tile, 1), lambda j: (row_tile(j), 0))
    key_mark_spec = pl.BlockSpec((1, 2 * keys), lambda j: (0, 0))
    wide = jax.ShapeDtypeStruct((total, HEAD), BF)
    return pl.pallas_call(
        attention_body,
        grid=(2 * TP,),
        in_specs=[
            query_spec,
            row_spec,
            key_spec,
            key_spec,
            key_spec,
            key_spec,
            own_key,
            own_value,
            table_spec,
            table_spec,
            key_table,
            key_table,
            key_table,
            key_table,
            mark_spec,
            key_mark_spec,
        ],
        out_specs=[out_spec, out_spec, own_both, both, key_spec, key_spec],
        out_shape=[
            wide,
            wide,
            jax.ShapeDtypeStruct((keys, 2 * HEAD), BF),
            jax.ShapeDtypeStruct((keys, 2 * HEAD), F32),
            jax.ShapeDtypeStruct((keys, HEAD), BF),
            jax.ShapeDtypeStruct((keys, HEAD), BF),
        ],
        scratch_shapes=[pltpu.VMEM((keys, HEAD), F32)] * 4,
        compiler_params=pltpu.CompilerParams(vmem_limit_bytes=56 << 20),
        cost_estimate=cost("attention_both_ways"),
        name="attention_both_ways",
    )(
        queries,
        grads,
        *near,
        *far,
        own,
        own,
        *tables,
        *near_tables,
        *far_tables,
        query_mark,
        key_mark,
    )


def join_grads(query_grads, own_grads, near_grads, far_keys, far_values):
    total = query_grads[0].shape[0]
    tile = total // 4

    def body(*refs):
        out_ref, sum_ref = refs[-2:]
        dq, down, dnear, dfar_key, dfar_value = (
            refs[i * HEADS_HERE : (i + 1) * HEADS_HERE] for i in range(5)
        )
        step = pl.program_id(0)

        @pl.when(step == 0)
        def _():
            sum_ref[...] = jnp.zeros_like(sum_ref)

        for head in range(HEADS_HERE):
            at = head * HEAD
            key_at, value_at = slice(HCOLS + at, HCOLS + at + HEAD), slice(
                2 * HCOLS + at, 2 * HCOLS + at + HEAD
            )
            out_ref[:, at : at + HEAD] = dq[head][...]

            @pl.when(step < 2)
            def _(head=head, key_at=key_at, value_at=value_at):
                near = dnear[head][...]
                out_ref[:, key_at] = (near[:, :HEAD] + dfar_key[head][...].astype(F32)).astype(BF)
                out_ref[:, value_at] = (near[:, HEAD:] + dfar_value[head][...].astype(F32)).astype(BF)

            @pl.when(step >= 2)
            def _(head=head, key_at=key_at, value_at=value_at):
                out_ref[:, key_at] = down[head][:, :HEAD]
                out_ref[:, value_at] = down[head][:, HEAD:]

        sum_ref[...] += out_ref[...].astype(F32).sum(axis=0, keepdims=True)

    prompt_spec, cont_spec = part_specs(total // 2, tile, 2 * HEAD, 2)
    far_spec, _ = part_specs(total // 2, tile, HEAD, 2)
    return pl.pallas_call(
        body,
        grid=(4,),
        in_specs=[
            *([pl.BlockSpec((tile, HEAD), lambda i: (i, 0))] * HEADS_HERE),
            *([cont_spec] * HEADS_HERE),
            *([prompt_spec] * HEADS_HERE),
            *([far_spec] * (2 * HEADS_HERE)),
        ],
        out_specs=[
            pl.BlockSpec((tile, 3 * HCOLS), lambda i: (i, 0)),
            pl.BlockSpec((1, 3 * HCOLS), lambda i: (0, 0)),
        ],
        out_shape=[
            jax.ShapeDtypeStruct((total, 3 * HCOLS), BF),
            jax.ShapeDtypeStruct((1, 3 * HCOLS), F32),
        ],
        compiler_params=pltpu.CompilerParams(vmem_limit_bytes=56 << 20),
        cost_estimate=cost("join_grads"),
        name="join_grads",
    )(*query_grads, *own_grads, *near_grads, *far_keys, *far_values)


def square_plan(
    prompt,
    conts,
    assignment,
    offsets,
    ln1_gain,
    ln1_bias,
    ln2_gain,
    ln2_bias,
    qkv_weight,
    qkv_bias,
    out_weight,
    out_bias,
    up_weight,
    up_bias,
    down_weight,
    down_bias,
    prompt_cot,
    cont_cot,
):
    block, cont_rows = prompt.shape[1], conts.shape[2]
    shard = qkv_weight.shape[0]
    ff = up_weight.shape[1]
    ff_here = ff // TP
    half = D // 2
    grp_index, seq_index = lax.axis_index("grp"), lax.axis_index("seq")
    tp_rank, z_half = seq_index & 3, seq_index >> 2
    place_index = grp_index * 2 + z_half

    v = {}

    def wait(*names):
        v.update(zip(names, tie(*(v[name] for name in names))))

    branch_ids = jnp.arange(offsets.shape[1], dtype=jnp.int32)
    my_offset = jnp.sum(jnp.where(branch_ids == assignment[0, 0], offsets[0], 0)).reshape(1, 1)
    v["offsets"] = jnp.concatenate(
        [my_offset if bits == 0 else swap_seq(my_offset, bits) for bits in CONT_ORDER], axis=0
    )
    own1, v["side1"], far1 = split_columns([qkv_weight, out_weight.T], [3, 1], tp_rank)
    v["got1_y"] = swap_seq(v["side1"], 1)
    v["own_a"], v["own_b"] = reorder_runs([prompt[0], conts[0, 0]], place_index)
    own2, v["side2"], far2 = split_columns([up_weight], [1], tp_rank)
    wait("got1_y", "side2", "own_a", "own_b", "offsets")
    v["got1_z"] = swap_seq(onward(far1, v["got1_y"]), 2)
    v["got2_y"] = swap_seq(v["side2"], 1)
    own3, v["side3"], far3 = split_columns([down_weight.T], [1], tp_rank)
    qkv_bias_here = pick(qkv_bias.reshape(3, TP, HCOLS), tp_rank, 1).reshape(1, 3 * HCOLS)
    up_bias_here = pick(up_bias.reshape(TP, ff_here), tp_rank, 0)[None]
    vectors = jnp.stack([ln1_gain, ln1_bias, ln2_gain, ln2_bias, out_bias + down_bias])
    vectors = jnp.concatenate([vectors, jnp.zeros((3, D), F32)], axis=0)
    (vectors,) = reorder_runs([vectors], place_index)
    gain1, bias1, gain2, bias2, bias_out = (vectors[i : i + 1] for i in range(5))
    prompt_ranks = (tp_rank ^ jnp.array(PROMPT_ORDER, dtype=jnp.int32))[:, None]
    prompt_iota = jnp.arange(block, dtype=jnp.int32)[None, :]
    cont_iota = jnp.arange(cont_rows, dtype=jnp.int32)[None, :]
    near_mark = ((z_half * TP + prompt_ranks) * block + prompt_iota).reshape(-1)
    far_mark = (((z_half ^ 1) * TP + prompt_ranks) * block + prompt_iota).reshape(-1)
    cont_positions = (PROMPT + cont_iota + v["offsets"]).reshape(-1)
    v["mark"] = jnp.concatenate([near_mark, cont_positions]).astype(F32)
    query_mark = jnp.concatenate([near_mark, near_mark]).reshape(-1, 1)
    key_mark = jnp.concatenate([near_mark, far_mark]).reshape(1, -1)
    wait("got1_z", "got2_y", "own_a", "own_b", "side3")
    v["base1a"], v["base1b"] = stack_ranks(
        own1, v["got1_y"], v["got1_z"], (2 * HCOLS,) * 2, tp_rank
    )
    v["rows_az"] = swap_seq(v["own_a"], 2)
    v["rows_by"] = swap_seq(v["own_b"], 1)
    v["z1a"] = swap_seq(v["base1a"], 4)
    v["x1a"] = swap_grp(v["base1a"], 2)
    v["send2"] = onward(far2, v["got2_y"])
    v["cot_a"], v["cot_b"], cot_sum = reorder_runs(
        [prompt_cot[0], cont_cot[0, 0]], place_index, sums=True
    )
    wait("rows_az", "rows_by", "z1a", "x1a", "send2", "base1b", "own_a", "cot_a", "cot_b", "mark")
    v["z1b"] = swap_seq(v["base1b"], 4)
    v["got2_z"] = swap_seq(v["send2"], 2)
    v["rows_ay"] = swap_seq(v["own_a"], 1)
    v["x1b"] = swap_grp(v["base1b"], 2)
    v["zx1a"] = swap_grp(v["z1a"], 2)
    tables = rotary_tables(v["mark"])
    far_tables = rotary_tables(far_mark.astype(F32))
    v["tables0"], v["tables1"] = tables
    v["far0"], v["far1"] = far_tables
    wait(
        "z1b",
        "got2_z",
        "rows_ay",
        "x1b",
        "zx1a",
        "rows_az",
        "own_b",
        "tables0",
        "tables1",
        "far0",
        "far1",
    )
    tables, far_tables = (v["tables0"], v["tables1"]), (v["far0"], v["far1"])
    shared = (tables, tables, far_tables, query_mark, key_mark)
    v["base2a"], v["base2b"] = stack_ranks(
        own2, v["got2_y"], v["got2_z"], (ff_here // 2,) * 2, tp_rank
    )
    v["z2a"] = swap_seq(v["base2a"], 4)
    v["rows_azy"] = swap_seq(v["rows_az"], 1)
    v["rows_bz"] = swap_seq(v["own_b"], 2)
    v["zx1b"] = swap_grp(v["z1b"], 2)
    v["x2a"] = swap_grp(v["base2a"], 2)
    wait("z2a", "rows_azy", "rows_bz", "zx1b", "x2a", "side3", "rows_by", "base2b", "cot_b")
    v["got3_y"] = swap_seq(v["side3"], 1)
    v["rows_bzy"] = swap_seq(v["rows_by"], 2)
    v["z2b"] = swap_seq(v["base2b"], 4)
    v["x2b"] = swap_grp(v["base2b"], 2)
    v["zx2a"] = swap_grp(v["z2a"], 2)
    v["core1"] = beside(
        [(v["base1a"], v["base1b"]), (v["z1a"], v["z1b"]), (v["x1a"], v["x1b"]), (v["zx1a"], v["zx1b"])]
    )
    wait("got3_y", "rows_bzy", "z2b", "x2b", "zx2a", "core1", "cot_a", "cot_b")

    v["swapped1"] = swap_grp(v["core1"], 1)
    v["got3_z"] = swap_seq(onward(far3, v["got3_y"]), 2)
    v["cot_by"] = swap_seq(v["cot_b"], 1)
    v["zx2b"] = swap_grp(v["z2b"], 2)
    v["rows"], v["first_low"], v["second_low"], mean, spread = both_low_norms(
        [v[k] for k in ("own_a", "rows_az", "rows_ay", "rows_azy", "own_b", "rows_by", "rows_bz", "rows_bzy")],
        gain1,
        bias1,
        gain2,
        bias2,
    )
    wait("first_low", "second_low", "got3_z", "zx2b", "swapped1", "core1", "cot_a", "cot_by")
    v["cot_az"] = swap_seq(v["cot_a"], 2)
    v["cot_ay"] = swap_seq(v["cot_a"], 1)
    v["base3a"], v["base3b"] = stack_ranks(
        own3, v["got3_y"], v["got3_z"], (ff_here // 2,) * 2, tp_rank
    )
    v["z3a"] = swap_seq(v["base3a"], 4)
    v["x3a"] = swap_grp(v["base3a"], 2)
    v["core2"] = beside(
        [(v["base2a"], v["base2b"]), (v["z2a"], v["z2b"]), (v["x2a"], v["x2b"]), (v["zx2a"], v["zx2b"])]
    )
    v["swapped2"] = swap_grp(v["core2"], 1)
    weight1 = (v["core1"], v["swapped1"])
    v["query0"], v["key0"], v["value0"], own0 = project_qkv(
        0, v["first_low"], weight1, qkv_bias_here, *tables
    )
    wait("query0", "first_low")
    v["query1"], v["key1"], v["value1"], own1_kv = project_qkv(
        1, v["first_low"], weight1, qkv_bias_here, *tables
    )
    wait("query1", "second_low", "swapped2", "core2", "cot_az", "cot_ay", "cot_by", "cot_b", "z3a", "x3a", "base3b")
    v["cot_azy"] = swap_seq(v["cot_az"], 1)
    v["cots_b"] = stacked([v["cot_b"], v["cot_by"]])
    v["cots_far_b"] = swap_seq(v["cots_b"], 2)
    v["z3b"] = swap_seq(v["base3b"], 4)
    v["x3b"] = swap_grp(v["base3b"], 2)
    weight2 = (v["core2"], v["swapped2"])
    v["act_low"], v["slope"] = feed_forward_up(v["second_low"], weight2, up_bias_here)
    wait("act_low", "slope", "z3b", "x3b", "key0", "value0", "z3a", "cot_azy")
    v["far_key0"] = swap_seq(v["key0"], 4)
    v["zx3"] = swap_grp(stacked([v["z3a"], v["z3b"]]), 2)
    v["cots_a"] = stacked([v["cot_a"], v["cot_az"], v["cot_ay"], v["cot_azy"]])
    wait("cots_a", "cots_far_b", "cots_b")
    v["attn_grad"], v["cots"] = attention_grad(
        v["cots_a"], [v["cots_b"], v["cots_far_b"]], weight1, 3
    )
    wait("attn_grad", "cots", "act_low", "zx3", "far_key0", "value0")
    v["far_value0"] = swap_seq(v["value0"], 4)
    v["core3"] = beside(
        [(v["base3a"], v["base3b"]), (v["z3a"], v["z3b"]), (v["x3a"], v["x3b"])], v["zx3"]
    )
    v["swapped3"] = swap_grp(v["core3"], 1)
    v["down_away"] = weight_grad(v["cots"], [v["act_low"]])
    wait("down_away", "far_value0", "key1", "value1", "attn_grad", "swapped3", "core3")
    v["down_core"] = swap_grp(v["down_away"], 1)
    v["far_key1"] = swap_seq(v["key1"], 4)
    v["attn0"], dq0, down0, dnear0, v["dfar_key0"], v["dfar_value0"] = attend(
        0,
        v["query0"],
        v["attn_grad"],
        (v["key0"], v["value0"]),
        (v["far_key0"], v["far_value0"]),
        own0,
        *shared,
    )
    wait("attn0", "down_core", "cots", "act_low", "far_key1", "value1")
    v["far_value1"] = swap_seq(v["value1"], 4)
    v["down_mine"], v["down_send"] = weight_grad(v["cots"], [v["act_low"]], v["down_core"])
    wait("down_mine", "down_send", "cots", "slope", "core3", "swapped3")
    v["down_side"] = swap_grp(v["down_send"], 2)
    weight3 = (v["core3"], v["swapped3"])
    v["hidden_grad"], up_bias_term = feed_forward_back(v["cots"], weight3, v["slope"])
    wait("hidden_grad", "far_value1", "dfar_key0", "dfar_value0", "attn_grad")
    v["back_key0"] = swap_seq(v["dfar_key0"], 4)
    v["attn1"], dq1, down1, v["dnear1"], v["dfar_key1"], v["dfar_value1"] = attend(
        1,
        v["query1"],
        v["attn_grad"],
        (v["key1"], v["value1"]),
        (v["far_key1"], v["far_value1"]),
        own1_kv,
        *shared,
    )
    wait("attn1", "second_low", "hidden_grad", "back_key0", "dfar_value0", "down_side", "down_mine")
    v["back_value0"] = swap_seq(v["dfar_value0"], 4)
    v["up_away"] = weight_grad(v["second_low"], [v["hidden_grad"]])
    v["down_half_send"] = second_sum(v["down_mine"], v["down_side"])
    wait("up_away", "back_value0", "dfar_key1", "dfar_value1", "act_low", "down_half_send")
    v["up_core"] = swap_grp(v["up_away"], 1)
    v["back_key1"] = swap_seq(v["dfar_key1"], 4)
    branch = branch_outputs((v["attn0"], v["attn1"]), v["act_low"], weight1, 3, weight3)
    v["branch0"], v["branch1"], v["branch2"], v["branch3"] = branch
    wait(
        "branch0",
        "branch1",
        "branch2",
        "branch3",
        "up_core",
        "second_low",
        "hidden_grad",
        "back_key1",
        "dfar_value1",
    )
    v["got_a"] = swap_seq(v["branch1"], 1)
    v["got_b"] = swap_seq(v["branch3"], 2)
    v["back_value1"] = swap_seq(v["dfar_value1"], 4)
    v["up_mine"], v["up_send"] = weight_grad(v["second_low"], [v["hidden_grad"]], v["up_core"])
    wait("up_mine", "up_send", "cots", "hidden_grad", "dnear1", "back_value1", "down_half_send")
    v["up_side"] = swap_grp(v["up_send"], 2)
    v["down_half"] = swap_seq(v["down_half_send"], 4)
    second_parts, second_sums = norm_grad(
        v["hidden_grad"], weight2, gain2, v["rows"], mean, spread, (0, 1, 2, 3)
    )
    v["second0"], second1, second2, second3 = second_parts
    wait("second0", "back_key1", "dnear1", "got_a", "got_b", "branch0", "branch2")
    v["branch_a_far"] = second_sum(v["branch0"], v["got_a"])
    v["branch_b_far"] = second_sum(v["branch2"], v["got_b"])
    v["qkv_grad"], qkv_bias_term = join_grads(
        (dq0, dq1),
        (down0, down1),
        (dnear0, v["dnear1"]),
        (v["back_key0"], v["back_key1"]),
        (v["back_value0"], v["back_value1"]),
    )
    wait("qkv_grad", "first_low", "branch_a_far", "branch_b_far")
    v["qkv_away"] = weight_grad(v["first_low"], [v["qkv_grad"]])
    wait("qkv_away", "cots", "up_side", "up_mine", "down_half", "branch_a_far", "branch_b_far")
    v["qkv_core"] = swap_grp(v["qkv_away"], 1)
    v["branch_far_b"] = swap_seq(v["branch_b_far"], 1)
    down_own, v["down_side2"], v["down_far"] = split_rows(
        [(v["down_mine"], v["down_side"], v["down_half"])], tp_rank, 2
    )
    v["down_z"] = swap_seq(v["down_side2"], 2)
    v["up_half_send"] = second_sum(v["up_mine"], v["up_side"])
    v["out_away"] = weight_grad(v["cots"], [v["attn0"], v["attn1"]])
    wait(
        "out_away",
        "qkv_core",
        "first_low",
        "qkv_grad",
        "up_half_send",
        "down_z",
        "down_far",
        "branch_a_far",
    )
    v["out_core"] = swap_grp(v["out_away"], 1)
    v["up_half"] = swap_seq(v["up_half_send"], 4)
    v["down_y"] = swap_seq(onward(v["down_far"], v["down_z"]), 1)
    v["branch_far_a"] = swap_seq(v["branch_a_far"], 2)
    v["qkv_mine"], v["qkv_send"] = weight_grad(v["first_low"], [v["qkv_grad"]], v["qkv_core"])
    wait("qkv_mine", "qkv_send", "qkv_grad", "out_core")
    v["qkv_side"] = swap_grp(v["qkv_send"], 2)
    (v["entry1"], v["entry3"]), v["far_sums"] = norm_grad(
        v["qkv_grad"], weight1, gain1, v["rows"], mean, spread, (1, 3), (second1, second3)
    )
    wait("entry1", "entry3", "far_sums", "cots", "qkv_grad", "out_core", "down_y", "branch_far_a", "branch_far_b")
    v["entry_got_a"] = swap_seq(v["entry1"], 1)
    v["entry_got_b"] = swap_seq(v["entry3"], 2)
    v["out_mine"], v["out_send"] = weight_grad(
        v["cots"], [v["attn0"], v["attn1"]], v["out_core"]
    )
    wait("out_mine", "out_send", "qkv_grad", "second0", "up_half", "qkv_side", "qkv_mine")
    v["out_side"] = swap_grp(v["out_send"], 2)
    v["qkv_half_send"] = second_sum(v["qkv_mine"], v["qkv_side"])
    v["qkv_half"] = swap_seq(v["qkv_half_send"], 4)
    (v["entry0"], v["entry2"]), v["near_sums"] = norm_grad(
        v["qkv_grad"], weight1, gain1, v["rows"], mean, spread, (0, 2), (v["second0"], second2)
    )
    wait("near_sums", "branch_far_a", "branch0", "out_side", "out_mine", "up_half", "qkv_half_send")

    rank_ids = jnp.arange(TP, dtype=jnp.int32)
    first_sums = v["far_sums"] + v["near_sums"]
    wide_sums = jnp.concatenate(
        [first_sums[:2], second_sums[:2], cot_sum, jnp.zeros((3, D), F32)], axis=0
    )
    wide_sums = restore_runs(wide_sums, place_index)
    qkv_bias_term = qkv_bias_term.reshape(3, 1, HCOLS)
    v["sums"] = jnp.concatenate(
        [
            wide_sums[:5].reshape(-1),
            jnp.where((rank_ids == tp_rank)[None, :, None], qkv_bias_term, 0.0).reshape(-1),
            jnp.where((rank_ids == tp_rank)[:, None], up_bias_term, 0.0).reshape(-1),
        ]
    ).reshape(-1, LANES)
    v["sums_got"] = swap_grp(v["sums"], 1)
    v["out_half_send"] = second_sum(v["out_mine"], v["out_side"])
    v["out_half"] = swap_seq(v["out_half_send"], 4)
    up_own, v["up_side2"], v["up_far"] = split_rows(
        [(v["up_mine"], v["up_side"], v["up_half"])], tp_rank, 2
    )
    wait("entry_got_a", "entry_got_b", "entry0", "entry2", "sums", "sums_got", "up_side2", "out_half_send")
    v["sums"] = v["sums"] + v["sums_got"]
    v["sums_got"] = swap_grp(v["sums"], 2)
    v["entry_b_far"] = second_sum(v["entry2"], v["entry_got_b"])
    v["entry_far_b"] = swap_seq(v["entry_b_far"], 1)
    v["entry_a_far"] = second_sum(v["entry0"], v["entry_got_a"])
    v["entry_far_a"] = swap_seq(v["entry_a_far"], 2)
    wait("entry_a_far", "entry_b_far", "branch0", "sums", "sums_got", "up_side2")
    v["up_z"] = swap_seq(v["up_side2"], 2)
    v["sums"] = v["sums"] + v["sums_got"]
    v["sums_got"] = swap_seq(v["sums"], 1)
    v["layer_a"], v["layer_b"] = finish_outputs(
        (
            (v["branch0"], v["got_a"], v["branch_far_a"]),
            (v["branch2"], v["got_b"], v["branch_far_b"]),
        ),
        (v["own_a"], v["own_b"]),
        bias_out,
        place_index,
    )
    (v["down_grad"],) = join_columns(
        down_own, v["down_z"], v["down_y"], [(1, ff_here)], tp_rank, 2
    )
    wait("qkv_half", "out_half", "layer_a", "down_grad", "sums", "sums_got")
    v["sums"] = v["sums"] + v["sums_got"]
    v["sums_got"] = swap_seq(v["sums"], 2)
    late_own, late_side, late_far = split_rows(
        [
            (v["qkv_mine"], v["qkv_side"], v["qkv_half"]),
            (v["out_mine"], v["out_side"], v["out_half"]),
        ],
        tp_rank,
    )
    v["late_y"] = swap_seq(late_side, 1)
    wait("entry_far_a", "entry_far_b", "late_y", "sums", "sums_got", "up_z")
    v["late_z"] = swap_seq(onward(late_far, v["late_y"]), 2)
    v["up_y"] = swap_seq(onward(v["up_far"], v["up_z"]), 1)
    v["sums"] = v["sums"] + v["sums_got"]
    v["sums_got"] = swap_seq(v["sums"], 4)
    v["grad_a"], grad_b = finish_grads(
        (
            (v["entry0"], v["entry_got_a"], v["entry_far_a"]),
            (v["entry2"], v["entry_got_b"], v["entry_far_b"]),
        ),
        (v["own_a"], v["own_b"]),
        (v["cot_a"], v["cot_b"]),
        place_index,
    )
    grad_a, down_grad = v["grad_a"], v["down_grad"]
    wait("grad_a", "up_y", "late_z", "sums_got")
    (up_weight_grad,) = join_columns(up_own, v["up_z"], v["up_y"], [(1, ff_here)], tp_rank, 2)
    qkv_weight_grad, out_grad = join_columns(
        late_own, v["late_y"], v["late_z"], [(3, HCOLS), (1, HCOLS)], tp_rank
    )
    down_weight_grad, out_weight_grad = down_grad.T, out_grad.T
    sums = (v["sums"] + v["sums_got"]).reshape(-1)
    cuts = np.cumsum([D, D, D, D, D, 3 * D])
    gain_one, shift_one, gain_two, shift_two, out_sum, qkv_sum, up_sum = jnp.split(sums, cuts)

    return (
        v["layer_a"][None],
        v["layer_b"][None, None],
        grad_a[None],
        grad_b[None, None],
        gain_one,
        shift_one,
        gain_two,
        shift_two,
        qkv_weight_grad,
        qkv_sum,
        out_weight_grad,
        out_sum,
        up_weight_grad,
        up_sum,
        down_weight_grad,
        out_sum,
    )


def solution(mesh):
    in_specs = (
        P("grp", "seq", None),
        P("grp", "seq", None, None),
        P("grp", "seq"),
        P("grp", None),
        P(),
        P(),
        P(),
        P(),
        P(("grp", "seq"), None),
        P(),
        P(None, ("grp", "seq")),
        P(),
        P(("grp", "seq"), None),
        P(),
        P(None, ("grp", "seq")),
        P(),
        P("grp", "seq", None),
        P("grp", "seq", None, None),
    )
    out_specs = (
        P("grp", "seq", None),
        P("grp", "seq", None, None),
        P("grp", "seq", None),
        P("grp", "seq", None, None),
        P(),
        P(),
        P(),
        P(),
        P(("grp", "seq"), None),
        P(),
        P(None, ("grp", "seq")),
        P(),
        P(("grp", "seq"), None),
        P(),
        P(None, ("grp", "seq")),
        P(),
    )
    plan = square_plan if (mesh.shape["grp"], mesh.shape["seq"]) == (4, 8) else local
    return jax.shard_map(plan, mesh=mesh, in_specs=in_specs, out_specs=out_specs, check_vma=False)
```

```python
from functools import partial
import math

import jax
import jax.numpy as jnp
import numpy as np
from jax import lax
from jax.experimental import pallas as pl
from jax.experimental.pallas import tpu as pltpu
from jax.sharding import PartitionSpec as P

D = 2048
HEADS = 8
HEAD = 256
ROT = 64
PROMPT = 2048


EPSILON = 1e-05
NEG_FILL = -1e30
ROPE_BASE = 10000.0


def layer_norm(values, ln_gain, ln_shift):
    center = values - jnp.mean(values, axis=-1, keepdims=True)
    normed = center * lax.rsqrt(jnp.mean(center * center, axis=-1, keepdims=True) + EPSILON)
    return normed * ln_gain + ln_shift


def both_norms(values, gain_one, shift_one, gain_two, shift_two):
    return (layer_norm(values, gain_one, shift_one), layer_norm(values, gain_two, shift_two))


def rotate(head_data, positions, sign_flip):
    half_rot = ROT // 2
    inv_freq = ROPE_BASE ** (-(2.0 * jnp.arange(half_rot, dtype=jnp.float32)) / ROT)
    angles = positions[:, None] * inv_freq[None, :]
    cos_table = jnp.cos(angles)[:, None, :]
    sin_table = sign_flip * jnp.sin(angles)[:, None, :]
    first_half = head_data[..., :half_rot]
    second = head_data[..., half_rot:ROT]
    return jnp.concatenate(
        [
            first_half * cos_table - second * sin_table,
            second * cos_table + first_half * sin_table,
            head_data[..., ROT:],
        ],
        axis=-1,
    )


def contract_rows(left, right):
    return lax.dot_general(
        left, right, (((1,), (1,)), ((), ())), preferred_element_type=jnp.float32
    )


def contract_cols(left, right):
    return lax.dot_general(
        left, right, (((0,), (0,)), ((), ())), preferred_element_type=jnp.float32
    )


def local(
    prompt,
    conts,
    assignment,
    offsets,
    ln1_gain,
    ln1_bias,
    ln2_gain,
    ln2_bias,
    qkv_weight,
    qkv_bias,
    out_weight,
    out_bias,
    up_weight,
    up_bias,
    down_weight,
    down_bias,
    prompt_cot,
    cont_cot,
):
    prompt_rows = prompt.shape[1]
    cont_rows = conts.shape[2]
    row_total = prompt_rows + cont_rows
    score_scale = 1.0 / math.sqrt(HEAD)
    shard_index = lax.axis_index("seq")
    tokens = jnp.concatenate([prompt[0], conts[0, 0]], axis=0).astype(jnp.float32)
    branch_ids = jnp.arange(offsets.shape[1], dtype=jnp.int32)
    my_offset = jnp.sum(jnp.where(branch_ids == assignment[0, 0], offsets[0], 0))
    prompt_mark = shard_index * prompt_rows + jnp.arange(prompt_rows, dtype=jnp.int32)
    cont_mark = PROMPT + jnp.arange(cont_rows, dtype=jnp.int32)
    query_mark = jnp.concatenate([prompt_mark, cont_mark])
    positions = jnp.concatenate([prompt_mark, cont_mark + my_offset]).astype(jnp.float32)
    (first_norm, second_norm), norm_pullback = jax.vjp(
        both_norms, tokens, ln1_gain, ln1_bias, ln2_gain, ln2_bias
    )
    first_low = first_norm.astype(jnp.bfloat16)
    second_low = second_norm.astype(jnp.bfloat16)
    qkv_full, up_full = (
        lax.all_gather(qkv_weight, ("grp", "seq"), axis=0, tiled=True),
        lax.all_gather(up_weight, ("grp", "seq"), axis=0, tiled=True),
    )
    qkv_acc = jnp.dot(first_low, qkv_full, preferred_element_type=jnp.float32)
    up_acc = jnp.dot(second_low, up_full, preferred_element_type=jnp.float32)
    split_qkv = (qkv_acc + qkv_bias).reshape(row_total, 3, HEADS, HEAD)
    queries = rotate(split_qkv[:, 0], positions, 1.0).astype(jnp.bfloat16)
    keys_rot = rotate(split_qkv[:, 1], positions, 1.0).astype(jnp.bfloat16)
    values_low = split_qkv[:, 2].astype(jnp.bfloat16)
    hidden_pre = up_acc + up_bias
    activated, gelu_pullback = jax.vjp(partial(jax.nn.gelu, approximate=False), hidden_pre)
    act_low = activated.astype(jnp.bfloat16)

    def score_block(key_block, key_mark):
        raw_scores = (
            jnp.einsum("qhd,khd->hqk", queries, key_block, preferred_element_type=jnp.float32)
            * score_scale
        )
        allowed = key_mark[None, :] <= query_mark[:, None]
        return (raw_scores, allowed)

    def absorb(soft_state, key_block, value_block, key_mark):
        run_max, run_sum, run_acc = soft_state
        raw_scores, allowed = score_block(key_block, key_mark)
        masked = jnp.where(allowed[None], raw_scores, NEG_FILL)
        new_max = jnp.maximum(run_max, jnp.max(masked, axis=-1))
        exp_scores = jnp.where(allowed[None], jnp.exp(masked - new_max[..., None]), 0.0)
        factor = jnp.exp(run_max - new_max)
        mixed_heads = jnp.einsum(
            "hqk,khd->qhd",
            exp_scores.astype(jnp.bfloat16),
            value_block,
            preferred_element_type=jnp.float32,
        )
        return (
            new_max,
            run_sum * factor + jnp.sum(exp_scores, axis=-1),
            run_acc * factor.T[:, :, None] + mixed_heads,
        )

    cont_keys = keys_rot[prompt_rows:]
    cont_values = values_low[prompt_rows:]
    start_state = (
        jnp.full((HEADS, row_total), NEG_FILL, jnp.float32),
        jnp.zeros((HEADS, row_total), jnp.float32),
        jnp.zeros((row_total, HEADS, HEAD), jnp.float32),
    )
    start_state = absorb(start_state, cont_keys, cont_values, cont_mark)
    prompt_keys_send = keys_rot[:prompt_rows].reshape(prompt_rows, D)
    prompt_values_send = values_low[:prompt_rows].reshape(prompt_rows, D)
    key_piece = lax.all_gather(prompt_keys_send, "seq", axis=0, tiled=True)
    value_piece = lax.all_gather(prompt_values_send, "seq", axis=0, tiled=True)
    piece_width = key_piece.shape[0]
    key_mark = jnp.arange(piece_width, dtype=jnp.int32)
    run_max, run_sum, run_acc = absorb(
        start_state,
        key_piece.reshape(piece_width, HEADS, HEAD),
        value_piece.reshape(piece_width, HEADS, HEAD),
        key_mark,
    )
    attention = run_acc / run_sum.T[:, :, None]
    log_total = run_max + jnp.log(run_sum)
    attention_low = attention.reshape(row_total, D).astype(jnp.bfloat16)
    out_full, down_full = (
        lax.all_gather(out_weight, ("grp", "seq"), axis=1, tiled=True),
        lax.all_gather(down_weight, ("grp", "seq"), axis=1, tiled=True),
    )
    branch_sum = jnp.dot(attention_low, out_full, preferred_element_type=jnp.float32) + jnp.dot(
        act_low, down_full, preferred_element_type=jnp.float32
    )
    layer_out = tokens + branch_sum + out_bias + down_bias
    grad_out = jnp.concatenate([prompt_cot[0], cont_cot[0, 0]], axis=0)
    grad_f32 = grad_out.astype(jnp.float32)
    bias_out_term = jnp.sum(grad_f32, axis=0)
    out_again, down_again = (
        lax.all_gather(out_weight, ("grp", "seq"), axis=1, tiled=True),
        lax.all_gather(down_weight, ("grp", "seq"), axis=1, tiled=True),
    )
    attn_grad = contract_rows(grad_out, out_again)
    act_grad = contract_rows(grad_out, down_again)
    attn_grad_low = attn_grad.astype(jnp.bfloat16)
    (hidden_grad,) = gelu_pullback(act_grad)
    hidden_grad_low = hidden_grad.astype(jnp.bfloat16)
    up_bias_term = jnp.sum(hidden_grad_low.astype(jnp.float32), axis=0)
    grad_heads = attn_grad_low.reshape(row_total, HEADS, HEAD)
    row_delta = jnp.sum(grad_heads.astype(jnp.float32) * attention, axis=-1).T

    def back_block(key_block, value_block, key_mark):
        raw_scores, allowed = score_block(key_block, key_mark)
        probabilities = jnp.exp(
            jnp.where(allowed[None], raw_scores - log_total[..., None], NEG_FILL)
        )
        prob_grad = jnp.einsum(
            "qhd,khd->hqk", grad_heads, value_block, preferred_element_type=jnp.float32
        )
        score_grad = (probabilities * (prob_grad - row_delta[..., None])).astype(jnp.bfloat16)
        query_term = (
            jnp.einsum("hqk,khd->qhd", score_grad, key_block, preferred_element_type=jnp.float32)
            * score_scale
        )
        key_term = (
            jnp.einsum("hqk,qhd->khd", score_grad, queries, preferred_element_type=jnp.float32)
            * score_scale
        )
        value_term = jnp.einsum(
            "hqk,qhd->khd",
            probabilities.astype(jnp.bfloat16),
            grad_heads,
            preferred_element_type=jnp.float32,
        )
        return (query_term, key_term, value_term)

    query_local, key_local, value_local = back_block(cont_keys, cont_values, cont_mark)
    gathered_keys, gathered_values = (
        lax.all_gather(prompt_keys_send, "seq", axis=0, tiled=True),
        lax.all_gather(prompt_values_send, "seq", axis=0, tiled=True),
    )
    key_block_size = min(512, PROMPT)
    block_count = PROMPT // key_block_size

    def scan_step(query_total, inputs):
        key_block, value_block, block_start = inputs
        key_mark = block_start + jnp.arange(key_block_size, dtype=jnp.int32)
        query_term, key_term, value_term = back_block(
            key_block.reshape(key_block_size, HEADS, HEAD),
            value_block.reshape(key_block_size, HEADS, HEAD),
            key_mark,
        )
        return (
            query_total + query_term,
            (key_term.reshape(key_block_size, D), value_term.reshape(key_block_size, D)),
        )

    query_grad, (key_terms, value_terms) = lax.scan(
        scan_step,
        query_local,
        (
            gathered_keys.reshape(block_count, key_block_size, D),
            gathered_values.reshape(block_count, key_block_size, D),
            jnp.arange(block_count, dtype=jnp.int32) * key_block_size,
        ),
    )
    key_prompt_grad, value_prompt_grad = (
        lax.psum_scatter(
            key_terms.reshape(PROMPT, D).astype(jnp.bfloat16),
            "seq",
            scatter_dimension=0,
            tiled=True,
        ).astype(jnp.float32),
        lax.psum_scatter(
            value_terms.reshape(PROMPT, D).astype(jnp.bfloat16),
            "seq",
            scatter_dimension=0,
            tiled=True,
        ).astype(jnp.float32),
    )
    key_grad = jnp.concatenate([key_prompt_grad, key_local.reshape(cont_rows, D)], axis=0).reshape(
        row_total, HEADS, HEAD
    )
    value_grad = jnp.concatenate(
        [value_prompt_grad, value_local.reshape(cont_rows, D)], axis=0
    ).reshape(row_total, HEADS, HEAD)
    qkv_grad = (
        jnp.stack(
            [rotate(query_grad, positions, -1.0), rotate(key_grad, positions, -1.0), value_grad],
            axis=1,
        )
        .reshape(row_total, 3 * D)
        .astype(jnp.bfloat16)
    )
    qkv_bias_term = jnp.sum(qkv_grad.astype(jnp.float32), axis=0)
    qkv_again, up_again = (
        lax.all_gather(qkv_weight, ("grp", "seq"), axis=0, tiled=True),
        lax.all_gather(up_weight, ("grp", "seq"), axis=0, tiled=True),
    )
    first_grad = contract_rows(qkv_grad, qkv_again)
    second_grad = contract_rows(hidden_grad_low, up_again)
    token_grad, gain_one, shift_one, gain_two, shift_two = norm_pullback((first_grad, second_grad))
    token_grad = token_grad + grad_f32
    small_sums = lax.psum(
        (gain_one, shift_one, gain_two, shift_two, qkv_bias_term, bias_out_term, up_bias_term),
        ("grp", "seq"),
    )
    out_sources = jnp.concatenate([attention_low, act_low], axis=1)
    in_group = lax.psum_scatter(
        jnp.concatenate(
            [contract_cols(first_low, qkv_grad), contract_cols(second_low, hidden_grad_low)], axis=1
        ).astype(jnp.bfloat16),
        "grp",
        scatter_dimension=0,
        tiled=True,
    )
    in_share = lax.psum_scatter(in_group, "seq", scatter_dimension=0, tiled=True).astype(
        jnp.float32
    )
    out_group = lax.psum_scatter(
        contract_cols(grad_out, out_sources).astype(jnp.bfloat16),
        "grp",
        scatter_dimension=0,
        tiled=True,
    )
    out_share = lax.psum_scatter(out_group, "seq", scatter_dimension=0, tiled=True).astype(
        jnp.float32
    )
    qkv_weight_grad = in_share[:, : 3 * D]
    up_weight_grad = in_share[:, 3 * D :]
    out_weight_grad = out_share[:, :D].T
    down_weight_grad = out_share[:, D:].T
    prompt_result = layer_out[:prompt_rows][None]
    cont_result = layer_out[prompt_rows:][None, None]
    prompt_grad = token_grad[:prompt_rows][None]
    cont_grad = token_grad[prompt_rows:][None, None]
    return (
        prompt_result,
        cont_result,
        prompt_grad,
        cont_grad,
        small_sums[0],
        small_sums[1],
        small_sums[2],
        small_sums[3],
        qkv_weight_grad,
        small_sums[4],
        out_weight_grad,
        small_sums[5],
        up_weight_grad,
        small_sums[6],
        down_weight_grad,
        small_sums[5],
    )


PROMPT_ORDER = (0, 2, 1, 3)
CONT_ORDER = (0, 1, 2, 3)
WIDTH_ORDER = (0, 1, 4, 5, 2, 3, 6, 7)
TP = 4
HEADS_HERE = HEADS // TP
HCOLS = HEADS_HERE * HEAD
LANES = 128
COST_UNIT = 1.0e6
COSTS = {
    "norms": 15,
    "qkv_rotary": 12,
    "feed_forward_up": 30,
    "attention_grad": 11,
    "weight_grad": 14,
    "attention_both_ways": 28,
    "feed_forward_back": 25,
    "branch_outputs": 34,
    "norm_grad": 25,
    "join_grads": 8,
    "finish_outputs": 7,
    "finish_grads": 9,
}
BF = jnp.bfloat16
F32 = jnp.float32


def swap_grp(array, bits):
    return lax.ppermute(array, "grp", [(i, i ^ bits) for i in range(4)])


def swap_seq(array, bits):
    return lax.ppermute(array, "seq", [(i, i ^ bits) for i in range(8)])


def matmul_nn(left, right):
    return jnp.dot(left, right, preferred_element_type=F32)


def pick(array, index, axis):
    return lax.dynamic_index_in_dim(array, index, axis, keepdims=False)


def place(buffer, piece, index):
    return lax.dynamic_update_index_in_dim(buffer, piece, index, 0)


def tie(*arrays):
    return lax.optimization_barrier(arrays)


def whole(shape):
    return pl.BlockSpec(shape, lambda i, rank: (0,) * len(shape))


def cost(name):
    flops = int(COSTS.get(name, 2) * COST_UNIT)
    return pl.CostEstimate(flops=flops, transcendentals=0, bytes_accessed=0)


def ranked_call(body, rank, ins, shapes, name, blocks=None):
    return pl.pallas_call(
        body,
        grid_spec=pltpu.PrefetchScalarGridSpec(
            num_scalar_prefetch=1,
            grid=(1,),
            in_specs=[whole(shape) for shape in blocks or [a.shape for a in ins]],
            out_specs=[whole(s.shape) for s in shapes],
        ),
        out_shape=shapes,
        compiler_params=pltpu.CompilerParams(vmem_limit_bytes=56 << 20),
        cost_estimate=cost(name),
        name=name,
    )(rank.reshape(1), *ins)


def split_columns(shards, groups, tp_rank):
    rows = shards[0].shape[0]
    widths = [shard.shape[1] // (TP * count) for shard, count in zip(shards, groups)]
    cols = sum(width * count for width, count in zip(widths, groups))

    def body(rank_ref, *refs):
        ins, (own_ref, side_ref, far_ref) = refs[: len(shards)], refs[len(shards) :]
        at = 0
        for ref, count, width in zip(ins, groups, widths):
            for part in range(count):
                for bits in range(TP):
                    start = pl.multiple_of((part * TP + (rank_ref[0] ^ bits)) * width, width)
                    run = ref[:, pl.ds(start, width)]
                    here = slice(at, at + width)
                    if bits == 0:
                        own_ref[:, here] = run
                    elif bits == 2:
                        far_ref[:, here] = run
                    else:
                        side_ref[bits // 2, :, here] = run
                at += width

    shapes = [
        jax.ShapeDtypeStruct((rows, cols), BF),
        jax.ShapeDtypeStruct((2, rows, cols), BF),
        jax.ShapeDtypeStruct((rows, cols), BF),
    ]
    return ranked_call(body, tp_rank, list(shards), shapes, "split_columns")


def stack_ranks(own, over_y, over_z, cuts, tp_rank, uncut=False):
    rows, cols = own.shape
    runs = [slice(sum(cuts[:i]), sum(cuts[: i + 1])) for i in range(len(cuts))]
    if uncut:
        runs.append(slice(0, cols))

    def body(rank_ref, own_ref, y_ref, z_ref, *outs):
        for out, here in zip(outs, runs):
            pieces = (own_ref[:, here], y_ref[0, :, here], z_ref[0, :, here], z_ref[1, :, here])
            for bits, piece in enumerate(pieces):
                start = pl.multiple_of((rank_ref[0] ^ bits) * rows, rows)
                out[pl.ds(start, rows), :] = piece

    shapes = [jax.ShapeDtypeStruct((TP * rows, run.stop - run.start), BF) for run in runs]
    return ranked_call(body, tp_rank, [own, over_y, over_z], shapes, "stack_ranks")


def split_rows(groups, tp_rank, first=1):
    rows = groups[0][2][0].shape[0] // TP
    cols = sum(terms[0].shape[1] for terms in groups)
    flat = [array for kept, got_x, got_z in groups for array in (kept, got_x, *got_z)]

    def body(rank_ref, *refs):
        ins, (own_ref, side_ref, far_ref) = list(refs[: len(flat)]), refs[len(flat) :]
        at = 0
        for _, _, got_z in groups:
            kept, got_x = ins.pop(0), ins.pop(0)
            inside = 0
            for _ in got_z:
                run_ref = ins.pop(0)
                width = run_ref.shape[1]
                here, cut = slice(at, at + width), slice(inside, inside + width)
                at, inside = at + width, inside + width
                for bits in range(TP):
                    lines = pl.ds(pl.multiple_of((rank_ref[0] ^ bits) * rows, rows), rows)
                    total = kept[lines, cut].astype(F32) + got_x[lines, cut].astype(F32)
                    run = (total + run_ref[lines, :].astype(F32)).astype(BF)
                    if bits == 0:
                        own_ref[:, here] = run
                    elif bits == 3 - first:
                        far_ref[:, here] = run
                    else:
                        side_ref[int(bits == 3), :, here] = run

    shapes = [
        jax.ShapeDtypeStruct((rows, cols), BF),
        jax.ShapeDtypeStruct((2, rows, cols), BF),
        jax.ShapeDtypeStruct((rows, cols), BF),
    ]
    blocks = [(TP * rows, term.shape[1]) for term in flat]
    return ranked_call(body, tp_rank, flat, shapes, "split_rows", blocks)


def join_columns(own, got_first, got_second, parts, tp_rank, first=1):
    rows = own.shape[0]

    def body(rank_ref, own_ref, first_ref, second_ref, *outs):
        at = 0
        for out, (count, width) in zip(outs, parts):
            for part in range(count):
                here = slice(at, at + width)
                pieces = {
                    0: own_ref[:, here],
                    first: first_ref[0, :, here],
                    3 - first: second_ref[0, :, here],
                    3: second_ref[1, :, here],
                }
                for bits, piece in pieces.items():
                    start = pl.multiple_of((part * TP + (rank_ref[0] ^ bits)) * width, width)
                    out[:, pl.ds(start, width)] = piece.astype(F32)
                at += width

    shapes = [jax.ShapeDtypeStruct((rows, TP * count * width), F32) for count, width in parts]
    return ranked_call(body, tp_rank, [own, got_first, got_second], shapes, "join_columns")


def reorder_runs(arrays, place_index, sums=False):
    run = D // 8
    shapes = [jax.ShapeDtypeStruct(a.shape, a.dtype) for a in arrays]
    if sums:
        shapes.append(jax.ShapeDtypeStruct((1, D), F32))

    def body(index_ref, *refs):
        ins, outs = refs[: len(arrays)], refs[len(arrays) :]
        for j, bits in enumerate(WIDTH_ORDER):
            start = pl.multiple_of((index_ref[0] ^ bits) * run, run)
            here = slice(j * run, (j + 1) * run)
            for in_ref, out_ref in zip(ins, outs):
                out_ref[:, here] = in_ref[:, pl.ds(start, run)]
        if sums:
            total = outs[0][...].astype(F32).sum(axis=0, keepdims=True)
            for out_ref in outs[1 : len(arrays)]:
                total = total + out_ref[...].astype(F32).sum(axis=0, keepdims=True)
            outs[-1][...] = total

    return ranked_call(body, place_index, list(arrays), shapes, "reorder_runs")


def restore_runs(array, place_index):
    run = D // 8

    def body(index_ref, in_ref, out_ref):
        for j, bits in enumerate(WIDTH_ORDER):
            start = pl.multiple_of((index_ref[0] ^ bits) * run, run)
            out_ref[:, pl.ds(start, run)] = in_ref[:, j * run : (j + 1) * run]

    shapes = [jax.ShapeDtypeStruct(array.shape, array.dtype)]
    return ranked_call(body, place_index, [array], shapes, "restore_runs")[0]


def finish_outputs(parts, tokens, bias, place_index):
    run = D // 8
    rows = tokens[0].shape[0]
    flat = [term for terms in parts for term in terms]

    def body(index_ref, *refs):
        ins, outs = refs[: len(flat) + len(tokens) + 1], refs[len(flat) + len(tokens) + 1 :]
        bias_ref = ins[-1]
        for i, out_ref in enumerate(outs):
            own, got, got_far = ins[3 * i : 3 * i + 3]
            token_ref = ins[len(flat) + i]
            value = token_ref[...].astype(F32) + own[...].astype(F32) + got[...].astype(F32)
            value = value + got_far[...].astype(F32) + bias_ref[...]
            for j, bits in enumerate(WIDTH_ORDER):
                start = pl.multiple_of((index_ref[0] ^ bits) * run, run)
                out_ref[:, pl.ds(start, run)] = value[:, j * run : (j + 1) * run]

    shapes = [jax.ShapeDtypeStruct((rows, D), F32) for _ in tokens]
    blocks = [(rows, D)] * (len(flat) + len(tokens)) + [bias.shape]
    return ranked_call(
        body, place_index, flat + list(tokens) + [bias], shapes, "finish_outputs", blocks
    )


def finish_grads(parts, tokens, cots, place_index):
    run = D // 8
    rows = tokens[0].shape[0]
    count = len(tokens)
    flat = [term for terms in parts for term in terms]

    def body(index_ref, *refs):
        ins, outs = refs[: 5 * count], refs[5 * count :]
        for i, out_ref in enumerate(outs):
            own, got, got_far = ins[3 * i : 3 * i + 3]
            token = ins[3 * count + i][...].astype(F32)
            cot = ins[4 * count + i][...].astype(F32)
            entry = own[...].astype(F32) + got[...].astype(F32) + got_far[...].astype(F32)
            center = token - jnp.mean(token, axis=1, keepdims=True)
            spread = lax.rsqrt(jnp.mean(center * center, axis=1, keepdims=True) + EPSILON)
            normed = center * spread
            entry_mean = jnp.mean(entry, axis=1, keepdims=True)
            entry_dot = jnp.mean(entry * normed, axis=1, keepdims=True)
            value = cot + spread * (entry - entry_mean - normed * entry_dot)
            for j, bits in enumerate(WIDTH_ORDER):
                start = pl.multiple_of((index_ref[0] ^ bits) * run, run)
                out_ref[:, pl.ds(start, run)] = value[:, j * run : (j + 1) * run]

    shapes = [jax.ShapeDtypeStruct((rows, D), F32) for _ in tokens]
    return ranked_call(
        body,
        place_index,
        flat + list(tokens) + list(cots),
        shapes,
        "finish_grads",
        [(rows, D)] * (5 * count),
    )


def part_specs(rows, tile, width, parts):
    per_part = rows // tile

    def spec(k):
        return pl.BlockSpec((tile, width), lambda i: (jnp.clip(i - k * per_part, 0, per_part - 1), 0))

    return [spec(k) for k in range(parts)]


def norms_body(gain1, bias1, gain2, bias2, *refs):
    *parts, rows_ref, first_ref, second_ref, mean_ref, spread_ref = refs
    step = pl.program_id(0)
    per_part = pl.num_programs(0) // len(parts)
    for k, part in enumerate(parts):

        @pl.when(step // per_part == k)
        def _(part=part):
            rows_ref[...] = part[...]
            values = part[...].astype(F32)
            mean = jnp.mean(values, axis=1, keepdims=True)
            center = values - mean
            spread = lax.rsqrt(jnp.mean(center * center, axis=1, keepdims=True) + EPSILON)
            normed = center * spread
            first_ref[...] = (normed * gain1[...] + bias1[...]).astype(BF)
            second_ref[...] = (normed * gain2[...] + bias2[...]).astype(BF)
            mean_ref[...] = mean
            spread_ref[...] = spread


def both_low_norms(parts, gain1, bias1, gain2, bias2):
    tile = parts[0].shape[0]
    total = tile * len(parts)
    vector = pl.BlockSpec((1, D), lambda i: (0, 0))
    wide = pl.BlockSpec((tile, D), lambda i: (i, 0))
    thin = pl.BlockSpec((tile, 1), lambda i: (i, 0))
    return pl.pallas_call(
        norms_body,
        grid=(total // tile,),
        in_specs=[vector] * 4 + part_specs(tile, tile, D, len(parts)),
        out_specs=[wide, wide, wide, thin, thin],
        out_shape=[
            jax.ShapeDtypeStruct((total, D), BF),
            jax.ShapeDtypeStruct((total, D), BF),
            jax.ShapeDtypeStruct((total, D), BF),
            jax.ShapeDtypeStruct((total, 1), F32),
            jax.ShapeDtypeStruct((total, 1), F32),
        ],
        compiler_params=pltpu.CompilerParams(vmem_limit_bytes=56 << 20),
        cost_estimate=cost("norms"),
        name="norms",
    )(gain1, bias1, gain2, bias2, *parts)


def resident(array, block=None, at=(0, 0)):
    return pl.BlockSpec(block or array.shape, lambda i: at, pipeline_mode=pl.Buffered(1))


def times(rows, halves, columns):
    upper, lower = halves
    half = upper.shape[0]
    return matmul_nn(rows[:, :half], upper[:, columns]) + matmul_nn(rows[:, half:], lower[:, columns])


def runs_of(width, run):
    return [slice(at, at + run) for at in range(0, width, run)]


def kernel(body, steps, in_specs, out_specs, out_shape, name, scratch=()):
    return pl.pallas_call(
        body,
        grid=(steps,),
        in_specs=in_specs,
        out_specs=out_specs,
        out_shape=out_shape,
        scratch_shapes=scratch,
        compiler_params=pltpu.CompilerParams(vmem_limit_bytes=58 << 20),
        cost_estimate=cost(name),
        name=name,
    )


def stacked(parts):
    tile, width = parts[0].shape

    def body(*refs):
        *ins, out_ref = refs
        for k, part in enumerate(ins):

            @pl.when(pl.program_id(0) == k)
            def _(part=part):
                out_ref[...] = part[...]

    return kernel(
        body,
        len(parts),
        part_specs(tile, tile, width, len(parts)),
        by_rows(tile, width),
        jax.ShapeDtypeStruct((tile * len(parts), width), BF),
        "stacked",
    )(*parts)


def beside(entries):
    tile, width = entries[0][0].shape
    specs, arrays = [], []
    for entry in entries:
        if isinstance(entry, tuple):
            specs += [pl.BlockSpec((tile, width), lambda i: (0, 0))] * 2
            arrays += entry
        elif entry.shape[0] == tile:
            specs += [pl.BlockSpec((tile, width), lambda i, h=h: (0, h)) for h in range(2)]
            arrays += [entry, entry]
        else:
            specs += [pl.BlockSpec((tile, width), lambda i, h=h: (h, 0)) for h in range(2)]
            arrays += [entry, entry]

    def body(*refs):
        *ins, out_ref = refs
        for k in range(len(entries)):

            @pl.when(pl.program_id(0) == k)
            def _(k=k):
                out_ref[:, :width] = ins[2 * k][...]
                out_ref[:, width:] = ins[2 * k + 1][...]

    return kernel(
        body,
        len(entries),
        specs,
        by_rows(tile, 2 * width),
        jax.ShapeDtypeStruct((tile * len(entries), 2 * width), BF),
        "beside",
    )(*arrays)


def second_sum(left, right, part=None):
    rows, width = left.shape[0] // 2, left.shape[1] // (1 if part is None else 2)
    wide = 1024 if width % 1024 == 0 else 512
    first = (part or 0) * (width // wide)

    def body(left_ref, right_ref, out_ref):
        out_ref[...] = (left_ref[...].astype(F32) + right_ref[...].astype(F32)).astype(BF)

    lower = pl.BlockSpec((rows, wide), lambda i: (1, first + i))
    at = right.shape[0] // rows - 1
    return kernel(
        body,
        width // wide,
        [lower, pl.BlockSpec((rows, wide), lambda i: (at, first + i))],
        pl.BlockSpec((rows, wide), lambda i: (0, i)),
        jax.ShapeDtypeStruct((rows, width), BF),
        "second_sum",
    )(left, right)


def onward(far, over_y):
    rows, width = far.shape

    def body(far_ref, y_ref, out_ref):
        out_ref[0] = far_ref[...]
        out_ref[1] = y_ref[0]

    return kernel(
        body,
        1,
        [
            pl.BlockSpec((rows, width), lambda i: (0, 0)),
            pl.BlockSpec((1, rows, width), lambda i: (1, 0, 0)),
        ],
        pl.BlockSpec((2, rows, width), lambda i: (0, 0, 0)),
        jax.ShapeDtypeStruct((2, rows, width), BF),
        "onward",
    )(far, over_y)


def by_rows(tile, width, tiles=lambda i: i):
    return pl.BlockSpec((tile, width), lambda i: (tiles(i), 0))


def attention_grad(parts, halves, column_block):
    tile = parts[0].shape[0]
    total = tile * len(parts)

    def body(upper, lower, *refs):
        *ins, out_ref, rows_ref, held = refs
        for k, part in enumerate(ins):

            @pl.when(pl.program_id(0) == k)
            def _(part=part):
                held[...] = part[...]

        rows = held[...]
        rows_ref[...] = rows
        out_ref[...] = times(rows, (upper, lower), slice(0, HCOLS)).astype(BF)

    weight_spec = resident(halves[0], (D // 2, HCOLS), (0, column_block))
    return kernel(
        body,
        len(parts),
        [weight_spec, weight_spec] + part_specs(tile, tile, D, len(parts)),
        [by_rows(tile, HCOLS), by_rows(tile, D)],
        [jax.ShapeDtypeStruct((total, HCOLS), BF), jax.ShapeDtypeStruct((total, D), BF)],
        "attention_grad",
        [pltpu.VMEM((tile, D), BF)],
    )(*halves, *parts)


def feed_forward_up(rows, halves, bias):
    total, ff_here = rows.shape[0], bias.shape[1]
    tile, wide = total // 4, ff_here // 2
    half = D // 2

    def body(rows_ref, upper, lower, bias_ref, act_ref, slope_ref):
        values = rows_ref[...]
        for run in runs_of(wide, 256):
            pre = times(values, (upper, lower), run) + bias_ref[:, run]
            cdf = 0.5 * (1.0 + lax.erf(pre * math.sqrt(0.5)))
            density = jnp.exp(-0.5 * pre * pre) * (1.0 / math.sqrt(2.0 * math.pi))
            act_ref[:, run] = (pre * cdf).astype(BF)
            slope_ref[:, run] = (cdf + pre * density).astype(BF)

    weight_spec = pl.BlockSpec((half, wide), lambda i: (0, i // 4))
    out_spec = pl.BlockSpec((tile, wide), lambda i: (i % 4, i // 4))
    return kernel(
        body,
        8,
        [
            by_rows(tile, D, lambda i: i % 4),
            weight_spec,
            weight_spec,
            pl.BlockSpec((1, wide), lambda i: (0, i // 4)),
        ],
        [out_spec] * 2,
        [jax.ShapeDtypeStruct((total, ff_here), BF)] * 2,
        "feed_forward_up",
    )(rows, *halves, bias)


def feed_forward_back(cots, halves, slope):
    total, ff_here = slope.shape
    tile, wide = total // 2, ff_here // 2
    half = D // 2

    def body(cot_ref, upper, lower, slope_ref, out_ref, sum_ref):
        @pl.when(pl.program_id(0) % 2 == 0)
        def _():
            sum_ref[...] = jnp.zeros_like(sum_ref)

        values = cot_ref[...]
        for run in runs_of(wide, 512):
            grad = times(values, (upper, lower), run) * slope_ref[:, run].astype(F32)
            low = grad.astype(BF)
            out_ref[:, run] = low
            sum_ref[:, run] += low.astype(F32).sum(axis=0, keepdims=True)

    weight_spec = pl.BlockSpec((half, wide), lambda i: (0, i // 2))
    both = pl.BlockSpec((tile, wide), lambda i: (i % 2, i // 2))
    return kernel(
        body,
        4,
        [by_rows(tile, D, lambda i: i % 2), weight_spec, weight_spec, both],
        [both, pl.BlockSpec((1, wide), lambda i: (0, i // 2))],
        [jax.ShapeDtypeStruct((total, ff_here), BF), jax.ShapeDtypeStruct((1, ff_here), F32)],
        "feed_forward_back",
    )(cots, *halves, slope)


def weight_grad(left, rights, core_got=None):
    total = left.shape[0]
    width = sum(right.shape[1] for right in rights)
    half = D // 2
    wide = 512
    steps = width // wide if len(rights) == 1 else 1
    keep = core_got is not None

    def body(left_ref, *refs):
        ins, rest = refs[: len(rights)], refs[len(rights) :]
        values = left_ref[...]
        at = 0
        for right in ins:
            here = slice(at, at + right.shape[1])
            at += right.shape[1]
            product = contract_cols(values, right[...])
            if keep:
                got_ref, mine_ref, side_ref = rest
                product = product + got_ref[:, here].astype(F32)
                mine_ref[:, here] = product[: half // 2].astype(BF)
                side_ref[:, here] = product[half // 2 :].astype(BF)
            else:
                rest[0][:, here] = product.astype(BF)

    if len(rights) == 1:
        right_specs = [pl.BlockSpec((total, wide), lambda i: (0, i))]
    else:
        right_specs = [resident(right) for right in rights]
    rows = half // 2 if keep else half
    count = 2 if keep else 1
    outs = kernel(
        body,
        steps,
        [resident(left, (total, half), (0, 0 if keep else 1))]
        + right_specs
        + ([pl.BlockSpec((half, wide), lambda i: (0, i))] if keep else []),
        [pl.BlockSpec((rows, wide), lambda i: (0, i))] * count,
        [jax.ShapeDtypeStruct((rows, width), BF)] * count,
        "weight_grad",
    )(left, *rights, *([core_got] if keep else []))
    return outs if keep else outs[0]


def width_tile(halves, height, columns, block=0):
    per_half = halves[0].shape[0] // height
    return [
        pl.BlockSpec((height, columns), lambda i: (jnp.minimum(i, per_half - 1), block)),
        pl.BlockSpec((height, columns), lambda i: (jnp.maximum(i - per_half, 0), block)),
    ]


def chosen(upper, lower):
    in_upper = pl.program_id(0) < pl.num_programs(0) // 2
    return jnp.where(in_upper, upper[...], lower[...])


def quarter_rows(tile):
    return [tile, tile // 2, tile // 2] * 2


def quarter_specs(tile, wide):
    return [pl.BlockSpec((rows, wide), lambda i: (0, i)) for rows in quarter_rows(tile)]


def put_quarter(outs, k, value):
    at = 3 * (k // 2)
    if k % 2 == 0:
        outs[at][...] = value
    else:
        half = value.shape[0] // 2
        outs[at + 1][...] = value[:half]
        outs[at + 2][...] = value[half:]


def branch_outputs(heads_low, act_low, attn_halves, column_block, down_halves):
    total, ff_here = act_low.shape
    tile = total // 4
    wide = 512

    def body(*refs):
        heads = [refs[h * 4 : h * 4 + 4] for h in range(HEADS_HERE)]
        refs = refs[4 * HEADS_HERE :]
        acts, attn, down, outs = refs[:4], refs[4:6], refs[6:8], refs[8:]
        attn_tile, down_tile = chosen(*attn), chosen(*down)
        for k in range(4):
            value = contract_rows(acts[k][...], down_tile)
            for head in range(HEADS_HERE):
                cut = slice(head * HEAD, (head + 1) * HEAD)
                value = value + contract_rows(heads[head][k][...], attn_tile[:, cut])
            put_quarter(outs, k, value.astype(BF))

    return kernel(
        body,
        D // wide,
        [resident(h, (tile, HEAD), (k, 0)) for h in heads_low for k in range(4)]
        + [resident(act_low, (tile, ff_here), (k, 0)) for k in range(4)]
        + width_tile(attn_halves, wide, HCOLS, column_block)
        + width_tile(down_halves, wide, ff_here),
        quarter_specs(tile, wide),
        [jax.ShapeDtypeStruct((rows, D), BF) for rows in quarter_rows(tile)],
        "branch_outputs",
    )(*[h for h in heads_low for _ in range(4)], *([act_low] * 4), *attn_halves, *down_halves)


def norm_grad(grads, halves, gain, tokens, mean, spread, row_blocks, addends=(), cut=False):
    tile = grads.shape[0] // 4
    count = len(row_blocks)
    width = grads.shape[1]
    wide = 512

    def body(upper, lower, gain_ref, *refs):
        rows, means, spreads, token_refs = (refs[i * count : (i + 1) * count] for i in range(4))
        rest = refs[4 * count :]
        adds, outs, sum_ref = rest[: len(addends)], rest[len(addends) : -1], rest[-1]
        weight = chosen(upper, lower)
        dots = jnp.zeros((1, wide), F32)
        totals = jnp.zeros((1, wide), F32)
        for k in range(count):
            value = contract_rows(rows[k][...], weight)
            scaled = value * gain_ref[...]
            if adds:
                scaled = scaled + adds[k][...].astype(F32)
            low = scaled.astype(BF)
            if cut:
                outs[2 * k][...] = low[: tile // 2]
                outs[2 * k + 1][...] = low[tile // 2 :]
            else:
                outs[k][...] = low
            normed = (token_refs[k][...].astype(F32) - means[k][...]) * spreads[k][...]
            dots = dots + (value * normed).sum(axis=0, keepdims=True)
            totals = totals + value.sum(axis=0, keepdims=True)
        sum_ref[0:1, :] = dots
        sum_ref[1:2, :] = totals

    column = pl.BlockSpec((tile, wide), lambda i: (0, i))
    out_rows = [tile // 2] * (2 * count) if cut else [tile] * count
    outs = kernel(
        body,
        D // wide,
        [
            *width_tile(halves, wide, width),
            pl.BlockSpec((1, wide), lambda i: (0, i)),
            *[resident(grads, (tile, width), (k, 0)) for k in row_blocks],
            *[resident(mean, (tile, 1), (k, 0)) for k in row_blocks],
            *[resident(spread, (tile, 1), (k, 0)) for k in row_blocks],
            *[pl.BlockSpec((tile, wide), lambda i, k=k: (k, i)) for k in row_blocks],
            *([column] * len(addends)),
        ],
        [pl.BlockSpec((rows, wide), lambda i: (0, i)) for rows in out_rows]
        + [pl.BlockSpec((8, wide), lambda i: (0, i))],
        [jax.ShapeDtypeStruct((rows, D), BF) for rows in out_rows]
        + [jax.ShapeDtypeStruct((8, D), F32)],
        "norm_grad",
    )(
        *halves,
        gain,
        *([grads] * count),
        *([mean] * count),
        *([spread] * count),
        *([tokens] * count),
        *addends,
    )
    return outs[:-1], outs[-1]


def rotary_tables(positions):
    lane = jnp.arange(LANES, dtype=jnp.int32)
    half_rot = ROT // 2
    exponent = -(2.0 * (lane % half_rot).astype(F32)) / ROT
    angles = positions[:, None] * (ROPE_BASE**exponent)[None, :]
    turning = (lane < ROT)[None, :]
    cos_table = jnp.where(turning, jnp.cos(angles), 1.0)
    sin_part = jnp.sin(angles)
    sin_table = jnp.where((lane < half_rot)[None, :], -sin_part, sin_part)
    return cos_table, jnp.where(turning, sin_table, 0.0)


def swapped_halves(values):
    half_rot = ROT // 2
    lane = lax.broadcasted_iota(jnp.int32, values.shape, 1)
    return jnp.where(
        lane < half_rot,
        pltpu.roll(values, LANES - half_rot, 1),
        pltpu.roll(values, half_rot, 1),
    )


def turned(values, cos_table, sin_table):
    first = values[:, :LANES]
    return jnp.concatenate(
        [first * cos_table + swapped_halves(first) * sin_table, values[:, LANES:]], axis=1
    )


def project_qkv(head, rows, halves, bias, cos_table, sin_table):
    total = rows.shape[0]
    tile = total // 2
    half = D // 2

    def body(rows_ref, *refs):
        weights, biases = refs[:6], refs[6:9]
        cos_ref, sin_ref, q_ref, near_key_ref, near_value_ref, own_ref = refs[9:]
        values = rows_ref[...]
        cos_here, sin_here = cos_ref[...], sin_ref[...]

        def product(kind):
            whole_run = slice(0, HEAD)
            return times(values, weights[2 * kind : 2 * kind + 2], whole_run) + biases[kind][...]

        query = turned(product(0), cos_here, sin_here)
        q_ref[...] = (query * (1.0 / math.sqrt(HEAD))).astype(BF)
        key = turned(product(1), cos_here, sin_here).astype(BF)
        value = product(2).astype(BF)

        @pl.when(pl.program_id(0) == 0)
        def _():
            near_key_ref[...] = key
            near_value_ref[...] = value

        @pl.when(pl.program_id(0) == 1)
        def _():
            own_ref[:, :HEAD] = key
            own_ref[:, HEAD:] = value

    columns = [kind * HEADS_HERE + head for kind in range(3)]
    both = jax.ShapeDtypeStruct((tile, 2 * HEAD), BF)
    one = jax.ShapeDtypeStruct((tile, HEAD), BF)
    kept_both = pl.BlockSpec((tile, 2 * HEAD), lambda i: (0, 0))
    kept = pl.BlockSpec((tile, HEAD), lambda i: (0, 0))
    return kernel(
        body,
        2,
        [
            by_rows(tile, D),
            *[resident(h, (half, HEAD), (0, c)) for c in columns for h in halves],
            *[resident(bias, (1, HEAD), (0, c)) for c in columns],
            by_rows(tile, LANES),
            by_rows(tile, LANES),
        ],
        [by_rows(tile, HEAD), kept, kept, kept_both],
        [jax.ShapeDtypeStruct((total, HEAD), BF), one, one, both],
        "qkv_rotary",
    )(rows, *[h for _ in columns for h in halves], *([bias] * 3), cos_table, sin_table)


def attention_body(
    q_ref,
    do_ref,
    kl_ref,
    vl_ref,
    kr_ref,
    vr_ref,
    kc_ref,
    vc_ref,
    cos_ref,
    sin_ref,
    cosl_ref,
    sinl_ref,
    cosr_ref,
    sinr_ref,
    qmark_ref,
    kmark_ref,
    o_ref,
    dq_ref,
    down_ref,
    dnear_ref,
    dfar_key_ref,
    dfar_value_ref,
    akl,
    avl,
    akr,
    avr,
):
    step = pl.program_id(0)
    last = pl.num_programs(0) - 1
    near = kl_ref.shape[0]

    @pl.when(step == 0)
    def _():
        for acc in (akl, avl, akr, avr):
            acc[...] = jnp.zeros_like(acc)

    query, grad = q_ref[...], do_ref[...]

    def work(own):
        scores = [contract_rows(query, kl_ref[...]), contract_rows(query, kr_ref[...])]
        if own:
            mine = contract_rows(query, kc_ref[...])
            at_row = lax.broadcasted_iota(jnp.int32, mine.shape, 0)
            at_col = lax.broadcasted_iota(jnp.int32, mine.shape, 1)
            scores.append(jnp.where(at_col <= at_row, mine, NEG_FILL))
        else:
            marks = kmark_ref[...]
            own_mark = qmark_ref[...]
            scores[0] = jnp.where(marks[:, :near] <= own_mark, scores[0], NEG_FILL)
            scores[1] = jnp.where(marks[:, near:] <= own_mark, scores[1], NEG_FILL)
        top = scores[0].max(axis=1, keepdims=True)
        for part in scores[1:]:
            top = jnp.maximum(top, part.max(axis=1, keepdims=True))
        probs = [jnp.exp(part - top) for part in scores]
        total = probs[0].sum(axis=1, keepdims=True)
        for part in probs[1:]:
            total = total + part.sum(axis=1, keepdims=True)
        share = 1.0 / total
        probs = [part * share for part in probs]
        low = [part.astype(BF) for part in probs]
        values = [vl_ref, vr_ref] + ([vc_ref] if own else [])
        keys = [kl_ref, kr_ref] + ([kc_ref] if own else [])
        mixed = matmul_nn(low[0], values[0][...])
        for part, ref in zip(low[1:], values[1:]):
            mixed = mixed + matmul_nn(part, ref[...])
        o_ref[...] = mixed.astype(BF)
        prob_grad = [contract_rows(grad, ref[...]) for ref in values]
        delta = (probs[0] * prob_grad[0]).sum(axis=1, keepdims=True)
        for part, grad_part in zip(probs[1:], prob_grad[1:]):
            delta = delta + (part * grad_part).sum(axis=1, keepdims=True)
        slopes = [
            (part * (grad_part - delta)).astype(BF) for part, grad_part in zip(probs, prob_grad)
        ]
        query_grad = matmul_nn(slopes[0], keys[0][...])
        for part, ref in zip(slopes[1:], keys[1:]):
            query_grad = query_grad + matmul_nn(part, ref[...])
        query_grad = query_grad * (1.0 / math.sqrt(HEAD))
        dq_ref[...] = turned(query_grad, cos_ref[...], -sin_ref[...]).astype(BF)
        akl[...] += contract_cols(slopes[0], query)
        akr[...] += contract_cols(slopes[1], query)
        avl[...] += contract_cols(low[0], grad)
        avr[...] += contract_cols(low[1], grad)
        if own:
            key_grad = contract_cols(slopes[2], query)
            down_ref[:, :HEAD] = turned(key_grad, cos_ref[...], -sin_ref[...]).astype(BF)
            down_ref[:, HEAD:] = contract_cols(low[2], grad).astype(BF)

    @pl.when(step < TP)
    def _():
        work(False)

    @pl.when(step >= TP)
    def _():
        work(True)

    @pl.when(step == last)
    def _():
        dnear_ref[:, :HEAD] = turned(akl[...], cosl_ref[...], -sinl_ref[...])
        dnear_ref[:, HEAD:] = avl[...]
        dfar_key_ref[...] = turned(akr[...], cosr_ref[...], -sinr_ref[...]).astype(BF)
        dfar_value_ref[...] = avr[...].astype(BF)


def attend(
    head, queries, grads, near, far, own, tables, near_tables, far_tables, query_mark, key_mark
):
    total = queries.shape[0]
    tile = total // (2 * TP)
    keys = near[0].shape[0]

    def row_tile(j):
        return j

    def cont_tile(j):
        return jnp.maximum(j - TP, 0)

    query_spec = pl.BlockSpec((tile, HEAD), lambda j: (row_tile(j), 0))
    row_spec = pl.BlockSpec((tile, HEAD), lambda j: (row_tile(j), head))
    out_spec = pl.BlockSpec((tile, HEAD), lambda j: (row_tile(j), 0))
    key_spec = pl.BlockSpec((keys, HEAD), lambda j: (0, 0))
    own_key = pl.BlockSpec((tile, HEAD), lambda j: (cont_tile(j), 0))
    own_value = pl.BlockSpec((tile, HEAD), lambda j: (cont_tile(j), 1))
    own_both = pl.BlockSpec((tile, 2 * HEAD), lambda j: (cont_tile(j), 0))
    both = pl.BlockSpec((keys, 2 * HEAD), lambda j: (0, 0))
    table_spec = pl.BlockSpec((tile, LANES), lambda j: (row_tile(j), 0))
    key_table = pl.BlockSpec((keys, LANES), lambda j: (0, 0))
    mark_spec = pl.BlockSpec((tile, 1), lambda j: (row_tile(j), 0))
    key_mark_spec = pl.BlockSpec((1, 2 * keys), lambda j: (0, 0))
    wide = jax.ShapeDtypeStruct((total, HEAD), BF)
    return pl.pallas_call(
        attention_body,
        grid=(2 * TP,),
        in_specs=[
            query_spec,
            row_spec,
            key_spec,
            key_spec,
            key_spec,
            key_spec,
            own_key,
            own_value,
            table_spec,
            table_spec,
            key_table,
            key_table,
            key_table,
            key_table,
            mark_spec,
            key_mark_spec,
        ],
        out_specs=[out_spec, out_spec, own_both, both, key_spec, key_spec],
        out_shape=[
            wide,
            wide,
            jax.ShapeDtypeStruct((keys, 2 * HEAD), BF),
            jax.ShapeDtypeStruct((keys, 2 * HEAD), F32),
            jax.ShapeDtypeStruct((keys, HEAD), BF),
            jax.ShapeDtypeStruct((keys, HEAD), BF),
        ],
        scratch_shapes=[pltpu.VMEM((keys, HEAD), F32)] * 4,
        compiler_params=pltpu.CompilerParams(vmem_limit_bytes=56 << 20),
        cost_estimate=cost("attention_both_ways"),
        name="attention_both_ways",
    )(
        queries,
        grads,
        *near,
        *far,
        own,
        own,
        *tables,
        *near_tables,
        *far_tables,
        query_mark,
        key_mark,
    )


def join_grads(query_grads, own_grads, near_grads, far_keys, far_values):
    total = query_grads[0].shape[0]
    tile = total // 4

    def body(*refs):
        out_ref, sum_ref = refs[-2:]
        dq, down, dnear, dfar_key, dfar_value = (
            refs[i * HEADS_HERE : (i + 1) * HEADS_HERE] for i in range(5)
        )
        step = pl.program_id(0)

        @pl.when(step == 0)
        def _():
            sum_ref[...] = jnp.zeros_like(sum_ref)

        for head in range(HEADS_HERE):
            at = head * HEAD
            key_at, value_at = slice(HCOLS + at, HCOLS + at + HEAD), slice(
                2 * HCOLS + at, 2 * HCOLS + at + HEAD
            )
            out_ref[:, at : at + HEAD] = dq[head][...]

            @pl.when(step < 2)
            def _(head=head, key_at=key_at, value_at=value_at):
                near = dnear[head][...]
                out_ref[:, key_at] = (near[:, :HEAD] + dfar_key[head][...].astype(F32)).astype(BF)
                out_ref[:, value_at] = (near[:, HEAD:] + dfar_value[head][...].astype(F32)).astype(BF)

            @pl.when(step >= 2)
            def _(head=head, key_at=key_at, value_at=value_at):
                out_ref[:, key_at] = down[head][:, :HEAD]
                out_ref[:, value_at] = down[head][:, HEAD:]

        sum_ref[...] += out_ref[...].astype(F32).sum(axis=0, keepdims=True)

    prompt_spec, cont_spec = part_specs(total // 2, tile, 2 * HEAD, 2)
    far_spec, _ = part_specs(total // 2, tile, HEAD, 2)
    return pl.pallas_call(
        body,
        grid=(4,),
        in_specs=[
            *([pl.BlockSpec((tile, HEAD), lambda i: (i, 0))] * HEADS_HERE),
            *([cont_spec] * HEADS_HERE),
            *([prompt_spec] * HEADS_HERE),
            *([far_spec] * (2 * HEADS_HERE)),
        ],
        out_specs=[
            pl.BlockSpec((tile, 3 * HCOLS), lambda i: (i, 0)),
            pl.BlockSpec((1, 3 * HCOLS), lambda i: (0, 0)),
        ],
        out_shape=[
            jax.ShapeDtypeStruct((total, 3 * HCOLS), BF),
            jax.ShapeDtypeStruct((1, 3 * HCOLS), F32),
        ],
        compiler_params=pltpu.CompilerParams(vmem_limit_bytes=56 << 20),
        cost_estimate=cost("join_grads"),
        name="join_grads",
    )(*query_grads, *own_grads, *near_grads, *far_keys, *far_values)


class Values:
    pass


def square_plan(
    prompt,
    conts,
    assignment,
    offsets,
    ln1_gain,
    ln1_bias,
    ln2_gain,
    ln2_bias,
    qkv_weight,
    qkv_bias,
    out_weight,
    out_bias,
    up_weight,
    up_bias,
    down_weight,
    down_bias,
    prompt_cot,
    cont_cot,
):
    block, cont_rows = prompt.shape[1], conts.shape[2]
    shard = qkv_weight.shape[0]
    ff = up_weight.shape[1]
    ff_here = ff // TP
    half = D // 2
    grp_index, seq_index = lax.axis_index("grp"), lax.axis_index("seq")
    tp_rank, z_half = seq_index & 3, seq_index >> 2
    place_index = grp_index * 2 + z_half

    v = Values()


    branch_ids = jnp.arange(offsets.shape[1], dtype=jnp.int32)
    my_offset = jnp.sum(jnp.where(branch_ids == assignment[0, 0], offsets[0], 0)).reshape(1, 1)
    v.offsets = jnp.concatenate(
        [my_offset if bits == 0 else swap_seq(my_offset, bits) for bits in CONT_ORDER], axis=0
    )
    own1, v.side1, far1 = split_columns([qkv_weight, out_weight.T], [3, 1], tp_rank)
    v.got1_y = swap_seq(v.side1, 1)
    v.own_a, v.own_b = reorder_runs([prompt[0], conts[0, 0]], place_index)
    own2, v.side2, far2 = split_columns([up_weight], [1], tp_rank)
    (
        v.got1_y, v.side2, v.own_a, v.own_b, v.offsets,
    ) = tie(
        v.got1_y, v.side2, v.own_a, v.own_b, v.offsets,
    )
    v.got1_z = swap_seq(onward(far1, v.got1_y), 2)
    v.got2_y = swap_seq(v.side2, 1)
    own3, v.side3, far3 = split_columns([down_weight.T], [1], tp_rank)
    qkv_bias_here = pick(qkv_bias.reshape(3, TP, HCOLS), tp_rank, 1).reshape(1, 3 * HCOLS)
    up_bias_here = pick(up_bias.reshape(TP, ff_here), tp_rank, 0)[None]
    vectors = jnp.stack([ln1_gain, ln1_bias, ln2_gain, ln2_bias, out_bias + down_bias])
    vectors = jnp.concatenate([vectors, jnp.zeros((3, D), F32)], axis=0)
    (v.vectors,) = reorder_runs([vectors], place_index)
    prompt_ranks = (tp_rank ^ jnp.array(PROMPT_ORDER, dtype=jnp.int32))[:, None]
    prompt_iota = jnp.arange(block, dtype=jnp.int32)[None, :]
    cont_iota = jnp.arange(cont_rows, dtype=jnp.int32)[None, :]
    near_mark = ((z_half * TP + prompt_ranks) * block + prompt_iota).reshape(-1)
    far_mark = (((z_half ^ 1) * TP + prompt_ranks) * block + prompt_iota).reshape(-1)
    cont_positions = (PROMPT + cont_iota + v.offsets).reshape(-1)
    v.mark = jnp.concatenate([near_mark, cont_positions]).astype(F32)
    query_mark = jnp.concatenate([near_mark, near_mark]).reshape(-1, 1)
    key_mark = jnp.concatenate([near_mark, far_mark]).reshape(1, -1)
    (
        v.got1_z, v.got2_y, v.own_a, v.own_b, v.side3,
    ) = tie(
        v.got1_z, v.got2_y, v.own_a, v.own_b, v.side3,
    )
    v.base1a, v.base1b = stack_ranks(
        own1, v.got1_y, v.got1_z, (2 * HCOLS,) * 2, tp_rank
    )
    v.rows_az = swap_seq(v.own_a, 2)
    v.rows_ay = swap_seq(v.own_a, 1)
    v.z1a = swap_seq(v.base1a, 4)
    v.x1a = swap_grp(v.base1a, 2)
    v.send2 = onward(far2, v.got2_y)
    v.cot_a, v.cot_b, cot_sum = reorder_runs(
        [prompt_cot[0], cont_cot[0, 0]], place_index, sums=True
    )
    (
        v.rows_az, v.rows_ay, v.z1a, v.x1a, v.send2, v.base1b, v.own_b, v.cot_a, v.cot_b, v.mark,
    ) = tie(
        v.rows_az, v.rows_ay, v.z1a, v.x1a, v.send2, v.base1b, v.own_b, v.cot_a, v.cot_b, v.mark,
    )
    v.z1b = swap_seq(v.base1b, 4)
    v.got2_z = swap_seq(v.send2, 2)
    v.rows_by = swap_seq(v.own_b, 1)
    v.x1b = swap_grp(v.base1b, 2)
    v.zx1a = swap_grp(v.z1a, 2)
    tables = rotary_tables(v.mark)
    far_tables = rotary_tables(far_mark.astype(F32))
    v.tables0, v.tables1 = tables
    v.far0, v.far1 = far_tables
    (
        v.vectors, v.z1b, v.got2_z, v.rows_by, v.x1b, v.zx1a, v.rows_az, v.own_b, v.side3,
        v.tables0, v.tables1, v.far0, v.far1,
    ) = tie(
        v.vectors, v.z1b, v.got2_z, v.rows_by, v.x1b, v.zx1a, v.rows_az, v.own_b, v.side3,
        v.tables0, v.tables1, v.far0, v.far1,
    )
    tables, far_tables = (v.tables0, v.tables1), (v.far0, v.far1)
    shared = (tables, tables, far_tables, query_mark, key_mark)
    v.got3_y = swap_seq(v.side3, 1)
    v.rows_azy = swap_seq(v.rows_az, 1)
    v.rows_bz = swap_seq(v.own_b, 2)
    v.zx1b = swap_grp(v.z1b, 2)
    v.base2a, v.base2b, v.base2 = stack_ranks(
        own2, v.got2_y, v.got2_z, (ff_here // 2,) * 2, tp_rank, True
    )
    v.z2a = swap_seq(v.base2a, 4)
    (
        v.z2a, v.rows_azy, v.rows_bz, v.zx1b, v.got3_y, v.base2b, v.base2,
    ) = tie(
        v.z2a, v.rows_azy, v.rows_bz, v.zx1b, v.got3_y, v.base2b, v.base2,
    )
    v.rows_bzy = swap_seq(v.rows_bz, 1)
    v.z2b = swap_seq(v.base2b, 4)
    v.x2 = swap_grp(v.base2, 2)
    v.got3_z = swap_seq(onward(far3, v.got3_y), 2)
    v.core1 = beside(
        [(v.base1a, v.base1b), (v.z1a, v.z1b), (v.x1a, v.x1b), (v.zx1a, v.zx1b)]
    )
    gain1, bias1, gain2, bias2, bias_out = (v.vectors[i : i + 1] for i in range(5))
    (
        v.rows_bzy, v.z2a, v.z2b, v.x2, v.got3_z, v.core1, v.cot_a, v.cot_b,
    ) = tie(
        v.rows_bzy, v.z2a, v.z2b, v.x2, v.got3_z, v.core1, v.cot_a, v.cot_b,
    )

    v.swapped1 = swap_grp(v.core1, 1)
    v.cot_az = swap_seq(v.cot_a, 2)
    v.cot_ay = swap_seq(v.cot_a, 1)
    v.zx2 = swap_grp(stacked([v.z2a, v.z2b]), 2)
    v.base3a, v.base3b, v.base3 = stack_ranks(
        own3, v.got3_y, v.got3_z, (ff_here // 2,) * 2, tp_rank, True
    )
    v.z3a = swap_seq(v.base3a, 4)
    v.rows, v.first_low, v.second_low, mean, spread = both_low_norms(
        [v.own_a, v.rows_az, v.rows_ay, v.rows_azy, v.own_b, v.rows_by, v.rows_bz, v.rows_bzy],
        gain1,
        bias1,
        gain2,
        bias2,
    )
    (
        v.first_low, v.second_low, v.zx2, v.swapped1, v.core1, v.base3, v.base3b, v.cot_az,
        v.cot_ay, v.z3a, v.cot_b,
    ) = tie(
        v.first_low, v.second_low, v.zx2, v.swapped1, v.core1, v.base3, v.base3b, v.cot_az,
        v.cot_ay, v.z3a, v.cot_b,
    )
    v.cot_by = swap_seq(v.cot_b, 1)
    v.cot_bz = swap_seq(v.cot_b, 2)
    v.z3b = swap_seq(v.base3b, 4)
    v.x3 = swap_grp(v.base3, 2)
    v.core2 = beside(
        [(v.base2a, v.base2b), (v.z2a, v.z2b), v.x2, v.zx2]
    )
    v.swapped2 = swap_grp(v.core2, 1)
    weight1 = (v.core1, v.swapped1)
    v.query0, v.key0, v.value0, own0 = project_qkv(
        0, v.first_low, weight1, qkv_bias_here, *tables
    )
    v.query0, v.first_low = tie(v.query0, v.first_low)
    v.query1, v.key1, v.value1, own1_kv = project_qkv(
        1, v.first_low, weight1, qkv_bias_here, *tables
    )
    (
        v.query1, v.second_low, v.swapped2, v.core2, v.cot_az, v.x3, v.cot_by, v.cot_bz, v.z3b,
        v.key0, v.z3a,
    ) = tie(
        v.query1, v.second_low, v.swapped2, v.core2, v.cot_az, v.x3, v.cot_by, v.cot_bz, v.z3b,
        v.key0, v.z3a,
    )
    v.cot_azy = swap_seq(v.cot_az, 1)
    v.cot_bzy = swap_seq(v.cot_by, 2)
    v.far_key0 = swap_seq(v.key0, 4)
    v.zx3 = swap_grp(stacked([v.z3a, v.z3b]), 2)
    weight2 = (v.core2, v.swapped2)
    v.act_low, v.slope = feed_forward_up(v.second_low, weight2, up_bias_here)
    (
        v.act_low, v.slope, v.cot_azy, v.cot_bzy, v.far_key0, v.zx3, v.value0,
    ) = tie(
        v.act_low, v.slope, v.cot_azy, v.cot_bzy, v.far_key0, v.zx3, v.value0,
    )
    v.far_value0 = swap_seq(v.value0, 4)
    v.core3 = beside(
        [(v.base3a, v.base3b), (v.z3a, v.z3b), v.x3, v.zx3]
    )
    v.swapped3 = swap_grp(v.core3, 1)
    v.attn_grad, v.cots = attention_grad(
        [v.cot_a, v.cot_az, v.cot_ay, v.cot_azy, v.cot_b, v.cot_by, v.cot_bz, v.cot_bzy],
        weight1,
        3,
    )
    v.attn_grad, v.cots, v.act_low = tie(v.attn_grad, v.cots, v.act_low)
    v.down_away = weight_grad(v.cots, [v.act_low])
    (
        v.down_away, v.far_value0, v.key1, v.value1, v.attn_grad, v.swapped3, v.core3,
    ) = tie(
        v.down_away, v.far_value0, v.key1, v.value1, v.attn_grad, v.swapped3, v.core3,
    )
    v.down_core = swap_grp(v.down_away, 1)
    v.far_key1 = swap_seq(v.key1, 4)
    v.attn0, dq0, down0, dnear0, v.dfar_key0, v.dfar_value0 = attend(
        0,
        v.query0,
        v.attn_grad,
        (v.key0, v.value0),
        (v.far_key0, v.far_value0),
        own0,
        *shared,
    )
    (
        v.attn0, v.down_core, v.cots, v.act_low, v.far_key1, v.value1,
    ) = tie(
        v.attn0, v.down_core, v.cots, v.act_low, v.far_key1, v.value1,
    )
    v.far_value1 = swap_seq(v.value1, 4)
    v.down_mine, v.down_send = weight_grad(v.cots, [v.act_low], v.down_core)
    (
        v.down_mine, v.down_send, v.cots, v.slope, v.core3, v.swapped3,
    ) = tie(
        v.down_mine, v.down_send, v.cots, v.slope, v.core3, v.swapped3,
    )
    v.down_side = swap_grp(v.down_send, 2)
    weight3 = (v.core3, v.swapped3)
    v.hidden_grad, up_bias_term = feed_forward_back(v.cots, weight3, v.slope)
    (
        v.hidden_grad, v.far_value1, v.dfar_key0, v.dfar_value0, v.attn_grad,
    ) = tie(
        v.hidden_grad, v.far_value1, v.dfar_key0, v.dfar_value0, v.attn_grad,
    )
    v.back_key0 = swap_seq(v.dfar_key0, 4)
    v.attn1, dq1, down1, v.dnear1, v.dfar_key1, v.dfar_value1 = attend(
        1,
        v.query1,
        v.attn_grad,
        (v.key1, v.value1),
        (v.far_key1, v.far_value1),
        own1_kv,
        *shared,
    )
    (
        v.attn1, v.second_low, v.hidden_grad, v.back_key0, v.dfar_value0, v.down_side,
        v.down_mine,
    ) = tie(
        v.attn1, v.second_low, v.hidden_grad, v.back_key0, v.dfar_value0, v.down_side,
        v.down_mine,
    )
    v.back_value0 = swap_seq(v.dfar_value0, 4)
    v.up_away = weight_grad(v.second_low, [v.hidden_grad])
    v.down_half_send = second_sum(v.down_mine, v.down_side)
    (
        v.up_away, v.back_value0, v.dfar_key1, v.dfar_value1, v.act_low, v.down_half_send,
    ) = tie(
        v.up_away, v.back_value0, v.dfar_key1, v.dfar_value1, v.act_low, v.down_half_send,
    )
    v.up_core = swap_grp(v.up_away, 1)
    v.back_key1 = swap_seq(v.dfar_key1, 4)
    branch = branch_outputs((v.attn0, v.attn1), v.act_low, weight1, 3, weight3)
    v.branch0, v.branch_y, v.branch_zy, v.branch2, v.branch_z, v.branch_yz = branch
    (
        v.branch0, v.branch_y, v.branch_zy, v.branch2, v.branch_z, v.branch_yz, v.up_core,
        v.second_low, v.hidden_grad, v.back_key1, v.dfar_value1,
    ) = tie(
        v.branch0, v.branch_y, v.branch_zy, v.branch2, v.branch_z, v.branch_yz, v.up_core,
        v.second_low, v.hidden_grad, v.back_key1, v.dfar_value1,
    )
    v.got_zy = swap_seq(v.branch_zy, 1)
    v.got_yz = swap_seq(v.branch_yz, 2)
    v.back_value1 = swap_seq(v.dfar_value1, 4)
    v.up_mine, v.up_send = weight_grad(v.second_low, [v.hidden_grad], v.up_core)
    v.up_mine, v.hidden_grad = tie(v.up_mine, v.hidden_grad)
    second_parts, second_sums = norm_grad(
        v.hidden_grad, weight2, gain2, v.rows, mean, spread, (0, 1, 2, 3)
    )
    v.second0, second1, second2, second3 = second_parts
    (
        v.second0, v.back_value1, v.dnear1, v.cots, v.down_half_send, v.up_send, v.got_zy,
        v.got_yz, v.branch0, v.branch2, v.branch_y, v.branch_z,
    ) = tie(
        v.second0, v.back_value1, v.dnear1, v.cots, v.down_half_send, v.up_send, v.got_zy,
        v.got_yz, v.branch0, v.branch2, v.branch_y, v.branch_z,
    )
    v.up_side = swap_grp(v.up_send, 2)
    v.down_half = swap_seq(v.down_half_send, 4)
    v.got_y = swap_seq(v.branch_y, 1)
    v.got_z = swap_seq(v.branch_z, 2)
    v.branch_a_far = second_sum(v.branch0, v.got_zy)
    v.branch_b_far = second_sum(v.branch2, v.got_yz)
    v.qkv_grad, qkv_bias_term = join_grads(
        (dq0, dq1),
        (down0, down1),
        (dnear0, v.dnear1),
        (v.back_key0, v.back_key1),
        (v.back_value0, v.back_value1),
    )
    v.qkv_grad, v.first_low, v.cots = tie(v.qkv_grad, v.first_low, v.cots)
    v.qkv_away = weight_grad(v.first_low, [v.qkv_grad])
    v.qkv_away, v.cots = tie(v.qkv_away, v.cots)
    v.out_away = weight_grad(v.cots, [v.attn0, v.attn1])
    (
        v.out_away, v.qkv_away, v.got_y, v.got_z, v.branch_a_far, v.branch_b_far, v.down_half,
        v.up_side, v.up_mine, v.qkv_grad,
    ) = tie(
        v.out_away, v.qkv_away, v.got_y, v.got_z, v.branch_a_far, v.branch_b_far, v.down_half,
        v.up_side, v.up_mine, v.qkv_grad,
    )
    v.qkv_core = swap_grp(v.qkv_away, 1)
    v.up_send_a = second_sum(v.up_mine, v.up_side, 0)
    v.up_half_a = swap_seq(v.up_send_a, 4)
    v.branch_far_a = swap_seq(v.branch_a_far, 2)
    v.branch_far_b = swap_seq(v.branch_b_far, 1)
    v.up_send_b = second_sum(v.up_mine, v.up_side, 1)
    (
        v.qkv_core, v.first_low, v.qkv_grad, v.up_send_b,
    ) = tie(
        v.qkv_core, v.first_low, v.qkv_grad, v.up_send_b,
    )
    v.qkv_mine, v.qkv_send = weight_grad(v.first_low, [v.qkv_grad], v.qkv_core)
    v.qkv_mine, v.qkv_send, v.qkv_grad = tie(v.qkv_mine, v.qkv_send, v.qkv_grad)
    v.qkv_side = swap_grp(v.qkv_send, 2)
    entry_far, v.far_sums = norm_grad(
        v.qkv_grad, weight1, gain1, v.rows, mean, spread, (1, 3), (second1, second3), True
    )
    v.entry_y, v.entry_zy, v.entry_z, v.entry_yz = entry_far
    (
        v.entry_y, v.entry_zy, v.entry_z, v.entry_yz, v.far_sums, v.out_away, v.branch_far_a,
        v.branch_far_b, v.up_half_a, v.up_send_b, v.qkv_grad, v.second0,
    ) = tie(
        v.entry_y, v.entry_zy, v.entry_z, v.entry_yz, v.far_sums, v.out_away, v.branch_far_a,
        v.branch_far_b, v.up_half_a, v.up_send_b, v.qkv_grad, v.second0,
    )
    v.entry_got_zy = swap_seq(v.entry_zy, 1)
    v.entry_got_yz = swap_seq(v.entry_yz, 2)
    v.out_core = swap_grp(v.out_away, 1)
    v.up_half_b = swap_seq(v.up_send_b, 4)
    (v.entry0, v.entry2), v.near_sums = norm_grad(
        v.qkv_grad, weight1, gain1, v.rows, mean, spread, (0, 2), (v.second0, second2)
    )
    (
        v.near_sums, v.out_core, v.cots, v.qkv_side, v.qkv_mine, v.up_half_b, v.branch0,
        v.entry_got_zy, v.entry_got_yz, v.entry_y, v.entry_z, v.entry0, v.entry2,
    ) = tie(
        v.near_sums, v.out_core, v.cots, v.qkv_side, v.qkv_mine, v.up_half_b, v.branch0,
        v.entry_got_zy, v.entry_got_yz, v.entry_y, v.entry_z, v.entry0, v.entry2,
    )
    v.entry_got_y = swap_seq(v.entry_y, 1)
    v.entry_got_z = swap_seq(v.entry_z, 2)
    v.qkv_half_send = second_sum(v.qkv_mine, v.qkv_side)
    v.qkv_half = swap_seq(v.qkv_half_send, 4)
    v.out_mine, v.out_send = weight_grad(
        v.cots, [v.attn0, v.attn1], v.out_core
    )
    v.out_side = swap_grp(v.out_send, 2)

    rank_ids = jnp.arange(TP, dtype=jnp.int32)
    first_sums = v.far_sums + v.near_sums
    wide_sums = jnp.concatenate(
        [first_sums[:2], second_sums[:2], cot_sum, jnp.zeros((3, D), F32)], axis=0
    )
    wide_sums = restore_runs(wide_sums, place_index)
    qkv_bias_term = qkv_bias_term.reshape(3, 1, HCOLS)
    v.sums = jnp.concatenate(
        [
            wide_sums[:5].reshape(-1),
            jnp.where((rank_ids == tp_rank)[None, :, None], qkv_bias_term, 0.0).reshape(-1),
            jnp.where((rank_ids == tp_rank)[:, None], up_bias_term, 0.0).reshape(-1),
        ]
    ).reshape(-1, LANES)
    v.entry_a_far = second_sum(v.entry0, v.entry_got_zy)
    v.entry_b_far = second_sum(v.entry2, v.entry_got_yz)
    (
        v.sums, v.out_send, v.out_mine, v.entry_got_y, v.entry_got_z, v.entry_a_far,
        v.entry_b_far, v.branch0, v.up_half_b,
    ) = tie(
        v.sums, v.out_send, v.out_mine, v.entry_got_y, v.entry_got_z, v.entry_a_far,
        v.entry_b_far, v.branch0, v.up_half_b,
    )
    v.entry_far_a = swap_seq(v.entry_a_far, 2)
    v.entry_far_b = swap_seq(v.entry_b_far, 1)
    v.sums_got = swap_grp(v.sums, 1)
    v.layer_a, v.layer_b = finish_outputs(
        (
            (v.branch0, v.got_y, v.branch_far_a),
            (v.branch2, v.got_z, v.branch_far_b),
        ),
        (v.own_a, v.own_b),
        bias_out,
        place_index,
    )
    down_own, v.down_side2, v.down_far = split_rows(
        [(v.down_mine, v.down_side, (v.down_half,))], tp_rank, 2
    )
    up_own, v.up_side2, v.up_far = split_rows(
        [(v.up_mine, v.up_side, (v.up_half_a, v.up_half_b))], tp_rank, 2
    )
    (
        v.layer_a, v.sums, v.sums_got, v.down_side2, v.up_side2, v.out_side, v.out_mine,
        v.qkv_half,
    ) = tie(
        v.layer_a, v.sums, v.sums_got, v.down_side2, v.up_side2, v.out_side, v.out_mine,
        v.qkv_half,
    )
    v.out_half_send = second_sum(v.out_mine, v.out_side)
    v.out_half = swap_seq(v.out_half_send, 4)
    v.sums = v.sums + v.sums_got
    v.sums_got = swap_grp(v.sums, 2)
    (
        v.entry_far_a, v.entry_far_b, v.out_half, v.down_side2, v.down_far, v.up_side2, v.sums,
        v.sums_got,
    ) = tie(
        v.entry_far_a, v.entry_far_b, v.out_half, v.down_side2, v.down_far, v.up_side2, v.sums,
        v.sums_got,
    )
    late_own, late_side, late_far = split_rows(
        [
            (v.qkv_mine, v.qkv_side, (v.qkv_half,)),
            (v.out_mine, v.out_side, (v.out_half,)),
        ],
        tp_rank,
    )
    v.late_y = swap_seq(late_side, 1)
    v.down_z = swap_seq(v.down_side2, 2)
    v.sums = v.sums + v.sums_got
    v.sums_got = swap_seq(v.sums, 1)
    v.grad_a, grad_b = finish_grads(
        (
            (v.entry0, v.entry_got_y, v.entry_far_a),
            (v.entry2, v.entry_got_z, v.entry_far_b),
        ),
        (v.own_a, v.own_b),
        (v.cot_a, v.cot_b),
        place_index,
    )
    (
        v.grad_a, v.late_y, v.down_z, v.up_side2, v.up_far, v.sums, v.sums_got, v.down_far,
    ) = tie(
        v.grad_a, v.late_y, v.down_z, v.up_side2, v.up_far, v.sums, v.sums_got, v.down_far,
    )
    v.late_z = swap_seq(onward(late_far, v.late_y), 2)
    v.down_y = swap_seq(onward(v.down_far, v.down_z), 1)
    v.up_z = swap_seq(v.up_side2, 2)
    v.sums = v.sums + v.sums_got
    v.sums_got = swap_seq(v.sums, 2)
    (
        v.sums, v.sums_got, v.up_z, v.down_y, v.up_far,
    ) = tie(
        v.sums, v.sums_got, v.up_z, v.down_y, v.up_far,
    )
    v.up_y = swap_seq(onward(v.up_far, v.up_z), 1)
    v.sums = v.sums + v.sums_got
    v.sums_got = swap_seq(v.sums, 4)
    (v.down_grad,) = join_columns(
        down_own, v.down_z, v.down_y, [(1, ff_here)], tp_rank, 2
    )
    (v.up_grad,) = join_columns(up_own, v.up_z, v.up_y, [(1, ff_here)], tp_rank, 2)
    grad_a, down_grad, up_weight_grad = v.grad_a, v.down_grad, v.up_grad
    qkv_weight_grad, out_grad = join_columns(
        late_own, v.late_y, v.late_z, [(3, HCOLS), (1, HCOLS)], tp_rank
    )
    down_weight_grad, out_weight_grad = down_grad.T, out_grad.T
    sums = (v.sums + v.sums_got).reshape(-1)
    cuts = np.cumsum([D, D, D, D, D, 3 * D])
    gain_one, shift_one, gain_two, shift_two, out_sum, qkv_sum, up_sum = jnp.split(sums, cuts)

    return (
        v.layer_a[None],
        v.layer_b[None, None],
        grad_a[None],
        grad_b[None, None],
        gain_one,
        shift_one,
        gain_two,
        shift_two,
        qkv_weight_grad,
        qkv_sum,
        out_weight_grad,
        out_sum,
        up_weight_grad,
        up_sum,
        down_weight_grad,
        out_sum,
    )


def solution(mesh):
    in_specs = (
        P("grp", "seq", None),
        P("grp", "seq", None, None),
        P("grp", "seq"),
        P("grp", None),
        P(),
        P(),
        P(),
        P(),
        P(("grp", "seq"), None),
        P(),
        P(None, ("grp", "seq")),
        P(),
        P(("grp", "seq"), None),
        P(),
        P(None, ("grp", "seq")),
        P(),
        P("grp", "seq", None),
        P("grp", "seq", None, None),
    )
    out_specs = (
        P("grp", "seq", None),
        P("grp", "seq", None, None),
        P("grp", "seq", None),
        P("grp", "seq", None, None),
        P(),
        P(),
        P(),
        P(),
        P(("grp", "seq"), None),
        P(),
        P(None, ("grp", "seq")),
        P(),
        P(("grp", "seq"), None),
        P(),
        P(None, ("grp", "seq")),
        P(),
    )
    plan = square_plan if (mesh.shape["grp"], mesh.shape["seq"]) == (4, 8) else local
    return jax.shard_map(plan, mesh=mesh, in_specs=in_specs, out_specs=out_specs, check_vma=False)
```

```python
from functools import partial
import math

import jax
import jax.numpy as jnp
import numpy as np
from jax import lax
from jax.experimental import pallas as pl
from jax.experimental.pallas import tpu as pltpu
from jax.sharding import PartitionSpec as P

D = 2048
HEADS = 8
HEAD = 256
ROT = 64
PROMPT = 2048


EPSILON = 1e-05
NEG_FILL = -1e30
ROPE_BASE = 10000.0


def layer_norm(values, ln_gain, ln_shift):
    center = values - jnp.mean(values, axis=-1, keepdims=True)
    normed = center * lax.rsqrt(jnp.mean(center * center, axis=-1, keepdims=True) + EPSILON)
    return normed * ln_gain + ln_shift


def both_norms(values, gain_one, shift_one, gain_two, shift_two):
    return (layer_norm(values, gain_one, shift_one), layer_norm(values, gain_two, shift_two))


def rotate(head_data, positions, sign_flip):
    half_rot = ROT // 2
    inv_freq = ROPE_BASE ** (-(2.0 * jnp.arange(half_rot, dtype=jnp.float32)) / ROT)
    angles = positions[:, None] * inv_freq[None, :]
    cos_table = jnp.cos(angles)[:, None, :]
    sin_table = sign_flip * jnp.sin(angles)[:, None, :]
    first_half = head_data[..., :half_rot]
    second = head_data[..., half_rot:ROT]
    return jnp.concatenate(
        [
            first_half * cos_table - second * sin_table,
            second * cos_table + first_half * sin_table,
            head_data[..., ROT:],
        ],
        axis=-1,
    )


def contract_rows(left, right):
    return lax.dot_general(
        left, right, (((1,), (1,)), ((), ())), preferred_element_type=jnp.float32
    )


def contract_cols(left, right):
    return lax.dot_general(
        left, right, (((0,), (0,)), ((), ())), preferred_element_type=jnp.float32
    )


def local(
    prompt,
    conts,
    assignment,
    offsets,
    ln1_gain,
    ln1_bias,
    ln2_gain,
    ln2_bias,
    qkv_weight,
    qkv_bias,
    out_weight,
    out_bias,
    up_weight,
    up_bias,
    down_weight,
    down_bias,
    prompt_cot,
    cont_cot,
):
    prompt_rows = prompt.shape[1]
    cont_rows = conts.shape[2]
    row_total = prompt_rows + cont_rows
    score_scale = 1.0 / math.sqrt(HEAD)
    shard_index = lax.axis_index("seq")
    tokens = jnp.concatenate([prompt[0], conts[0, 0]], axis=0).astype(jnp.float32)
    branch_ids = jnp.arange(offsets.shape[1], dtype=jnp.int32)
    my_offset = jnp.sum(jnp.where(branch_ids == assignment[0, 0], offsets[0], 0))
    prompt_mark = shard_index * prompt_rows + jnp.arange(prompt_rows, dtype=jnp.int32)
    cont_mark = PROMPT + jnp.arange(cont_rows, dtype=jnp.int32)
    query_mark = jnp.concatenate([prompt_mark, cont_mark])
    positions = jnp.concatenate([prompt_mark, cont_mark + my_offset]).astype(jnp.float32)
    (first_norm, second_norm), norm_pullback = jax.vjp(
        both_norms, tokens, ln1_gain, ln1_bias, ln2_gain, ln2_bias
    )
    first_low = first_norm.astype(jnp.bfloat16)
    second_low = second_norm.astype(jnp.bfloat16)
    qkv_full, up_full = (
        lax.all_gather(qkv_weight, ("grp", "seq"), axis=0, tiled=True),
        lax.all_gather(up_weight, ("grp", "seq"), axis=0, tiled=True),
    )
    qkv_acc = jnp.dot(first_low, qkv_full, preferred_element_type=jnp.float32)
    up_acc = jnp.dot(second_low, up_full, preferred_element_type=jnp.float32)
    split_qkv = (qkv_acc + qkv_bias).reshape(row_total, 3, HEADS, HEAD)
    queries = rotate(split_qkv[:, 0], positions, 1.0).astype(jnp.bfloat16)
    keys_rot = rotate(split_qkv[:, 1], positions, 1.0).astype(jnp.bfloat16)
    values_low = split_qkv[:, 2].astype(jnp.bfloat16)
    hidden_pre = up_acc + up_bias
    activated, gelu_pullback = jax.vjp(partial(jax.nn.gelu, approximate=False), hidden_pre)
    act_low = activated.astype(jnp.bfloat16)

    def score_block(key_block, key_mark):
        raw_scores = (
            jnp.einsum("qhd,khd->hqk", queries, key_block, preferred_element_type=jnp.float32)
            * score_scale
        )
        allowed = key_mark[None, :] <= query_mark[:, None]
        return (raw_scores, allowed)

    def absorb(soft_state, key_block, value_block, key_mark):
        run_max, run_sum, run_acc = soft_state
        raw_scores, allowed = score_block(key_block, key_mark)
        masked = jnp.where(allowed[None], raw_scores, NEG_FILL)
        new_max = jnp.maximum(run_max, jnp.max(masked, axis=-1))
        exp_scores = jnp.where(allowed[None], jnp.exp(masked - new_max[..., None]), 0.0)
        factor = jnp.exp(run_max - new_max)
        mixed_heads = jnp.einsum(
            "hqk,khd->qhd",
            exp_scores.astype(jnp.bfloat16),
            value_block,
            preferred_element_type=jnp.float32,
        )
        return (
            new_max,
            run_sum * factor + jnp.sum(exp_scores, axis=-1),
            run_acc * factor.T[:, :, None] + mixed_heads,
        )

    cont_keys = keys_rot[prompt_rows:]
    cont_values = values_low[prompt_rows:]
    start_state = (
        jnp.full((HEADS, row_total), NEG_FILL, jnp.float32),
        jnp.zeros((HEADS, row_total), jnp.float32),
        jnp.zeros((row_total, HEADS, HEAD), jnp.float32),
    )
    start_state = absorb(start_state, cont_keys, cont_values, cont_mark)
    prompt_keys_send = keys_rot[:prompt_rows].reshape(prompt_rows, D)
    prompt_values_send = values_low[:prompt_rows].reshape(prompt_rows, D)
    key_piece = lax.all_gather(prompt_keys_send, "seq", axis=0, tiled=True)
    value_piece = lax.all_gather(prompt_values_send, "seq", axis=0, tiled=True)
    piece_width = key_piece.shape[0]
    key_mark = jnp.arange(piece_width, dtype=jnp.int32)
    run_max, run_sum, run_acc = absorb(
        start_state,
        key_piece.reshape(piece_width, HEADS, HEAD),
        value_piece.reshape(piece_width, HEADS, HEAD),
        key_mark,
    )
    attention = run_acc / run_sum.T[:, :, None]
    log_total = run_max + jnp.log(run_sum)
    attention_low = attention.reshape(row_total, D).astype(jnp.bfloat16)
    out_full, down_full = (
        lax.all_gather(out_weight, ("grp", "seq"), axis=1, tiled=True),
        lax.all_gather(down_weight, ("grp", "seq"), axis=1, tiled=True),
    )
    branch_sum = jnp.dot(attention_low, out_full, preferred_element_type=jnp.float32) + jnp.dot(
        act_low, down_full, preferred_element_type=jnp.float32
    )
    layer_out = tokens + branch_sum + out_bias + down_bias
    grad_out = jnp.concatenate([prompt_cot[0], cont_cot[0, 0]], axis=0)
    grad_f32 = grad_out.astype(jnp.float32)
    bias_out_term = jnp.sum(grad_f32, axis=0)
    out_again, down_again = (
        lax.all_gather(out_weight, ("grp", "seq"), axis=1, tiled=True),
        lax.all_gather(down_weight, ("grp", "seq"), axis=1, tiled=True),
    )
    attn_grad = contract_rows(grad_out, out_again)
    act_grad = contract_rows(grad_out, down_again)
    attn_grad_low = attn_grad.astype(jnp.bfloat16)
    (hidden_grad,) = gelu_pullback(act_grad)
    hidden_grad_low = hidden_grad.astype(jnp.bfloat16)
    up_bias_term = jnp.sum(hidden_grad_low.astype(jnp.float32), axis=0)
    grad_heads = attn_grad_low.reshape(row_total, HEADS, HEAD)
    row_delta = jnp.sum(grad_heads.astype(jnp.float32) * attention, axis=-1).T

    def back_block(key_block, value_block, key_mark):
        raw_scores, allowed = score_block(key_block, key_mark)
        probabilities = jnp.exp(
            jnp.where(allowed[None], raw_scores - log_total[..., None], NEG_FILL)
        )
        prob_grad = jnp.einsum(
            "qhd,khd->hqk", grad_heads, value_block, preferred_element_type=jnp.float32
        )
        score_grad = (probabilities * (prob_grad - row_delta[..., None])).astype(jnp.bfloat16)
        query_term = (
            jnp.einsum("hqk,khd->qhd", score_grad, key_block, preferred_element_type=jnp.float32)
            * score_scale
        )
        key_term = (
            jnp.einsum("hqk,qhd->khd", score_grad, queries, preferred_element_type=jnp.float32)
            * score_scale
        )
        value_term = jnp.einsum(
            "hqk,qhd->khd",
            probabilities.astype(jnp.bfloat16),
            grad_heads,
            preferred_element_type=jnp.float32,
        )
        return (query_term, key_term, value_term)

    query_local, key_local, value_local = back_block(cont_keys, cont_values, cont_mark)
    gathered_keys, gathered_values = (
        lax.all_gather(prompt_keys_send, "seq", axis=0, tiled=True),
        lax.all_gather(prompt_values_send, "seq", axis=0, tiled=True),
    )
    key_block_size = min(512, PROMPT)
    block_count = PROMPT // key_block_size

    def scan_step(query_total, inputs):
        key_block, value_block, block_start = inputs
        key_mark = block_start + jnp.arange(key_block_size, dtype=jnp.int32)
        query_term, key_term, value_term = back_block(
            key_block.reshape(key_block_size, HEADS, HEAD),
            value_block.reshape(key_block_size, HEADS, HEAD),
            key_mark,
        )
        return (
            query_total + query_term,
            (key_term.reshape(key_block_size, D), value_term.reshape(key_block_size, D)),
        )

    query_grad, (key_terms, value_terms) = lax.scan(
        scan_step,
        query_local,
        (
            gathered_keys.reshape(block_count, key_block_size, D),
            gathered_values.reshape(block_count, key_block_size, D),
            jnp.arange(block_count, dtype=jnp.int32) * key_block_size,
        ),
    )
    key_prompt_grad, value_prompt_grad = (
        lax.psum_scatter(
            key_terms.reshape(PROMPT, D).astype(jnp.bfloat16),
            "seq",
            scatter_dimension=0,
            tiled=True,
        ).astype(jnp.float32),
        lax.psum_scatter(
            value_terms.reshape(PROMPT, D).astype(jnp.bfloat16),
            "seq",
            scatter_dimension=0,
            tiled=True,
        ).astype(jnp.float32),
    )
    key_grad = jnp.concatenate([key_prompt_grad, key_local.reshape(cont_rows, D)], axis=0).reshape(
        row_total, HEADS, HEAD
    )
    value_grad = jnp.concatenate(
        [value_prompt_grad, value_local.reshape(cont_rows, D)], axis=0
    ).reshape(row_total, HEADS, HEAD)
    qkv_grad = (
        jnp.stack(
            [rotate(query_grad, positions, -1.0), rotate(key_grad, positions, -1.0), value_grad],
            axis=1,
        )
        .reshape(row_total, 3 * D)
        .astype(jnp.bfloat16)
    )
    qkv_bias_term = jnp.sum(qkv_grad.astype(jnp.float32), axis=0)
    qkv_again, up_again = (
        lax.all_gather(qkv_weight, ("grp", "seq"), axis=0, tiled=True),
        lax.all_gather(up_weight, ("grp", "seq"), axis=0, tiled=True),
    )
    first_grad = contract_rows(qkv_grad, qkv_again)
    second_grad = contract_rows(hidden_grad_low, up_again)
    token_grad, gain_one, shift_one, gain_two, shift_two = norm_pullback((first_grad, second_grad))
    token_grad = token_grad + grad_f32
    small_sums = lax.psum(
        (gain_one, shift_one, gain_two, shift_two, qkv_bias_term, bias_out_term, up_bias_term),
        ("grp", "seq"),
    )
    out_sources = jnp.concatenate([attention_low, act_low], axis=1)
    in_group = lax.psum_scatter(
        jnp.concatenate(
            [contract_cols(first_low, qkv_grad), contract_cols(second_low, hidden_grad_low)], axis=1
        ).astype(jnp.bfloat16),
        "grp",
        scatter_dimension=0,
        tiled=True,
    )
    in_share = lax.psum_scatter(in_group, "seq", scatter_dimension=0, tiled=True).astype(
        jnp.float32
    )
    out_group = lax.psum_scatter(
        contract_cols(grad_out, out_sources).astype(jnp.bfloat16),
        "grp",
        scatter_dimension=0,
        tiled=True,
    )
    out_share = lax.psum_scatter(out_group, "seq", scatter_dimension=0, tiled=True).astype(
        jnp.float32
    )
    qkv_weight_grad = in_share[:, : 3 * D]
    up_weight_grad = in_share[:, 3 * D :]
    out_weight_grad = out_share[:, :D].T
    down_weight_grad = out_share[:, D:].T
    prompt_result = layer_out[:prompt_rows][None]
    cont_result = layer_out[prompt_rows:][None, None]
    prompt_grad = token_grad[:prompt_rows][None]
    cont_grad = token_grad[prompt_rows:][None, None]
    return (
        prompt_result,
        cont_result,
        prompt_grad,
        cont_grad,
        small_sums[0],
        small_sums[1],
        small_sums[2],
        small_sums[3],
        qkv_weight_grad,
        small_sums[4],
        out_weight_grad,
        small_sums[5],
        up_weight_grad,
        small_sums[6],
        down_weight_grad,
        small_sums[5],
    )


PROMPT_ORDER = (0, 2, 1, 3)
CONT_ORDER = (0, 1, 2, 3)
WIDTH_ORDER = (0, 1, 4, 5, 2, 3, 6, 7)
TP = 4
HEADS_HERE = HEADS // TP
HCOLS = HEADS_HERE * HEAD
LANES = 128
COST_UNIT = 1.0e6
COSTS = {
    "norms": 15,
    "qkv_rotary": 12,
    "feed_forward_up": 30,
    "attention_grad": 11,
    "weight_grad": 14,
    "attention_both_ways": 28,
    "feed_forward_back": 25,
    "branch_outputs": 34,
    "norm_grad": 25,
    "join_grads": 8,
    "finish_outputs": 7,
    "finish_grads": 9,
}
BF = jnp.bfloat16
F32 = jnp.float32


def swap_grp(array, bits):
    return lax.ppermute(array, "grp", [(i, i ^ bits) for i in range(4)])


def swap_seq(array, bits):
    return lax.ppermute(array, "seq", [(i, i ^ bits) for i in range(8)])


def matmul_nn(left, right):
    return jnp.dot(left, right, preferred_element_type=F32)


def pick(array, index, axis):
    return lax.dynamic_index_in_dim(array, index, axis, keepdims=False)


def place(buffer, piece, index):
    return lax.dynamic_update_index_in_dim(buffer, piece, index, 0)


def tie(*arrays):
    return lax.optimization_barrier(arrays)


def whole(shape):
    return pl.BlockSpec(shape, lambda i, rank: (0,) * len(shape))


def cost(name):
    flops = int(COSTS.get(name, 2) * COST_UNIT)
    return pl.CostEstimate(flops=flops, transcendentals=0, bytes_accessed=0)


def ranked_call(body, rank, ins, shapes, name, blocks=None):
    return pl.pallas_call(
        body,
        grid_spec=pltpu.PrefetchScalarGridSpec(
            num_scalar_prefetch=1,
            grid=(1,),
            in_specs=[whole(shape) for shape in blocks or [a.shape for a in ins]],
            out_specs=[whole(s.shape) for s in shapes],
        ),
        out_shape=shapes,
        compiler_params=pltpu.CompilerParams(vmem_limit_bytes=56 << 20),
        cost_estimate=cost(name),
        name=name,
    )(rank.reshape(1), *ins)


def split_columns(shards, groups, tp_rank):
    rows = shards[0].shape[0]
    widths = [shard.shape[1] // (TP * count) for shard, count in zip(shards, groups)]
    cols = sum(width * count for width, count in zip(widths, groups))

    def body(rank_ref, *refs):
        ins, (own_ref, side_ref, far_ref) = refs[: len(shards)], refs[len(shards) :]
        at = 0
        for ref, count, width in zip(ins, groups, widths):
            for part in range(count):
                for bits in range(TP):
                    start = pl.multiple_of((part * TP + (rank_ref[0] ^ bits)) * width, width)
                    run = ref[:, pl.ds(start, width)]
                    here = slice(at, at + width)
                    if bits == 0:
                        own_ref[:, here] = run
                    elif bits == 2:
                        far_ref[:, here] = run
                    else:
                        side_ref[bits // 2, :, here] = run
                at += width

    shapes = [
        jax.ShapeDtypeStruct((rows, cols), BF),
        jax.ShapeDtypeStruct((2, rows, cols), BF),
        jax.ShapeDtypeStruct((rows, cols), BF),
    ]
    return ranked_call(body, tp_rank, list(shards), shapes, "split_columns")


def stack_ranks(own, over_y, over_z, cuts, tp_rank, uncut=False):
    rows, cols = own.shape
    runs = [slice(sum(cuts[:i]), sum(cuts[: i + 1])) for i in range(len(cuts))]
    if uncut:
        runs.append(slice(0, cols))

    def body(rank_ref, own_ref, y_ref, z_ref, *outs):
        for out, here in zip(outs, runs):
            pieces = (own_ref[:, here], y_ref[0, :, here], z_ref[0, :, here], z_ref[1, :, here])
            for bits, piece in enumerate(pieces):
                start = pl.multiple_of((rank_ref[0] ^ bits) * rows, rows)
                out[pl.ds(start, rows), :] = piece

    shapes = [jax.ShapeDtypeStruct((TP * rows, run.stop - run.start), BF) for run in runs]
    return ranked_call(body, tp_rank, [own, over_y, over_z], shapes, "stack_ranks")


def split_rows(groups, tp_rank, first=1):
    rows = groups[0][2][0].shape[0] // TP
    cols = sum(terms[0].shape[1] for terms in groups)
    flat = [array for kept, got_x, got_z in groups for array in (kept, got_x, *got_z)]

    def body(rank_ref, *refs):
        ins, (own_ref, side_ref, far_ref) = list(refs[: len(flat)]), refs[len(flat) :]
        at = 0
        for _, _, got_z in groups:
            kept, got_x = ins.pop(0), ins.pop(0)
            inside = 0
            for _ in got_z:
                run_ref = ins.pop(0)
                width = run_ref.shape[1]
                here, cut = slice(at, at + width), slice(inside, inside + width)
                at, inside = at + width, inside + width
                for bits in range(TP):
                    lines = pl.ds(pl.multiple_of((rank_ref[0] ^ bits) * rows, rows), rows)
                    total = kept[lines, cut].astype(F32) + got_x[lines, cut].astype(F32)
                    run = (total + run_ref[lines, :].astype(F32)).astype(BF)
                    if bits == 0:
                        own_ref[:, here] = run
                    elif bits == 3 - first:
                        far_ref[:, here] = run
                    else:
                        side_ref[int(bits == 3), :, here] = run

    shapes = [
        jax.ShapeDtypeStruct((rows, cols), BF),
        jax.ShapeDtypeStruct((2, rows, cols), BF),
        jax.ShapeDtypeStruct((rows, cols), BF),
    ]
    blocks = [(TP * rows, term.shape[1]) for term in flat]
    return ranked_call(body, tp_rank, flat, shapes, "split_rows", blocks)


def join_columns(own, got_first, got_second, parts, tp_rank, first=1):
    rows = own.shape[0]

    def body(rank_ref, own_ref, first_ref, second_ref, *outs):
        at = 0
        for out, (count, width) in zip(outs, parts):
            for part in range(count):
                here = slice(at, at + width)
                pieces = {
                    0: own_ref[:, here],
                    first: first_ref[0, :, here],
                    3 - first: second_ref[0, :, here],
                    3: second_ref[1, :, here],
                }
                for bits, piece in pieces.items():
                    start = pl.multiple_of((part * TP + (rank_ref[0] ^ bits)) * width, width)
                    out[:, pl.ds(start, width)] = piece.astype(F32)
                at += width

    shapes = [jax.ShapeDtypeStruct((rows, TP * count * width), F32) for count, width in parts]
    return ranked_call(body, tp_rank, [own, got_first, got_second], shapes, "join_columns")


def reorder_runs(arrays, place_index, sums=False):
    run = D // 8
    shapes = [jax.ShapeDtypeStruct(a.shape, a.dtype) for a in arrays]
    if sums:
        shapes.append(jax.ShapeDtypeStruct((1, D), F32))

    def body(index_ref, *refs):
        ins, outs = refs[: len(arrays)], refs[len(arrays) :]
        for j, bits in enumerate(WIDTH_ORDER):
            start = pl.multiple_of((index_ref[0] ^ bits) * run, run)
            here = slice(j * run, (j + 1) * run)
            for in_ref, out_ref in zip(ins, outs):
                out_ref[:, here] = in_ref[:, pl.ds(start, run)]
        if sums:
            total = outs[0][...].astype(F32).sum(axis=0, keepdims=True)
            for out_ref in outs[1 : len(arrays)]:
                total = total + out_ref[...].astype(F32).sum(axis=0, keepdims=True)
            outs[-1][...] = total

    return ranked_call(body, place_index, list(arrays), shapes, "reorder_runs")


def restore_runs(array, place_index):
    run = D // 8

    def body(index_ref, in_ref, out_ref):
        for j, bits in enumerate(WIDTH_ORDER):
            start = pl.multiple_of((index_ref[0] ^ bits) * run, run)
            out_ref[:, pl.ds(start, run)] = in_ref[:, j * run : (j + 1) * run]

    shapes = [jax.ShapeDtypeStruct(array.shape, array.dtype)]
    return ranked_call(body, place_index, [array], shapes, "restore_runs")[0]


def finish_outputs(parts, tokens, bias, place_index):
    run = D // 8
    rows = tokens[0].shape[0]
    flat = [term for terms in parts for term in terms]

    def body(index_ref, *refs):
        ins, outs = refs[: len(flat) + len(tokens) + 1], refs[len(flat) + len(tokens) + 1 :]
        bias_ref = ins[-1]
        for i, out_ref in enumerate(outs):
            own, got, got_far = ins[3 * i : 3 * i + 3]
            token_ref = ins[len(flat) + i]
            value = token_ref[...].astype(F32) + own[...].astype(F32) + got[...].astype(F32)
            value = value + got_far[...].astype(F32) + bias_ref[...]
            for j, bits in enumerate(WIDTH_ORDER):
                start = pl.multiple_of((index_ref[0] ^ bits) * run, run)
                out_ref[:, pl.ds(start, run)] = value[:, j * run : (j + 1) * run]

    shapes = [jax.ShapeDtypeStruct((rows, D), F32) for _ in tokens]
    blocks = [(rows, D)] * (len(flat) + len(tokens)) + [bias.shape]
    return ranked_call(
        body, place_index, flat + list(tokens) + [bias], shapes, "finish_outputs", blocks
    )


def finish_grads(parts, tokens, cots, place_index):
    run = D // 8
    rows = tokens[0].shape[0]
    count = len(tokens)
    flat = [term for terms in parts for term in terms]

    def body(index_ref, *refs):
        ins, outs = refs[: 5 * count], refs[5 * count :]
        for i, out_ref in enumerate(outs):
            own, got, got_far = ins[3 * i : 3 * i + 3]
            token = ins[3 * count + i][...].astype(F32)
            cot = ins[4 * count + i][...].astype(F32)
            entry = own[...].astype(F32) + got[...].astype(F32) + got_far[...].astype(F32)
            center = token - jnp.mean(token, axis=1, keepdims=True)
            spread = lax.rsqrt(jnp.mean(center * center, axis=1, keepdims=True) + EPSILON)
            normed = center * spread
            entry_mean = jnp.mean(entry, axis=1, keepdims=True)
            entry_dot = jnp.mean(entry * normed, axis=1, keepdims=True)
            value = cot + spread * (entry - entry_mean - normed * entry_dot)
            for j, bits in enumerate(WIDTH_ORDER):
                start = pl.multiple_of((index_ref[0] ^ bits) * run, run)
                out_ref[:, pl.ds(start, run)] = value[:, j * run : (j + 1) * run]

    shapes = [jax.ShapeDtypeStruct((rows, D), F32) for _ in tokens]
    return ranked_call(
        body,
        place_index,
        flat + list(tokens) + list(cots),
        shapes,
        "finish_grads",
        [(rows, D)] * (5 * count),
    )


def part_specs(rows, tile, width, parts):
    per_part = rows // tile

    def spec(k):
        return pl.BlockSpec((tile, width), lambda i: (jnp.clip(i - k * per_part, 0, per_part - 1), 0))

    return [spec(k) for k in range(parts)]


def norms_body(gain1, bias1, gain2, bias2, *refs):
    *parts, rows_ref, first_ref, second_ref, mean_ref, spread_ref = refs
    step = pl.program_id(0)
    per_part = pl.num_programs(0) // len(parts)
    for k, part in enumerate(parts):

        @pl.when(step // per_part == k)
        def _(part=part):
            rows_ref[...] = part[...]
            values = part[...].astype(F32)
            mean = jnp.mean(values, axis=1, keepdims=True)
            center = values - mean
            spread = lax.rsqrt(jnp.mean(center * center, axis=1, keepdims=True) + EPSILON)
            normed = center * spread
            first_ref[...] = (normed * gain1[...] + bias1[...]).astype(BF)
            second_ref[...] = (normed * gain2[...] + bias2[...]).astype(BF)
            mean_ref[...] = mean
            spread_ref[...] = spread


def both_low_norms(parts, gain1, bias1, gain2, bias2):
    tile = parts[0].shape[0]
    total = tile * len(parts)
    vector = pl.BlockSpec((1, D), lambda i: (0, 0))
    wide = pl.BlockSpec((tile, D), lambda i: (i, 0))
    thin = pl.BlockSpec((tile, 1), lambda i: (i, 0))
    return pl.pallas_call(
        norms_body,
        grid=(total // tile,),
        in_specs=[vector] * 4 + part_specs(tile, tile, D, len(parts)),
        out_specs=[wide, wide, wide, thin, thin],
        out_shape=[
            jax.ShapeDtypeStruct((total, D), BF),
            jax.ShapeDtypeStruct((total, D), BF),
            jax.ShapeDtypeStruct((total, D), BF),
            jax.ShapeDtypeStruct((total, 1), F32),
            jax.ShapeDtypeStruct((total, 1), F32),
        ],
        compiler_params=pltpu.CompilerParams(vmem_limit_bytes=56 << 20),
        cost_estimate=cost("norms"),
        name="norms",
    )(gain1, bias1, gain2, bias2, *parts)


def resident(array, block=None, at=(0, 0)):
    return pl.BlockSpec(block or array.shape, lambda i: at, pipeline_mode=pl.Buffered(1))


def times(rows, halves, columns):
    upper, lower = halves
    half = upper.shape[0]
    return matmul_nn(rows[:, :half], upper[:, columns]) + matmul_nn(rows[:, half:], lower[:, columns])


def runs_of(width, run):
    return [slice(at, at + run) for at in range(0, width, run)]


def kernel(body, steps, in_specs, out_specs, out_shape, name, scratch=()):
    return pl.pallas_call(
        body,
        grid=(steps,),
        in_specs=in_specs,
        out_specs=out_specs,
        out_shape=out_shape,
        scratch_shapes=scratch,
        compiler_params=pltpu.CompilerParams(vmem_limit_bytes=58 << 20),
        cost_estimate=cost(name),
        name=name,
    )


def stacked(parts):
    tile, width = parts[0].shape

    def body(*refs):
        *ins, out_ref = refs
        for k, part in enumerate(ins):

            @pl.when(pl.program_id(0) == k)
            def _(part=part):
                out_ref[...] = part[...]

    return kernel(
        body,
        len(parts),
        part_specs(tile, tile, width, len(parts)),
        by_rows(tile, width),
        jax.ShapeDtypeStruct((tile * len(parts), width), BF),
        "stacked",
    )(*parts)


def beside(entries):
    tile, width = entries[0][0].shape
    specs, arrays = [], []
    for entry in entries:
        if isinstance(entry, tuple):
            specs += [pl.BlockSpec((tile, width), lambda i: (0, 0))] * 2
            arrays += entry
        elif entry.shape[0] == tile:
            specs += [pl.BlockSpec((tile, width), lambda i, h=h: (0, h)) for h in range(2)]
            arrays += [entry, entry]
        else:
            specs += [pl.BlockSpec((tile, width), lambda i, h=h: (h, 0)) for h in range(2)]
            arrays += [entry, entry]

    def body(*refs):
        *ins, out_ref = refs
        for k in range(len(entries)):

            @pl.when(pl.program_id(0) == k)
            def _(k=k):
                out_ref[:, :width] = ins[2 * k][...]
                out_ref[:, width:] = ins[2 * k + 1][...]

    return kernel(
        body,
        len(entries),
        specs,
        by_rows(tile, 2 * width),
        jax.ShapeDtypeStruct((tile * len(entries), 2 * width), BF),
        "beside",
    )(*arrays)


def second_sum(left, right, part=None):
    rows, width = left.shape[0] // 2, left.shape[1] // (1 if part is None else 2)
    wide = 1024 if width % 1024 == 0 else 512
    first = (part or 0) * (width // wide)

    def body(left_ref, right_ref, out_ref):
        out_ref[...] = (left_ref[...].astype(F32) + right_ref[...].astype(F32)).astype(BF)

    lower = pl.BlockSpec((rows, wide), lambda i: (1, first + i))
    at = right.shape[0] // rows - 1
    return kernel(
        body,
        width // wide,
        [lower, pl.BlockSpec((rows, wide), lambda i: (at, first + i))],
        pl.BlockSpec((rows, wide), lambda i: (0, i)),
        jax.ShapeDtypeStruct((rows, width), BF),
        "second_sum",
    )(left, right)


def onward(far, over_y):
    rows, width = far.shape

    def body(far_ref, y_ref, out_ref):
        out_ref[0] = far_ref[...]
        out_ref[1] = y_ref[0]

    return kernel(
        body,
        1,
        [
            pl.BlockSpec((rows, width), lambda i: (0, 0)),
            pl.BlockSpec((1, rows, width), lambda i: (1, 0, 0)),
        ],
        pl.BlockSpec((2, rows, width), lambda i: (0, 0, 0)),
        jax.ShapeDtypeStruct((2, rows, width), BF),
        "onward",
    )(far, over_y)


def by_rows(tile, width, tiles=lambda i: i):
    return pl.BlockSpec((tile, width), lambda i: (tiles(i), 0))


def attention_grad(parts, halves, column_block):
    tile = parts[0].shape[0]
    total = tile * len(parts)

    def body(upper, lower, *refs):
        *ins, out_ref, rows_ref, held = refs
        for k, part in enumerate(ins):

            @pl.when(pl.program_id(0) == k)
            def _(part=part):
                held[...] = part[...]

        rows = held[...]
        rows_ref[...] = rows
        out_ref[...] = times(rows, (upper, lower), slice(0, HCOLS)).astype(BF)

    weight_spec = resident(halves[0], (D // 2, HCOLS), (0, column_block))
    return kernel(
        body,
        len(parts),
        [weight_spec, weight_spec] + part_specs(tile, tile, D, len(parts)),
        [by_rows(tile, HCOLS), by_rows(tile, D)],
        [jax.ShapeDtypeStruct((total, HCOLS), BF), jax.ShapeDtypeStruct((total, D), BF)],
        "attention_grad",
        [pltpu.VMEM((tile, D), BF)],
    )(*halves, *parts)


def feed_forward_up(rows, halves, bias):
    total, ff_here = rows.shape[0], bias.shape[1]
    tile, wide = total // 4, ff_here // 2
    half = D // 2

    def body(rows_ref, upper, lower, bias_ref, act_ref, slope_ref):
        values = rows_ref[...]
        for run in runs_of(wide, 256):
            pre = times(values, (upper, lower), run) + bias_ref[:, run]
            cdf = 0.5 * (1.0 + lax.erf(pre * math.sqrt(0.5)))
            density = jnp.exp(-0.5 * pre * pre) * (1.0 / math.sqrt(2.0 * math.pi))
            act_ref[:, run] = (pre * cdf).astype(BF)
            slope_ref[:, run] = (cdf + pre * density).astype(BF)

    weight_spec = pl.BlockSpec((half, wide), lambda i: (0, i // 4))
    out_spec = pl.BlockSpec((tile, wide), lambda i: (i % 4, i // 4))
    return kernel(
        body,
        8,
        [
            by_rows(tile, D, lambda i: i % 4),
            weight_spec,
            weight_spec,
            pl.BlockSpec((1, wide), lambda i: (0, i // 4)),
        ],
        [out_spec] * 2,
        [jax.ShapeDtypeStruct((total, ff_here), BF)] * 2,
        "feed_forward_up",
    )(rows, *halves, bias)


def feed_forward_back(cots, halves, slope):
    total, ff_here = slope.shape
    tile, wide = total // 2, ff_here // 2
    half = D // 2

    def body(cot_ref, upper, lower, slope_ref, out_ref, sum_ref):
        @pl.when(pl.program_id(0) % 2 == 0)
        def _():
            sum_ref[...] = jnp.zeros_like(sum_ref)

        values = cot_ref[...]
        for run in runs_of(wide, 512):
            grad = times(values, (upper, lower), run) * slope_ref[:, run].astype(F32)
            low = grad.astype(BF)
            out_ref[:, run] = low
            sum_ref[:, run] += low.astype(F32).sum(axis=0, keepdims=True)

    weight_spec = pl.BlockSpec((half, wide), lambda i: (0, i // 2))
    both = pl.BlockSpec((tile, wide), lambda i: (i % 2, i // 2))
    return kernel(
        body,
        4,
        [by_rows(tile, D, lambda i: i % 2), weight_spec, weight_spec, both],
        [both, pl.BlockSpec((1, wide), lambda i: (0, i // 2))],
        [jax.ShapeDtypeStruct((total, ff_here), BF), jax.ShapeDtypeStruct((1, ff_here), F32)],
        "feed_forward_back",
    )(cots, *halves, slope)


def weight_grad(left, rights, core_got=None):
    total = left.shape[0]
    width = sum(right.shape[1] for right in rights)
    half = D // 2
    wide = 512
    steps = width // wide if len(rights) == 1 else 1
    keep = core_got is not None

    def body(left_ref, *refs):
        ins, rest = refs[: len(rights)], refs[len(rights) :]
        values = left_ref[...]
        at = 0
        for right in ins:
            here = slice(at, at + right.shape[1])
            at += right.shape[1]
            product = contract_cols(values, right[...])
            if keep:
                got_ref, mine_ref, side_ref = rest
                product = product + got_ref[:, here].astype(F32)
                mine_ref[:, here] = product[: half // 2].astype(BF)
                side_ref[:, here] = product[half // 2 :].astype(BF)
            else:
                rest[0][:, here] = product.astype(BF)

    if len(rights) == 1:
        right_specs = [pl.BlockSpec((total, wide), lambda i: (0, i))]
    else:
        right_specs = [resident(right) for right in rights]
    rows = half // 2 if keep else half
    count = 2 if keep else 1
    outs = kernel(
        body,
        steps,
        [resident(left, (total, half), (0, 0 if keep else 1))]
        + right_specs
        + ([pl.BlockSpec((half, wide), lambda i: (0, i))] if keep else []),
        [pl.BlockSpec((rows, wide), lambda i: (0, i))] * count,
        [jax.ShapeDtypeStruct((rows, width), BF)] * count,
        "weight_grad",
    )(left, *rights, *([core_got] if keep else []))
    return outs if keep else outs[0]


def width_tile(halves, height, columns, block=0):
    per_half = halves[0].shape[0] // height
    return [
        pl.BlockSpec((height, columns), lambda i: (jnp.minimum(i, per_half - 1), block)),
        pl.BlockSpec((height, columns), lambda i: (jnp.maximum(i - per_half, 0), block)),
    ]


def chosen(upper, lower):
    in_upper = pl.program_id(0) < pl.num_programs(0) // 2
    return jnp.where(in_upper, upper[...], lower[...])


def quarter_rows(tile):
    return [tile, tile // 2, tile // 2] * 2


def quarter_specs(tile, wide):
    return [pl.BlockSpec((rows, wide), lambda i: (0, i)) for rows in quarter_rows(tile)]


def put_quarter(outs, k, value):
    at = 3 * (k // 2)
    if k % 2 == 0:
        outs[at][...] = value
    else:
        half = value.shape[0] // 2
        outs[at + 1][...] = value[:half]
        outs[at + 2][...] = value[half:]


def branch_outputs(heads_low, act_low, attn_halves, column_block, down_halves):
    total, ff_here = act_low.shape
    tile = total // 4
    wide = 512

    def body(*refs):
        heads = [refs[h * 4 : h * 4 + 4] for h in range(HEADS_HERE)]
        refs = refs[4 * HEADS_HERE :]
        acts, attn, down, outs = refs[:4], refs[4:6], refs[6:8], refs[8:]
        attn_tile, down_tile = chosen(*attn), chosen(*down)
        for k in range(4):
            value = contract_rows(acts[k][...], down_tile)
            for head in range(HEADS_HERE):
                cut = slice(head * HEAD, (head + 1) * HEAD)
                value = value + contract_rows(heads[head][k][...], attn_tile[:, cut])
            put_quarter(outs, k, value.astype(BF))

    return kernel(
        body,
        D // wide,
        [resident(h, (tile, HEAD), (k, 0)) for h in heads_low for k in range(4)]
        + [resident(act_low, (tile, ff_here), (k, 0)) for k in range(4)]
        + width_tile(attn_halves, wide, HCOLS, column_block)
        + width_tile(down_halves, wide, ff_here),
        quarter_specs(tile, wide),
        [jax.ShapeDtypeStruct((rows, D), BF) for rows in quarter_rows(tile)],
        "branch_outputs",
    )(*[h for h in heads_low for _ in range(4)], *([act_low] * 4), *attn_halves, *down_halves)


def norm_grad(grads, halves, gain, tokens, mean, spread, row_blocks, addends=(), cut=False):
    tile = grads.shape[0] // 4
    count = len(row_blocks)
    width = grads.shape[1]
    wide = 512

    def body(upper, lower, gain_ref, *refs):
        rows, means, spreads, token_refs = (refs[i * count : (i + 1) * count] for i in range(4))
        rest = refs[4 * count :]
        adds, outs, sum_ref = rest[: len(addends)], rest[len(addends) : -1], rest[-1]
        weight = chosen(upper, lower)
        dots = jnp.zeros((1, wide), F32)
        totals = jnp.zeros((1, wide), F32)
        for k in range(count):
            value = contract_rows(rows[k][...], weight)
            scaled = value * gain_ref[...]
            if adds:
                scaled = scaled + adds[k][...].astype(F32)
            low = scaled.astype(BF)
            if cut:
                outs[2 * k][...] = low[: tile // 2]
                outs[2 * k + 1][...] = low[tile // 2 :]
            else:
                outs[k][...] = low
            normed = (token_refs[k][...].astype(F32) - means[k][...]) * spreads[k][...]
            dots = dots + (value * normed).sum(axis=0, keepdims=True)
            totals = totals + value.sum(axis=0, keepdims=True)
        sum_ref[0:1, :] = dots
        sum_ref[1:2, :] = totals

    column = pl.BlockSpec((tile, wide), lambda i: (0, i))
    out_rows = [tile // 2] * (2 * count) if cut else [tile] * count
    outs = kernel(
        body,
        D // wide,
        [
            *width_tile(halves, wide, width),
            pl.BlockSpec((1, wide), lambda i: (0, i)),
            *[resident(grads, (tile, width), (k, 0)) for k in row_blocks],
            *[resident(mean, (tile, 1), (k, 0)) for k in row_blocks],
            *[resident(spread, (tile, 1), (k, 0)) for k in row_blocks],
            *[pl.BlockSpec((tile, wide), lambda i, k=k: (k, i)) for k in row_blocks],
            *([column] * len(addends)),
        ],
        [pl.BlockSpec((rows, wide), lambda i: (0, i)) for rows in out_rows]
        + [pl.BlockSpec((8, wide), lambda i: (0, i))],
        [jax.ShapeDtypeStruct((rows, D), BF) for rows in out_rows]
        + [jax.ShapeDtypeStruct((8, D), F32)],
        "norm_grad",
    )(
        *halves,
        gain,
        *([grads] * count),
        *([mean] * count),
        *([spread] * count),
        *([tokens] * count),
        *addends,
    )
    return outs[:-1], outs[-1]


def rotary_tables(positions):
    lane = jnp.arange(LANES, dtype=jnp.int32)
    half_rot = ROT // 2
    exponent = -(2.0 * (lane % half_rot).astype(F32)) / ROT
    angles = positions[:, None] * (ROPE_BASE**exponent)[None, :]
    turning = (lane < ROT)[None, :]
    cos_table = jnp.where(turning, jnp.cos(angles), 1.0)
    sin_part = jnp.sin(angles)
    sin_table = jnp.where((lane < half_rot)[None, :], -sin_part, sin_part)
    return cos_table, jnp.where(turning, sin_table, 0.0)


def swapped_halves(values):
    half_rot = ROT // 2
    lane = lax.broadcasted_iota(jnp.int32, values.shape, 1)
    return jnp.where(
        lane < half_rot,
        pltpu.roll(values, LANES - half_rot, 1),
        pltpu.roll(values, half_rot, 1),
    )


def turned(values, cos_table, sin_table):
    first = values[:, :LANES]
    return jnp.concatenate(
        [first * cos_table + swapped_halves(first) * sin_table, values[:, LANES:]], axis=1
    )


def project_qkv(head, rows, halves, bias, cos_table, sin_table):
    total = rows.shape[0]
    tile = total // 2
    half = D // 2

    def body(rows_ref, *refs):
        weights, biases = refs[:6], refs[6:9]
        cos_ref, sin_ref, q_ref, near_key_ref, near_value_ref, own_ref = refs[9:]
        values = rows_ref[...]
        cos_here, sin_here = cos_ref[...], sin_ref[...]

        def product(kind):
            whole_run = slice(0, HEAD)
            return times(values, weights[2 * kind : 2 * kind + 2], whole_run) + biases[kind][...]

        query = turned(product(0), cos_here, sin_here)
        q_ref[...] = (query * (1.0 / math.sqrt(HEAD))).astype(BF)
        key = turned(product(1), cos_here, sin_here).astype(BF)
        value = product(2).astype(BF)

        @pl.when(pl.program_id(0) == 0)
        def _():
            near_key_ref[...] = key
            near_value_ref[...] = value

        @pl.when(pl.program_id(0) == 1)
        def _():
            own_ref[:, :HEAD] = key
            own_ref[:, HEAD:] = value

    columns = [kind * HEADS_HERE + head for kind in range(3)]
    both = jax.ShapeDtypeStruct((tile, 2 * HEAD), BF)
    one = jax.ShapeDtypeStruct((tile, HEAD), BF)
    kept_both = pl.BlockSpec((tile, 2 * HEAD), lambda i: (0, 0))
    kept = pl.BlockSpec((tile, HEAD), lambda i: (0, 0))
    return kernel(
        body,
        2,
        [
            by_rows(tile, D),
            *[resident(h, (half, HEAD), (0, c)) for c in columns for h in halves],
            *[resident(bias, (1, HEAD), (0, c)) for c in columns],
            by_rows(tile, LANES),
            by_rows(tile, LANES),
        ],
        [by_rows(tile, HEAD), kept, kept, kept_both],
        [jax.ShapeDtypeStruct((total, HEAD), BF), one, one, both],
        "qkv_rotary",
    )(rows, *[h for _ in columns for h in halves], *([bias] * 3), cos_table, sin_table)


def attention_body(
    q_ref,
    do_ref,
    kl_ref,
    vl_ref,
    kr_ref,
    vr_ref,
    kc_ref,
    vc_ref,
    cos_ref,
    sin_ref,
    cosl_ref,
    sinl_ref,
    cosr_ref,
    sinr_ref,
    qmark_ref,
    kmark_ref,
    o_ref,
    dq_ref,
    down_ref,
    dnear_ref,
    dfar_key_ref,
    dfar_value_ref,
    akl,
    avl,
    akr,
    avr,
):
    step = pl.program_id(0)
    last = pl.num_programs(0) - 1
    near = kl_ref.shape[0]

    @pl.when(step == 0)
    def _():
        for acc in (akl, avl, akr, avr):
            acc[...] = jnp.zeros_like(acc)

    query, grad = q_ref[...], do_ref[...]

    def work(own):
        scores = [contract_rows(query, kl_ref[...]), contract_rows(query, kr_ref[...])]
        if own:
            mine = contract_rows(query, kc_ref[...])
            at_row = lax.broadcasted_iota(jnp.int32, mine.shape, 0)
            at_col = lax.broadcasted_iota(jnp.int32, mine.shape, 1)
            scores.append(jnp.where(at_col <= at_row, mine, NEG_FILL))
        else:
            marks = kmark_ref[...]
            own_mark = qmark_ref[...]
            scores[0] = jnp.where(marks[:, :near] <= own_mark, scores[0], NEG_FILL)
            scores[1] = jnp.where(marks[:, near:] <= own_mark, scores[1], NEG_FILL)
        top = scores[0].max(axis=1, keepdims=True)
        for part in scores[1:]:
            top = jnp.maximum(top, part.max(axis=1, keepdims=True))
        probs = [jnp.exp(part - top) for part in scores]
        total = probs[0].sum(axis=1, keepdims=True)
        for part in probs[1:]:
            total = total + part.sum(axis=1, keepdims=True)
        share = 1.0 / total
        probs = [part * share for part in probs]
        low = [part.astype(BF) for part in probs]
        values = [vl_ref, vr_ref] + ([vc_ref] if own else [])
        keys = [kl_ref, kr_ref] + ([kc_ref] if own else [])
        mixed = matmul_nn(low[0], values[0][...])
        for part, ref in zip(low[1:], values[1:]):
            mixed = mixed + matmul_nn(part, ref[...])
        o_ref[...] = mixed.astype(BF)
        prob_grad = [contract_rows(grad, ref[...]) for ref in values]
        delta = (probs[0] * prob_grad[0]).sum(axis=1, keepdims=True)
        for part, grad_part in zip(probs[1:], prob_grad[1:]):
            delta = delta + (part * grad_part).sum(axis=1, keepdims=True)
        slopes = [
            (part * (grad_part - delta)).astype(BF) for part, grad_part in zip(probs, prob_grad)
        ]
        query_grad = matmul_nn(slopes[0], keys[0][...])
        for part, ref in zip(slopes[1:], keys[1:]):
            query_grad = query_grad + matmul_nn(part, ref[...])
        query_grad = query_grad * (1.0 / math.sqrt(HEAD))
        dq_ref[...] = turned(query_grad, cos_ref[...], -sin_ref[...]).astype(BF)
        akl[...] += contract_cols(slopes[0], query)
        akr[...] += contract_cols(slopes[1], query)
        avl[...] += contract_cols(low[0], grad)
        avr[...] += contract_cols(low[1], grad)
        if own:
            key_grad = contract_cols(slopes[2], query)
            down_ref[:, :HEAD] = turned(key_grad, cos_ref[...], -sin_ref[...]).astype(BF)
            down_ref[:, HEAD:] = contract_cols(low[2], grad).astype(BF)

    @pl.when(step < TP)
    def _():
        work(False)

    @pl.when(step >= TP)
    def _():
        work(True)

    @pl.when(step == last)
    def _():
        dnear_ref[:, :HEAD] = turned(akl[...], cosl_ref[...], -sinl_ref[...])
        dnear_ref[:, HEAD:] = avl[...]
        dfar_key_ref[...] = turned(akr[...], cosr_ref[...], -sinr_ref[...]).astype(BF)
        dfar_value_ref[...] = avr[...].astype(BF)


def attend(
    head, queries, grads, near, far, own, tables, near_tables, far_tables, query_mark, key_mark
):
    total = queries.shape[0]
    tile = total // (2 * TP)
    keys = near[0].shape[0]

    def row_tile(j):
        return j

    def cont_tile(j):
        return jnp.maximum(j - TP, 0)

    query_spec = pl.BlockSpec((tile, HEAD), lambda j: (row_tile(j), 0))
    row_spec = pl.BlockSpec((tile, HEAD), lambda j: (row_tile(j), head))
    out_spec = pl.BlockSpec((tile, HEAD), lambda j: (row_tile(j), 0))
    key_spec = pl.BlockSpec((keys, HEAD), lambda j: (0, 0))
    own_key = pl.BlockSpec((tile, HEAD), lambda j: (cont_tile(j), 0))
    own_value = pl.BlockSpec((tile, HEAD), lambda j: (cont_tile(j), 1))
    own_both = pl.BlockSpec((tile, 2 * HEAD), lambda j: (cont_tile(j), 0))
    both = pl.BlockSpec((keys, 2 * HEAD), lambda j: (0, 0))
    table_spec = pl.BlockSpec((tile, LANES), lambda j: (row_tile(j), 0))
    key_table = pl.BlockSpec((keys, LANES), lambda j: (0, 0))
    mark_spec = pl.BlockSpec((tile, 1), lambda j: (row_tile(j), 0))
    key_mark_spec = pl.BlockSpec((1, 2 * keys), lambda j: (0, 0))
    wide = jax.ShapeDtypeStruct((total, HEAD), BF)
    return pl.pallas_call(
        attention_body,
        grid=(2 * TP,),
        in_specs=[
            query_spec,
            row_spec,
            key_spec,
            key_spec,
            key_spec,
            key_spec,
            own_key,
            own_value,
            table_spec,
            table_spec,
            key_table,
            key_table,
            key_table,
            key_table,
            mark_spec,
            key_mark_spec,
        ],
        out_specs=[out_spec, out_spec, own_both, both, key_spec, key_spec],
        out_shape=[
            wide,
            wide,
            jax.ShapeDtypeStruct((keys, 2 * HEAD), BF),
            jax.ShapeDtypeStruct((keys, 2 * HEAD), F32),
            jax.ShapeDtypeStruct((keys, HEAD), BF),
            jax.ShapeDtypeStruct((keys, HEAD), BF),
        ],
        scratch_shapes=[pltpu.VMEM((keys, HEAD), F32)] * 4,
        compiler_params=pltpu.CompilerParams(vmem_limit_bytes=56 << 20),
        cost_estimate=cost("attention_both_ways"),
        name="attention_both_ways",
    )(
        queries,
        grads,
        *near,
        *far,
        own,
        own,
        *tables,
        *near_tables,
        *far_tables,
        query_mark,
        key_mark,
    )


def join_grads(query_grads, own_grads, near_grads, far_keys, far_values):
    total = query_grads[0].shape[0]
    tile = total // 4

    def body(*refs):
        out_ref, sum_ref = refs[-2:]
        dq, down, dnear, dfar_key, dfar_value = (
            refs[i * HEADS_HERE : (i + 1) * HEADS_HERE] for i in range(5)
        )
        step = pl.program_id(0)

        @pl.when(step == 0)
        def _():
            sum_ref[...] = jnp.zeros_like(sum_ref)

        for head in range(HEADS_HERE):
            at = head * HEAD
            key_at, value_at = slice(HCOLS + at, HCOLS + at + HEAD), slice(
                2 * HCOLS + at, 2 * HCOLS + at + HEAD
            )
            out_ref[:, at : at + HEAD] = dq[head][...]

            @pl.when(step < 2)
            def _(head=head, key_at=key_at, value_at=value_at):
                near = dnear[head][...]
                out_ref[:, key_at] = (near[:, :HEAD] + dfar_key[head][...].astype(F32)).astype(BF)
                out_ref[:, value_at] = (near[:, HEAD:] + dfar_value[head][...].astype(F32)).astype(BF)

            @pl.when(step >= 2)
            def _(head=head, key_at=key_at, value_at=value_at):
                out_ref[:, key_at] = down[head][:, :HEAD]
                out_ref[:, value_at] = down[head][:, HEAD:]

        sum_ref[...] += out_ref[...].astype(F32).sum(axis=0, keepdims=True)

    prompt_spec, cont_spec = part_specs(total // 2, tile, 2 * HEAD, 2)
    far_spec, _ = part_specs(total // 2, tile, HEAD, 2)
    return pl.pallas_call(
        body,
        grid=(4,),
        in_specs=[
            *([pl.BlockSpec((tile, HEAD), lambda i: (i, 0))] * HEADS_HERE),
            *([cont_spec] * HEADS_HERE),
            *([prompt_spec] * HEADS_HERE),
            *([far_spec] * (2 * HEADS_HERE)),
        ],
        out_specs=[
            pl.BlockSpec((tile, 3 * HCOLS), lambda i: (i, 0)),
            pl.BlockSpec((1, 3 * HCOLS), lambda i: (0, 0)),
        ],
        out_shape=[
            jax.ShapeDtypeStruct((total, 3 * HCOLS), BF),
            jax.ShapeDtypeStruct((1, 3 * HCOLS), F32),
        ],
        compiler_params=pltpu.CompilerParams(vmem_limit_bytes=56 << 20),
        cost_estimate=cost("join_grads"),
        name="join_grads",
    )(*query_grads, *own_grads, *near_grads, *far_keys, *far_values)


class Values:
    pass


def square_plan(
    prompt,
    conts,
    assignment,
    offsets,
    ln1_gain,
    ln1_bias,
    ln2_gain,
    ln2_bias,
    qkv_weight,
    qkv_bias,
    out_weight,
    out_bias,
    up_weight,
    up_bias,
    down_weight,
    down_bias,
    prompt_cot,
    cont_cot,
):
    block, cont_rows = prompt.shape[1], conts.shape[2]
    shard = qkv_weight.shape[0]
    ff = up_weight.shape[1]
    ff_here = ff // TP
    half = D // 2
    grp_index, seq_index = lax.axis_index("grp"), lax.axis_index("seq")
    tp_rank, z_half = seq_index & 3, seq_index >> 2
    place_index = grp_index * 2 + z_half

    v = Values()


    branch_ids = jnp.arange(offsets.shape[1], dtype=jnp.int32)
    my_offset = jnp.sum(jnp.where(branch_ids == assignment[0, 0], offsets[0], 0)).reshape(1, 1)
    v.offsets = jnp.concatenate(
        [my_offset if bits == 0 else swap_seq(my_offset, bits) for bits in CONT_ORDER], axis=0
    )
    own1, v.side1, far1 = split_columns([qkv_weight, out_weight.T], [3, 1], tp_rank)
    v.got1_y = swap_seq(v.side1, 1)
    v.own_a, v.own_b = reorder_runs([prompt[0], conts[0, 0]], place_index)
    own2, v.side2, far2 = split_columns([up_weight], [1], tp_rank)
    v.got1_y, v.side2 = tie(v.got1_y, v.side2)
    v.got1_z = swap_seq(onward(far1, v.got1_y), 2)
    v.got2_y = swap_seq(v.side2, 1)
    own3, v.side3, far3 = split_columns([down_weight.T], [1], tp_rank)
    qkv_bias_here = pick(qkv_bias.reshape(3, TP, HCOLS), tp_rank, 1).reshape(1, 3 * HCOLS)
    up_bias_here = pick(up_bias.reshape(TP, ff_here), tp_rank, 0)[None]
    vectors = jnp.stack([ln1_gain, ln1_bias, ln2_gain, ln2_bias, out_bias + down_bias])
    vectors = jnp.concatenate([vectors, jnp.zeros((3, D), F32)], axis=0)
    (v.vectors,) = reorder_runs([vectors], place_index)
    prompt_ranks = (tp_rank ^ jnp.array(PROMPT_ORDER, dtype=jnp.int32))[:, None]
    prompt_iota = jnp.arange(block, dtype=jnp.int32)[None, :]
    cont_iota = jnp.arange(cont_rows, dtype=jnp.int32)[None, :]
    near_mark = ((z_half * TP + prompt_ranks) * block + prompt_iota).reshape(-1)
    far_mark = (((z_half ^ 1) * TP + prompt_ranks) * block + prompt_iota).reshape(-1)
    cont_positions = (PROMPT + cont_iota + v.offsets).reshape(-1)
    v.mark = jnp.concatenate([near_mark, cont_positions]).astype(F32)
    query_mark = jnp.concatenate([near_mark, near_mark]).reshape(-1, 1)
    key_mark = jnp.concatenate([near_mark, far_mark]).reshape(1, -1)
    (
        v.got1_z, v.got2_y, v.own_a, v.own_b, v.side3, v.offsets,
    ) = tie(
        v.got1_z, v.got2_y, v.own_a, v.own_b, v.side3, v.offsets,
    )
    v.base1a, v.base1b = stack_ranks(
        own1, v.got1_y, v.got1_z, (2 * HCOLS,) * 2, tp_rank
    )
    v.rows_az = swap_seq(v.own_a, 2)
    v.rows_ay = swap_seq(v.own_a, 1)
    v.z1a = swap_seq(v.base1a, 4)
    v.x1a = swap_grp(v.base1a, 2)
    v.send2 = onward(far2, v.got2_y)
    v.cot0, v.cot1 = prompt_cot[0], cont_cot[0, 0]
    v.cot0, v.cot1, v.base1b = tie(v.cot0, v.cot1, v.base1b)
    v.cot_a, v.cot_b, cot_sum = reorder_runs([v.cot0, v.cot1], place_index, sums=True)
    (
        v.rows_az, v.rows_ay, v.z1a, v.x1a, v.send2, v.base1b, v.own_b, v.cot_a, v.cot_b, v.mark,
    ) = tie(
        v.rows_az, v.rows_ay, v.z1a, v.x1a, v.send2, v.base1b, v.own_b, v.cot_a, v.cot_b, v.mark,
    )
    v.z1b = swap_seq(v.base1b, 4)
    v.got2_z = swap_seq(v.send2, 2)
    v.rows_by = swap_seq(v.own_b, 1)
    v.x1b = swap_grp(v.base1b, 2)
    v.zx1a = swap_grp(v.z1a, 2)
    v.base2a, v.base2b, v.base2 = stack_ranks(
        own2, v.got2_y, v.got2_z, (ff_here // 2,) * 2, tp_rank, True
    )
    tables = rotary_tables(v.mark)
    far_tables = rotary_tables(far_mark.astype(F32))
    v.tables0, v.tables1 = tables
    v.far0, v.far1 = far_tables
    (
        v.vectors, v.z1b, v.base2a, v.base2b, v.base2, v.rows_by, v.x1b, v.zx1a, v.rows_az,
        v.own_b, v.side3, v.tables0, v.tables1, v.far0, v.far1,
    ) = tie(
        v.vectors, v.z1b, v.base2a, v.base2b, v.base2, v.rows_by, v.x1b, v.zx1a, v.rows_az,
        v.own_b, v.side3, v.tables0, v.tables1, v.far0, v.far1,
    )
    tables, far_tables = (v.tables0, v.tables1), (v.far0, v.far1)
    shared = (tables, tables, far_tables, query_mark, key_mark)
    v.got3_y = swap_seq(v.side3, 1)
    v.rows_azy = swap_seq(v.rows_az, 1)
    v.rows_bz = swap_seq(v.own_b, 2)
    v.zx1b = swap_grp(v.z1b, 2)
    v.z2a = swap_seq(v.base2a, 4)
    (
        v.z2a, v.rows_azy, v.rows_bz, v.zx1b, v.got3_y, v.base2b, v.base2,
    ) = tie(
        v.z2a, v.rows_azy, v.rows_bz, v.zx1b, v.got3_y, v.base2b, v.base2,
    )
    v.rows_bzy = swap_seq(v.rows_bz, 1)
    v.z2b = swap_seq(v.base2b, 4)
    v.x2 = swap_grp(v.base2, 2)
    v.got3_z = swap_seq(onward(far3, v.got3_y), 2)
    v.base3a, v.base3b, v.base3 = stack_ranks(
        own3, v.got3_y, v.got3_z, (ff_here // 2,) * 2, tp_rank, True
    )
    v.core1 = beside(
        [(v.base1a, v.base1b), (v.z1a, v.z1b), (v.x1a, v.x1b), (v.zx1a, v.zx1b)]
    )
    gain1, bias1, gain2, bias2, bias_out = (v.vectors[i : i + 1] for i in range(5))
    (
        v.rows_bzy, v.z2a, v.z2b, v.x2, v.base3a, v.base3b, v.base3, v.core1, v.cot_a, v.cot_b,
    ) = tie(
        v.rows_bzy, v.z2a, v.z2b, v.x2, v.base3a, v.base3b, v.base3, v.core1, v.cot_a, v.cot_b,
    )

    v.swapped1 = swap_grp(v.core1, 1)
    v.cot_az = swap_seq(v.cot_a, 2)
    v.cot_ay = swap_seq(v.cot_a, 1)
    v.zx2 = swap_grp(stacked([v.z2a, v.z2b]), 2)
    v.z3a = swap_seq(v.base3a, 4)
    v.rows, v.first_low, v.second_low, mean, spread = both_low_norms(
        [v.own_a, v.rows_az, v.rows_ay, v.rows_azy, v.own_b, v.rows_by, v.rows_bz, v.rows_bzy],
        gain1,
        bias1,
        gain2,
        bias2,
    )
    v.core2 = beside(
        [(v.base2a, v.base2b), (v.z2a, v.z2b), v.x2, v.zx2]
    )
    (
        v.first_low, v.second_low, v.core2, v.swapped1, v.core1, v.base3, v.base3b, v.cot_az,
        v.cot_ay, v.z3a, v.cot_b,
    ) = tie(
        v.first_low, v.second_low, v.core2, v.swapped1, v.core1, v.base3, v.base3b, v.cot_az,
        v.cot_ay, v.z3a, v.cot_b,
    )
    v.cot_by = swap_seq(v.cot_b, 1)
    v.cot_bz = swap_seq(v.cot_b, 2)
    v.z3b = swap_seq(v.base3b, 4)
    v.x3 = swap_grp(v.base3, 2)
    v.swapped2 = swap_grp(v.core2, 1)
    weight1 = (v.core1, v.swapped1)
    v.query0, v.key0, v.value0, own0 = project_qkv(
        0, v.first_low, weight1, qkv_bias_here, *tables
    )
    v.query0, v.first_low = tie(v.query0, v.first_low)
    v.query1, v.key1, v.value1, own1_kv = project_qkv(
        1, v.first_low, weight1, qkv_bias_here, *tables
    )
    (
        v.query1, v.second_low, v.swapped2, v.core2, v.cot_az, v.x3, v.cot_by, v.cot_bz, v.z3b,
        v.key0, v.z3a,
    ) = tie(
        v.query1, v.second_low, v.swapped2, v.core2, v.cot_az, v.x3, v.cot_by, v.cot_bz, v.z3b,
        v.key0, v.z3a,
    )
    v.cot_azy = swap_seq(v.cot_az, 1)
    v.cot_bzy = swap_seq(v.cot_by, 2)
    v.far_key0 = swap_seq(v.key0, 4)
    v.zx3 = swap_grp(stacked([v.z3a, v.z3b]), 2)
    weight2 = (v.core2, v.swapped2)
    v.act_low, v.slope = feed_forward_up(v.second_low, weight2, up_bias_here)
    (
        v.act_low, v.slope, v.cot_azy, v.cot_bzy, v.far_key0, v.zx3, v.value0,
    ) = tie(
        v.act_low, v.slope, v.cot_azy, v.cot_bzy, v.far_key0, v.zx3, v.value0,
    )
    v.far_value0 = swap_seq(v.value0, 4)
    v.core3 = beside(
        [(v.base3a, v.base3b), (v.z3a, v.z3b), v.x3, v.zx3]
    )
    v.swapped3 = swap_grp(v.core3, 1)
    v.attn_grad, v.cots = attention_grad(
        [v.cot_a, v.cot_az, v.cot_ay, v.cot_azy, v.cot_b, v.cot_by, v.cot_bz, v.cot_bzy],
        weight1,
        3,
    )
    v.attn_grad, v.cots, v.act_low = tie(v.attn_grad, v.cots, v.act_low)
    v.down_away = weight_grad(v.cots, [v.act_low])
    (
        v.down_away, v.far_value0, v.key1, v.value1, v.attn_grad, v.swapped3, v.core3,
    ) = tie(
        v.down_away, v.far_value0, v.key1, v.value1, v.attn_grad, v.swapped3, v.core3,
    )
    v.down_core = swap_grp(v.down_away, 1)
    v.far_key1 = swap_seq(v.key1, 4)
    v.attn0, dq0, down0, dnear0, v.dfar_key0, v.dfar_value0 = attend(
        0,
        v.query0,
        v.attn_grad,
        (v.key0, v.value0),
        (v.far_key0, v.far_value0),
        own0,
        *shared,
    )
    (
        v.attn0, v.down_core, v.cots, v.act_low, v.far_key1, v.value1,
    ) = tie(
        v.attn0, v.down_core, v.cots, v.act_low, v.far_key1, v.value1,
    )
    v.far_value1 = swap_seq(v.value1, 4)
    v.down_mine, v.down_send = weight_grad(v.cots, [v.act_low], v.down_core)
    (
        v.down_mine, v.down_send, v.cots, v.slope, v.core3, v.swapped3, v.dfar_key0,
    ) = tie(
        v.down_mine, v.down_send, v.cots, v.slope, v.core3, v.swapped3, v.dfar_key0,
    )
    v.back_key0 = swap_seq(v.dfar_key0, 4)
    v.down_side = swap_grp(v.down_send, 2)
    weight3 = (v.core3, v.swapped3)
    v.hidden_grad, up_bias_term = feed_forward_back(v.cots, weight3, v.slope)
    (
        v.hidden_grad, v.far_value1, v.dfar_value0, v.attn_grad,
    ) = tie(
        v.hidden_grad, v.far_value1, v.dfar_value0, v.attn_grad,
    )
    v.back_value0 = swap_seq(v.dfar_value0, 4)
    v.attn1, dq1, down1, v.dnear1, v.dfar_key1, v.dfar_value1 = attend(
        1,
        v.query1,
        v.attn_grad,
        (v.key1, v.value1),
        (v.far_key1, v.far_value1),
        own1_kv,
        *shared,
    )
    (
        v.attn1, v.second_low, v.hidden_grad, v.back_key0, v.down_side, v.down_mine,
    ) = tie(
        v.attn1, v.second_low, v.hidden_grad, v.back_key0, v.down_side, v.down_mine,
    )
    v.up_away = weight_grad(v.second_low, [v.hidden_grad])
    v.down_half_send = second_sum(v.down_mine, v.down_side)
    (
        v.up_away, v.back_value0, v.dfar_key1, v.dfar_value1, v.act_low, v.down_half_send,
    ) = tie(
        v.up_away, v.back_value0, v.dfar_key1, v.dfar_value1, v.act_low, v.down_half_send,
    )
    v.up_core = swap_grp(v.up_away, 1)
    v.back_key1 = swap_seq(v.dfar_key1, 4)
    branch = branch_outputs((v.attn0, v.attn1), v.act_low, weight1, 3, weight3)
    v.branch0, v.branch_y, v.branch_zy, v.branch2, v.branch_z, v.branch_yz = branch
    (
        v.branch0, v.branch_y, v.branch_zy, v.branch2, v.branch_z, v.branch_yz, v.up_core,
        v.second_low, v.hidden_grad, v.back_key1, v.dfar_value1,
    ) = tie(
        v.branch0, v.branch_y, v.branch_zy, v.branch2, v.branch_z, v.branch_yz, v.up_core,
        v.second_low, v.hidden_grad, v.back_key1, v.dfar_value1,
    )
    v.got_zy = swap_seq(v.branch_zy, 1)
    v.got_yz = swap_seq(v.branch_yz, 2)
    v.back_value1 = swap_seq(v.dfar_value1, 4)
    v.up_mine, v.up_send = weight_grad(v.second_low, [v.hidden_grad], v.up_core)
    v.up_mine, v.hidden_grad = tie(v.up_mine, v.hidden_grad)
    second_parts, second_sums = norm_grad(
        v.hidden_grad, weight2, gain2, v.rows, mean, spread, (0, 1, 2, 3)
    )
    v.second0, second1, second2, second3 = second_parts
    (
        v.second0, v.back_value1, v.dnear1, v.cots, v.down_half_send, v.up_send, v.got_zy,
        v.got_yz, v.branch0, v.branch2, v.branch_y, v.branch_z,
    ) = tie(
        v.second0, v.back_value1, v.dnear1, v.cots, v.down_half_send, v.up_send, v.got_zy,
        v.got_yz, v.branch0, v.branch2, v.branch_y, v.branch_z,
    )
    v.up_side = swap_grp(v.up_send, 2)
    v.down_half = swap_seq(v.down_half_send, 4)
    v.got_y = swap_seq(v.branch_y, 1)
    v.got_z = swap_seq(v.branch_z, 2)
    v.branch_a_far = second_sum(v.branch0, v.got_zy)
    v.branch_b_far = second_sum(v.branch2, v.got_yz)
    v.qkv_grad, qkv_bias_term = join_grads(
        (dq0, dq1),
        (down0, down1),
        (dnear0, v.dnear1),
        (v.back_key0, v.back_key1),
        (v.back_value0, v.back_value1),
    )
    v.qkv_grad, v.first_low, v.cots = tie(v.qkv_grad, v.first_low, v.cots)
    v.qkv_away = weight_grad(v.first_low, [v.qkv_grad])
    v.qkv_away, v.cots = tie(v.qkv_away, v.cots)
    v.out_away = weight_grad(v.cots, [v.attn0, v.attn1])
    (
        v.out_away, v.qkv_away, v.got_y, v.got_z, v.branch_a_far, v.branch_b_far, v.down_half,
        v.up_side, v.up_mine, v.qkv_grad,
    ) = tie(
        v.out_away, v.qkv_away, v.got_y, v.got_z, v.branch_a_far, v.branch_b_far, v.down_half,
        v.up_side, v.up_mine, v.qkv_grad,
    )
    v.qkv_core = swap_grp(v.qkv_away, 1)
    down_own, v.down_side2, v.down_far = split_rows(
        [(v.down_mine, v.down_side, (v.down_half,))], tp_rank
    )
    v.up_send_a = second_sum(v.up_mine, v.up_side, 0)
    v.up_half_a = swap_seq(v.up_send_a, 4)
    v.branch_far_a = swap_seq(v.branch_a_far, 2)
    v.branch_far_b = swap_seq(v.branch_b_far, 1)
    v.down_y = swap_seq(v.down_side2, 1)
    v.up_send_b = second_sum(v.up_mine, v.up_side, 1)
    (
        v.qkv_core, v.first_low, v.qkv_grad, v.up_send_b,
    ) = tie(
        v.qkv_core, v.first_low, v.qkv_grad, v.up_send_b,
    )
    v.qkv_mine, v.qkv_send = weight_grad(v.first_low, [v.qkv_grad], v.qkv_core)
    v.qkv_mine, v.qkv_send, v.qkv_grad = tie(v.qkv_mine, v.qkv_send, v.qkv_grad)
    v.qkv_side = swap_grp(v.qkv_send, 2)
    entry_far, v.far_sums = norm_grad(
        v.qkv_grad, weight1, gain1, v.rows, mean, spread, (1, 3), (second1, second3), True
    )
    v.entry_y, v.entry_zy, v.entry_z, v.entry_yz = entry_far
    (
        v.entry_y, v.entry_zy, v.entry_z, v.entry_yz, v.far_sums, v.out_away, v.branch_far_a,
        v.branch_far_b, v.down_y, v.down_far, v.up_half_a, v.up_send_b, v.qkv_grad, v.second0,
    ) = tie(
        v.entry_y, v.entry_zy, v.entry_z, v.entry_yz, v.far_sums, v.out_away, v.branch_far_a,
        v.branch_far_b, v.down_y, v.down_far, v.up_half_a, v.up_send_b, v.qkv_grad, v.second0,
    )
    v.entry_got_zy = swap_seq(v.entry_zy, 1)
    v.entry_got_yz = swap_seq(v.entry_yz, 2)
    v.out_core = swap_grp(v.out_away, 1)
    v.up_half_b = swap_seq(v.up_send_b, 4)
    (v.entry0, v.entry2), v.near_sums = norm_grad(
        v.qkv_grad, weight1, gain1, v.rows, mean, spread, (0, 2), (v.second0, second2)
    )
    (
        v.near_sums, v.out_core, v.cots, v.qkv_side, v.qkv_mine, v.up_half_b, v.branch0,
        v.entry_got_zy, v.entry_got_yz, v.entry_y, v.entry_z, v.entry0, v.entry2,
    ) = tie(
        v.near_sums, v.out_core, v.cots, v.qkv_side, v.qkv_mine, v.up_half_b, v.branch0,
        v.entry_got_zy, v.entry_got_yz, v.entry_y, v.entry_z, v.entry0, v.entry2,
    )
    v.entry_got_y = swap_seq(v.entry_y, 1)
    v.entry_got_z = swap_seq(v.entry_z, 2)
    v.qkv_half_send = second_sum(v.qkv_mine, v.qkv_side)
    v.qkv_half = swap_seq(v.qkv_half_send, 4)
    v.out_mine, v.out_send = weight_grad(
        v.cots, [v.attn0, v.attn1], v.out_core
    )
    v.out_side = swap_grp(v.out_send, 2)

    rank_ids = jnp.arange(TP, dtype=jnp.int32)
    first_sums = v.far_sums + v.near_sums
    wide_sums = jnp.concatenate(
        [first_sums[:2], second_sums[:2], cot_sum, jnp.zeros((3, D), F32)], axis=0
    )
    wide_sums = restore_runs(wide_sums, place_index)
    qkv_bias_term = qkv_bias_term.reshape(3, 1, HCOLS)
    v.sums = jnp.concatenate(
        [
            wide_sums[:5].reshape(-1),
            jnp.where((rank_ids == tp_rank)[None, :, None], qkv_bias_term, 0.0).reshape(-1),
            jnp.where((rank_ids == tp_rank)[:, None], up_bias_term, 0.0).reshape(-1),
        ]
    ).reshape(-1, LANES)
    v.sums_got = swap_grp(v.sums, 1)
    v.entry_a_far = second_sum(v.entry0, v.entry_got_zy)
    v.entry_b_far = second_sum(v.entry2, v.entry_got_yz)
    (
        v.sums, v.sums_got, v.out_send, v.out_mine, v.entry_got_y, v.entry_got_z, v.entry_a_far,
        v.entry_b_far, v.branch0, v.up_half_b,
    ) = tie(
        v.sums, v.sums_got, v.out_send, v.out_mine, v.entry_got_y, v.entry_got_z, v.entry_a_far,
        v.entry_b_far, v.branch0, v.up_half_b,
    )
    v.entry_far_a = swap_seq(v.entry_a_far, 2)
    v.entry_far_b = swap_seq(v.entry_b_far, 1)
    v.sums = v.sums + v.sums_got
    v.sums_got = swap_grp(v.sums, 2)
    v.layer_a, v.layer_b = finish_outputs(
        (
            (v.branch0, v.got_y, v.branch_far_a),
            (v.branch2, v.got_z, v.branch_far_b),
        ),
        (v.own_a, v.own_b),
        bias_out,
        place_index,
    )
    up_own, v.up_side2, v.up_far = split_rows(
        [(v.up_mine, v.up_side, (v.up_half_a, v.up_half_b))], tp_rank
    )
    (
        v.layer_a, v.sums, v.sums_got, v.up_side2, v.out_side, v.out_mine, v.qkv_half,
    ) = tie(
        v.layer_a, v.sums, v.sums_got, v.up_side2, v.out_side, v.out_mine, v.qkv_half,
    )
    v.out_half_send = second_sum(v.out_mine, v.out_side)
    v.out_half = swap_seq(v.out_half_send, 4)
    v.up_y = swap_seq(v.up_side2, 1)
    v.sums = v.sums + v.sums_got
    v.sums_got = swap_seq(v.sums, 4)
    (
        v.entry_far_a, v.entry_far_b, v.out_half, v.up_y, v.up_far, v.down_far, v.sums,
        v.sums_got,
    ) = tie(
        v.entry_far_a, v.entry_far_b, v.out_half, v.up_y, v.up_far, v.down_far, v.sums,
        v.sums_got,
    )
    late_own, late_side, late_far = split_rows(
        [
            (v.qkv_mine, v.qkv_side, (v.qkv_half,)),
            (v.out_mine, v.out_side, (v.out_half,)),
        ],
        tp_rank,
    )
    v.late_y = swap_seq(late_side, 1)
    v.down_z = swap_seq(onward(v.down_far, v.down_y), 2)
    v.up_z = swap_seq(onward(v.up_far, v.up_y), 2)
    v.sums = v.sums + v.sums_got
    v.sums_got = swap_seq(v.sums, 1)
    v.grad_a, grad_b = finish_grads(
        (
            (v.entry0, v.entry_got_y, v.entry_far_a),
            (v.entry2, v.entry_got_z, v.entry_far_b),
        ),
        (v.own_a, v.own_b),
        (v.cot_a, v.cot_b),
        place_index,
    )
    (
        v.grad_a, v.late_y, v.down_z, v.up_z, v.sums, v.sums_got,
    ) = tie(
        v.grad_a, v.late_y, v.down_z, v.up_z, v.sums, v.sums_got,
    )
    v.late_z = swap_seq(onward(late_far, v.late_y), 2)
    v.sums = v.sums + v.sums_got
    v.sums_got = swap_seq(v.sums, 2)
    (v.down_grad,) = join_columns(
        down_own, v.down_y, v.down_z, [(1, ff_here)], tp_rank
    )
    (v.up_grad,) = join_columns(up_own, v.up_y, v.up_z, [(1, ff_here)], tp_rank)
    grad_a, down_grad, up_weight_grad = v.grad_a, v.down_grad, v.up_grad
    qkv_weight_grad, out_grad = join_columns(
        late_own, v.late_y, v.late_z, [(3, HCOLS), (1, HCOLS)], tp_rank
    )
    down_weight_grad, out_weight_grad = down_grad.T, out_grad.T
    sums = (v.sums + v.sums_got).reshape(-1)
    cuts = np.cumsum([D, D, D, D, D, 3 * D])
    gain_one, shift_one, gain_two, shift_two, out_sum, qkv_sum, up_sum = jnp.split(sums, cuts)

    return (
        v.layer_a[None],
        v.layer_b[None, None],
        grad_a[None],
        grad_b[None, None],
        gain_one,
        shift_one,
        gain_two,
        shift_two,
        qkv_weight_grad,
        qkv_sum,
        out_weight_grad,
        out_sum,
        up_weight_grad,
        up_sum,
        down_weight_grad,
        out_sum,
    )


def solution(mesh):
    in_specs = (
        P("grp", "seq", None),
        P("grp", "seq", None, None),
        P("grp", "seq"),
        P("grp", None),
        P(),
        P(),
        P(),
        P(),
        P(("grp", "seq"), None),
        P(),
        P(None, ("grp", "seq")),
        P(),
        P(("grp", "seq"), None),
        P(),
        P(None, ("grp", "seq")),
        P(),
        P("grp", "seq", None),
        P("grp", "seq", None, None),
    )
    out_specs = (
        P("grp", "seq", None),
        P("grp", "seq", None, None),
        P("grp", "seq", None),
        P("grp", "seq", None, None),
        P(),
        P(),
        P(),
        P(),
        P(("grp", "seq"), None),
        P(),
        P(None, ("grp", "seq")),
        P(),
        P(("grp", "seq"), None),
        P(),
        P(None, ("grp", "seq")),
        P(),
    )
    plan = square_plan if (mesh.shape["grp"], mesh.shape["seq"]) == (4, 8) else local
    return jax.shard_map(plan, mesh=mesh, in_specs=in_specs, out_specs=out_specs, check_vma=False)
```

```python
from functools import partial
import math

import jax
import jax.numpy as jnp
import numpy as np
from jax import lax
from jax.experimental import pallas as pl
from jax.experimental.pallas import tpu as pltpu
from jax.sharding import PartitionSpec as P

D = 2048
HEADS = 8
HEAD = 256
ROT = 64
PROMPT = 2048


EPSILON = 1e-05
NEG_FILL = -1e30
ROPE_BASE = 10000.0


def layer_norm(values, ln_gain, ln_shift):
    center = values - jnp.mean(values, axis=-1, keepdims=True)
    normed = center * lax.rsqrt(jnp.mean(center * center, axis=-1, keepdims=True) + EPSILON)
    return normed * ln_gain + ln_shift


def both_norms(values, gain_one, shift_one, gain_two, shift_two):
    return (layer_norm(values, gain_one, shift_one), layer_norm(values, gain_two, shift_two))


def rotate(head_data, positions, sign_flip):
    half_rot = ROT // 2
    inv_freq = ROPE_BASE ** (-(2.0 * jnp.arange(half_rot, dtype=jnp.float32)) / ROT)
    angles = positions[:, None] * inv_freq[None, :]
    cos_table = jnp.cos(angles)[:, None, :]
    sin_table = sign_flip * jnp.sin(angles)[:, None, :]
    first_half = head_data[..., :half_rot]
    second = head_data[..., half_rot:ROT]
    return jnp.concatenate(
        [
            first_half * cos_table - second * sin_table,
            second * cos_table + first_half * sin_table,
            head_data[..., ROT:],
        ],
        axis=-1,
    )


def contract_rows(left, right):
    return lax.dot_general(
        left, right, (((1,), (1,)), ((), ())), preferred_element_type=jnp.float32
    )


def contract_cols(left, right):
    return lax.dot_general(
        left, right, (((0,), (0,)), ((), ())), preferred_element_type=jnp.float32
    )


def local(
    prompt,
    conts,
    assignment,
    offsets,
    ln1_gain,
    ln1_bias,
    ln2_gain,
    ln2_bias,
    qkv_weight,
    qkv_bias,
    out_weight,
    out_bias,
    up_weight,
    up_bias,
    down_weight,
    down_bias,
    prompt_cot,
    cont_cot,
):
    prompt_rows = prompt.shape[1]
    cont_rows = conts.shape[2]
    row_total = prompt_rows + cont_rows
    score_scale = 1.0 / math.sqrt(HEAD)
    shard_index = lax.axis_index("seq")
    tokens = jnp.concatenate([prompt[0], conts[0, 0]], axis=0).astype(jnp.float32)
    branch_ids = jnp.arange(offsets.shape[1], dtype=jnp.int32)
    my_offset = jnp.sum(jnp.where(branch_ids == assignment[0, 0], offsets[0], 0))
    prompt_mark = shard_index * prompt_rows + jnp.arange(prompt_rows, dtype=jnp.int32)
    cont_mark = PROMPT + jnp.arange(cont_rows, dtype=jnp.int32)
    query_mark = jnp.concatenate([prompt_mark, cont_mark])
    positions = jnp.concatenate([prompt_mark, cont_mark + my_offset]).astype(jnp.float32)
    (first_norm, second_norm), norm_pullback = jax.vjp(
        both_norms, tokens, ln1_gain, ln1_bias, ln2_gain, ln2_bias
    )
    first_low = first_norm.astype(jnp.bfloat16)
    second_low = second_norm.astype(jnp.bfloat16)
    qkv_full, up_full = (
        lax.all_gather(qkv_weight, ("grp", "seq"), axis=0, tiled=True),
        lax.all_gather(up_weight, ("grp", "seq"), axis=0, tiled=True),
    )
    qkv_acc = jnp.dot(first_low, qkv_full, preferred_element_type=jnp.float32)
    up_acc = jnp.dot(second_low, up_full, preferred_element_type=jnp.float32)
    split_qkv = (qkv_acc + qkv_bias).reshape(row_total, 3, HEADS, HEAD)
    queries = rotate(split_qkv[:, 0], positions, 1.0).astype(jnp.bfloat16)
    keys_rot = rotate(split_qkv[:, 1], positions, 1.0).astype(jnp.bfloat16)
    values_low = split_qkv[:, 2].astype(jnp.bfloat16)
    hidden_pre = up_acc + up_bias
    activated, gelu_pullback = jax.vjp(partial(jax.nn.gelu, approximate=False), hidden_pre)
    act_low = activated.astype(jnp.bfloat16)

    def score_block(key_block, key_mark):
        raw_scores = (
            jnp.einsum("qhd,khd->hqk", queries, key_block, preferred_element_type=jnp.float32)
            * score_scale
        )
        allowed = key_mark[None, :] <= query_mark[:, None]
        return (raw_scores, allowed)

    def absorb(soft_state, key_block, value_block, key_mark):
        run_max, run_sum, run_acc = soft_state
        raw_scores, allowed = score_block(key_block, key_mark)
        masked = jnp.where(allowed[None], raw_scores, NEG_FILL)
        new_max = jnp.maximum(run_max, jnp.max(masked, axis=-1))
        exp_scores = jnp.where(allowed[None], jnp.exp(masked - new_max[..., None]), 0.0)
        factor = jnp.exp(run_max - new_max)
        mixed_heads = jnp.einsum(
            "hqk,khd->qhd",
            exp_scores.astype(jnp.bfloat16),
            value_block,
            preferred_element_type=jnp.float32,
        )
        return (
            new_max,
            run_sum * factor + jnp.sum(exp_scores, axis=-1),
            run_acc * factor.T[:, :, None] + mixed_heads,
        )

    cont_keys = keys_rot[prompt_rows:]
    cont_values = values_low[prompt_rows:]
    start_state = (
        jnp.full((HEADS, row_total), NEG_FILL, jnp.float32),
        jnp.zeros((HEADS, row_total), jnp.float32),
        jnp.zeros((row_total, HEADS, HEAD), jnp.float32),
    )
    start_state = absorb(start_state, cont_keys, cont_values, cont_mark)
    prompt_keys_send = keys_rot[:prompt_rows].reshape(prompt_rows, D)
    prompt_values_send = values_low[:prompt_rows].reshape(prompt_rows, D)
    key_piece = lax.all_gather(prompt_keys_send, "seq", axis=0, tiled=True)
    value_piece = lax.all_gather(prompt_values_send, "seq", axis=0, tiled=True)
    piece_width = key_piece.shape[0]
    key_mark = jnp.arange(piece_width, dtype=jnp.int32)
    run_max, run_sum, run_acc = absorb(
        start_state,
        key_piece.reshape(piece_width, HEADS, HEAD),
        value_piece.reshape(piece_width, HEADS, HEAD),
        key_mark,
    )
    attention = run_acc / run_sum.T[:, :, None]
    log_total = run_max + jnp.log(run_sum)
    attention_low = attention.reshape(row_total, D).astype(jnp.bfloat16)
    out_full, down_full = (
        lax.all_gather(out_weight, ("grp", "seq"), axis=1, tiled=True),
        lax.all_gather(down_weight, ("grp", "seq"), axis=1, tiled=True),
    )
    branch_sum = jnp.dot(attention_low, out_full, preferred_element_type=jnp.float32) + jnp.dot(
        act_low, down_full, preferred_element_type=jnp.float32
    )
    layer_out = tokens + branch_sum + out_bias + down_bias
    grad_out = jnp.concatenate([prompt_cot[0], cont_cot[0, 0]], axis=0)
    grad_f32 = grad_out.astype(jnp.float32)
    bias_out_term = jnp.sum(grad_f32, axis=0)
    out_again, down_again = (
        lax.all_gather(out_weight, ("grp", "seq"), axis=1, tiled=True),
        lax.all_gather(down_weight, ("grp", "seq"), axis=1, tiled=True),
    )
    attn_grad = contract_rows(grad_out, out_again)
    act_grad = contract_rows(grad_out, down_again)
    attn_grad_low = attn_grad.astype(jnp.bfloat16)
    (hidden_grad,) = gelu_pullback(act_grad)
    hidden_grad_low = hidden_grad.astype(jnp.bfloat16)
    up_bias_term = jnp.sum(hidden_grad_low.astype(jnp.float32), axis=0)
    grad_heads = attn_grad_low.reshape(row_total, HEADS, HEAD)
    row_delta = jnp.sum(grad_heads.astype(jnp.float32) * attention, axis=-1).T

    def back_block(key_block, value_block, key_mark):
        raw_scores, allowed = score_block(key_block, key_mark)
        probabilities = jnp.exp(
            jnp.where(allowed[None], raw_scores - log_total[..., None], NEG_FILL)
        )
        prob_grad = jnp.einsum(
            "qhd,khd->hqk", grad_heads, value_block, preferred_element_type=jnp.float32
        )
        score_grad = (probabilities * (prob_grad - row_delta[..., None])).astype(jnp.bfloat16)
        query_term = (
            jnp.einsum("hqk,khd->qhd", score_grad, key_block, preferred_element_type=jnp.float32)
            * score_scale
        )
        key_term = (
            jnp.einsum("hqk,qhd->khd", score_grad, queries, preferred_element_type=jnp.float32)
            * score_scale
        )
        value_term = jnp.einsum(
            "hqk,qhd->khd",
            probabilities.astype(jnp.bfloat16),
            grad_heads,
            preferred_element_type=jnp.float32,
        )
        return (query_term, key_term, value_term)

    query_local, key_local, value_local = back_block(cont_keys, cont_values, cont_mark)
    gathered_keys, gathered_values = (
        lax.all_gather(prompt_keys_send, "seq", axis=0, tiled=True),
        lax.all_gather(prompt_values_send, "seq", axis=0, tiled=True),
    )
    key_block_size = min(512, PROMPT)
    block_count = PROMPT // key_block_size

    def scan_step(query_total, inputs):
        key_block, value_block, block_start = inputs
        key_mark = block_start + jnp.arange(key_block_size, dtype=jnp.int32)
        query_term, key_term, value_term = back_block(
            key_block.reshape(key_block_size, HEADS, HEAD),
            value_block.reshape(key_block_size, HEADS, HEAD),
            key_mark,
        )
        return (
            query_total + query_term,
            (key_term.reshape(key_block_size, D), value_term.reshape(key_block_size, D)),
        )

    query_grad, (key_terms, value_terms) = lax.scan(
        scan_step,
        query_local,
        (
            gathered_keys.reshape(block_count, key_block_size, D),
            gathered_values.reshape(block_count, key_block_size, D),
            jnp.arange(block_count, dtype=jnp.int32) * key_block_size,
        ),
    )
    key_prompt_grad, value_prompt_grad = (
        lax.psum_scatter(
            key_terms.reshape(PROMPT, D).astype(jnp.bfloat16),
            "seq",
            scatter_dimension=0,
            tiled=True,
        ).astype(jnp.float32),
        lax.psum_scatter(
            value_terms.reshape(PROMPT, D).astype(jnp.bfloat16),
            "seq",
            scatter_dimension=0,
            tiled=True,
        ).astype(jnp.float32),
    )
    key_grad = jnp.concatenate([key_prompt_grad, key_local.reshape(cont_rows, D)], axis=0).reshape(
        row_total, HEADS, HEAD
    )
    value_grad = jnp.concatenate(
        [value_prompt_grad, value_local.reshape(cont_rows, D)], axis=0
    ).reshape(row_total, HEADS, HEAD)
    qkv_grad = (
        jnp.stack(
            [rotate(query_grad, positions, -1.0), rotate(key_grad, positions, -1.0), value_grad],
            axis=1,
        )
        .reshape(row_total, 3 * D)
        .astype(jnp.bfloat16)
    )
    qkv_bias_term = jnp.sum(qkv_grad.astype(jnp.float32), axis=0)
    qkv_again, up_again = (
        lax.all_gather(qkv_weight, ("grp", "seq"), axis=0, tiled=True),
        lax.all_gather(up_weight, ("grp", "seq"), axis=0, tiled=True),
    )
    first_grad = contract_rows(qkv_grad, qkv_again)
    second_grad = contract_rows(hidden_grad_low, up_again)
    token_grad, gain_one, shift_one, gain_two, shift_two = norm_pullback((first_grad, second_grad))
    token_grad = token_grad + grad_f32
    small_sums = lax.psum(
        (gain_one, shift_one, gain_two, shift_two, qkv_bias_term, bias_out_term, up_bias_term),
        ("grp", "seq"),
    )
    out_sources = jnp.concatenate([attention_low, act_low], axis=1)
    in_group = lax.psum_scatter(
        jnp.concatenate(
            [contract_cols(first_low, qkv_grad), contract_cols(second_low, hidden_grad_low)], axis=1
        ).astype(jnp.bfloat16),
        "grp",
        scatter_dimension=0,
        tiled=True,
    )
    in_share = lax.psum_scatter(in_group, "seq", scatter_dimension=0, tiled=True).astype(
        jnp.float32
    )
    out_group = lax.psum_scatter(
        contract_cols(grad_out, out_sources).astype(jnp.bfloat16),
        "grp",
        scatter_dimension=0,
        tiled=True,
    )
    out_share = lax.psum_scatter(out_group, "seq", scatter_dimension=0, tiled=True).astype(
        jnp.float32
    )
    qkv_weight_grad = in_share[:, : 3 * D]
    up_weight_grad = in_share[:, 3 * D :]
    out_weight_grad = out_share[:, :D].T
    down_weight_grad = out_share[:, D:].T
    prompt_result = layer_out[:prompt_rows][None]
    cont_result = layer_out[prompt_rows:][None, None]
    prompt_grad = token_grad[:prompt_rows][None]
    cont_grad = token_grad[prompt_rows:][None, None]
    return (
        prompt_result,
        cont_result,
        prompt_grad,
        cont_grad,
        small_sums[0],
        small_sums[1],
        small_sums[2],
        small_sums[3],
        qkv_weight_grad,
        small_sums[4],
        out_weight_grad,
        small_sums[5],
        up_weight_grad,
        small_sums[6],
        down_weight_grad,
        small_sums[5],
    )


PROMPT_ORDER = (0, 2, 1, 3)
CONT_ORDER = (0, 1, 2, 3)
WIDTH_ORDER = (0, 1, 4, 5, 2, 3, 6, 7)
TP = 4
HEADS_HERE = HEADS // TP
HCOLS = HEADS_HERE * HEAD
LANES = 128
COST_UNIT = 1.0e6
COSTS = {
    "norms": 15,
    "qkv_rotary": 12,
    "feed_forward_up": 30,
    "attention_grad": 11,
    "weight_grad": 14,
    "attention_both_ways": 28,
    "feed_forward_back": 25,
    "branch_outputs": 34,
    "norm_grad": 25,
    "join_grads": 8,
    "finish_outputs": 7,
    "finish_grads": 9,
}
BF = jnp.bfloat16
F32 = jnp.float32


def swap_grp(array, bits):
    return lax.ppermute(array, "grp", [(i, i ^ bits) for i in range(4)])


def swap_seq(array, bits):
    return lax.ppermute(array, "seq", [(i, i ^ bits) for i in range(8)])


def matmul_nn(left, right):
    return jnp.dot(left, right, preferred_element_type=F32)


def pick(array, index, axis):
    return lax.dynamic_index_in_dim(array, index, axis, keepdims=False)


def place(buffer, piece, index):
    return lax.dynamic_update_index_in_dim(buffer, piece, index, 0)


def tie(*arrays):
    return lax.optimization_barrier(arrays)


def whole(shape):
    return pl.BlockSpec(shape, lambda i, rank: (0,) * len(shape))


def cost(name):
    flops = int(COSTS.get(name, 2) * COST_UNIT)
    return pl.CostEstimate(flops=flops, transcendentals=0, bytes_accessed=0)


def ranked_call(body, rank, ins, shapes, name, blocks=None):
    return pl.pallas_call(
        body,
        grid_spec=pltpu.PrefetchScalarGridSpec(
            num_scalar_prefetch=1,
            grid=(1,),
            in_specs=[whole(shape) for shape in blocks or [a.shape for a in ins]],
            out_specs=[whole(s.shape) for s in shapes],
        ),
        out_shape=shapes,
        compiler_params=pltpu.CompilerParams(vmem_limit_bytes=56 << 20),
        cost_estimate=cost(name),
        name=name,
    )(rank.reshape(1), *ins)


def split_columns(shards, groups, tp_rank):
    rows = shards[0].shape[0]
    widths = [shard.shape[1] // (TP * count) for shard, count in zip(shards, groups)]
    cols = sum(width * count for width, count in zip(widths, groups))

    def body(rank_ref, *refs):
        ins, (own_ref, side_ref, far_ref) = refs[: len(shards)], refs[len(shards) :]
        at = 0
        for ref, count, width in zip(ins, groups, widths):
            for part in range(count):
                for bits in range(TP):
                    start = pl.multiple_of((part * TP + (rank_ref[0] ^ bits)) * width, width)
                    run = ref[:, pl.ds(start, width)]
                    here = slice(at, at + width)
                    if bits == 0:
                        own_ref[:, here] = run
                    elif bits == 2:
                        far_ref[:, here] = run
                    else:
                        side_ref[bits // 2, :, here] = run
                at += width

    shapes = [
        jax.ShapeDtypeStruct((rows, cols), BF),
        jax.ShapeDtypeStruct((2, rows, cols), BF),
        jax.ShapeDtypeStruct((rows, cols), BF),
    ]
    return ranked_call(body, tp_rank, list(shards), shapes, "split_columns")


def stack_ranks(own, over_y, over_z, cuts, tp_rank, uncut=False):
    rows, cols = own.shape
    runs = [slice(sum(cuts[:i]), sum(cuts[: i + 1])) for i in range(len(cuts))]
    if uncut:
        runs.append(slice(0, cols))

    def body(rank_ref, own_ref, y_ref, z_ref, *outs):
        for out, here in zip(outs, runs):
            pieces = (own_ref[:, here], y_ref[0, :, here], z_ref[0, :, here], z_ref[1, :, here])
            for bits, piece in enumerate(pieces):
                start = pl.multiple_of((rank_ref[0] ^ bits) * rows, rows)
                out[pl.ds(start, rows), :] = piece

    shapes = [jax.ShapeDtypeStruct((TP * rows, run.stop - run.start), BF) for run in runs]
    return ranked_call(body, tp_rank, [own, over_y, over_z], shapes, "stack_ranks")


def split_rows(groups, tp_rank, first=1):
    rows = groups[0][2][0].shape[0] // TP
    cols = sum(terms[0].shape[1] for terms in groups)
    flat = [array for kept, got_x, got_z in groups for array in (kept, got_x, *got_z)]

    def body(rank_ref, *refs):
        ins, (own_ref, side_ref, far_ref) = list(refs[: len(flat)]), refs[len(flat) :]
        at = 0
        for _, _, got_z in groups:
            kept, got_x = ins.pop(0), ins.pop(0)
            inside = 0
            for _ in got_z:
                run_ref = ins.pop(0)
                width = run_ref.shape[1]
                here, cut = slice(at, at + width), slice(inside, inside + width)
                at, inside = at + width, inside + width
                for bits in range(TP):
                    lines = pl.ds(pl.multiple_of((rank_ref[0] ^ bits) * rows, rows), rows)
                    total = kept[lines, cut].astype(F32) + got_x[lines, cut].astype(F32)
                    run = (total + run_ref[lines, :].astype(F32)).astype(BF)
                    if bits == 0:
                        own_ref[:, here] = run
                    elif bits == 3 - first:
                        far_ref[:, here] = run
                    else:
                        side_ref[int(bits == 3), :, here] = run

    shapes = [
        jax.ShapeDtypeStruct((rows, cols), BF),
        jax.ShapeDtypeStruct((2, rows, cols), BF),
        jax.ShapeDtypeStruct((rows, cols), BF),
    ]
    blocks = [(TP * rows, term.shape[1]) for term in flat]
    return ranked_call(body, tp_rank, flat, shapes, "split_rows", blocks)


def join_columns(own, got_first, got_second, parts, tp_rank, first=1):
    rows = own.shape[0]

    def body(rank_ref, own_ref, first_ref, second_ref, *outs):
        at = 0
        for out, (count, width) in zip(outs, parts):
            for part in range(count):
                here = slice(at, at + width)
                pieces = {
                    0: own_ref[:, here],
                    first: first_ref[0, :, here],
                    3 - first: second_ref[0, :, here],
                    3: second_ref[1, :, here],
                }
                for bits, piece in pieces.items():
                    start = pl.multiple_of((part * TP + (rank_ref[0] ^ bits)) * width, width)
                    out[:, pl.ds(start, width)] = piece.astype(F32)
                at += width

    shapes = [jax.ShapeDtypeStruct((rows, TP * count * width), F32) for count, width in parts]
    return ranked_call(body, tp_rank, [own, got_first, got_second], shapes, "join_columns")


def reorder_runs(arrays, place_index, sums=False):
    run = D // 8
    shapes = [jax.ShapeDtypeStruct(a.shape, a.dtype) for a in arrays]
    if sums:
        shapes.append(jax.ShapeDtypeStruct((1, D), F32))

    def body(index_ref, *refs):
        ins, outs = refs[: len(arrays)], refs[len(arrays) :]
        for j, bits in enumerate(WIDTH_ORDER):
            start = pl.multiple_of((index_ref[0] ^ bits) * run, run)
            here = slice(j * run, (j + 1) * run)
            for in_ref, out_ref in zip(ins, outs):
                out_ref[:, here] = in_ref[:, pl.ds(start, run)]
        if sums:
            total = outs[0][...].astype(F32).sum(axis=0, keepdims=True)
            for out_ref in outs[1 : len(arrays)]:
                total = total + out_ref[...].astype(F32).sum(axis=0, keepdims=True)
            outs[-1][...] = total

    return ranked_call(body, place_index, list(arrays), shapes, "reorder_runs")


def restore_runs(array, place_index):
    run = D // 8

    def body(index_ref, in_ref, out_ref):
        for j, bits in enumerate(WIDTH_ORDER):
            start = pl.multiple_of((index_ref[0] ^ bits) * run, run)
            out_ref[:, pl.ds(start, run)] = in_ref[:, j * run : (j + 1) * run]

    shapes = [jax.ShapeDtypeStruct(array.shape, array.dtype)]
    return ranked_call(body, place_index, [array], shapes, "restore_runs")[0]


def finish_outputs(parts, tokens, bias, place_index):
    run = D // 8
    rows = tokens[0].shape[0]
    flat = [term for terms in parts for term in terms]

    def body(index_ref, *refs):
        ins, outs = refs[: len(flat) + len(tokens) + 1], refs[len(flat) + len(tokens) + 1 :]
        bias_ref = ins[-1]
        for i, out_ref in enumerate(outs):
            own, got, got_far = ins[3 * i : 3 * i + 3]
            token_ref = ins[len(flat) + i]
            value = token_ref[...].astype(F32) + own[...].astype(F32) + got[...].astype(F32)
            value = value + got_far[...].astype(F32) + bias_ref[...]
            for j, bits in enumerate(WIDTH_ORDER):
                start = pl.multiple_of((index_ref[0] ^ bits) * run, run)
                out_ref[:, pl.ds(start, run)] = value[:, j * run : (j + 1) * run]

    shapes = [jax.ShapeDtypeStruct((rows, D), F32) for _ in tokens]
    blocks = [(rows, D)] * (len(flat) + len(tokens)) + [bias.shape]
    return ranked_call(
        body, place_index, flat + list(tokens) + [bias], shapes, "finish_outputs", blocks
    )


def finish_grads(parts, tokens, cots, place_index):
    run = D // 8
    rows = tokens[0].shape[0]
    count = len(tokens)
    flat = [term for terms in parts for term in terms]

    def body(index_ref, *refs):
        ins, outs = refs[: 5 * count], refs[5 * count :]
        for i, out_ref in enumerate(outs):
            own, got, got_far = ins[3 * i : 3 * i + 3]
            token = ins[3 * count + i][...].astype(F32)
            cot = ins[4 * count + i][...].astype(F32)
            entry = own[...].astype(F32) + got[...].astype(F32) + got_far[...].astype(F32)
            center = token - jnp.mean(token, axis=1, keepdims=True)
            spread = lax.rsqrt(jnp.mean(center * center, axis=1, keepdims=True) + EPSILON)
            normed = center * spread
            entry_mean = jnp.mean(entry, axis=1, keepdims=True)
            entry_dot = jnp.mean(entry * normed, axis=1, keepdims=True)
            value = cot + spread * (entry - entry_mean - normed * entry_dot)
            for j, bits in enumerate(WIDTH_ORDER):
                start = pl.multiple_of((index_ref[0] ^ bits) * run, run)
                out_ref[:, pl.ds(start, run)] = value[:, j * run : (j + 1) * run]

    shapes = [jax.ShapeDtypeStruct((rows, D), F32) for _ in tokens]
    return ranked_call(
        body,
        place_index,
        flat + list(tokens) + list(cots),
        shapes,
        "finish_grads",
        [(rows, D)] * (5 * count),
    )


def part_specs(rows, tile, width, parts):
    per_part = rows // tile

    def spec(k):
        return pl.BlockSpec((tile, width), lambda i: (jnp.clip(i - k * per_part, 0, per_part - 1), 0))

    return [spec(k) for k in range(parts)]


def norms_body(gain1, bias1, gain2, bias2, *refs):
    *parts, rows_ref, first_ref, second_ref, mean_ref, spread_ref = refs
    step = pl.program_id(0)
    per_part = pl.num_programs(0) // len(parts)
    for k, part in enumerate(parts):

        @pl.when(step // per_part == k)
        def _(part=part):
            rows_ref[...] = part[...]
            values = part[...].astype(F32)
            mean = jnp.mean(values, axis=1, keepdims=True)
            center = values - mean
            spread = lax.rsqrt(jnp.mean(center * center, axis=1, keepdims=True) + EPSILON)
            normed = center * spread
            first_ref[...] = (normed * gain1[...] + bias1[...]).astype(BF)
            second_ref[...] = (normed * gain2[...] + bias2[...]).astype(BF)
            mean_ref[...] = mean
            spread_ref[...] = spread


def both_low_norms(parts, gain1, bias1, gain2, bias2):
    tile = parts[0].shape[0]
    total = tile * len(parts)
    vector = pl.BlockSpec((1, D), lambda i: (0, 0))
    wide = pl.BlockSpec((tile, D), lambda i: (i, 0))
    thin = pl.BlockSpec((tile, 1), lambda i: (i, 0))
    return pl.pallas_call(
        norms_body,
        grid=(total // tile,),
        in_specs=[vector] * 4 + part_specs(tile, tile, D, len(parts)),
        out_specs=[wide, wide, wide, thin, thin],
        out_shape=[
            jax.ShapeDtypeStruct((total, D), BF),
            jax.ShapeDtypeStruct((total, D), BF),
            jax.ShapeDtypeStruct((total, D), BF),
            jax.ShapeDtypeStruct((total, 1), F32),
            jax.ShapeDtypeStruct((total, 1), F32),
        ],
        compiler_params=pltpu.CompilerParams(vmem_limit_bytes=56 << 20),
        cost_estimate=cost("norms"),
        name="norms",
    )(gain1, bias1, gain2, bias2, *parts)


def resident(array, block=None, at=(0, 0)):
    return pl.BlockSpec(block or array.shape, lambda i: at, pipeline_mode=pl.Buffered(1))


def times(rows, halves, columns):
    upper, lower = halves
    half = upper.shape[0]
    return matmul_nn(rows[:, :half], upper[:, columns]) + matmul_nn(rows[:, half:], lower[:, columns])


def runs_of(width, run):
    return [slice(at, at + run) for at in range(0, width, run)]


def kernel(body, steps, in_specs, out_specs, out_shape, name, scratch=()):
    return pl.pallas_call(
        body,
        grid=(steps,),
        in_specs=in_specs,
        out_specs=out_specs,
        out_shape=out_shape,
        scratch_shapes=scratch,
        compiler_params=pltpu.CompilerParams(vmem_limit_bytes=58 << 20),
        cost_estimate=cost(name),
        name=name,
    )


def stacked(parts):
    tile, width = parts[0].shape

    def body(*refs):
        *ins, out_ref = refs
        for k, part in enumerate(ins):

            @pl.when(pl.program_id(0) == k)
            def _(part=part):
                out_ref[...] = part[...]

    return kernel(
        body,
        len(parts),
        part_specs(tile, tile, width, len(parts)),
        by_rows(tile, width),
        jax.ShapeDtypeStruct((tile * len(parts), width), BF),
        "stacked",
    )(*parts)


def beside(entries):
    tile, width = entries[0][0].shape
    specs, arrays = [], []
    for entry in entries:
        if isinstance(entry, tuple):
            specs += [pl.BlockSpec((tile, width), lambda i: (0, 0))] * 2
            arrays += entry
        elif entry.shape[0] == tile:
            specs += [pl.BlockSpec((tile, width), lambda i, h=h: (0, h)) for h in range(2)]
            arrays += [entry, entry]
        else:
            specs += [pl.BlockSpec((tile, width), lambda i, h=h: (h, 0)) for h in range(2)]
            arrays += [entry, entry]

    def body(*refs):
        *ins, out_ref = refs
        for k in range(len(entries)):

            @pl.when(pl.program_id(0) == k)
            def _(k=k):
                out_ref[:, :width] = ins[2 * k][...]
                out_ref[:, width:] = ins[2 * k + 1][...]

    return kernel(
        body,
        len(entries),
        specs,
        by_rows(tile, 2 * width),
        jax.ShapeDtypeStruct((tile * len(entries), 2 * width), BF),
        "beside",
    )(*arrays)


def second_sum(left, right, part=None):
    rows, width = left.shape[0] // 2, left.shape[1] // (1 if part is None else 2)
    wide = 1024 if width % 1024 == 0 else 512
    first = (part or 0) * (width // wide)

    def body(left_ref, right_ref, out_ref):
        out_ref[...] = (left_ref[...].astype(F32) + right_ref[...].astype(F32)).astype(BF)

    lower = pl.BlockSpec((rows, wide), lambda i: (1, first + i))
    at = right.shape[0] // rows - 1
    return kernel(
        body,
        width // wide,
        [lower, pl.BlockSpec((rows, wide), lambda i: (at, first + i))],
        pl.BlockSpec((rows, wide), lambda i: (0, i)),
        jax.ShapeDtypeStruct((rows, width), BF),
        "second_sum",
    )(left, right)


def onward(far, over_y):
    rows, width = far.shape

    def body(far_ref, y_ref, out_ref):
        out_ref[0] = far_ref[...]
        out_ref[1] = y_ref[0]

    return kernel(
        body,
        1,
        [
            pl.BlockSpec((rows, width), lambda i: (0, 0)),
            pl.BlockSpec((1, rows, width), lambda i: (1, 0, 0)),
        ],
        pl.BlockSpec((2, rows, width), lambda i: (0, 0, 0)),
        jax.ShapeDtypeStruct((2, rows, width), BF),
        "onward",
    )(far, over_y)


def by_rows(tile, width, tiles=lambda i: i):
    return pl.BlockSpec((tile, width), lambda i: (tiles(i), 0))


def attention_grad(parts, halves, column_block):
    tile = parts[0].shape[0]
    total = tile * len(parts)

    def body(upper, lower, *refs):
        *ins, out_ref, rows_ref, held = refs
        for k, part in enumerate(ins):

            @pl.when(pl.program_id(0) == k)
            def _(part=part):
                held[...] = part[...]

        rows = held[...]
        rows_ref[...] = rows
        out_ref[...] = times(rows, (upper, lower), slice(0, HCOLS)).astype(BF)

    weight_spec = resident(halves[0], (D // 2, HCOLS), (0, column_block))
    return kernel(
        body,
        len(parts),
        [weight_spec, weight_spec] + part_specs(tile, tile, D, len(parts)),
        [by_rows(tile, HCOLS), by_rows(tile, D)],
        [jax.ShapeDtypeStruct((total, HCOLS), BF), jax.ShapeDtypeStruct((total, D), BF)],
        "attention_grad",
        [pltpu.VMEM((tile, D), BF)],
    )(*halves, *parts)


def feed_forward_up(rows, halves, bias):
    total, ff_here = rows.shape[0], bias.shape[1]
    tile, wide = total // 4, ff_here // 2
    half = D // 2

    def body(rows_ref, upper, lower, bias_ref, act_ref, slope_ref):
        values = rows_ref[...]
        for run in runs_of(wide, 256):
            pre = times(values, (upper, lower), run) + bias_ref[:, run]
            cdf = 0.5 * (1.0 + lax.erf(pre * math.sqrt(0.5)))
            density = jnp.exp(-0.5 * pre * pre) * (1.0 / math.sqrt(2.0 * math.pi))
            act_ref[:, run] = (pre * cdf).astype(BF)
            slope_ref[:, run] = (cdf + pre * density).astype(BF)

    weight_spec = pl.BlockSpec((half, wide), lambda i: (0, i // 4))
    out_spec = pl.BlockSpec((tile, wide), lambda i: (i % 4, i // 4))
    return kernel(
        body,
        8,
        [
            by_rows(tile, D, lambda i: i % 4),
            weight_spec,
            weight_spec,
            pl.BlockSpec((1, wide), lambda i: (0, i // 4)),
        ],
        [out_spec] * 2,
        [jax.ShapeDtypeStruct((total, ff_here), BF)] * 2,
        "feed_forward_up",
    )(rows, *halves, bias)


def feed_forward_back(cots, halves, slope):
    total, ff_here = slope.shape
    tile, wide = total // 2, ff_here // 2
    half = D // 2

    def body(cot_ref, upper, lower, slope_ref, out_ref, sum_ref):
        @pl.when(pl.program_id(0) % 2 == 0)
        def _():
            sum_ref[...] = jnp.zeros_like(sum_ref)

        values = cot_ref[...]
        for run in runs_of(wide, 512):
            grad = times(values, (upper, lower), run) * slope_ref[:, run].astype(F32)
            low = grad.astype(BF)
            out_ref[:, run] = low
            sum_ref[:, run] += low.astype(F32).sum(axis=0, keepdims=True)

    weight_spec = pl.BlockSpec((half, wide), lambda i: (0, i // 2))
    both = pl.BlockSpec((tile, wide), lambda i: (i % 2, i // 2))
    return kernel(
        body,
        4,
        [by_rows(tile, D, lambda i: i % 2), weight_spec, weight_spec, both],
        [both, pl.BlockSpec((1, wide), lambda i: (0, i // 2))],
        [jax.ShapeDtypeStruct((total, ff_here), BF), jax.ShapeDtypeStruct((1, ff_here), F32)],
        "feed_forward_back",
    )(cots, *halves, slope)


def weight_grad(left, rights, core_got=None):
    total = left.shape[0]
    width = sum(right.shape[1] for right in rights)
    half = D // 2
    wide = 512
    steps = width // wide if len(rights) == 1 else 1
    keep = core_got is not None

    def body(left_ref, *refs):
        ins, rest = refs[: len(rights)], refs[len(rights) :]
        values = left_ref[...]
        at = 0
        for right in ins:
            here = slice(at, at + right.shape[1])
            at += right.shape[1]
            product = contract_cols(values, right[...])
            if keep:
                got_ref, mine_ref, side_ref = rest
                product = product + got_ref[:, here].astype(F32)
                mine_ref[:, here] = product[: half // 2].astype(BF)
                side_ref[:, here] = product[half // 2 :].astype(BF)
            else:
                rest[0][:, here] = product.astype(BF)

    if len(rights) == 1:
        right_specs = [pl.BlockSpec((total, wide), lambda i: (0, i))]
    else:
        right_specs = [resident(right) for right in rights]
    rows = half // 2 if keep else half
    count = 2 if keep else 1
    outs = kernel(
        body,
        steps,
        [resident(left, (total, half), (0, 0 if keep else 1))]
        + right_specs
        + ([pl.BlockSpec((half, wide), lambda i: (0, i))] if keep else []),
        [pl.BlockSpec((rows, wide), lambda i: (0, i))] * count,
        [jax.ShapeDtypeStruct((rows, width), BF)] * count,
        "weight_grad",
    )(left, *rights, *([core_got] if keep else []))
    return outs if keep else outs[0]


def width_tile(halves, height, columns, block=0):
    per_half = halves[0].shape[0] // height
    return [
        pl.BlockSpec((height, columns), lambda i: (jnp.minimum(i, per_half - 1), block)),
        pl.BlockSpec((height, columns), lambda i: (jnp.maximum(i - per_half, 0), block)),
    ]


def chosen(upper, lower):
    in_upper = pl.program_id(0) < pl.num_programs(0) // 2
    return jnp.where(in_upper, upper[...], lower[...])


def quarter_rows(tile):
    return [tile, tile // 2, tile // 2] * 2


def quarter_specs(tile, wide):
    return [pl.BlockSpec((rows, wide), lambda i: (0, i)) for rows in quarter_rows(tile)]


def put_quarter(outs, k, value):
    at = 3 * (k // 2)
    if k % 2 == 0:
        outs[at][...] = value
    else:
        half = value.shape[0] // 2
        outs[at + 1][...] = value[:half]
        outs[at + 2][...] = value[half:]


def branch_outputs(heads_low, act_low, attn_halves, column_block, down_halves):
    total, ff_here = act_low.shape
    tile = total // 4
    wide = 512

    def body(*refs):
        heads = [refs[h * 4 : h * 4 + 4] for h in range(HEADS_HERE)]
        refs = refs[4 * HEADS_HERE :]
        acts, attn, down, outs = refs[:4], refs[4:6], refs[6:8], refs[8:]
        attn_tile, down_tile = chosen(*attn), chosen(*down)
        for k in range(4):
            value = contract_rows(acts[k][...], down_tile)
            for head in range(HEADS_HERE):
                cut = slice(head * HEAD, (head + 1) * HEAD)
                value = value + contract_rows(heads[head][k][...], attn_tile[:, cut])
            put_quarter(outs, k, value.astype(BF))

    return kernel(
        body,
        D // wide,
        [resident(h, (tile, HEAD), (k, 0)) for h in heads_low for k in range(4)]
        + [resident(act_low, (tile, ff_here), (k, 0)) for k in range(4)]
        + width_tile(attn_halves, wide, HCOLS, column_block)
        + width_tile(down_halves, wide, ff_here),
        quarter_specs(tile, wide),
        [jax.ShapeDtypeStruct((rows, D), BF) for rows in quarter_rows(tile)],
        "branch_outputs",
    )(*[h for h in heads_low for _ in range(4)], *([act_low] * 4), *attn_halves, *down_halves)


def norm_grad(grads, halves, gain, tokens, mean, spread, row_blocks, addends=(), cut=False):
    tile = grads.shape[0] // 4
    count = len(row_blocks)
    width = grads.shape[1]
    wide = 512

    def body(upper, lower, gain_ref, *refs):
        rows, means, spreads, token_refs = (refs[i * count : (i + 1) * count] for i in range(4))
        rest = refs[4 * count :]
        adds, outs, sum_ref = rest[: len(addends)], rest[len(addends) : -1], rest[-1]
        weight = chosen(upper, lower)
        dots = jnp.zeros((1, wide), F32)
        totals = jnp.zeros((1, wide), F32)
        for k in range(count):
            value = contract_rows(rows[k][...], weight)
            scaled = value * gain_ref[...]
            if adds:
                scaled = scaled + adds[k][...].astype(F32)
            low = scaled.astype(BF)
            if cut:
                outs[2 * k][...] = low[: tile // 2]
                outs[2 * k + 1][...] = low[tile // 2 :]
            else:
                outs[k][...] = low
            normed = (token_refs[k][...].astype(F32) - means[k][...]) * spreads[k][...]
            dots = dots + (value * normed).sum(axis=0, keepdims=True)
            totals = totals + value.sum(axis=0, keepdims=True)
        sum_ref[0:1, :] = dots
        sum_ref[1:2, :] = totals

    column = pl.BlockSpec((tile, wide), lambda i: (0, i))
    out_rows = [tile // 2] * (2 * count) if cut else [tile] * count
    outs = kernel(
        body,
        D // wide,
        [
            *width_tile(halves, wide, width),
            pl.BlockSpec((1, wide), lambda i: (0, i)),
            *[resident(grads, (tile, width), (k, 0)) for k in row_blocks],
            *[resident(mean, (tile, 1), (k, 0)) for k in row_blocks],
            *[resident(spread, (tile, 1), (k, 0)) for k in row_blocks],
            *[pl.BlockSpec((tile, wide), lambda i, k=k: (k, i)) for k in row_blocks],
            *([column] * len(addends)),
        ],
        [pl.BlockSpec((rows, wide), lambda i: (0, i)) for rows in out_rows]
        + [pl.BlockSpec((8, wide), lambda i: (0, i))],
        [jax.ShapeDtypeStruct((rows, D), BF) for rows in out_rows]
        + [jax.ShapeDtypeStruct((8, D), F32)],
        "norm_grad",
    )(
        *halves,
        gain,
        *([grads] * count),
        *([mean] * count),
        *([spread] * count),
        *([tokens] * count),
        *addends,
    )
    return outs[:-1], outs[-1]


def rotary_tables(positions):
    lane = jnp.arange(LANES, dtype=jnp.int32)
    half_rot = ROT // 2
    exponent = -(2.0 * (lane % half_rot).astype(F32)) / ROT
    angles = positions[:, None] * (ROPE_BASE**exponent)[None, :]
    turning = (lane < ROT)[None, :]
    cos_table = jnp.where(turning, jnp.cos(angles), 1.0)
    sin_part = jnp.sin(angles)
    sin_table = jnp.where((lane < half_rot)[None, :], -sin_part, sin_part)
    return cos_table, jnp.where(turning, sin_table, 0.0)


def swapped_halves(values):
    half_rot = ROT // 2
    lane = lax.broadcasted_iota(jnp.int32, values.shape, 1)
    return jnp.where(
        lane < half_rot,
        pltpu.roll(values, LANES - half_rot, 1),
        pltpu.roll(values, half_rot, 1),
    )


def turned(values, cos_table, sin_table):
    first = values[:, :LANES]
    return jnp.concatenate(
        [first * cos_table + swapped_halves(first) * sin_table, values[:, LANES:]], axis=1
    )


def project_qkv(head, rows, halves, bias, cos_table, sin_table):
    total = rows.shape[0]
    tile = total // 2
    half = D // 2

    def body(rows_ref, *refs):
        weights, biases = refs[:6], refs[6:9]
        cos_ref, sin_ref, q_ref, near_key_ref, near_value_ref, own_ref = refs[9:]
        values = rows_ref[...]
        cos_here, sin_here = cos_ref[...], sin_ref[...]

        def product(kind):
            whole_run = slice(0, HEAD)
            return times(values, weights[2 * kind : 2 * kind + 2], whole_run) + biases[kind][...]

        query = turned(product(0), cos_here, sin_here)
        q_ref[...] = (query * (1.0 / math.sqrt(HEAD))).astype(BF)
        key = turned(product(1), cos_here, sin_here).astype(BF)
        value = product(2).astype(BF)

        @pl.when(pl.program_id(0) == 0)
        def _():
            near_key_ref[...] = key
            near_value_ref[...] = value

        @pl.when(pl.program_id(0) == 1)
        def _():
            own_ref[:, :HEAD] = key
            own_ref[:, HEAD:] = value

    columns = [kind * HEADS_HERE + head for kind in range(3)]
    both = jax.ShapeDtypeStruct((tile, 2 * HEAD), BF)
    one = jax.ShapeDtypeStruct((tile, HEAD), BF)
    kept_both = pl.BlockSpec((tile, 2 * HEAD), lambda i: (0, 0))
    kept = pl.BlockSpec((tile, HEAD), lambda i: (0, 0))
    return kernel(
        body,
        2,
        [
            by_rows(tile, D),
            *[resident(h, (half, HEAD), (0, c)) for c in columns for h in halves],
            *[resident(bias, (1, HEAD), (0, c)) for c in columns],
            by_rows(tile, LANES),
            by_rows(tile, LANES),
        ],
        [by_rows(tile, HEAD), kept, kept, kept_both],
        [jax.ShapeDtypeStruct((total, HEAD), BF), one, one, both],
        "qkv_rotary",
    )(rows, *[h for _ in columns for h in halves], *([bias] * 3), cos_table, sin_table)


def attention_body(
    q_ref,
    do_ref,
    kl_ref,
    vl_ref,
    kr_ref,
    vr_ref,
    kc_ref,
    vc_ref,
    cos_ref,
    sin_ref,
    cosl_ref,
    sinl_ref,
    cosr_ref,
    sinr_ref,
    qmark_ref,
    kmark_ref,
    o_ref,
    dq_ref,
    down_ref,
    dnear_ref,
    dfar_key_ref,
    dfar_value_ref,
    akl,
    avl,
    akr,
    avr,
):
    step = pl.program_id(0)
    last = pl.num_programs(0) - 1
    near = kl_ref.shape[0]

    @pl.when(step == 0)
    def _():
        for acc in (akl, avl, akr, avr):
            acc[...] = jnp.zeros_like(acc)

    query, grad = q_ref[...], do_ref[...]

    def work(own):
        scores = [contract_rows(query, kl_ref[...]), contract_rows(query, kr_ref[...])]
        if own:
            mine = contract_rows(query, kc_ref[...])
            at_row = lax.broadcasted_iota(jnp.int32, mine.shape, 0)
            at_col = lax.broadcasted_iota(jnp.int32, mine.shape, 1)
            scores.append(jnp.where(at_col <= at_row, mine, NEG_FILL))
        else:
            marks = kmark_ref[...]
            own_mark = qmark_ref[...]
            scores[0] = jnp.where(marks[:, :near] <= own_mark, scores[0], NEG_FILL)
            scores[1] = jnp.where(marks[:, near:] <= own_mark, scores[1], NEG_FILL)
        top = scores[0].max(axis=1, keepdims=True)
        for part in scores[1:]:
            top = jnp.maximum(top, part.max(axis=1, keepdims=True))
        probs = [jnp.exp(part - top) for part in scores]
        total = probs[0].sum(axis=1, keepdims=True)
        for part in probs[1:]:
            total = total + part.sum(axis=1, keepdims=True)
        share = 1.0 / total
        probs = [part * share for part in probs]
        low = [part.astype(BF) for part in probs]
        values = [vl_ref, vr_ref] + ([vc_ref] if own else [])
        keys = [kl_ref, kr_ref] + ([kc_ref] if own else [])
        mixed = matmul_nn(low[0], values[0][...])
        for part, ref in zip(low[1:], values[1:]):
            mixed = mixed + matmul_nn(part, ref[...])
        o_ref[...] = mixed.astype(BF)
        prob_grad = [contract_rows(grad, ref[...]) for ref in values]
        delta = (probs[0] * prob_grad[0]).sum(axis=1, keepdims=True)
        for part, grad_part in zip(probs[1:], prob_grad[1:]):
            delta = delta + (part * grad_part).sum(axis=1, keepdims=True)
        slopes = [
            (part * (grad_part - delta)).astype(BF) for part, grad_part in zip(probs, prob_grad)
        ]
        query_grad = matmul_nn(slopes[0], keys[0][...])
        for part, ref in zip(slopes[1:], keys[1:]):
            query_grad = query_grad + matmul_nn(part, ref[...])
        query_grad = query_grad * (1.0 / math.sqrt(HEAD))
        dq_ref[...] = turned(query_grad, cos_ref[...], -sin_ref[...]).astype(BF)
        akl[...] += contract_cols(slopes[0], query)
        akr[...] += contract_cols(slopes[1], query)
        avl[...] += contract_cols(low[0], grad)
        avr[...] += contract_cols(low[1], grad)
        if own:
            key_grad = contract_cols(slopes[2], query)
            down_ref[:, :HEAD] = turned(key_grad, cos_ref[...], -sin_ref[...]).astype(BF)
            down_ref[:, HEAD:] = contract_cols(low[2], grad).astype(BF)

    @pl.when(step < TP)
    def _():
        work(False)

    @pl.when(step >= TP)
    def _():
        work(True)

    @pl.when(step == last)
    def _():
        dnear_ref[:, :HEAD] = turned(akl[...], cosl_ref[...], -sinl_ref[...])
        dnear_ref[:, HEAD:] = avl[...]
        dfar_key_ref[...] = turned(akr[...], cosr_ref[...], -sinr_ref[...]).astype(BF)
        dfar_value_ref[...] = avr[...].astype(BF)


def attend(
    head, queries, grads, near, far, own, tables, near_tables, far_tables, query_mark, key_mark
):
    total = queries.shape[0]
    tile = total // (2 * TP)
    keys = near[0].shape[0]

    def row_tile(j):
        return j

    def cont_tile(j):
        return jnp.maximum(j - TP, 0)

    query_spec = pl.BlockSpec((tile, HEAD), lambda j: (row_tile(j), 0))
    row_spec = pl.BlockSpec((tile, HEAD), lambda j: (row_tile(j), head))
    out_spec = pl.BlockSpec((tile, HEAD), lambda j: (row_tile(j), 0))
    key_spec = pl.BlockSpec((keys, HEAD), lambda j: (0, 0))
    own_key = pl.BlockSpec((tile, HEAD), lambda j: (cont_tile(j), 0))
    own_value = pl.BlockSpec((tile, HEAD), lambda j: (cont_tile(j), 1))
    own_both = pl.BlockSpec((tile, 2 * HEAD), lambda j: (cont_tile(j), 0))
    both = pl.BlockSpec((keys, 2 * HEAD), lambda j: (0, 0))
    table_spec = pl.BlockSpec((tile, LANES), lambda j: (row_tile(j), 0))
    key_table = pl.BlockSpec((keys, LANES), lambda j: (0, 0))
    mark_spec = pl.BlockSpec((tile, 1), lambda j: (row_tile(j), 0))
    key_mark_spec = pl.BlockSpec((1, 2 * keys), lambda j: (0, 0))
    wide = jax.ShapeDtypeStruct((total, HEAD), BF)
    return pl.pallas_call(
        attention_body,
        grid=(2 * TP,),
        in_specs=[
            query_spec,
            row_spec,
            key_spec,
            key_spec,
            key_spec,
            key_spec,
            own_key,
            own_value,
            table_spec,
            table_spec,
            key_table,
            key_table,
            key_table,
            key_table,
            mark_spec,
            key_mark_spec,
        ],
        out_specs=[out_spec, out_spec, own_both, both, key_spec, key_spec],
        out_shape=[
            wide,
            wide,
            jax.ShapeDtypeStruct((keys, 2 * HEAD), BF),
            jax.ShapeDtypeStruct((keys, 2 * HEAD), F32),
            jax.ShapeDtypeStruct((keys, HEAD), BF),
            jax.ShapeDtypeStruct((keys, HEAD), BF),
        ],
        scratch_shapes=[pltpu.VMEM((keys, HEAD), F32)] * 4,
        compiler_params=pltpu.CompilerParams(vmem_limit_bytes=56 << 20),
        cost_estimate=cost("attention_both_ways"),
        name="attention_both_ways",
    )(
        queries,
        grads,
        *near,
        *far,
        own,
        own,
        *tables,
        *near_tables,
        *far_tables,
        query_mark,
        key_mark,
    )


def join_grads(query_grads, own_grads, near_grads, far_keys, far_values):
    total = query_grads[0].shape[0]
    tile = total // 4

    def body(*refs):
        out_ref, sum_ref = refs[-2:]
        dq, down, dnear, dfar_key, dfar_value = (
            refs[i * HEADS_HERE : (i + 1) * HEADS_HERE] for i in range(5)
        )
        step = pl.program_id(0)

        @pl.when(step == 0)
        def _():
            sum_ref[...] = jnp.zeros_like(sum_ref)

        for head in range(HEADS_HERE):
            at = head * HEAD
            key_at, value_at = slice(HCOLS + at, HCOLS + at + HEAD), slice(
                2 * HCOLS + at, 2 * HCOLS + at + HEAD
            )
            out_ref[:, at : at + HEAD] = dq[head][...]

            @pl.when(step < 2)
            def _(head=head, key_at=key_at, value_at=value_at):
                near = dnear[head][...]
                out_ref[:, key_at] = (near[:, :HEAD] + dfar_key[head][...].astype(F32)).astype(BF)
                out_ref[:, value_at] = (near[:, HEAD:] + dfar_value[head][...].astype(F32)).astype(BF)

            @pl.when(step >= 2)
            def _(head=head, key_at=key_at, value_at=value_at):
                out_ref[:, key_at] = down[head][:, :HEAD]
                out_ref[:, value_at] = down[head][:, HEAD:]

        sum_ref[...] += out_ref[...].astype(F32).sum(axis=0, keepdims=True)

    prompt_spec, cont_spec = part_specs(total // 2, tile, 2 * HEAD, 2)
    far_spec, _ = part_specs(total // 2, tile, HEAD, 2)
    return pl.pallas_call(
        body,
        grid=(4,),
        in_specs=[
            *([pl.BlockSpec((tile, HEAD), lambda i: (i, 0))] * HEADS_HERE),
            *([cont_spec] * HEADS_HERE),
            *([prompt_spec] * HEADS_HERE),
            *([far_spec] * (2 * HEADS_HERE)),
        ],
        out_specs=[
            pl.BlockSpec((tile, 3 * HCOLS), lambda i: (i, 0)),
            pl.BlockSpec((1, 3 * HCOLS), lambda i: (0, 0)),
        ],
        out_shape=[
            jax.ShapeDtypeStruct((total, 3 * HCOLS), BF),
            jax.ShapeDtypeStruct((1, 3 * HCOLS), F32),
        ],
        compiler_params=pltpu.CompilerParams(vmem_limit_bytes=56 << 20),
        cost_estimate=cost("join_grads"),
        name="join_grads",
    )(*query_grads, *own_grads, *near_grads, *far_keys, *far_values)


class Values:
    pass


def square_plan(
    prompt,
    conts,
    assignment,
    offsets,
    ln1_gain,
    ln1_bias,
    ln2_gain,
    ln2_bias,
    qkv_weight,
    qkv_bias,
    out_weight,
    out_bias,
    up_weight,
    up_bias,
    down_weight,
    down_bias,
    prompt_cot,
    cont_cot,
):
    block, cont_rows = prompt.shape[1], conts.shape[2]
    shard = qkv_weight.shape[0]
    ff = up_weight.shape[1]
    ff_here = ff // TP
    half = D // 2
    grp_index, seq_index = lax.axis_index("grp"), lax.axis_index("seq")
    tp_rank, z_half = seq_index & 3, seq_index >> 2
    place_index = grp_index * 2 + z_half

    v = Values()


    branch_ids = jnp.arange(offsets.shape[1], dtype=jnp.int32)
    my_offset = jnp.sum(jnp.where(branch_ids == assignment[0, 0], offsets[0], 0)).reshape(1, 1)
    v.offsets = jnp.concatenate(
        [my_offset if bits == 0 else swap_seq(my_offset, bits) for bits in CONT_ORDER], axis=0
    )
    own1, v.side1, far1 = split_columns([qkv_weight, out_weight.T], [3, 1], tp_rank)
    v.got1_y = swap_seq(v.side1, 1)
    v.own_a, v.own_b = reorder_runs([prompt[0], conts[0, 0]], place_index)
    own2, v.side2, far2 = split_columns([up_weight], [1], tp_rank)
    v.got1_y, v.side2 = tie(v.got1_y, v.side2)
    v.got1_z = swap_seq(onward(far1, v.got1_y), 2)
    v.got2_y = swap_seq(v.side2, 1)
    own3, v.side3, far3 = split_columns([down_weight.T], [1], tp_rank)
    qkv_bias_here = pick(qkv_bias.reshape(3, TP, HCOLS), tp_rank, 1).reshape(1, 3 * HCOLS)
    up_bias_here = pick(up_bias.reshape(TP, ff_here), tp_rank, 0)[None]
    vectors = jnp.stack([ln1_gain, ln1_bias, ln2_gain, ln2_bias, out_bias + down_bias])
    vectors = jnp.concatenate([vectors, jnp.zeros((3, D), F32)], axis=0)
    (v.vectors,) = reorder_runs([vectors], place_index)
    prompt_ranks = (tp_rank ^ jnp.array(PROMPT_ORDER, dtype=jnp.int32))[:, None]
    prompt_iota = jnp.arange(block, dtype=jnp.int32)[None, :]
    cont_iota = jnp.arange(cont_rows, dtype=jnp.int32)[None, :]
    near_mark = ((z_half * TP + prompt_ranks) * block + prompt_iota).reshape(-1)
    far_mark = (((z_half ^ 1) * TP + prompt_ranks) * block + prompt_iota).reshape(-1)
    cont_positions = (PROMPT + cont_iota + v.offsets).reshape(-1)
    v.mark = jnp.concatenate([near_mark, cont_positions]).astype(F32)
    query_mark = jnp.concatenate([near_mark, near_mark]).reshape(-1, 1)
    key_mark = jnp.concatenate([near_mark, far_mark]).reshape(1, -1)
    (
        v.got1_z, v.got2_y, v.own_a, v.own_b, v.side3, v.offsets,
    ) = tie(
        v.got1_z, v.got2_y, v.own_a, v.own_b, v.side3, v.offsets,
    )
    v.base1a, v.base1b = stack_ranks(
        own1, v.got1_y, v.got1_z, (2 * HCOLS,) * 2, tp_rank
    )
    v.rows_az = swap_seq(v.own_a, 2)
    v.rows_ay = swap_seq(v.own_a, 1)
    v.z1a = swap_seq(v.base1a, 4)
    v.x1a = swap_grp(v.base1a, 2)
    v.send2 = onward(far2, v.got2_y)
    v.cot0, v.cot1 = prompt_cot[0], cont_cot[0, 0]
    v.cot0, v.cot1, v.base1b = tie(v.cot0, v.cot1, v.base1b)
    v.cot_a, v.cot_b, cot_sum = reorder_runs([v.cot0, v.cot1], place_index, sums=True)
    (
        v.rows_az, v.rows_ay, v.z1a, v.x1a, v.send2, v.base1b, v.own_b, v.cot_a, v.cot_b, v.mark,
    ) = tie(
        v.rows_az, v.rows_ay, v.z1a, v.x1a, v.send2, v.base1b, v.own_b, v.cot_a, v.cot_b, v.mark,
    )
    v.z1b = swap_seq(v.base1b, 4)
    v.got2_z = swap_seq(v.send2, 2)
    v.rows_by = swap_seq(v.own_b, 1)
    v.x1b = swap_grp(v.base1b, 2)
    v.zx1a = swap_grp(v.z1a, 2)
    v.base2a, v.base2b, v.base2 = stack_ranks(
        own2, v.got2_y, v.got2_z, (ff_here // 2,) * 2, tp_rank, True
    )
    tables = rotary_tables(v.mark)
    far_tables = rotary_tables(far_mark.astype(F32))
    v.tables0, v.tables1 = tables
    v.far0, v.far1 = far_tables
    (
        v.vectors, v.z1b, v.base2a, v.base2b, v.base2, v.rows_by, v.x1b, v.zx1a, v.rows_az,
        v.own_b, v.side3, v.tables0, v.tables1, v.far0, v.far1,
    ) = tie(
        v.vectors, v.z1b, v.base2a, v.base2b, v.base2, v.rows_by, v.x1b, v.zx1a, v.rows_az,
        v.own_b, v.side3, v.tables0, v.tables1, v.far0, v.far1,
    )
    tables, far_tables = (v.tables0, v.tables1), (v.far0, v.far1)
    shared = (tables, tables, far_tables, query_mark, key_mark)
    v.got3_y = swap_seq(v.side3, 1)
    v.rows_azy = swap_seq(v.rows_az, 1)
    v.rows_bz = swap_seq(v.own_b, 2)
    v.zx1b = swap_grp(v.z1b, 2)
    v.z2a = swap_seq(v.base2a, 4)
    (
        v.z2a, v.rows_azy, v.rows_bz, v.zx1b, v.got3_y, v.base2b, v.base2,
    ) = tie(
        v.z2a, v.rows_azy, v.rows_bz, v.zx1b, v.got3_y, v.base2b, v.base2,
    )
    v.rows_bzy = swap_seq(v.rows_bz, 1)
    v.z2b = swap_seq(v.base2b, 4)
    v.x2 = swap_grp(v.base2, 2)
    v.got3_z = swap_seq(onward(far3, v.got3_y), 2)
    v.base3a, v.base3b, v.base3 = stack_ranks(
        own3, v.got3_y, v.got3_z, (ff_here // 2,) * 2, tp_rank, True
    )
    v.core1 = beside(
        [(v.base1a, v.base1b), (v.z1a, v.z1b), (v.x1a, v.x1b), (v.zx1a, v.zx1b)]
    )
    gain1, bias1, gain2, bias2, bias_out = (v.vectors[i : i + 1] for i in range(5))
    (
        v.rows_bzy, v.z2a, v.z2b, v.x2, v.base3a, v.base3b, v.base3, v.core1, v.cot_a, v.cot_b,
    ) = tie(
        v.rows_bzy, v.z2a, v.z2b, v.x2, v.base3a, v.base3b, v.base3, v.core1, v.cot_a, v.cot_b,
    )

    v.swapped1 = swap_grp(v.core1, 1)
    v.cot_az = swap_seq(v.cot_a, 2)
    v.cot_ay = swap_seq(v.cot_a, 1)
    v.zx2 = swap_grp(stacked([v.z2a, v.z2b]), 2)
    v.z3a = swap_seq(v.base3a, 4)
    v.rows, v.first_low, v.second_low, mean, spread = both_low_norms(
        [v.own_a, v.rows_az, v.rows_ay, v.rows_azy, v.own_b, v.rows_by, v.rows_bz, v.rows_bzy],
        gain1,
        bias1,
        gain2,
        bias2,
    )
    v.core2 = beside(
        [(v.base2a, v.base2b), (v.z2a, v.z2b), v.x2, v.zx2]
    )
    (
        v.first_low, v.second_low, v.core2, v.swapped1, v.core1, v.base3, v.base3b, v.cot_az,
        v.cot_ay, v.z3a, v.cot_b,
    ) = tie(
        v.first_low, v.second_low, v.core2, v.swapped1, v.core1, v.base3, v.base3b, v.cot_az,
        v.cot_ay, v.z3a, v.cot_b,
    )
    v.cot_by = swap_seq(v.cot_b, 1)
    v.cot_bz = swap_seq(v.cot_b, 2)
    v.z3b = swap_seq(v.base3b, 4)
    v.x3 = swap_grp(v.base3, 2)
    v.swapped2 = swap_grp(v.core2, 1)
    weight1 = (v.core1, v.swapped1)
    v.query0, v.key0, v.value0, own0 = project_qkv(
        0, v.first_low, weight1, qkv_bias_here, *tables
    )
    v.query0, v.first_low = tie(v.query0, v.first_low)
    v.query1, v.key1, v.value1, own1_kv = project_qkv(
        1, v.first_low, weight1, qkv_bias_here, *tables
    )
    (
        v.query1, v.second_low, v.swapped2, v.core2, v.cot_az, v.x3, v.cot_by, v.cot_bz, v.z3b,
        v.key0, v.z3a,
    ) = tie(
        v.query1, v.second_low, v.swapped2, v.core2, v.cot_az, v.x3, v.cot_by, v.cot_bz, v.z3b,
        v.key0, v.z3a,
    )
    v.cot_azy = swap_seq(v.cot_az, 1)
    v.cot_bzy = swap_seq(v.cot_by, 2)
    v.far_key0 = swap_seq(v.key0, 4)
    v.zx3 = swap_grp(stacked([v.z3a, v.z3b]), 2)
    weight2 = (v.core2, v.swapped2)
    v.act_low, v.slope = feed_forward_up(v.second_low, weight2, up_bias_here)
    (
        v.act_low, v.slope, v.cot_azy, v.cot_bzy, v.far_key0, v.zx3, v.value0,
    ) = tie(
        v.act_low, v.slope, v.cot_azy, v.cot_bzy, v.far_key0, v.zx3, v.value0,
    )
    v.far_value0 = swap_seq(v.value0, 4)
    v.core3 = beside(
        [(v.base3a, v.base3b), (v.z3a, v.z3b), v.x3, v.zx3]
    )
    v.swapped3 = swap_grp(v.core3, 1)
    v.attn_grad, v.cots = attention_grad(
        [v.cot_a, v.cot_az, v.cot_ay, v.cot_azy, v.cot_b, v.cot_by, v.cot_bz, v.cot_bzy],
        weight1,
        3,
    )
    v.attn_grad, v.cots, v.act_low = tie(v.attn_grad, v.cots, v.act_low)
    v.down_away = weight_grad(v.cots, [v.act_low])
    (
        v.down_away, v.far_value0, v.key1, v.value1, v.attn_grad, v.swapped3, v.core3,
    ) = tie(
        v.down_away, v.far_value0, v.key1, v.value1, v.attn_grad, v.swapped3, v.core3,
    )
    v.down_core = swap_grp(v.down_away, 1)
    v.far_key1 = swap_seq(v.key1, 4)
    v.attn0, dq0, down0, dnear0, v.dfar_key0, v.dfar_value0 = attend(
        0,
        v.query0,
        v.attn_grad,
        (v.key0, v.value0),
        (v.far_key0, v.far_value0),
        own0,
        *shared,
    )
    (
        v.attn0, v.down_core, v.cots, v.act_low, v.far_key1, v.value1,
    ) = tie(
        v.attn0, v.down_core, v.cots, v.act_low, v.far_key1, v.value1,
    )
    v.far_value1 = swap_seq(v.value1, 4)
    v.down_mine, v.down_send = weight_grad(v.cots, [v.act_low], v.down_core)
    (
        v.down_mine, v.down_send, v.cots, v.slope, v.core3, v.swapped3,
    ) = tie(
        v.down_mine, v.down_send, v.cots, v.slope, v.core3, v.swapped3,
    )
    v.down_side = swap_grp(v.down_send, 2)
    weight3 = (v.core3, v.swapped3)
    v.hidden_grad, up_bias_term = feed_forward_back(v.cots, weight3, v.slope)
    (
        v.hidden_grad, v.far_value1, v.dfar_key0, v.dfar_value0, v.attn_grad,
    ) = tie(
        v.hidden_grad, v.far_value1, v.dfar_key0, v.dfar_value0, v.attn_grad,
    )
    v.back_key0 = swap_seq(v.dfar_key0, 4)
    v.back_value0 = swap_seq(v.dfar_value0, 4)
    v.attn1, dq1, down1, v.dnear1, v.dfar_key1, v.dfar_value1 = attend(
        1,
        v.query1,
        v.attn_grad,
        (v.key1, v.value1),
        (v.far_key1, v.far_value1),
        own1_kv,
        *shared,
    )
    (
        v.attn1, v.second_low, v.hidden_grad, v.down_side, v.down_mine,
    ) = tie(
        v.attn1, v.second_low, v.hidden_grad, v.down_side, v.down_mine,
    )
    v.up_away = weight_grad(v.second_low, [v.hidden_grad])
    v.down_half_send = second_sum(v.down_mine, v.down_side)
    (
        v.up_away, v.back_key0, v.back_value0, v.dfar_key1, v.dfar_value1, v.act_low,
        v.down_half_send,
    ) = tie(
        v.up_away, v.back_key0, v.back_value0, v.dfar_key1, v.dfar_value1, v.act_low,
        v.down_half_send,
    )
    v.up_core = swap_grp(v.up_away, 1)
    v.back_key1 = swap_seq(v.dfar_key1, 4)
    branch = branch_outputs((v.attn0, v.attn1), v.act_low, weight1, 3, weight3)
    v.branch0, v.branch_y, v.branch_zy, v.branch2, v.branch_z, v.branch_yz = branch
    (
        v.branch0, v.branch_y, v.branch_zy, v.branch2, v.branch_z, v.branch_yz, v.up_core,
        v.second_low, v.hidden_grad, v.back_key1, v.dfar_value1,
    ) = tie(
        v.branch0, v.branch_y, v.branch_zy, v.branch2, v.branch_z, v.branch_yz, v.up_core,
        v.second_low, v.hidden_grad, v.back_key1, v.dfar_value1,
    )
    v.got_zy = swap_seq(v.branch_zy, 1)
    v.got_yz = swap_seq(v.branch_yz, 2)
    v.back_value1 = swap_seq(v.dfar_value1, 4)
    v.up_mine, v.up_send = weight_grad(v.second_low, [v.hidden_grad], v.up_core)
    v.up_mine, v.hidden_grad = tie(v.up_mine, v.hidden_grad)
    second_parts, second_sums = norm_grad(
        v.hidden_grad, weight2, gain2, v.rows, mean, spread, (0, 1, 2, 3)
    )
    v.second0, second1, second2, second3 = second_parts
    (
        v.second0, v.back_value1, v.dnear1, v.cots, v.down_half_send, v.up_send, v.got_zy,
        v.got_yz, v.branch0, v.branch2, v.branch_y, v.branch_z,
    ) = tie(
        v.second0, v.back_value1, v.dnear1, v.cots, v.down_half_send, v.up_send, v.got_zy,
        v.got_yz, v.branch0, v.branch2, v.branch_y, v.branch_z,
    )
    v.up_side = swap_grp(v.up_send, 2)
    v.down_half = swap_seq(v.down_half_send, 4)
    v.got_y = swap_seq(v.branch_y, 1)
    v.got_z = swap_seq(v.branch_z, 2)
    v.branch_a_far = second_sum(v.branch0, v.got_zy)
    v.branch_b_far = second_sum(v.branch2, v.got_yz)
    v.qkv_grad, qkv_bias_term = join_grads(
        (dq0, dq1),
        (down0, down1),
        (dnear0, v.dnear1),
        (v.back_key0, v.back_key1),
        (v.back_value0, v.back_value1),
    )
    v.qkv_grad, v.first_low, v.cots = tie(v.qkv_grad, v.first_low, v.cots)
    v.qkv_away = weight_grad(v.first_low, [v.qkv_grad])
    v.qkv_away, v.cots = tie(v.qkv_away, v.cots)
    v.out_away = weight_grad(v.cots, [v.attn0, v.attn1])
    (
        v.out_away, v.qkv_away, v.got_y, v.got_z, v.branch_a_far, v.branch_b_far, v.down_half,
        v.up_side, v.up_mine, v.qkv_grad,
    ) = tie(
        v.out_away, v.qkv_away, v.got_y, v.got_z, v.branch_a_far, v.branch_b_far, v.down_half,
        v.up_side, v.up_mine, v.qkv_grad,
    )
    v.qkv_core = swap_grp(v.qkv_away, 1)
    down_own, v.down_side2, v.down_far = split_rows(
        [(v.down_mine, v.down_side, (v.down_half,))], tp_rank
    )
    v.up_send_a = second_sum(v.up_mine, v.up_side, 0)
    v.up_half_a = swap_seq(v.up_send_a, 4)
    v.branch_far_a = swap_seq(v.branch_a_far, 2)
    v.branch_far_b = swap_seq(v.branch_b_far, 1)
    v.down_y = swap_seq(v.down_side2, 1)
    v.up_send_b = second_sum(v.up_mine, v.up_side, 1)
    (
        v.qkv_core, v.first_low, v.qkv_grad, v.up_send_b,
    ) = tie(
        v.qkv_core, v.first_low, v.qkv_grad, v.up_send_b,
    )
    v.qkv_mine, v.qkv_send = weight_grad(v.first_low, [v.qkv_grad], v.qkv_core)
    v.qkv_mine, v.qkv_send, v.qkv_grad = tie(v.qkv_mine, v.qkv_send, v.qkv_grad)
    v.qkv_side = swap_grp(v.qkv_send, 2)
    entry_far, v.far_sums = norm_grad(
        v.qkv_grad, weight1, gain1, v.rows, mean, spread, (1, 3), (second1, second3), True
    )
    v.entry_y, v.entry_zy, v.entry_z, v.entry_yz = entry_far
    (
        v.entry_y, v.entry_zy, v.entry_z, v.entry_yz, v.far_sums, v.out_away, v.branch_far_a,
        v.branch_far_b, v.down_y, v.down_far, v.up_half_a, v.up_send_b, v.qkv_grad, v.second0,
    ) = tie(
        v.entry_y, v.entry_zy, v.entry_z, v.entry_yz, v.far_sums, v.out_away, v.branch_far_a,
        v.branch_far_b, v.down_y, v.down_far, v.up_half_a, v.up_send_b, v.qkv_grad, v.second0,
    )
    v.entry_got_zy = swap_seq(v.entry_zy, 1)
    v.entry_got_yz = swap_seq(v.entry_yz, 2)
    v.out_core = swap_grp(v.out_away, 1)
    v.up_half_b = swap_seq(v.up_send_b, 4)
    (v.entry0, v.entry2), v.near_sums = norm_grad(
        v.qkv_grad, weight1, gain1, v.rows, mean, spread, (0, 2), (v.second0, second2)
    )
    (
        v.near_sums, v.out_core, v.cots, v.qkv_side, v.qkv_mine, v.up_half_b, v.branch0,
        v.entry_got_zy, v.entry_got_yz, v.entry_y, v.entry_z, v.entry0, v.entry2,
    ) = tie(
        v.near_sums, v.out_core, v.cots, v.qkv_side, v.qkv_mine, v.up_half_b, v.branch0,
        v.entry_got_zy, v.entry_got_yz, v.entry_y, v.entry_z, v.entry0, v.entry2,
    )
    v.entry_got_y = swap_seq(v.entry_y, 1)
    v.entry_got_z = swap_seq(v.entry_z, 2)
    v.qkv_half_send = second_sum(v.qkv_mine, v.qkv_side)
    v.qkv_half = swap_seq(v.qkv_half_send, 4)
    v.out_mine, v.out_send = weight_grad(
        v.cots, [v.attn0, v.attn1], v.out_core
    )
    v.out_side = swap_grp(v.out_send, 2)

    rank_ids = jnp.arange(TP, dtype=jnp.int32)
    first_sums = v.far_sums + v.near_sums
    wide_sums = jnp.concatenate(
        [first_sums[:2], second_sums[:2], cot_sum, jnp.zeros((3, D), F32)], axis=0
    )
    wide_sums = restore_runs(wide_sums, place_index)
    qkv_bias_term = qkv_bias_term.reshape(3, 1, HCOLS)
    v.sums = jnp.concatenate(
        [
            wide_sums[:5].reshape(-1),
            jnp.where((rank_ids == tp_rank)[None, :, None], qkv_bias_term, 0.0).reshape(-1),
            jnp.where((rank_ids == tp_rank)[:, None], up_bias_term, 0.0).reshape(-1),
        ]
    ).reshape(-1, LANES)
    v.sums_got = swap_grp(v.sums, 1)
    v.entry_a_far = second_sum(v.entry0, v.entry_got_zy)
    v.entry_b_far = second_sum(v.entry2, v.entry_got_yz)
    (
        v.sums, v.sums_got, v.out_send, v.out_mine, v.entry_got_y, v.entry_got_z, v.entry_a_far,
        v.entry_b_far, v.branch0, v.up_half_b,
    ) = tie(
        v.sums, v.sums_got, v.out_send, v.out_mine, v.entry_got_y, v.entry_got_z, v.entry_a_far,
        v.entry_b_far, v.branch0, v.up_half_b,
    )
    v.entry_far_a = swap_seq(v.entry_a_far, 2)
    v.entry_far_b = swap_seq(v.entry_b_far, 1)
    v.sums = v.sums + v.sums_got
    v.sums_got = swap_grp(v.sums, 2)
    v.layer_a, v.layer_b = finish_outputs(
        (
            (v.branch0, v.got_y, v.branch_far_a),
            (v.branch2, v.got_z, v.branch_far_b),
        ),
        (v.own_a, v.own_b),
        bias_out,
        place_index,
    )
    up_own, v.up_side2, v.up_far = split_rows(
        [(v.up_mine, v.up_side, (v.up_half_a, v.up_half_b))], tp_rank
    )
    (
        v.layer_a, v.sums, v.sums_got, v.up_side2, v.out_side, v.out_mine, v.qkv_half,
    ) = tie(
        v.layer_a, v.sums, v.sums_got, v.up_side2, v.out_side, v.out_mine, v.qkv_half,
    )
    v.out_half_send = second_sum(v.out_mine, v.out_side)
    v.out_half = swap_seq(v.out_half_send, 4)
    v.up_y = swap_seq(v.up_side2, 1)
    v.sums = v.sums + v.sums_got
    v.sums_got = swap_seq(v.sums, 4)
    (
        v.entry_far_a, v.entry_far_b, v.out_half, v.up_y, v.up_far, v.down_far, v.sums,
        v.sums_got,
    ) = tie(
        v.entry_far_a, v.entry_far_b, v.out_half, v.up_y, v.up_far, v.down_far, v.sums,
        v.sums_got,
    )
    late_own, late_side, late_far = split_rows(
        [
            (v.qkv_mine, v.qkv_side, (v.qkv_half,)),
            (v.out_mine, v.out_side, (v.out_half,)),
        ],
        tp_rank,
    )
    v.late_y = swap_seq(late_side, 1)
    v.down_z = swap_seq(onward(v.down_far, v.down_y), 2)
    v.up_z = swap_seq(onward(v.up_far, v.up_y), 2)
    v.sums = v.sums + v.sums_got
    v.sums_got = swap_seq(v.sums, 1)
    v.grad_a, grad_b = finish_grads(
        (
            (v.entry0, v.entry_got_y, v.entry_far_a),
            (v.entry2, v.entry_got_z, v.entry_far_b),
        ),
        (v.own_a, v.own_b),
        (v.cot_a, v.cot_b),
        place_index,
    )
    (
        v.grad_a, v.late_y, v.down_z, v.up_z, v.sums, v.sums_got,
    ) = tie(
        v.grad_a, v.late_y, v.down_z, v.up_z, v.sums, v.sums_got,
    )
    v.late_z = swap_seq(onward(late_far, v.late_y), 2)
    v.sums = v.sums + v.sums_got
    v.sums_got = swap_seq(v.sums, 2)
    (v.down_grad,) = join_columns(
        down_own, v.down_y, v.down_z, [(1, ff_here)], tp_rank
    )
    (v.up_grad,) = join_columns(up_own, v.up_y, v.up_z, [(1, ff_here)], tp_rank)
    grad_a, down_grad, up_weight_grad = v.grad_a, v.down_grad, v.up_grad
    qkv_weight_grad, out_grad = join_columns(
        late_own, v.late_y, v.late_z, [(3, HCOLS), (1, HCOLS)], tp_rank
    )
    down_weight_grad, out_weight_grad = down_grad.T, out_grad.T
    sums = (v.sums + v.sums_got).reshape(-1)
    cuts = np.cumsum([D, D, D, D, D, 3 * D])
    gain_one, shift_one, gain_two, shift_two, out_sum, qkv_sum, up_sum = jnp.split(sums, cuts)

    return (
        v.layer_a[None],
        v.layer_b[None, None],
        grad_a[None],
        grad_b[None, None],
        gain_one,
        shift_one,
        gain_two,
        shift_two,
        qkv_weight_grad,
        qkv_sum,
        out_weight_grad,
        out_sum,
        up_weight_grad,
        up_sum,
        down_weight_grad,
        out_sum,
    )


def solution(mesh):
    in_specs = (
        P("grp", "seq", None),
        P("grp", "seq", None, None),
        P("grp", "seq"),
        P("grp", None),
        P(),
        P(),
        P(),
        P(),
        P(("grp", "seq"), None),
        P(),
        P(None, ("grp", "seq")),
        P(),
        P(("grp", "seq"), None),
        P(),
        P(None, ("grp", "seq")),
        P(),
        P("grp", "seq", None),
        P("grp", "seq", None, None),
    )
    out_specs = (
        P("grp", "seq", None),
        P("grp", "seq", None, None),
        P("grp", "seq", None),
        P("grp", "seq", None, None),
        P(),
        P(),
        P(),
        P(),
        P(("grp", "seq"), None),
        P(),
        P(None, ("grp", "seq")),
        P(),
        P(("grp", "seq"), None),
        P(),
        P(None, ("grp", "seq")),
        P(),
    )
    plan = square_plan if (mesh.shape["grp"], mesh.shape["seq"]) == (4, 8) else local
    return jax.shard_map(plan, mesh=mesh, in_specs=in_specs, out_specs=out_specs, check_vma=False)
```

```python
from functools import partial
import math

import jax
import jax.numpy as jnp
import numpy as np
from jax import lax
from jax.experimental import pallas as pl
from jax.experimental.pallas import tpu as pltpu
from jax.sharding import PartitionSpec as P

D = 2048
HEADS = 8
HEAD = 256
ROT = 64
PROMPT = 2048


EPSILON = 1e-05
NEG_FILL = -1e30
ROPE_BASE = 10000.0


def layer_norm(values, ln_gain, ln_shift):
    center = values - jnp.mean(values, axis=-1, keepdims=True)
    normed = center * lax.rsqrt(jnp.mean(center * center, axis=-1, keepdims=True) + EPSILON)
    return normed * ln_gain + ln_shift


def both_norms(values, gain_one, shift_one, gain_two, shift_two):
    return (layer_norm(values, gain_one, shift_one), layer_norm(values, gain_two, shift_two))


def rotate(head_data, positions, sign_flip):
    half_rot = ROT // 2
    inv_freq = ROPE_BASE ** (-(2.0 * jnp.arange(half_rot, dtype=jnp.float32)) / ROT)
    angles = positions[:, None] * inv_freq[None, :]
    cos_table = jnp.cos(angles)[:, None, :]
    sin_table = sign_flip * jnp.sin(angles)[:, None, :]
    first_half = head_data[..., :half_rot]
    second = head_data[..., half_rot:ROT]
    return jnp.concatenate(
        [
            first_half * cos_table - second * sin_table,
            second * cos_table + first_half * sin_table,
            head_data[..., ROT:],
        ],
        axis=-1,
    )


def contract_rows(left, right):
    return lax.dot_general(
        left, right, (((1,), (1,)), ((), ())), preferred_element_type=jnp.float32
    )


def contract_cols(left, right):
    return lax.dot_general(
        left, right, (((0,), (0,)), ((), ())), preferred_element_type=jnp.float32
    )


def local(
    prompt,
    conts,
    assignment,
    offsets,
    ln1_gain,
    ln1_bias,
    ln2_gain,
    ln2_bias,
    qkv_weight,
    qkv_bias,
    out_weight,
    out_bias,
    up_weight,
    up_bias,
    down_weight,
    down_bias,
    prompt_cot,
    cont_cot,
):
    prompt_rows = prompt.shape[1]
    cont_rows = conts.shape[2]
    row_total = prompt_rows + cont_rows
    score_scale = 1.0 / math.sqrt(HEAD)
    shard_index = lax.axis_index("seq")
    tokens = jnp.concatenate([prompt[0], conts[0, 0]], axis=0).astype(jnp.float32)
    branch_ids = jnp.arange(offsets.shape[1], dtype=jnp.int32)
    my_offset = jnp.sum(jnp.where(branch_ids == assignment[0, 0], offsets[0], 0))
    prompt_mark = shard_index * prompt_rows + jnp.arange(prompt_rows, dtype=jnp.int32)
    cont_mark = PROMPT + jnp.arange(cont_rows, dtype=jnp.int32)
    query_mark = jnp.concatenate([prompt_mark, cont_mark])
    positions = jnp.concatenate([prompt_mark, cont_mark + my_offset]).astype(jnp.float32)
    (first_norm, second_norm), norm_pullback = jax.vjp(
        both_norms, tokens, ln1_gain, ln1_bias, ln2_gain, ln2_bias
    )
    first_low = first_norm.astype(jnp.bfloat16)
    second_low = second_norm.astype(jnp.bfloat16)
    qkv_full, up_full = (
        lax.all_gather(qkv_weight, ("grp", "seq"), axis=0, tiled=True),
        lax.all_gather(up_weight, ("grp", "seq"), axis=0, tiled=True),
    )
    qkv_acc = jnp.dot(first_low, qkv_full, preferred_element_type=jnp.float32)
    up_acc = jnp.dot(second_low, up_full, preferred_element_type=jnp.float32)
    split_qkv = (qkv_acc + qkv_bias).reshape(row_total, 3, HEADS, HEAD)
    queries = rotate(split_qkv[:, 0], positions, 1.0).astype(jnp.bfloat16)
    keys_rot = rotate(split_qkv[:, 1], positions, 1.0).astype(jnp.bfloat16)
    values_low = split_qkv[:, 2].astype(jnp.bfloat16)
    hidden_pre = up_acc + up_bias
    activated, gelu_pullback = jax.vjp(partial(jax.nn.gelu, approximate=False), hidden_pre)
    act_low = activated.astype(jnp.bfloat16)

    def score_block(key_block, key_mark):
        raw_scores = (
            jnp.einsum("qhd,khd->hqk", queries, key_block, preferred_element_type=jnp.float32)
            * score_scale
        )
        allowed = key_mark[None, :] <= query_mark[:, None]
        return (raw_scores, allowed)

    def absorb(soft_state, key_block, value_block, key_mark):
        run_max, run_sum, run_acc = soft_state
        raw_scores, allowed = score_block(key_block, key_mark)
        masked = jnp.where(allowed[None], raw_scores, NEG_FILL)
        new_max = jnp.maximum(run_max, jnp.max(masked, axis=-1))
        exp_scores = jnp.where(allowed[None], jnp.exp(masked - new_max[..., None]), 0.0)
        factor = jnp.exp(run_max - new_max)
        mixed_heads = jnp.einsum(
            "hqk,khd->qhd",
            exp_scores.astype(jnp.bfloat16),
            value_block,
            preferred_element_type=jnp.float32,
        )
        return (
            new_max,
            run_sum * factor + jnp.sum(exp_scores, axis=-1),
            run_acc * factor.T[:, :, None] + mixed_heads,
        )

    cont_keys = keys_rot[prompt_rows:]
    cont_values = values_low[prompt_rows:]
    start_state = (
        jnp.full((HEADS, row_total), NEG_FILL, jnp.float32),
        jnp.zeros((HEADS, row_total), jnp.float32),
        jnp.zeros((row_total, HEADS, HEAD), jnp.float32),
    )
    start_state = absorb(start_state, cont_keys, cont_values, cont_mark)
    prompt_keys_send = keys_rot[:prompt_rows].reshape(prompt_rows, D)
    prompt_values_send = values_low[:prompt_rows].reshape(prompt_rows, D)
    key_piece = lax.all_gather(prompt_keys_send, "seq", axis=0, tiled=True)
    value_piece = lax.all_gather(prompt_values_send, "seq", axis=0, tiled=True)
    piece_width = key_piece.shape[0]
    key_mark = jnp.arange(piece_width, dtype=jnp.int32)
    run_max, run_sum, run_acc = absorb(
        start_state,
        key_piece.reshape(piece_width, HEADS, HEAD),
        value_piece.reshape(piece_width, HEADS, HEAD),
        key_mark,
    )
    attention = run_acc / run_sum.T[:, :, None]
    log_total = run_max + jnp.log(run_sum)
    attention_low = attention.reshape(row_total, D).astype(jnp.bfloat16)
    out_full, down_full = (
        lax.all_gather(out_weight, ("grp", "seq"), axis=1, tiled=True),
        lax.all_gather(down_weight, ("grp", "seq"), axis=1, tiled=True),
    )
    branch_sum = jnp.dot(attention_low, out_full, preferred_element_type=jnp.float32) + jnp.dot(
        act_low, down_full, preferred_element_type=jnp.float32
    )
    layer_out = tokens + branch_sum + out_bias + down_bias
    grad_out = jnp.concatenate([prompt_cot[0], cont_cot[0, 0]], axis=0)
    grad_f32 = grad_out.astype(jnp.float32)
    bias_out_term = jnp.sum(grad_f32, axis=0)
    out_again, down_again = (
        lax.all_gather(out_weight, ("grp", "seq"), axis=1, tiled=True),
        lax.all_gather(down_weight, ("grp", "seq"), axis=1, tiled=True),
    )
    attn_grad = contract_rows(grad_out, out_again)
    act_grad = contract_rows(grad_out, down_again)
    attn_grad_low = attn_grad.astype(jnp.bfloat16)
    (hidden_grad,) = gelu_pullback(act_grad)
    hidden_grad_low = hidden_grad.astype(jnp.bfloat16)
    up_bias_term = jnp.sum(hidden_grad_low.astype(jnp.float32), axis=0)
    grad_heads = attn_grad_low.reshape(row_total, HEADS, HEAD)
    row_delta = jnp.sum(grad_heads.astype(jnp.float32) * attention, axis=-1).T

    def back_block(key_block, value_block, key_mark):
        raw_scores, allowed = score_block(key_block, key_mark)
        probabilities = jnp.exp(
            jnp.where(allowed[None], raw_scores - log_total[..., None], NEG_FILL)
        )
        prob_grad = jnp.einsum(
            "qhd,khd->hqk", grad_heads, value_block, preferred_element_type=jnp.float32
        )
        score_grad = (probabilities * (prob_grad - row_delta[..., None])).astype(jnp.bfloat16)
        query_term = (
            jnp.einsum("hqk,khd->qhd", score_grad, key_block, preferred_element_type=jnp.float32)
            * score_scale
        )
        key_term = (
            jnp.einsum("hqk,qhd->khd", score_grad, queries, preferred_element_type=jnp.float32)
            * score_scale
        )
        value_term = jnp.einsum(
            "hqk,qhd->khd",
            probabilities.astype(jnp.bfloat16),
            grad_heads,
            preferred_element_type=jnp.float32,
        )
        return (query_term, key_term, value_term)

    query_local, key_local, value_local = back_block(cont_keys, cont_values, cont_mark)
    gathered_keys, gathered_values = (
        lax.all_gather(prompt_keys_send, "seq", axis=0, tiled=True),
        lax.all_gather(prompt_values_send, "seq", axis=0, tiled=True),
    )
    key_block_size = min(512, PROMPT)
    block_count = PROMPT // key_block_size

    def scan_step(query_total, inputs):
        key_block, value_block, block_start = inputs
        key_mark = block_start + jnp.arange(key_block_size, dtype=jnp.int32)
        query_term, key_term, value_term = back_block(
            key_block.reshape(key_block_size, HEADS, HEAD),
            value_block.reshape(key_block_size, HEADS, HEAD),
            key_mark,
        )
        return (
            query_total + query_term,
            (key_term.reshape(key_block_size, D), value_term.reshape(key_block_size, D)),
        )

    query_grad, (key_terms, value_terms) = lax.scan(
        scan_step,
        query_local,
        (
            gathered_keys.reshape(block_count, key_block_size, D),
            gathered_values.reshape(block_count, key_block_size, D),
            jnp.arange(block_count, dtype=jnp.int32) * key_block_size,
        ),
    )
    key_prompt_grad, value_prompt_grad = (
        lax.psum_scatter(
            key_terms.reshape(PROMPT, D).astype(jnp.bfloat16),
            "seq",
            scatter_dimension=0,
            tiled=True,
        ).astype(jnp.float32),
        lax.psum_scatter(
            value_terms.reshape(PROMPT, D).astype(jnp.bfloat16),
            "seq",
            scatter_dimension=0,
            tiled=True,
        ).astype(jnp.float32),
    )
    key_grad = jnp.concatenate([key_prompt_grad, key_local.reshape(cont_rows, D)], axis=0).reshape(
        row_total, HEADS, HEAD
    )
    value_grad = jnp.concatenate(
        [value_prompt_grad, value_local.reshape(cont_rows, D)], axis=0
    ).reshape(row_total, HEADS, HEAD)
    qkv_grad = (
        jnp.stack(
            [rotate(query_grad, positions, -1.0), rotate(key_grad, positions, -1.0), value_grad],
            axis=1,
        )
        .reshape(row_total, 3 * D)
        .astype(jnp.bfloat16)
    )
    qkv_bias_term = jnp.sum(qkv_grad.astype(jnp.float32), axis=0)
    qkv_again, up_again = (
        lax.all_gather(qkv_weight, ("grp", "seq"), axis=0, tiled=True),
        lax.all_gather(up_weight, ("grp", "seq"), axis=0, tiled=True),
    )
    first_grad = contract_rows(qkv_grad, qkv_again)
    second_grad = contract_rows(hidden_grad_low, up_again)
    token_grad, gain_one, shift_one, gain_two, shift_two = norm_pullback((first_grad, second_grad))
    token_grad = token_grad + grad_f32
    small_sums = lax.psum(
        (gain_one, shift_one, gain_two, shift_two, qkv_bias_term, bias_out_term, up_bias_term),
        ("grp", "seq"),
    )
    out_sources = jnp.concatenate([attention_low, act_low], axis=1)
    in_group = lax.psum_scatter(
        jnp.concatenate(
            [contract_cols(first_low, qkv_grad), contract_cols(second_low, hidden_grad_low)], axis=1
        ).astype(jnp.bfloat16),
        "grp",
        scatter_dimension=0,
        tiled=True,
    )
    in_share = lax.psum_scatter(in_group, "seq", scatter_dimension=0, tiled=True).astype(
        jnp.float32
    )
    out_group = lax.psum_scatter(
        contract_cols(grad_out, out_sources).astype(jnp.bfloat16),
        "grp",
        scatter_dimension=0,
        tiled=True,
    )
    out_share = lax.psum_scatter(out_group, "seq", scatter_dimension=0, tiled=True).astype(
        jnp.float32
    )
    qkv_weight_grad = in_share[:, : 3 * D]
    up_weight_grad = in_share[:, 3 * D :]
    out_weight_grad = out_share[:, :D].T
    down_weight_grad = out_share[:, D:].T
    prompt_result = layer_out[:prompt_rows][None]
    cont_result = layer_out[prompt_rows:][None, None]
    prompt_grad = token_grad[:prompt_rows][None]
    cont_grad = token_grad[prompt_rows:][None, None]
    return (
        prompt_result,
        cont_result,
        prompt_grad,
        cont_grad,
        small_sums[0],
        small_sums[1],
        small_sums[2],
        small_sums[3],
        qkv_weight_grad,
        small_sums[4],
        out_weight_grad,
        small_sums[5],
        up_weight_grad,
        small_sums[6],
        down_weight_grad,
        small_sums[5],
    )


PROMPT_ORDER = (0, 2, 1, 3)
CONT_ORDER = (0, 1, 2, 3)
WIDTH_ORDER = (0, 1, 4, 5, 2, 3, 6, 7)
TP = 4
HEADS_HERE = HEADS // TP
HCOLS = HEADS_HERE * HEAD
LANES = 128
COST_UNIT = 1.0e6
COSTS = {
    "norms": 15,
    "qkv_rotary": 12,
    "feed_forward_up": 30,
    "attention_grad": 11,
    "weight_grad": 14,
    "attention_both_ways": 28,
    "feed_forward_back": 25,
    "branch_outputs": 34,
    "norm_grad": 25,
    "join_grads": 8,
    "finish_outputs": 7,
    "finish_grads": 9,
}
BF = jnp.bfloat16
F32 = jnp.float32


def swap_grp(array, bits):
    return lax.ppermute(array, "grp", [(i, i ^ bits) for i in range(4)])


def swap_seq(array, bits):
    return lax.ppermute(array, "seq", [(i, i ^ bits) for i in range(8)])


def matmul_nn(left, right):
    return jnp.dot(left, right, preferred_element_type=F32)


def pick(array, index, axis):
    return lax.dynamic_index_in_dim(array, index, axis, keepdims=False)


def place(buffer, piece, index):
    return lax.dynamic_update_index_in_dim(buffer, piece, index, 0)


def tie(*arrays):
    return lax.optimization_barrier(arrays)


def whole(shape):
    return pl.BlockSpec(shape, lambda i, rank: (0,) * len(shape))


def cost(name):
    flops = int(COSTS.get(name, 2) * COST_UNIT)
    return pl.CostEstimate(flops=flops, transcendentals=0, bytes_accessed=0)


def ranked_call(body, rank, ins, shapes, name, blocks=None):
    return pl.pallas_call(
        body,
        grid_spec=pltpu.PrefetchScalarGridSpec(
            num_scalar_prefetch=1,
            grid=(1,),
            in_specs=[whole(shape) for shape in blocks or [a.shape for a in ins]],
            out_specs=[whole(s.shape) for s in shapes],
        ),
        out_shape=shapes,
        compiler_params=pltpu.CompilerParams(vmem_limit_bytes=56 << 20),
        cost_estimate=cost(name),
        name=name,
    )(rank.reshape(1), *ins)


def split_columns(shards, groups, tp_rank):
    rows = shards[0].shape[0]
    widths = [shard.shape[1] // (TP * count) for shard, count in zip(shards, groups)]
    cols = sum(width * count for width, count in zip(widths, groups))

    def body(rank_ref, *refs):
        ins, (own_ref, side_ref, far_ref) = refs[: len(shards)], refs[len(shards) :]
        at = 0
        for ref, count, width in zip(ins, groups, widths):
            for part in range(count):
                for bits in range(TP):
                    start = pl.multiple_of((part * TP + (rank_ref[0] ^ bits)) * width, width)
                    run = ref[:, pl.ds(start, width)]
                    here = slice(at, at + width)
                    if bits == 0:
                        own_ref[:, here] = run
                    elif bits == 2:
                        far_ref[:, here] = run
                    else:
                        side_ref[bits // 2, :, here] = run
                at += width

    shapes = [
        jax.ShapeDtypeStruct((rows, cols), BF),
        jax.ShapeDtypeStruct((2, rows, cols), BF),
        jax.ShapeDtypeStruct((rows, cols), BF),
    ]
    return ranked_call(body, tp_rank, list(shards), shapes, "split_columns")


def stack_ranks(own, over_y, over_z, cuts, tp_rank, uncut=False):
    rows, cols = own.shape
    runs = [slice(sum(cuts[:i]), sum(cuts[: i + 1])) for i in range(len(cuts))]
    if uncut:
        runs.append(slice(0, cols))

    def body(rank_ref, own_ref, y_ref, z_ref, *outs):
        for out, here in zip(outs, runs):
            pieces = (own_ref[:, here], y_ref[0, :, here], z_ref[0, :, here], z_ref[1, :, here])
            for bits, piece in enumerate(pieces):
                start = pl.multiple_of((rank_ref[0] ^ bits) * rows, rows)
                out[pl.ds(start, rows), :] = piece

    shapes = [jax.ShapeDtypeStruct((TP * rows, run.stop - run.start), BF) for run in runs]
    return ranked_call(body, tp_rank, [own, over_y, over_z], shapes, "stack_ranks")


def split_rows(groups, tp_rank, first=1):
    rows = groups[0][2][0].shape[0] // TP
    cols = sum(terms[0].shape[1] for terms in groups)
    flat = [array for kept, got_x, got_z in groups for array in (kept, got_x, *got_z)]

    def body(rank_ref, *refs):
        ins, (own_ref, side_ref, far_ref) = list(refs[: len(flat)]), refs[len(flat) :]
        at = 0
        for _, _, got_z in groups:
            kept, got_x = ins.pop(0), ins.pop(0)
            inside = 0
            for _ in got_z:
                run_ref = ins.pop(0)
                width = run_ref.shape[1]
                here, cut = slice(at, at + width), slice(inside, inside + width)
                at, inside = at + width, inside + width
                for bits in range(TP):
                    lines = pl.ds(pl.multiple_of((rank_ref[0] ^ bits) * rows, rows), rows)
                    total = kept[lines, cut].astype(F32) + got_x[lines, cut].astype(F32)
                    run = (total + run_ref[lines, :].astype(F32)).astype(BF)
                    if bits == 0:
                        own_ref[:, here] = run
                    elif bits == 3 - first:
                        far_ref[:, here] = run
                    else:
                        side_ref[int(bits == 3), :, here] = run

    shapes = [
        jax.ShapeDtypeStruct((rows, cols), BF),
        jax.ShapeDtypeStruct((2, rows, cols), BF),
        jax.ShapeDtypeStruct((rows, cols), BF),
    ]
    blocks = [(TP * rows, term.shape[1]) for term in flat]
    return ranked_call(body, tp_rank, flat, shapes, "split_rows", blocks)


def join_columns(own, got_first, got_second, parts, tp_rank, first=1):
    rows = own.shape[0]

    def body(rank_ref, own_ref, first_ref, second_ref, *outs):
        at = 0
        for out, (count, width) in zip(outs, parts):
            for part in range(count):
                here = slice(at, at + width)
                pieces = {
                    0: own_ref[:, here],
                    first: first_ref[0, :, here],
                    3 - first: second_ref[0, :, here],
                    3: second_ref[1, :, here],
                }
                for bits, piece in pieces.items():
                    start = pl.multiple_of((part * TP + (rank_ref[0] ^ bits)) * width, width)
                    out[:, pl.ds(start, width)] = piece.astype(F32)
                at += width

    shapes = [jax.ShapeDtypeStruct((rows, TP * count * width), F32) for count, width in parts]
    return ranked_call(body, tp_rank, [own, got_first, got_second], shapes, "join_columns")


def reorder_runs(arrays, place_index, sums=False):
    run = D // 8
    shapes = [jax.ShapeDtypeStruct(a.shape, a.dtype) for a in arrays]
    if sums:
        shapes.append(jax.ShapeDtypeStruct((1, D), F32))

    def body(index_ref, *refs):
        ins, outs = refs[: len(arrays)], refs[len(arrays) :]
        for j, bits in enumerate(WIDTH_ORDER):
            start = pl.multiple_of((index_ref[0] ^ bits) * run, run)
            here = slice(j * run, (j + 1) * run)
            for in_ref, out_ref in zip(ins, outs):
                out_ref[:, here] = in_ref[:, pl.ds(start, run)]
        if sums:
            total = outs[0][...].astype(F32).sum(axis=0, keepdims=True)
            for out_ref in outs[1 : len(arrays)]:
                total = total + out_ref[...].astype(F32).sum(axis=0, keepdims=True)
            outs[-1][...] = total

    return ranked_call(body, place_index, list(arrays), shapes, "reorder_runs")


def restore_runs(array, place_index):
    run = D // 8

    def body(index_ref, in_ref, out_ref):
        for j, bits in enumerate(WIDTH_ORDER):
            start = pl.multiple_of((index_ref[0] ^ bits) * run, run)
            out_ref[:, pl.ds(start, run)] = in_ref[:, j * run : (j + 1) * run]

    shapes = [jax.ShapeDtypeStruct(array.shape, array.dtype)]
    return ranked_call(body, place_index, [array], shapes, "restore_runs")[0]


def finish_outputs(parts, tokens, bias, place_index):
    run = D // 8
    rows = tokens[0].shape[0]
    flat = [term for terms in parts for term in terms]

    def body(index_ref, *refs):
        ins, outs = refs[: len(flat) + len(tokens) + 1], refs[len(flat) + len(tokens) + 1 :]
        bias_ref = ins[-1]
        for i, out_ref in enumerate(outs):
            own, got, got_far = ins[3 * i : 3 * i + 3]
            token_ref = ins[len(flat) + i]
            value = token_ref[...].astype(F32) + own[...].astype(F32) + got[...].astype(F32)
            value = value + got_far[...].astype(F32) + bias_ref[...]
            for j, bits in enumerate(WIDTH_ORDER):
                start = pl.multiple_of((index_ref[0] ^ bits) * run, run)
                out_ref[:, pl.ds(start, run)] = value[:, j * run : (j + 1) * run]

    shapes = [jax.ShapeDtypeStruct((rows, D), F32) for _ in tokens]
    blocks = [(rows, D)] * (len(flat) + len(tokens)) + [bias.shape]
    return ranked_call(
        body, place_index, flat + list(tokens) + [bias], shapes, "finish_outputs", blocks
    )


def finish_grads(parts, tokens, cots, place_index):
    run = D // 8
    rows = tokens[0].shape[0]
    count = len(tokens)
    flat = [term for terms in parts for term in terms]

    def body(index_ref, *refs):
        ins, outs = refs[: 5 * count], refs[5 * count :]
        for i, out_ref in enumerate(outs):
            own, got, got_far = ins[3 * i : 3 * i + 3]
            token = ins[3 * count + i][...].astype(F32)
            cot = ins[4 * count + i][...].astype(F32)
            entry = own[...].astype(F32) + got[...].astype(F32) + got_far[...].astype(F32)
            center = token - jnp.mean(token, axis=1, keepdims=True)
            spread = lax.rsqrt(jnp.mean(center * center, axis=1, keepdims=True) + EPSILON)
            normed = center * spread
            entry_mean = jnp.mean(entry, axis=1, keepdims=True)
            entry_dot = jnp.mean(entry * normed, axis=1, keepdims=True)
            value = cot + spread * (entry - entry_mean - normed * entry_dot)
            for j, bits in enumerate(WIDTH_ORDER):
                start = pl.multiple_of((index_ref[0] ^ bits) * run, run)
                out_ref[:, pl.ds(start, run)] = value[:, j * run : (j + 1) * run]

    shapes = [jax.ShapeDtypeStruct((rows, D), F32) for _ in tokens]
    return ranked_call(
        body,
        place_index,
        flat + list(tokens) + list(cots),
        shapes,
        "finish_grads",
        [(rows, D)] * (5 * count),
    )


def part_specs(rows, tile, width, parts):
    per_part = rows // tile

    def spec(k):
        return pl.BlockSpec((tile, width), lambda i: (jnp.clip(i - k * per_part, 0, per_part - 1), 0))

    return [spec(k) for k in range(parts)]


def norms_body(gain1, bias1, gain2, bias2, *refs):
    *parts, rows_ref, first_ref, second_ref, mean_ref, spread_ref = refs
    step = pl.program_id(0)
    per_part = pl.num_programs(0) // len(parts)
    for k, part in enumerate(parts):

        @pl.when(step // per_part == k)
        def _(part=part):
            rows_ref[...] = part[...]
            values = part[...].astype(F32)
            mean = jnp.mean(values, axis=1, keepdims=True)
            center = values - mean
            spread = lax.rsqrt(jnp.mean(center * center, axis=1, keepdims=True) + EPSILON)
            normed = center * spread
            first_ref[...] = (normed * gain1[...] + bias1[...]).astype(BF)
            second_ref[...] = (normed * gain2[...] + bias2[...]).astype(BF)
            mean_ref[...] = mean
            spread_ref[...] = spread


def both_low_norms(parts, gain1, bias1, gain2, bias2):
    tile = parts[0].shape[0]
    total = tile * len(parts)
    vector = pl.BlockSpec((1, D), lambda i: (0, 0))
    wide = pl.BlockSpec((tile, D), lambda i: (i, 0))
    thin = pl.BlockSpec((tile, 1), lambda i: (i, 0))
    return pl.pallas_call(
        norms_body,
        grid=(total // tile,),
        in_specs=[vector] * 4 + part_specs(tile, tile, D, len(parts)),
        out_specs=[wide, wide, wide, thin, thin],
        out_shape=[
            jax.ShapeDtypeStruct((total, D), BF),
            jax.ShapeDtypeStruct((total, D), BF),
            jax.ShapeDtypeStruct((total, D), BF),
            jax.ShapeDtypeStruct((total, 1), F32),
            jax.ShapeDtypeStruct((total, 1), F32),
        ],
        compiler_params=pltpu.CompilerParams(vmem_limit_bytes=56 << 20),
        cost_estimate=cost("norms"),
        name="norms",
    )(gain1, bias1, gain2, bias2, *parts)


def resident(array, block=None, at=(0, 0)):
    return pl.BlockSpec(block or array.shape, lambda i: at, pipeline_mode=pl.Buffered(1))


def times(rows, halves, columns):
    upper, lower = halves
    half = upper.shape[0]
    return matmul_nn(rows[:, :half], upper[:, columns]) + matmul_nn(rows[:, half:], lower[:, columns])


def runs_of(width, run):
    return [slice(at, at + run) for at in range(0, width, run)]


def kernel(body, steps, in_specs, out_specs, out_shape, name, scratch=()):
    return pl.pallas_call(
        body,
        grid=(steps,),
        in_specs=in_specs,
        out_specs=out_specs,
        out_shape=out_shape,
        scratch_shapes=scratch,
        compiler_params=pltpu.CompilerParams(vmem_limit_bytes=58 << 20),
        cost_estimate=cost(name),
        name=name,
    )


def stacked(parts):
    tile, width = parts[0].shape

    def body(*refs):
        *ins, out_ref = refs
        for k, part in enumerate(ins):

            @pl.when(pl.program_id(0) == k)
            def _(part=part):
                out_ref[...] = part[...]

    return kernel(
        body,
        len(parts),
        part_specs(tile, tile, width, len(parts)),
        by_rows(tile, width),
        jax.ShapeDtypeStruct((tile * len(parts), width), BF),
        "stacked",
    )(*parts)


def beside(entries):
    tile, width = entries[0][0].shape
    specs, arrays = [], []
    for entry in entries:
        if isinstance(entry, tuple):
            specs += [pl.BlockSpec((tile, width), lambda i: (0, 0))] * 2
            arrays += entry
        elif entry.shape[0] == tile:
            specs += [pl.BlockSpec((tile, width), lambda i, h=h: (0, h)) for h in range(2)]
            arrays += [entry, entry]
        else:
            specs += [pl.BlockSpec((tile, width), lambda i, h=h: (h, 0)) for h in range(2)]
            arrays += [entry, entry]

    def body(*refs):
        *ins, out_ref = refs
        for k in range(len(entries)):

            @pl.when(pl.program_id(0) == k)
            def _(k=k):
                out_ref[:, :width] = ins[2 * k][...]
                out_ref[:, width:] = ins[2 * k + 1][...]

    return kernel(
        body,
        len(entries),
        specs,
        by_rows(tile, 2 * width),
        jax.ShapeDtypeStruct((tile * len(entries), 2 * width), BF),
        "beside",
    )(*arrays)


def second_sum(left, right, part=None):
    rows, width = left.shape[0] // 2, left.shape[1] // (1 if part is None else 2)
    wide = 1024 if width % 1024 == 0 else 512
    first = (part or 0) * (width // wide)

    def body(left_ref, right_ref, out_ref):
        out_ref[...] = (left_ref[...].astype(F32) + right_ref[...].astype(F32)).astype(BF)

    lower = pl.BlockSpec((rows, wide), lambda i: (1, first + i))
    at = right.shape[0] // rows - 1
    return kernel(
        body,
        width // wide,
        [lower, pl.BlockSpec((rows, wide), lambda i: (at, first + i))],
        pl.BlockSpec((rows, wide), lambda i: (0, i)),
        jax.ShapeDtypeStruct((rows, width), BF),
        "second_sum",
    )(left, right)


def onward(far, over_y):
    rows, width = far.shape

    def body(far_ref, y_ref, out_ref):
        out_ref[0] = far_ref[...]
        out_ref[1] = y_ref[0]

    return kernel(
        body,
        1,
        [
            pl.BlockSpec((rows, width), lambda i: (0, 0)),
            pl.BlockSpec((1, rows, width), lambda i: (1, 0, 0)),
        ],
        pl.BlockSpec((2, rows, width), lambda i: (0, 0, 0)),
        jax.ShapeDtypeStruct((2, rows, width), BF),
        "onward",
    )(far, over_y)


def by_rows(tile, width, tiles=lambda i: i):
    return pl.BlockSpec((tile, width), lambda i: (tiles(i), 0))


def attention_grad(parts, halves, column_block):
    tile = parts[0].shape[0]
    total = tile * len(parts)

    def body(upper, lower, *refs):
        *ins, out_ref, rows_ref, held = refs
        for k, part in enumerate(ins):

            @pl.when(pl.program_id(0) == k)
            def _(part=part):
                held[...] = part[...]

        rows = held[...]
        rows_ref[...] = rows
        out_ref[...] = times(rows, (upper, lower), slice(0, HCOLS)).astype(BF)

    weight_spec = resident(halves[0], (D // 2, HCOLS), (0, column_block))
    return kernel(
        body,
        len(parts),
        [weight_spec, weight_spec] + part_specs(tile, tile, D, len(parts)),
        [by_rows(tile, HCOLS), by_rows(tile, D)],
        [jax.ShapeDtypeStruct((total, HCOLS), BF), jax.ShapeDtypeStruct((total, D), BF)],
        "attention_grad",
        [pltpu.VMEM((tile, D), BF)],
    )(*halves, *parts)


def feed_forward_up(rows, halves, bias):
    total, ff_here = rows.shape[0], bias.shape[1]
    tile, wide = total // 4, ff_here // 2
    half = D // 2

    def body(rows_ref, upper, lower, bias_ref, act_ref, slope_ref):
        values = rows_ref[...]
        for run in runs_of(wide, 256):
            pre = times(values, (upper, lower), run) + bias_ref[:, run]
            cdf = 0.5 * (1.0 + lax.erf(pre * math.sqrt(0.5)))
            density = jnp.exp(-0.5 * pre * pre) * (1.0 / math.sqrt(2.0 * math.pi))
            act_ref[:, run] = (pre * cdf).astype(BF)
            slope_ref[:, run] = (cdf + pre * density).astype(BF)

    weight_spec = pl.BlockSpec((half, wide), lambda i: (0, i // 4))
    out_spec = pl.BlockSpec((tile, wide), lambda i: (i % 4, i // 4))
    return kernel(
        body,
        8,
        [
            by_rows(tile, D, lambda i: i % 4),
            weight_spec,
            weight_spec,
            pl.BlockSpec((1, wide), lambda i: (0, i // 4)),
        ],
        [out_spec] * 2,
        [jax.ShapeDtypeStruct((total, ff_here), BF)] * 2,
        "feed_forward_up",
    )(rows, *halves, bias)


def feed_forward_back(cots, halves, slope):
    total, ff_here = slope.shape
    tile, wide = total // 2, ff_here // 2
    half = D // 2

    def body(cot_ref, upper, lower, slope_ref, out_ref, sum_ref):
        @pl.when(pl.program_id(0) % 2 == 0)
        def _():
            sum_ref[...] = jnp.zeros_like(sum_ref)

        values = cot_ref[...]
        for run in runs_of(wide, 512):
            grad = times(values, (upper, lower), run) * slope_ref[:, run].astype(F32)
            low = grad.astype(BF)
            out_ref[:, run] = low
            sum_ref[:, run] += low.astype(F32).sum(axis=0, keepdims=True)

    weight_spec = pl.BlockSpec((half, wide), lambda i: (0, i // 2))
    both = pl.BlockSpec((tile, wide), lambda i: (i % 2, i // 2))
    return kernel(
        body,
        4,
        [by_rows(tile, D, lambda i: i % 2), weight_spec, weight_spec, both],
        [both, pl.BlockSpec((1, wide), lambda i: (0, i // 2))],
        [jax.ShapeDtypeStruct((total, ff_here), BF), jax.ShapeDtypeStruct((1, ff_here), F32)],
        "feed_forward_back",
    )(cots, *halves, slope)


def weight_grad(left, rights, core_got=None):
    total = left.shape[0]
    width = sum(right.shape[1] for right in rights)
    half = D // 2
    wide = 512
    steps = width // wide if len(rights) == 1 else 1
    keep = core_got is not None

    def body(left_ref, *refs):
        ins, rest = refs[: len(rights)], refs[len(rights) :]
        values = left_ref[...]
        at = 0
        for right in ins:
            here = slice(at, at + right.shape[1])
            at += right.shape[1]
            product = contract_cols(values, right[...])
            if keep:
                got_ref, mine_ref, side_ref = rest
                product = product + got_ref[:, here].astype(F32)
                mine_ref[:, here] = product[: half // 2].astype(BF)
                side_ref[:, here] = product[half // 2 :].astype(BF)
            else:
                rest[0][:, here] = product.astype(BF)

    if len(rights) == 1:
        right_specs = [pl.BlockSpec((total, wide), lambda i: (0, i))]
    else:
        right_specs = [resident(right) for right in rights]
    rows = half // 2 if keep else half
    count = 2 if keep else 1
    outs = kernel(
        body,
        steps,
        [resident(left, (total, half), (0, 0 if keep else 1))]
        + right_specs
        + ([pl.BlockSpec((half, wide), lambda i: (0, i))] if keep else []),
        [pl.BlockSpec((rows, wide), lambda i: (0, i))] * count,
        [jax.ShapeDtypeStruct((rows, width), BF)] * count,
        "weight_grad",
    )(left, *rights, *([core_got] if keep else []))
    return outs if keep else outs[0]


def width_tile(halves, height, columns, block=0):
    per_half = halves[0].shape[0] // height
    return [
        pl.BlockSpec((height, columns), lambda i: (jnp.minimum(i, per_half - 1), block)),
        pl.BlockSpec((height, columns), lambda i: (jnp.maximum(i - per_half, 0), block)),
    ]


def chosen(upper, lower):
    in_upper = pl.program_id(0) < pl.num_programs(0) // 2
    return jnp.where(in_upper, upper[...], lower[...])


def quarter_rows(tile):
    return [tile, tile // 2, tile // 2] * 2


def quarter_specs(tile, wide):
    return [pl.BlockSpec((rows, wide), lambda i: (0, i)) for rows in quarter_rows(tile)]


def put_quarter(outs, k, value):
    at = 3 * (k // 2)
    if k % 2 == 0:
        outs[at][...] = value
    else:
        half = value.shape[0] // 2
        outs[at + 1][...] = value[:half]
        outs[at + 2][...] = value[half:]


def branch_outputs(heads_low, act_low, attn_halves, column_block, down_halves):
    total, ff_here = act_low.shape
    tile = total // 4
    wide = 512

    def body(*refs):
        heads = [refs[h * 4 : h * 4 + 4] for h in range(HEADS_HERE)]
        refs = refs[4 * HEADS_HERE :]
        acts, attn, down, outs = refs[:4], refs[4:6], refs[6:8], refs[8:]
        attn_tile, down_tile = chosen(*attn), chosen(*down)
        for k in range(4):
            value = contract_rows(acts[k][...], down_tile)
            for head in range(HEADS_HERE):
                cut = slice(head * HEAD, (head + 1) * HEAD)
                value = value + contract_rows(heads[head][k][...], attn_tile[:, cut])
            put_quarter(outs, k, value.astype(BF))

    return kernel(
        body,
        D // wide,
        [resident(h, (tile, HEAD), (k, 0)) for h in heads_low for k in range(4)]
        + [resident(act_low, (tile, ff_here), (k, 0)) for k in range(4)]
        + width_tile(attn_halves, wide, HCOLS, column_block)
        + width_tile(down_halves, wide, ff_here),
        quarter_specs(tile, wide),
        [jax.ShapeDtypeStruct((rows, D), BF) for rows in quarter_rows(tile)],
        "branch_outputs",
    )(*[h for h in heads_low for _ in range(4)], *([act_low] * 4), *attn_halves, *down_halves)


def norm_grad(grads, halves, gain, tokens, mean, spread, row_blocks, addends=(), cut=False):
    tile = grads.shape[0] // 4
    count = len(row_blocks)
    width = grads.shape[1]
    wide = 512

    def body(upper, lower, gain_ref, *refs):
        rows, means, spreads, token_refs = (refs[i * count : (i + 1) * count] for i in range(4))
        rest = refs[4 * count :]
        adds, outs, sum_ref = rest[: len(addends)], rest[len(addends) : -1], rest[-1]
        weight = chosen(upper, lower)
        dots = jnp.zeros((1, wide), F32)
        totals = jnp.zeros((1, wide), F32)
        for k in range(count):
            value = contract_rows(rows[k][...], weight)
            scaled = value * gain_ref[...]
            if adds:
                scaled = scaled + adds[k][...].astype(F32)
            low = scaled.astype(BF)
            if cut:
                outs[2 * k][...] = low[: tile // 2]
                outs[2 * k + 1][...] = low[tile // 2 :]
            else:
                outs[k][...] = low
            normed = (token_refs[k][...].astype(F32) - means[k][...]) * spreads[k][...]
            dots = dots + (value * normed).sum(axis=0, keepdims=True)
            totals = totals + value.sum(axis=0, keepdims=True)
        sum_ref[0:1, :] = dots
        sum_ref[1:2, :] = totals

    column = pl.BlockSpec((tile, wide), lambda i: (0, i))
    out_rows = [tile // 2] * (2 * count) if cut else [tile] * count
    outs = kernel(
        body,
        D // wide,
        [
            *width_tile(halves, wide, width),
            pl.BlockSpec((1, wide), lambda i: (0, i)),
            *[resident(grads, (tile, width), (k, 0)) for k in row_blocks],
            *[resident(mean, (tile, 1), (k, 0)) for k in row_blocks],
            *[resident(spread, (tile, 1), (k, 0)) for k in row_blocks],
            *[pl.BlockSpec((tile, wide), lambda i, k=k: (k, i)) for k in row_blocks],
            *([column] * len(addends)),
        ],
        [pl.BlockSpec((rows, wide), lambda i: (0, i)) for rows in out_rows]
        + [pl.BlockSpec((8, wide), lambda i: (0, i))],
        [jax.ShapeDtypeStruct((rows, D), BF) for rows in out_rows]
        + [jax.ShapeDtypeStruct((8, D), F32)],
        "norm_grad",
    )(
        *halves,
        gain,
        *([grads] * count),
        *([mean] * count),
        *([spread] * count),
        *([tokens] * count),
        *addends,
    )
    return outs[:-1], outs[-1]


def rotary_tables(positions):
    lane = jnp.arange(LANES, dtype=jnp.int32)
    half_rot = ROT // 2
    exponent = -(2.0 * (lane % half_rot).astype(F32)) / ROT
    angles = positions[:, None] * (ROPE_BASE**exponent)[None, :]
    turning = (lane < ROT)[None, :]
    cos_table = jnp.where(turning, jnp.cos(angles), 1.0)
    sin_part = jnp.sin(angles)
    sin_table = jnp.where((lane < half_rot)[None, :], -sin_part, sin_part)
    return cos_table, jnp.where(turning, sin_table, 0.0)


def swapped_halves(values):
    half_rot = ROT // 2
    lane = lax.broadcasted_iota(jnp.int32, values.shape, 1)
    return jnp.where(
        lane < half_rot,
        pltpu.roll(values, LANES - half_rot, 1),
        pltpu.roll(values, half_rot, 1),
    )


def turned(values, cos_table, sin_table):
    first = values[:, :LANES]
    return jnp.concatenate(
        [first * cos_table + swapped_halves(first) * sin_table, values[:, LANES:]], axis=1
    )


def project_qkv(head, rows, halves, bias, cos_table, sin_table):
    total = rows.shape[0]
    tile = total // 2
    half = D // 2

    def body(rows_ref, *refs):
        weights, biases = refs[:6], refs[6:9]
        cos_ref, sin_ref, q_ref, near_key_ref, near_value_ref, own_ref = refs[9:]
        values = rows_ref[...]
        cos_here, sin_here = cos_ref[...], sin_ref[...]

        def product(kind):
            whole_run = slice(0, HEAD)
            return times(values, weights[2 * kind : 2 * kind + 2], whole_run) + biases[kind][...]

        query = turned(product(0), cos_here, sin_here)
        q_ref[...] = (query * (1.0 / math.sqrt(HEAD))).astype(BF)
        key = turned(product(1), cos_here, sin_here).astype(BF)
        value = product(2).astype(BF)

        @pl.when(pl.program_id(0) == 0)
        def _():
            near_key_ref[...] = key
            near_value_ref[...] = value

        @pl.when(pl.program_id(0) == 1)
        def _():
            own_ref[:, :HEAD] = key
            own_ref[:, HEAD:] = value

    columns = [kind * HEADS_HERE + head for kind in range(3)]
    both = jax.ShapeDtypeStruct((tile, 2 * HEAD), BF)
    one = jax.ShapeDtypeStruct((tile, HEAD), BF)
    kept_both = pl.BlockSpec((tile, 2 * HEAD), lambda i: (0, 0))
    kept = pl.BlockSpec((tile, HEAD), lambda i: (0, 0))
    return kernel(
        body,
        2,
        [
            by_rows(tile, D),
            *[resident(h, (half, HEAD), (0, c)) for c in columns for h in halves],
            *[resident(bias, (1, HEAD), (0, c)) for c in columns],
            by_rows(tile, LANES),
            by_rows(tile, LANES),
        ],
        [by_rows(tile, HEAD), kept, kept, kept_both],
        [jax.ShapeDtypeStruct((total, HEAD), BF), one, one, both],
        "qkv_rotary",
    )(rows, *[h for _ in columns for h in halves], *([bias] * 3), cos_table, sin_table)


def attention_body(
    q_ref,
    do_ref,
    kl_ref,
    vl_ref,
    kr_ref,
    vr_ref,
    kc_ref,
    vc_ref,
    cos_ref,
    sin_ref,
    cosl_ref,
    sinl_ref,
    cosr_ref,
    sinr_ref,
    qmark_ref,
    kmark_ref,
    o_ref,
    dq_ref,
    down_ref,
    dnear_ref,
    dfar_key_ref,
    dfar_value_ref,
    akl,
    avl,
    akr,
    avr,
):
    step = pl.program_id(0)
    last = pl.num_programs(0) - 1
    near = kl_ref.shape[0]

    @pl.when(step == 0)
    def _():
        for acc in (akl, avl, akr, avr):
            acc[...] = jnp.zeros_like(acc)

    query, grad = q_ref[...], do_ref[...]

    def work(own):
        scores = [contract_rows(query, kl_ref[...]), contract_rows(query, kr_ref[...])]
        if own:
            mine = contract_rows(query, kc_ref[...])
            at_row = lax.broadcasted_iota(jnp.int32, mine.shape, 0)
            at_col = lax.broadcasted_iota(jnp.int32, mine.shape, 1)
            scores.append(jnp.where(at_col <= at_row, mine, NEG_FILL))
        else:
            marks = kmark_ref[...]
            own_mark = qmark_ref[...]
            scores[0] = jnp.where(marks[:, :near] <= own_mark, scores[0], NEG_FILL)
            scores[1] = jnp.where(marks[:, near:] <= own_mark, scores[1], NEG_FILL)
        top = scores[0].max(axis=1, keepdims=True)
        for part in scores[1:]:
            top = jnp.maximum(top, part.max(axis=1, keepdims=True))
        probs = [jnp.exp(part - top) for part in scores]
        total = probs[0].sum(axis=1, keepdims=True)
        for part in probs[1:]:
            total = total + part.sum(axis=1, keepdims=True)
        share = 1.0 / total
        probs = [part * share for part in probs]
        low = [part.astype(BF) for part in probs]
        values = [vl_ref, vr_ref] + ([vc_ref] if own else [])
        keys = [kl_ref, kr_ref] + ([kc_ref] if own else [])
        mixed = matmul_nn(low[0], values[0][...])
        for part, ref in zip(low[1:], values[1:]):
            mixed = mixed + matmul_nn(part, ref[...])
        o_ref[...] = mixed.astype(BF)
        prob_grad = [contract_rows(grad, ref[...]) for ref in values]
        delta = (probs[0] * prob_grad[0]).sum(axis=1, keepdims=True)
        for part, grad_part in zip(probs[1:], prob_grad[1:]):
            delta = delta + (part * grad_part).sum(axis=1, keepdims=True)
        slopes = [
            (part * (grad_part - delta)).astype(BF) for part, grad_part in zip(probs, prob_grad)
        ]
        query_grad = matmul_nn(slopes[0], keys[0][...])
        for part, ref in zip(slopes[1:], keys[1:]):
            query_grad = query_grad + matmul_nn(part, ref[...])
        query_grad = query_grad * (1.0 / math.sqrt(HEAD))
        dq_ref[...] = turned(query_grad, cos_ref[...], -sin_ref[...]).astype(BF)
        akl[...] += contract_cols(slopes[0], query)
        akr[...] += contract_cols(slopes[1], query)
        avl[...] += contract_cols(low[0], grad)
        avr[...] += contract_cols(low[1], grad)
        if own:
            key_grad = contract_cols(slopes[2], query)
            down_ref[:, :HEAD] = turned(key_grad, cos_ref[...], -sin_ref[...]).astype(BF)
            down_ref[:, HEAD:] = contract_cols(low[2], grad).astype(BF)

    @pl.when(step < TP)
    def _():
        work(False)

    @pl.when(step >= TP)
    def _():
        work(True)

    @pl.when(step == last)
    def _():
        dnear_ref[:, :HEAD] = turned(akl[...], cosl_ref[...], -sinl_ref[...])
        dnear_ref[:, HEAD:] = avl[...]
        dfar_key_ref[...] = turned(akr[...], cosr_ref[...], -sinr_ref[...]).astype(BF)
        dfar_value_ref[...] = avr[...].astype(BF)


def attend(
    head, queries, grads, near, far, own, tables, near_tables, far_tables, query_mark, key_mark
):
    total = queries.shape[0]
    tile = total // (2 * TP)
    keys = near[0].shape[0]

    def row_tile(j):
        return j

    def cont_tile(j):
        return jnp.maximum(j - TP, 0)

    query_spec = pl.BlockSpec((tile, HEAD), lambda j: (row_tile(j), 0))
    row_spec = pl.BlockSpec((tile, HEAD), lambda j: (row_tile(j), head))
    out_spec = pl.BlockSpec((tile, HEAD), lambda j: (row_tile(j), 0))
    key_spec = pl.BlockSpec((keys, HEAD), lambda j: (0, 0))
    own_key = pl.BlockSpec((tile, HEAD), lambda j: (cont_tile(j), 0))
    own_value = pl.BlockSpec((tile, HEAD), lambda j: (cont_tile(j), 1))
    own_both = pl.BlockSpec((tile, 2 * HEAD), lambda j: (cont_tile(j), 0))
    both = pl.BlockSpec((keys, 2 * HEAD), lambda j: (0, 0))
    table_spec = pl.BlockSpec((tile, LANES), lambda j: (row_tile(j), 0))
    key_table = pl.BlockSpec((keys, LANES), lambda j: (0, 0))
    mark_spec = pl.BlockSpec((tile, 1), lambda j: (row_tile(j), 0))
    key_mark_spec = pl.BlockSpec((1, 2 * keys), lambda j: (0, 0))
    wide = jax.ShapeDtypeStruct((total, HEAD), BF)
    return pl.pallas_call(
        attention_body,
        grid=(2 * TP,),
        in_specs=[
            query_spec,
            row_spec,
            key_spec,
            key_spec,
            key_spec,
            key_spec,
            own_key,
            own_value,
            table_spec,
            table_spec,
            key_table,
            key_table,
            key_table,
            key_table,
            mark_spec,
            key_mark_spec,
        ],
        out_specs=[out_spec, out_spec, own_both, both, key_spec, key_spec],
        out_shape=[
            wide,
            wide,
            jax.ShapeDtypeStruct((keys, 2 * HEAD), BF),
            jax.ShapeDtypeStruct((keys, 2 * HEAD), F32),
            jax.ShapeDtypeStruct((keys, HEAD), BF),
            jax.ShapeDtypeStruct((keys, HEAD), BF),
        ],
        scratch_shapes=[pltpu.VMEM((keys, HEAD), F32)] * 4,
        compiler_params=pltpu.CompilerParams(vmem_limit_bytes=56 << 20),
        cost_estimate=cost("attention_both_ways"),
        name="attention_both_ways",
    )(
        queries,
        grads,
        *near,
        *far,
        own,
        own,
        *tables,
        *near_tables,
        *far_tables,
        query_mark,
        key_mark,
    )


def join_grads(query_grads, own_grads, near_grads, far_keys, far_values):
    total = query_grads[0].shape[0]
    tile = total // 4

    def body(*refs):
        out_ref, sum_ref = refs[-2:]
        dq, down, dnear, dfar_key, dfar_value = (
            refs[i * HEADS_HERE : (i + 1) * HEADS_HERE] for i in range(5)
        )
        step = pl.program_id(0)

        @pl.when(step == 0)
        def _():
            sum_ref[...] = jnp.zeros_like(sum_ref)

        for head in range(HEADS_HERE):
            at = head * HEAD
            key_at, value_at = slice(HCOLS + at, HCOLS + at + HEAD), slice(
                2 * HCOLS + at, 2 * HCOLS + at + HEAD
            )
            out_ref[:, at : at + HEAD] = dq[head][...]

            @pl.when(step < 2)
            def _(head=head, key_at=key_at, value_at=value_at):
                near = dnear[head][...]
                out_ref[:, key_at] = (near[:, :HEAD] + dfar_key[head][...].astype(F32)).astype(BF)
                out_ref[:, value_at] = (near[:, HEAD:] + dfar_value[head][...].astype(F32)).astype(BF)

            @pl.when(step >= 2)
            def _(head=head, key_at=key_at, value_at=value_at):
                out_ref[:, key_at] = down[head][:, :HEAD]
                out_ref[:, value_at] = down[head][:, HEAD:]

        sum_ref[...] += out_ref[...].astype(F32).sum(axis=0, keepdims=True)

    prompt_spec, cont_spec = part_specs(total // 2, tile, 2 * HEAD, 2)
    far_spec, _ = part_specs(total // 2, tile, HEAD, 2)
    return pl.pallas_call(
        body,
        grid=(4,),
        in_specs=[
            *([pl.BlockSpec((tile, HEAD), lambda i: (i, 0))] * HEADS_HERE),
            *([cont_spec] * HEADS_HERE),
            *([prompt_spec] * HEADS_HERE),
            *([far_spec] * (2 * HEADS_HERE)),
        ],
        out_specs=[
            pl.BlockSpec((tile, 3 * HCOLS), lambda i: (i, 0)),
            pl.BlockSpec((1, 3 * HCOLS), lambda i: (0, 0)),
        ],
        out_shape=[
            jax.ShapeDtypeStruct((total, 3 * HCOLS), BF),
            jax.ShapeDtypeStruct((1, 3 * HCOLS), F32),
        ],
        compiler_params=pltpu.CompilerParams(vmem_limit_bytes=56 << 20),
        cost_estimate=cost("join_grads"),
        name="join_grads",
    )(*query_grads, *own_grads, *near_grads, *far_keys, *far_values)


class Values:
    pass


def square_plan(
    prompt,
    conts,
    assignment,
    offsets,
    ln1_gain,
    ln1_bias,
    ln2_gain,
    ln2_bias,
    qkv_weight,
    qkv_bias,
    out_weight,
    out_bias,
    up_weight,
    up_bias,
    down_weight,
    down_bias,
    prompt_cot,
    cont_cot,
):
    block, cont_rows = prompt.shape[1], conts.shape[2]
    shard = qkv_weight.shape[0]
    ff = up_weight.shape[1]
    ff_here = ff // TP
    half = D // 2
    grp_index, seq_index = lax.axis_index("grp"), lax.axis_index("seq")
    tp_rank, z_half = seq_index & 3, seq_index >> 2
    place_index = grp_index * 2 + z_half

    v = Values()


    branch_ids = jnp.arange(offsets.shape[1], dtype=jnp.int32)
    my_offset = jnp.sum(jnp.where(branch_ids == assignment[0, 0], offsets[0], 0)).reshape(1, 1)
    v.offsets = jnp.concatenate(
        [my_offset if bits == 0 else swap_seq(my_offset, bits) for bits in CONT_ORDER], axis=0
    )
    own1, v.side1, far1 = split_columns([qkv_weight, out_weight.T], [3, 1], tp_rank)
    v.got1_y = swap_seq(v.side1, 1)
    v.own_a, v.own_b = reorder_runs([prompt[0], conts[0, 0]], place_index)
    own2, v.side2, far2 = split_columns([up_weight], [1], tp_rank)
    v.got1_y, v.side2 = tie(v.got1_y, v.side2)
    v.got1_z = swap_seq(onward(far1, v.got1_y), 2)
    v.got2_y = swap_seq(v.side2, 1)
    own3, v.side3, far3 = split_columns([down_weight.T], [1], tp_rank)
    qkv_bias_here = pick(qkv_bias.reshape(3, TP, HCOLS), tp_rank, 1).reshape(1, 3 * HCOLS)
    up_bias_here = pick(up_bias.reshape(TP, ff_here), tp_rank, 0)[None]
    vectors = jnp.stack([ln1_gain, ln1_bias, ln2_gain, ln2_bias, out_bias + down_bias])
    vectors = jnp.concatenate([vectors, jnp.zeros((3, D), F32)], axis=0)
    (v.vectors,) = reorder_runs([vectors], place_index)
    prompt_ranks = (tp_rank ^ jnp.array(PROMPT_ORDER, dtype=jnp.int32))[:, None]
    prompt_iota = jnp.arange(block, dtype=jnp.int32)[None, :]
    cont_iota = jnp.arange(cont_rows, dtype=jnp.int32)[None, :]
    near_mark = ((z_half * TP + prompt_ranks) * block + prompt_iota).reshape(-1)
    far_mark = (((z_half ^ 1) * TP + prompt_ranks) * block + prompt_iota).reshape(-1)
    cont_positions = (PROMPT + cont_iota + v.offsets).reshape(-1)
    v.mark = jnp.concatenate([near_mark, cont_positions]).astype(F32)
    query_mark = jnp.concatenate([near_mark, near_mark]).reshape(-1, 1)
    key_mark = jnp.concatenate([near_mark, far_mark]).reshape(1, -1)
    (
        v.got1_z, v.got2_y, v.own_a, v.own_b, v.side3, v.offsets,
    ) = tie(
        v.got1_z, v.got2_y, v.own_a, v.own_b, v.side3, v.offsets,
    )
    v.base1a, v.base1b = stack_ranks(
        own1, v.got1_y, v.got1_z, (2 * HCOLS,) * 2, tp_rank
    )
    v.rows_az = swap_seq(v.own_a, 2)
    v.rows_ay = swap_seq(v.own_a, 1)
    v.z1a = swap_seq(v.base1a, 4)
    v.x1a = swap_grp(v.base1a, 2)
    v.send2 = onward(far2, v.got2_y)
    v.cot0, v.cot1 = prompt_cot[0], cont_cot[0, 0]
    v.cot0, v.cot1, v.base1b = tie(v.cot0, v.cot1, v.base1b)
    v.cot_a, v.cot_b, cot_sum = reorder_runs([v.cot0, v.cot1], place_index, sums=True)
    (
        v.rows_az, v.rows_ay, v.z1a, v.x1a, v.send2, v.base1b, v.own_b, v.cot_a, v.cot_b, v.mark,
    ) = tie(
        v.rows_az, v.rows_ay, v.z1a, v.x1a, v.send2, v.base1b, v.own_b, v.cot_a, v.cot_b, v.mark,
    )
    v.z1b = swap_seq(v.base1b, 4)
    v.got2_z = swap_seq(v.send2, 2)
    v.rows_by = swap_seq(v.own_b, 1)
    v.x1b = swap_grp(v.base1b, 2)
    v.zx1a = swap_grp(v.z1a, 2)
    v.base2a, v.base2b, v.base2 = stack_ranks(
        own2, v.got2_y, v.got2_z, (ff_here // 2,) * 2, tp_rank, True
    )
    tables = rotary_tables(v.mark)
    far_tables = rotary_tables(far_mark.astype(F32))
    v.tables0, v.tables1 = tables
    v.far0, v.far1 = far_tables
    (
        v.vectors, v.z1b, v.base2a, v.base2b, v.base2, v.rows_by, v.x1b, v.zx1a, v.rows_az,
        v.own_b, v.side3, v.tables0, v.tables1, v.far0, v.far1,
    ) = tie(
        v.vectors, v.z1b, v.base2a, v.base2b, v.base2, v.rows_by, v.x1b, v.zx1a, v.rows_az,
        v.own_b, v.side3, v.tables0, v.tables1, v.far0, v.far1,
    )
    tables, far_tables = (v.tables0, v.tables1), (v.far0, v.far1)
    shared = (tables, tables, far_tables, query_mark, key_mark)
    v.got3_y = swap_seq(v.side3, 1)
    v.rows_azy = swap_seq(v.rows_az, 1)
    v.rows_bz = swap_seq(v.own_b, 2)
    v.zx1b = swap_grp(v.z1b, 2)
    v.z2a = swap_seq(v.base2a, 4)
    (
        v.z2a, v.rows_azy, v.rows_bz, v.zx1b, v.got3_y, v.base2b, v.base2,
    ) = tie(
        v.z2a, v.rows_azy, v.rows_bz, v.zx1b, v.got3_y, v.base2b, v.base2,
    )
    v.rows_bzy = swap_seq(v.rows_bz, 1)
    v.z2b = swap_seq(v.base2b, 4)
    v.x2 = swap_grp(v.base2, 2)
    v.got3_z = swap_seq(onward(far3, v.got3_y), 2)
    v.base3a, v.base3b, v.base3 = stack_ranks(
        own3, v.got3_y, v.got3_z, (ff_here // 2,) * 2, tp_rank, True
    )
    v.core1 = beside(
        [(v.base1a, v.base1b), (v.z1a, v.z1b), (v.x1a, v.x1b), (v.zx1a, v.zx1b)]
    )
    gain1, bias1, gain2, bias2, bias_out = (v.vectors[i : i + 1] for i in range(5))
    (
        v.rows_bzy, v.z2a, v.z2b, v.x2, v.base3a, v.base3b, v.base3, v.core1, v.cot_a, v.cot_b,
    ) = tie(
        v.rows_bzy, v.z2a, v.z2b, v.x2, v.base3a, v.base3b, v.base3, v.core1, v.cot_a, v.cot_b,
    )

    v.swapped1 = swap_grp(v.core1, 1)
    v.cot_az = swap_seq(v.cot_a, 2)
    v.cot_ay = swap_seq(v.cot_a, 1)
    v.zx2 = swap_grp(stacked([v.z2a, v.z2b]), 2)
    v.z3a = swap_seq(v.base3a, 4)
    v.rows, v.first_low, v.second_low, mean, spread = both_low_norms(
        [v.own_a, v.rows_az, v.rows_ay, v.rows_azy, v.own_b, v.rows_by, v.rows_bz, v.rows_bzy],
        gain1,
        bias1,
        gain2,
        bias2,
    )
    v.core2 = beside(
        [(v.base2a, v.base2b), (v.z2a, v.z2b), v.x2, v.zx2]
    )
    (
        v.first_low, v.second_low, v.core2, v.swapped1, v.core1, v.base3, v.base3b, v.cot_az,
        v.cot_ay, v.z3a, v.cot_b,
    ) = tie(
        v.first_low, v.second_low, v.core2, v.swapped1, v.core1, v.base3, v.base3b, v.cot_az,
        v.cot_ay, v.z3a, v.cot_b,
    )
    v.cot_by = swap_seq(v.cot_b, 1)
    v.cot_bz = swap_seq(v.cot_b, 2)
    v.z3b = swap_seq(v.base3b, 4)
    v.x3 = swap_grp(v.base3, 2)
    v.swapped2 = swap_grp(v.core2, 1)
    weight1 = (v.core1, v.swapped1)
    v.query0, v.key0, v.value0, own0 = project_qkv(
        0, v.first_low, weight1, qkv_bias_here, *tables
    )
    v.query0, v.first_low = tie(v.query0, v.first_low)
    v.query1, v.key1, v.value1, own1_kv = project_qkv(
        1, v.first_low, weight1, qkv_bias_here, *tables
    )
    (
        v.query1, v.second_low, v.swapped2, v.core2, v.cot_az, v.x3, v.cot_by, v.cot_bz, v.z3b,
        v.key0, v.z3a,
    ) = tie(
        v.query1, v.second_low, v.swapped2, v.core2, v.cot_az, v.x3, v.cot_by, v.cot_bz, v.z3b,
        v.key0, v.z3a,
    )
    v.cot_azy = swap_seq(v.cot_az, 1)
    v.cot_bzy = swap_seq(v.cot_by, 2)
    v.far_key0 = swap_seq(v.key0, 4)
    v.zx3a = swap_grp(v.z3a, 2)
    v.zx3b = swap_grp(v.z3b, 2)
    weight2 = (v.core2, v.swapped2)
    v.act_low, v.slope = feed_forward_up(v.second_low, weight2, up_bias_here)
    (
        v.act_low, v.slope, v.cot_azy, v.cot_bzy, v.far_key0, v.zx3a, v.zx3b, v.value0,
    ) = tie(
        v.act_low, v.slope, v.cot_azy, v.cot_bzy, v.far_key0, v.zx3a, v.zx3b, v.value0,
    )
    v.far_value0 = swap_seq(v.value0, 4)
    v.core3 = beside(
        [(v.base3a, v.base3b), (v.z3a, v.z3b), v.x3, (v.zx3a, v.zx3b)]
    )
    v.swapped3 = swap_grp(v.core3, 1)
    v.attn_grad, v.cots = attention_grad(
        [v.cot_a, v.cot_az, v.cot_ay, v.cot_azy, v.cot_b, v.cot_by, v.cot_bz, v.cot_bzy],
        weight1,
        3,
    )
    v.attn_grad, v.cots, v.act_low = tie(v.attn_grad, v.cots, v.act_low)
    v.down_away = weight_grad(v.cots, [v.act_low])
    (
        v.down_away, v.far_value0, v.key1, v.value1, v.attn_grad, v.swapped3, v.core3,
    ) = tie(
        v.down_away, v.far_value0, v.key1, v.value1, v.attn_grad, v.swapped3, v.core3,
    )
    v.down_core = swap_grp(v.down_away, 1)
    v.far_key1 = swap_seq(v.key1, 4)
    v.attn0, dq0, down0, dnear0, v.dfar_key0, v.dfar_value0 = attend(
        0,
        v.query0,
        v.attn_grad,
        (v.key0, v.value0),
        (v.far_key0, v.far_value0),
        own0,
        *shared,
    )
    (
        v.attn0, v.down_core, v.cots, v.act_low, v.far_key1, v.value1,
    ) = tie(
        v.attn0, v.down_core, v.cots, v.act_low, v.far_key1, v.value1,
    )
    v.far_value1 = swap_seq(v.value1, 4)
    v.down_mine, v.down_send = weight_grad(v.cots, [v.act_low], v.down_core)
    (
        v.down_mine, v.down_send, v.cots, v.slope, v.core3, v.swapped3,
    ) = tie(
        v.down_mine, v.down_send, v.cots, v.slope, v.core3, v.swapped3,
    )
    v.down_side = swap_grp(v.down_send, 2)
    weight3 = (v.core3, v.swapped3)
    v.hidden_grad, up_bias_term = feed_forward_back(v.cots, weight3, v.slope)
    (
        v.hidden_grad, v.far_value1, v.dfar_key0, v.dfar_value0, v.attn_grad,
    ) = tie(
        v.hidden_grad, v.far_value1, v.dfar_key0, v.dfar_value0, v.attn_grad,
    )
    v.back_key0 = swap_seq(v.dfar_key0, 4)
    v.back_value0 = swap_seq(v.dfar_value0, 4)
    v.attn1, dq1, down1, v.dnear1, v.dfar_key1, v.dfar_value1 = attend(
        1,
        v.query1,
        v.attn_grad,
        (v.key1, v.value1),
        (v.far_key1, v.far_value1),
        own1_kv,
        *shared,
    )
    (
        v.attn1, v.second_low, v.hidden_grad, v.down_side, v.down_mine,
    ) = tie(
        v.attn1, v.second_low, v.hidden_grad, v.down_side, v.down_mine,
    )
    v.up_away = weight_grad(v.second_low, [v.hidden_grad])
    v.down_half_send = second_sum(v.down_mine, v.down_side)
    (
        v.up_away, v.back_key0, v.back_value0, v.dfar_key1, v.dfar_value1, v.act_low,
        v.down_half_send,
    ) = tie(
        v.up_away, v.back_key0, v.back_value0, v.dfar_key1, v.dfar_value1, v.act_low,
        v.down_half_send,
    )
    v.up_core = swap_grp(v.up_away, 1)
    v.back_key1 = swap_seq(v.dfar_key1, 4)
    branch = branch_outputs((v.attn0, v.attn1), v.act_low, weight1, 3, weight3)
    v.branch0, v.branch_y, v.branch_zy, v.branch2, v.branch_z, v.branch_yz = branch
    (
        v.branch0, v.branch_y, v.branch_zy, v.branch2, v.branch_z, v.branch_yz, v.up_core,
        v.second_low, v.hidden_grad, v.back_key1, v.dfar_value1,
    ) = tie(
        v.branch0, v.branch_y, v.branch_zy, v.branch2, v.branch_z, v.branch_yz, v.up_core,
        v.second_low, v.hidden_grad, v.back_key1, v.dfar_value1,
    )
    v.got_zy = swap_seq(v.branch_zy, 1)
    v.got_yz = swap_seq(v.branch_yz, 2)
    v.back_value1 = swap_seq(v.dfar_value1, 4)
    v.up_mine, v.up_send = weight_grad(v.second_low, [v.hidden_grad], v.up_core)
    v.up_mine, v.hidden_grad = tie(v.up_mine, v.hidden_grad)
    second_parts, second_sums = norm_grad(
        v.hidden_grad, weight2, gain2, v.rows, mean, spread, (0, 1, 2, 3)
    )
    v.second0, second1, second2, second3 = second_parts
    (
        v.second0, v.back_value1, v.dnear1, v.cots, v.down_half_send, v.up_send, v.got_zy,
        v.got_yz, v.branch0, v.branch2, v.branch_y, v.branch_z,
    ) = tie(
        v.second0, v.back_value1, v.dnear1, v.cots, v.down_half_send, v.up_send, v.got_zy,
        v.got_yz, v.branch0, v.branch2, v.branch_y, v.branch_z,
    )
    v.up_side = swap_grp(v.up_send, 2)
    v.down_half = swap_seq(v.down_half_send, 4)
    v.got_y = swap_seq(v.branch_y, 1)
    v.got_z = swap_seq(v.branch_z, 2)
    v.branch_a_far = second_sum(v.branch0, v.got_zy)
    v.branch_b_far = second_sum(v.branch2, v.got_yz)
    v.qkv_grad, qkv_bias_term = join_grads(
        (dq0, dq1),
        (down0, down1),
        (dnear0, v.dnear1),
        (v.back_key0, v.back_key1),
        (v.back_value0, v.back_value1),
    )
    v.qkv_grad, v.first_low, v.cots = tie(v.qkv_grad, v.first_low, v.cots)
    v.qkv_away = weight_grad(v.first_low, [v.qkv_grad])
    v.qkv_away, v.cots = tie(v.qkv_away, v.cots)
    v.out_away = weight_grad(v.cots, [v.attn0, v.attn1])
    (
        v.out_away, v.qkv_away, v.got_y, v.got_z, v.branch_a_far, v.branch_b_far, v.down_half,
        v.up_side, v.up_mine, v.qkv_grad,
    ) = tie(
        v.out_away, v.qkv_away, v.got_y, v.got_z, v.branch_a_far, v.branch_b_far, v.down_half,
        v.up_side, v.up_mine, v.qkv_grad,
    )
    v.qkv_core = swap_grp(v.qkv_away, 1)
    down_own, v.down_side2, v.down_far = split_rows(
        [(v.down_mine, v.down_side, (v.down_half,))], tp_rank
    )
    v.up_send_a = second_sum(v.up_mine, v.up_side, 0)
    v.up_half_a = swap_seq(v.up_send_a, 4)
    v.branch_far_a = swap_seq(v.branch_a_far, 2)
    v.branch_far_b = swap_seq(v.branch_b_far, 1)
    v.down_y = swap_seq(v.down_side2, 1)
    v.up_send_b = second_sum(v.up_mine, v.up_side, 1)
    (
        v.qkv_core, v.first_low, v.qkv_grad, v.up_send_b,
    ) = tie(
        v.qkv_core, v.first_low, v.qkv_grad, v.up_send_b,
    )
    v.qkv_mine, v.qkv_send = weight_grad(v.first_low, [v.qkv_grad], v.qkv_core)
    v.qkv_mine, v.qkv_send, v.qkv_grad = tie(v.qkv_mine, v.qkv_send, v.qkv_grad)
    v.qkv_side = swap_grp(v.qkv_send, 2)
    entry_far, v.far_sums = norm_grad(
        v.qkv_grad, weight1, gain1, v.rows, mean, spread, (1, 3), (second1, second3), True
    )
    v.entry_y, v.entry_zy, v.entry_z, v.entry_yz = entry_far
    (
        v.entry_y, v.entry_zy, v.entry_z, v.entry_yz, v.far_sums, v.out_away, v.branch_far_a,
        v.branch_far_b, v.down_y, v.down_far, v.up_half_a, v.up_send_b, v.qkv_grad, v.second0,
    ) = tie(
        v.entry_y, v.entry_zy, v.entry_z, v.entry_yz, v.far_sums, v.out_away, v.branch_far_a,
        v.branch_far_b, v.down_y, v.down_far, v.up_half_a, v.up_send_b, v.qkv_grad, v.second0,
    )
    v.entry_got_zy = swap_seq(v.entry_zy, 1)
    v.entry_got_yz = swap_seq(v.entry_yz, 2)
    v.out_core = swap_grp(v.out_away, 1)
    v.up_half_b = swap_seq(v.up_send_b, 4)
    (v.entry0, v.entry2), v.near_sums = norm_grad(
        v.qkv_grad, weight1, gain1, v.rows, mean, spread, (0, 2), (v.second0, second2)
    )
    (
        v.near_sums, v.out_core, v.cots, v.qkv_side, v.qkv_mine, v.up_half_b, v.branch0,
        v.entry_got_zy, v.entry_got_yz, v.entry_y, v.entry_z, v.entry0, v.entry2,
    ) = tie(
        v.near_sums, v.out_core, v.cots, v.qkv_side, v.qkv_mine, v.up_half_b, v.branch0,
        v.entry_got_zy, v.entry_got_yz, v.entry_y, v.entry_z, v.entry0, v.entry2,
    )
    v.entry_got_y = swap_seq(v.entry_y, 1)
    v.entry_got_z = swap_seq(v.entry_z, 2)
    v.qkv_half_send = second_sum(v.qkv_mine, v.qkv_side)
    v.qkv_half = swap_seq(v.qkv_half_send, 4)
    v.out_mine, v.out_send = weight_grad(
        v.cots, [v.attn0, v.attn1], v.out_core
    )
    v.out_side = swap_grp(v.out_send, 2)

    rank_ids = jnp.arange(TP, dtype=jnp.int32)
    first_sums = v.far_sums + v.near_sums
    wide_sums = jnp.concatenate(
        [first_sums[:2], second_sums[:2], cot_sum, jnp.zeros((3, D), F32)], axis=0
    )
    wide_sums = restore_runs(wide_sums, place_index)
    qkv_bias_term = qkv_bias_term.reshape(3, 1, HCOLS)
    v.sums = jnp.concatenate(
        [
            wide_sums[:5].reshape(-1),
            jnp.where((rank_ids == tp_rank)[None, :, None], qkv_bias_term, 0.0).reshape(-1),
            jnp.where((rank_ids == tp_rank)[:, None], up_bias_term, 0.0).reshape(-1),
        ]
    ).reshape(-1, LANES)
    v.sums_got = swap_grp(v.sums, 1)
    v.entry_a_far = second_sum(v.entry0, v.entry_got_zy)
    v.entry_b_far = second_sum(v.entry2, v.entry_got_yz)
    (
        v.sums, v.sums_got, v.out_send, v.out_mine, v.entry_got_y, v.entry_got_z, v.entry_a_far,
        v.entry_b_far, v.branch0, v.up_half_b,
    ) = tie(
        v.sums, v.sums_got, v.out_send, v.out_mine, v.entry_got_y, v.entry_got_z, v.entry_a_far,
        v.entry_b_far, v.branch0, v.up_half_b,
    )
    v.entry_far_a = swap_seq(v.entry_a_far, 2)
    v.entry_far_b = swap_seq(v.entry_b_far, 1)
    v.sums = v.sums + v.sums_got
    v.sums_got = swap_grp(v.sums, 2)
    v.layer_a, v.layer_b = finish_outputs(
        (
            (v.branch0, v.got_y, v.branch_far_a),
            (v.branch2, v.got_z, v.branch_far_b),
        ),
        (v.own_a, v.own_b),
        bias_out,
        place_index,
    )
    up_own, v.up_side2, v.up_far = split_rows(
        [(v.up_mine, v.up_side, (v.up_half_a, v.up_half_b))], tp_rank
    )
    (
        v.layer_a, v.sums, v.sums_got, v.up_side2, v.out_side, v.out_mine, v.qkv_half,
    ) = tie(
        v.layer_a, v.sums, v.sums_got, v.up_side2, v.out_side, v.out_mine, v.qkv_half,
    )
    v.out_half_send = second_sum(v.out_mine, v.out_side)
    v.out_half = swap_seq(v.out_half_send, 4)
    v.up_y = swap_seq(v.up_side2, 1)
    v.sums = v.sums + v.sums_got
    v.sums_got = swap_seq(v.sums, 4)
    (
        v.entry_far_a, v.entry_far_b, v.out_half, v.up_y, v.up_far, v.down_far, v.sums,
        v.sums_got,
    ) = tie(
        v.entry_far_a, v.entry_far_b, v.out_half, v.up_y, v.up_far, v.down_far, v.sums,
        v.sums_got,
    )
    late_own, late_side, late_far = split_rows(
        [
            (v.qkv_mine, v.qkv_side, (v.qkv_half,)),
            (v.out_mine, v.out_side, (v.out_half,)),
        ],
        tp_rank,
    )
    v.late_y = swap_seq(late_side, 1)
    v.down_z = swap_seq(onward(v.down_far, v.down_y), 2)
    v.up_z = swap_seq(onward(v.up_far, v.up_y), 2)
    v.sums = v.sums + v.sums_got
    v.sums_got = swap_seq(v.sums, 1)
    v.grad_a, grad_b = finish_grads(
        (
            (v.entry0, v.entry_got_y, v.entry_far_a),
            (v.entry2, v.entry_got_z, v.entry_far_b),
        ),
        (v.own_a, v.own_b),
        (v.cot_a, v.cot_b),
        place_index,
    )
    (
        v.grad_a, v.late_y, v.down_z, v.up_z, v.sums, v.sums_got,
    ) = tie(
        v.grad_a, v.late_y, v.down_z, v.up_z, v.sums, v.sums_got,
    )
    v.late_z = swap_seq(onward(late_far, v.late_y), 2)
    v.sums = v.sums + v.sums_got
    v.sums_got = swap_seq(v.sums, 2)
    (v.down_grad,) = join_columns(
        down_own, v.down_y, v.down_z, [(1, ff_here)], tp_rank
    )
    (v.up_grad,) = join_columns(up_own, v.up_y, v.up_z, [(1, ff_here)], tp_rank)
    grad_a, down_grad, up_weight_grad = v.grad_a, v.down_grad, v.up_grad
    qkv_weight_grad, out_grad = join_columns(
        late_own, v.late_y, v.late_z, [(3, HCOLS), (1, HCOLS)], tp_rank
    )
    down_weight_grad, out_weight_grad = down_grad.T, out_grad.T
    sums = (v.sums + v.sums_got).reshape(-1)
    cuts = np.cumsum([D, D, D, D, D, 3 * D])
    gain_one, shift_one, gain_two, shift_two, out_sum, qkv_sum, up_sum = jnp.split(sums, cuts)

    return (
        v.layer_a[None],
        v.layer_b[None, None],
        grad_a[None],
        grad_b[None, None],
        gain_one,
        shift_one,
        gain_two,
        shift_two,
        qkv_weight_grad,
        qkv_sum,
        out_weight_grad,
        out_sum,
        up_weight_grad,
        up_sum,
        down_weight_grad,
        out_sum,
    )


def solution(mesh):
    in_specs = (
        P("grp", "seq", None),
        P("grp", "seq", None, None),
        P("grp", "seq"),
        P("grp", None),
        P(),
        P(),
        P(),
        P(),
        P(("grp", "seq"), None),
        P(),
        P(None, ("grp", "seq")),
        P(),
        P(("grp", "seq"), None),
        P(),
        P(None, ("grp", "seq")),
        P(),
        P("grp", "seq", None),
        P("grp", "seq", None, None),
    )
    out_specs = (
        P("grp", "seq", None),
        P("grp", "seq", None, None),
        P("grp", "seq", None),
        P("grp", "seq", None, None),
        P(),
        P(),
        P(),
        P(),
        P(("grp", "seq"), None),
        P(),
        P(None, ("grp", "seq")),
        P(),
        P(("grp", "seq"), None),
        P(),
        P(None, ("grp", "seq")),
        P(),
    )
    plan = square_plan if (mesh.shape["grp"], mesh.shape["seq"]) == (4, 8) else local
    return jax.shard_map(plan, mesh=mesh, in_specs=in_specs, out_specs=out_specs, check_vma=False)
```

```python
from functools import partial
import math

import jax
import jax.numpy as jnp
import numpy as np
from jax import lax
from jax.experimental import pallas as pl
from jax.experimental.pallas import tpu as pltpu
from jax.sharding import PartitionSpec as P

D = 2048
HEADS = 8
HEAD = 256
ROT = 64
PROMPT = 2048


EPSILON = 1e-05
NEG_FILL = -1e30
ROPE_BASE = 10000.0


def layer_norm(values, ln_gain, ln_shift):
    center = values - jnp.mean(values, axis=-1, keepdims=True)
    normed = center * lax.rsqrt(jnp.mean(center * center, axis=-1, keepdims=True) + EPSILON)
    return normed * ln_gain + ln_shift


def both_norms(values, gain_one, shift_one, gain_two, shift_two):
    return (layer_norm(values, gain_one, shift_one), layer_norm(values, gain_two, shift_two))


def rotate(head_data, positions, sign_flip):
    half_rot = ROT // 2
    inv_freq = ROPE_BASE ** (-(2.0 * jnp.arange(half_rot, dtype=jnp.float32)) / ROT)
    angles = positions[:, None] * inv_freq[None, :]
    cos_table = jnp.cos(angles)[:, None, :]
    sin_table = sign_flip * jnp.sin(angles)[:, None, :]
    first_half = head_data[..., :half_rot]
    second = head_data[..., half_rot:ROT]
    return jnp.concatenate(
        [
            first_half * cos_table - second * sin_table,
            second * cos_table + first_half * sin_table,
            head_data[..., ROT:],
        ],
        axis=-1,
    )


def contract_rows(left, right):
    return lax.dot_general(
        left, right, (((1,), (1,)), ((), ())), preferred_element_type=jnp.float32
    )


def contract_cols(left, right):
    return lax.dot_general(
        left, right, (((0,), (0,)), ((), ())), preferred_element_type=jnp.float32
    )


def local(
    prompt,
    conts,
    assignment,
    offsets,
    ln1_gain,
    ln1_bias,
    ln2_gain,
    ln2_bias,
    qkv_weight,
    qkv_bias,
    out_weight,
    out_bias,
    up_weight,
    up_bias,
    down_weight,
    down_bias,
    prompt_cot,
    cont_cot,
):
    prompt_rows = prompt.shape[1]
    cont_rows = conts.shape[2]
    row_total = prompt_rows + cont_rows
    score_scale = 1.0 / math.sqrt(HEAD)
    shard_index = lax.axis_index("seq")
    tokens = jnp.concatenate([prompt[0], conts[0, 0]], axis=0).astype(jnp.float32)
    branch_ids = jnp.arange(offsets.shape[1], dtype=jnp.int32)
    my_offset = jnp.sum(jnp.where(branch_ids == assignment[0, 0], offsets[0], 0))
    prompt_mark = shard_index * prompt_rows + jnp.arange(prompt_rows, dtype=jnp.int32)
    cont_mark = PROMPT + jnp.arange(cont_rows, dtype=jnp.int32)
    query_mark = jnp.concatenate([prompt_mark, cont_mark])
    positions = jnp.concatenate([prompt_mark, cont_mark + my_offset]).astype(jnp.float32)
    (first_norm, second_norm), norm_pullback = jax.vjp(
        both_norms, tokens, ln1_gain, ln1_bias, ln2_gain, ln2_bias
    )
    first_low = first_norm.astype(jnp.bfloat16)
    second_low = second_norm.astype(jnp.bfloat16)
    qkv_full, up_full = (
        lax.all_gather(qkv_weight, ("grp", "seq"), axis=0, tiled=True),
        lax.all_gather(up_weight, ("grp", "seq"), axis=0, tiled=True),
    )
    qkv_acc = jnp.dot(first_low, qkv_full, preferred_element_type=jnp.float32)
    up_acc = jnp.dot(second_low, up_full, preferred_element_type=jnp.float32)
    split_qkv = (qkv_acc + qkv_bias).reshape(row_total, 3, HEADS, HEAD)
    queries = rotate(split_qkv[:, 0], positions, 1.0).astype(jnp.bfloat16)
    keys_rot = rotate(split_qkv[:, 1], positions, 1.0).astype(jnp.bfloat16)
    values_low = split_qkv[:, 2].astype(jnp.bfloat16)
    hidden_pre = up_acc + up_bias
    activated, gelu_pullback = jax.vjp(partial(jax.nn.gelu, approximate=False), hidden_pre)
    act_low = activated.astype(jnp.bfloat16)

    def score_block(key_block, key_mark):
        raw_scores = (
            jnp.einsum("qhd,khd->hqk", queries, key_block, preferred_element_type=jnp.float32)
            * score_scale
        )
        allowed = key_mark[None, :] <= query_mark[:, None]
        return (raw_scores, allowed)

    def absorb(soft_state, key_block, value_block, key_mark):
        run_max, run_sum, run_acc = soft_state
        raw_scores, allowed = score_block(key_block, key_mark)
        masked = jnp.where(allowed[None], raw_scores, NEG_FILL)
        new_max = jnp.maximum(run_max, jnp.max(masked, axis=-1))
        exp_scores = jnp.where(allowed[None], jnp.exp(masked - new_max[..., None]), 0.0)
        factor = jnp.exp(run_max - new_max)
        mixed_heads = jnp.einsum(
            "hqk,khd->qhd",
            exp_scores.astype(jnp.bfloat16),
            value_block,
            preferred_element_type=jnp.float32,
        )
        return (
            new_max,
            run_sum * factor + jnp.sum(exp_scores, axis=-1),
            run_acc * factor.T[:, :, None] + mixed_heads,
        )

    cont_keys = keys_rot[prompt_rows:]
    cont_values = values_low[prompt_rows:]
    start_state = (
        jnp.full((HEADS, row_total), NEG_FILL, jnp.float32),
        jnp.zeros((HEADS, row_total), jnp.float32),
        jnp.zeros((row_total, HEADS, HEAD), jnp.float32),
    )
    start_state = absorb(start_state, cont_keys, cont_values, cont_mark)
    prompt_keys_send = keys_rot[:prompt_rows].reshape(prompt_rows, D)
    prompt_values_send = values_low[:prompt_rows].reshape(prompt_rows, D)
    key_piece = lax.all_gather(prompt_keys_send, "seq", axis=0, tiled=True)
    value_piece = lax.all_gather(prompt_values_send, "seq", axis=0, tiled=True)
    piece_width = key_piece.shape[0]
    key_mark = jnp.arange(piece_width, dtype=jnp.int32)
    run_max, run_sum, run_acc = absorb(
        start_state,
        key_piece.reshape(piece_width, HEADS, HEAD),
        value_piece.reshape(piece_width, HEADS, HEAD),
        key_mark,
    )
    attention = run_acc / run_sum.T[:, :, None]
    log_total = run_max + jnp.log(run_sum)
    attention_low = attention.reshape(row_total, D).astype(jnp.bfloat16)
    out_full, down_full = (
        lax.all_gather(out_weight, ("grp", "seq"), axis=1, tiled=True),
        lax.all_gather(down_weight, ("grp", "seq"), axis=1, tiled=True),
    )
    branch_sum = jnp.dot(attention_low, out_full, preferred_element_type=jnp.float32) + jnp.dot(
        act_low, down_full, preferred_element_type=jnp.float32
    )
    layer_out = tokens + branch_sum + out_bias + down_bias
    grad_out = jnp.concatenate([prompt_cot[0], cont_cot[0, 0]], axis=0)
    grad_f32 = grad_out.astype(jnp.float32)
    bias_out_term = jnp.sum(grad_f32, axis=0)
    out_again, down_again = (
        lax.all_gather(out_weight, ("grp", "seq"), axis=1, tiled=True),
        lax.all_gather(down_weight, ("grp", "seq"), axis=1, tiled=True),
    )
    attn_grad = contract_rows(grad_out, out_again)
    act_grad = contract_rows(grad_out, down_again)
    attn_grad_low = attn_grad.astype(jnp.bfloat16)
    (hidden_grad,) = gelu_pullback(act_grad)
    hidden_grad_low = hidden_grad.astype(jnp.bfloat16)
    up_bias_term = jnp.sum(hidden_grad_low.astype(jnp.float32), axis=0)
    grad_heads = attn_grad_low.reshape(row_total, HEADS, HEAD)
    row_delta = jnp.sum(grad_heads.astype(jnp.float32) * attention, axis=-1).T

    def back_block(key_block, value_block, key_mark):
        raw_scores, allowed = score_block(key_block, key_mark)
        probabilities = jnp.exp(
            jnp.where(allowed[None], raw_scores - log_total[..., None], NEG_FILL)
        )
        prob_grad = jnp.einsum(
            "qhd,khd->hqk", grad_heads, value_block, preferred_element_type=jnp.float32
        )
        score_grad = (probabilities * (prob_grad - row_delta[..., None])).astype(jnp.bfloat16)
        query_term = (
            jnp.einsum("hqk,khd->qhd", score_grad, key_block, preferred_element_type=jnp.float32)
            * score_scale
        )
        key_term = (
            jnp.einsum("hqk,qhd->khd", score_grad, queries, preferred_element_type=jnp.float32)
            * score_scale
        )
        value_term = jnp.einsum(
            "hqk,qhd->khd",
            probabilities.astype(jnp.bfloat16),
            grad_heads,
            preferred_element_type=jnp.float32,
        )
        return (query_term, key_term, value_term)

    query_local, key_local, value_local = back_block(cont_keys, cont_values, cont_mark)
    gathered_keys, gathered_values = (
        lax.all_gather(prompt_keys_send, "seq", axis=0, tiled=True),
        lax.all_gather(prompt_values_send, "seq", axis=0, tiled=True),
    )
    key_block_size = min(512, PROMPT)
    block_count = PROMPT // key_block_size

    def scan_step(query_total, inputs):
        key_block, value_block, block_start = inputs
        key_mark = block_start + jnp.arange(key_block_size, dtype=jnp.int32)
        query_term, key_term, value_term = back_block(
            key_block.reshape(key_block_size, HEADS, HEAD),
            value_block.reshape(key_block_size, HEADS, HEAD),
            key_mark,
        )
        return (
            query_total + query_term,
            (key_term.reshape(key_block_size, D), value_term.reshape(key_block_size, D)),
        )

    query_grad, (key_terms, value_terms) = lax.scan(
        scan_step,
        query_local,
        (
            gathered_keys.reshape(block_count, key_block_size, D),
            gathered_values.reshape(block_count, key_block_size, D),
            jnp.arange(block_count, dtype=jnp.int32) * key_block_size,
        ),
    )
    key_prompt_grad, value_prompt_grad = (
        lax.psum_scatter(
            key_terms.reshape(PROMPT, D).astype(jnp.bfloat16),
            "seq",
            scatter_dimension=0,
            tiled=True,
        ).astype(jnp.float32),
        lax.psum_scatter(
            value_terms.reshape(PROMPT, D).astype(jnp.bfloat16),
            "seq",
            scatter_dimension=0,
            tiled=True,
        ).astype(jnp.float32),
    )
    key_grad = jnp.concatenate([key_prompt_grad, key_local.reshape(cont_rows, D)], axis=0).reshape(
        row_total, HEADS, HEAD
    )
    value_grad = jnp.concatenate(
        [value_prompt_grad, value_local.reshape(cont_rows, D)], axis=0
    ).reshape(row_total, HEADS, HEAD)
    qkv_grad = (
        jnp.stack(
            [rotate(query_grad, positions, -1.0), rotate(key_grad, positions, -1.0), value_grad],
            axis=1,
        )
        .reshape(row_total, 3 * D)
        .astype(jnp.bfloat16)
    )
    qkv_bias_term = jnp.sum(qkv_grad.astype(jnp.float32), axis=0)
    qkv_again, up_again = (
        lax.all_gather(qkv_weight, ("grp", "seq"), axis=0, tiled=True),
        lax.all_gather(up_weight, ("grp", "seq"), axis=0, tiled=True),
    )
    first_grad = contract_rows(qkv_grad, qkv_again)
    second_grad = contract_rows(hidden_grad_low, up_again)
    token_grad, gain_one, shift_one, gain_two, shift_two = norm_pullback((first_grad, second_grad))
    token_grad = token_grad + grad_f32
    small_sums = lax.psum(
        (gain_one, shift_one, gain_two, shift_two, qkv_bias_term, bias_out_term, up_bias_term),
        ("grp", "seq"),
    )
    out_sources = jnp.concatenate([attention_low, act_low], axis=1)
    in_group = lax.psum_scatter(
        jnp.concatenate(
            [contract_cols(first_low, qkv_grad), contract_cols(second_low, hidden_grad_low)], axis=1
        ).astype(jnp.bfloat16),
        "grp",
        scatter_dimension=0,
        tiled=True,
    )
    in_share = lax.psum_scatter(in_group, "seq", scatter_dimension=0, tiled=True).astype(
        jnp.float32
    )
    out_group = lax.psum_scatter(
        contract_cols(grad_out, out_sources).astype(jnp.bfloat16),
        "grp",
        scatter_dimension=0,
        tiled=True,
    )
    out_share = lax.psum_scatter(out_group, "seq", scatter_dimension=0, tiled=True).astype(
        jnp.float32
    )
    qkv_weight_grad = in_share[:, : 3 * D]
    up_weight_grad = in_share[:, 3 * D :]
    out_weight_grad = out_share[:, :D].T
    down_weight_grad = out_share[:, D:].T
    prompt_result = layer_out[:prompt_rows][None]
    cont_result = layer_out[prompt_rows:][None, None]
    prompt_grad = token_grad[:prompt_rows][None]
    cont_grad = token_grad[prompt_rows:][None, None]
    return (
        prompt_result,
        cont_result,
        prompt_grad,
        cont_grad,
        small_sums[0],
        small_sums[1],
        small_sums[2],
        small_sums[3],
        qkv_weight_grad,
        small_sums[4],
        out_weight_grad,
        small_sums[5],
        up_weight_grad,
        small_sums[6],
        down_weight_grad,
        small_sums[5],
    )


PROMPT_ORDER = (0, 2, 1, 3)
CONT_ORDER = (0, 1, 2, 3)
WIDTH_ORDER = (0, 1, 4, 5, 2, 3, 6, 7)
TP = 4
HEADS_HERE = HEADS // TP
HCOLS = HEADS_HERE * HEAD
LANES = 128
COST_UNIT = 1.0e6
COSTS = {
    "norms": 15,
    "qkv_rotary": 12,
    "feed_forward_up": 30,
    "attention_grad": 11,
    "weight_grad": 14,
    "attention_both_ways": 28,
    "feed_forward_back": 25,
    "branch_outputs": 34,
    "norm_grad": 25,
    "join_grads": 8,
    "finish_outputs": 7,
    "finish_grads": 9,
}
BF = jnp.bfloat16
F32 = jnp.float32


def swap_grp(array, bits):
    return lax.ppermute(array, "grp", [(i, i ^ bits) for i in range(4)])


def swap_seq(array, bits):
    return lax.ppermute(array, "seq", [(i, i ^ bits) for i in range(8)])


def matmul_nn(left, right):
    return jnp.dot(left, right, preferred_element_type=F32)


def pick(array, index, axis):
    return lax.dynamic_index_in_dim(array, index, axis, keepdims=False)


def place(buffer, piece, index):
    return lax.dynamic_update_index_in_dim(buffer, piece, index, 0)


def tie(*arrays):
    return lax.optimization_barrier(arrays)


def whole(shape):
    return pl.BlockSpec(shape, lambda i, rank: (0,) * len(shape))


def cost(name):
    flops = int(COSTS.get(name, 2) * COST_UNIT)
    return pl.CostEstimate(flops=flops, transcendentals=0, bytes_accessed=0)


def ranked_call(body, rank, ins, shapes, name, blocks=None):
    return pl.pallas_call(
        body,
        grid_spec=pltpu.PrefetchScalarGridSpec(
            num_scalar_prefetch=1,
            grid=(1,),
            in_specs=[whole(shape) for shape in blocks or [a.shape for a in ins]],
            out_specs=[whole(s.shape) for s in shapes],
        ),
        out_shape=shapes,
        compiler_params=pltpu.CompilerParams(vmem_limit_bytes=56 << 20),
        cost_estimate=cost(name),
        name=name,
    )(rank.reshape(1), *ins)


def split_columns(shards, groups, tp_rank):
    rows = shards[0].shape[0]
    widths = [shard.shape[1] // (TP * count) for shard, count in zip(shards, groups)]
    cols = sum(width * count for width, count in zip(widths, groups))

    def body(rank_ref, *refs):
        ins, (own_ref, side_ref, far_ref) = refs[: len(shards)], refs[len(shards) :]
        at = 0
        for ref, count, width in zip(ins, groups, widths):
            for part in range(count):
                for bits in range(TP):
                    start = pl.multiple_of((part * TP + (rank_ref[0] ^ bits)) * width, width)
                    run = ref[:, pl.ds(start, width)]
                    here = slice(at, at + width)
                    if bits == 0:
                        own_ref[:, here] = run
                    elif bits == 2:
                        far_ref[:, here] = run
                    else:
                        side_ref[bits // 2, :, here] = run
                at += width

    shapes = [
        jax.ShapeDtypeStruct((rows, cols), BF),
        jax.ShapeDtypeStruct((2, rows, cols), BF),
        jax.ShapeDtypeStruct((rows, cols), BF),
    ]
    return ranked_call(body, tp_rank, list(shards), shapes, "split_columns")


def stack_ranks(own, over_y, over_z, cuts, tp_rank, uncut=False):
    rows, cols = own.shape
    runs = [slice(sum(cuts[:i]), sum(cuts[: i + 1])) for i in range(len(cuts))]
    if uncut:
        runs.append(slice(0, cols))

    def body(rank_ref, own_ref, y_ref, z_ref, *outs):
        for out, here in zip(outs, runs):
            pieces = (own_ref[:, here], y_ref[0, :, here], z_ref[0, :, here], z_ref[1, :, here])
            for bits, piece in enumerate(pieces):
                start = pl.multiple_of((rank_ref[0] ^ bits) * rows, rows)
                out[pl.ds(start, rows), :] = piece

    shapes = [jax.ShapeDtypeStruct((TP * rows, run.stop - run.start), BF) for run in runs]
    return ranked_call(body, tp_rank, [own, over_y, over_z], shapes, "stack_ranks")


def split_rows(groups, tp_rank, first=1):
    rows = groups[0][2][0].shape[0] // TP
    cols = sum(terms[0].shape[1] for terms in groups)
    flat = [array for kept, got_x, got_z in groups for array in (kept, got_x, *got_z)]

    def body(rank_ref, *refs):
        ins, (own_ref, side_ref, far_ref) = list(refs[: len(flat)]), refs[len(flat) :]
        at = 0
        for _, _, got_z in groups:
            kept, got_x = ins.pop(0), ins.pop(0)
            inside = 0
            for _ in got_z:
                run_ref = ins.pop(0)
                width = run_ref.shape[1]
                here, cut = slice(at, at + width), slice(inside, inside + width)
                at, inside = at + width, inside + width
                for bits in range(TP):
                    lines = pl.ds(pl.multiple_of((rank_ref[0] ^ bits) * rows, rows), rows)
                    total = kept[lines, cut].astype(F32) + got_x[lines, cut].astype(F32)
                    run = (total + run_ref[lines, :].astype(F32)).astype(BF)
                    if bits == 0:
                        own_ref[:, here] = run
                    elif bits == 3 - first:
                        far_ref[:, here] = run
                    else:
                        side_ref[int(bits == 3), :, here] = run

    shapes = [
        jax.ShapeDtypeStruct((rows, cols), BF),
        jax.ShapeDtypeStruct((2, rows, cols), BF),
        jax.ShapeDtypeStruct((rows, cols), BF),
    ]
    blocks = [(TP * rows, term.shape[1]) for term in flat]
    return ranked_call(body, tp_rank, flat, shapes, "split_rows", blocks)


def join_columns(own, got_first, got_second, parts, tp_rank, first=1):
    rows = own.shape[0]

    def body(rank_ref, own_ref, first_ref, second_ref, *outs):
        at = 0
        for out, (count, width) in zip(outs, parts):
            for part in range(count):
                here = slice(at, at + width)
                pieces = {
                    0: own_ref[:, here],
                    first: first_ref[0, :, here],
                    3 - first: second_ref[0, :, here],
                    3: second_ref[1, :, here],
                }
                for bits, piece in pieces.items():
                    start = pl.multiple_of((part * TP + (rank_ref[0] ^ bits)) * width, width)
                    out[:, pl.ds(start, width)] = piece.astype(F32)
                at += width

    shapes = [jax.ShapeDtypeStruct((rows, TP * count * width), F32) for count, width in parts]
    return ranked_call(body, tp_rank, [own, got_first, got_second], shapes, "join_columns")


def reorder_runs(arrays, place_index, sums=False):
    run = D // 8
    shapes = [jax.ShapeDtypeStruct(a.shape, a.dtype) for a in arrays]
    if sums:
        shapes.append(jax.ShapeDtypeStruct((1, D), F32))

    def body(index_ref, *refs):
        ins, outs = refs[: len(arrays)], refs[len(arrays) :]
        for j, bits in enumerate(WIDTH_ORDER):
            start = pl.multiple_of((index_ref[0] ^ bits) * run, run)
            here = slice(j * run, (j + 1) * run)
            for in_ref, out_ref in zip(ins, outs):
                out_ref[:, here] = in_ref[:, pl.ds(start, run)]
        if sums:
            total = outs[0][...].astype(F32).sum(axis=0, keepdims=True)
            for out_ref in outs[1 : len(arrays)]:
                total = total + out_ref[...].astype(F32).sum(axis=0, keepdims=True)
            outs[-1][...] = total

    return ranked_call(body, place_index, list(arrays), shapes, "reorder_runs")


def restore_runs(array, place_index):
    run = D // 8

    def body(index_ref, in_ref, out_ref):
        for j, bits in enumerate(WIDTH_ORDER):
            start = pl.multiple_of((index_ref[0] ^ bits) * run, run)
            out_ref[:, pl.ds(start, run)] = in_ref[:, j * run : (j + 1) * run]

    shapes = [jax.ShapeDtypeStruct(array.shape, array.dtype)]
    return ranked_call(body, place_index, [array], shapes, "restore_runs")[0]


def finish_outputs(parts, tokens, bias, place_index):
    run = D // 8
    rows = tokens[0].shape[0]
    flat = [term for terms in parts for term in terms]

    def body(index_ref, *refs):
        ins, outs = refs[: len(flat) + len(tokens) + 1], refs[len(flat) + len(tokens) + 1 :]
        bias_ref = ins[-1]
        for i, out_ref in enumerate(outs):
            own, got, got_far = ins[3 * i : 3 * i + 3]
            token_ref = ins[len(flat) + i]
            value = token_ref[...].astype(F32) + own[...].astype(F32) + got[...].astype(F32)
            value = value + got_far[...].astype(F32) + bias_ref[...]
            for j, bits in enumerate(WIDTH_ORDER):
                start = pl.multiple_of((index_ref[0] ^ bits) * run, run)
                out_ref[:, pl.ds(start, run)] = value[:, j * run : (j + 1) * run]

    shapes = [jax.ShapeDtypeStruct((rows, D), F32) for _ in tokens]
    blocks = [(rows, D)] * (len(flat) + len(tokens)) + [bias.shape]
    return ranked_call(
        body, place_index, flat + list(tokens) + [bias], shapes, "finish_outputs", blocks
    )


def finish_grads(parts, tokens, cots, place_index):
    run = D // 8
    rows = tokens[0].shape[0]
    count = len(tokens)
    flat = [term for terms in parts for term in terms]

    def body(index_ref, *refs):
        ins, outs = refs[: 5 * count], refs[5 * count :]
        for i, out_ref in enumerate(outs):
            own, got, got_far = ins[3 * i : 3 * i + 3]
            token = ins[3 * count + i][...].astype(F32)
            cot = ins[4 * count + i][...].astype(F32)
            entry = own[...].astype(F32) + got[...].astype(F32) + got_far[...].astype(F32)
            center = token - jnp.mean(token, axis=1, keepdims=True)
            spread = lax.rsqrt(jnp.mean(center * center, axis=1, keepdims=True) + EPSILON)
            normed = center * spread
            entry_mean = jnp.mean(entry, axis=1, keepdims=True)
            entry_dot = jnp.mean(entry * normed, axis=1, keepdims=True)
            value = cot + spread * (entry - entry_mean - normed * entry_dot)
            for j, bits in enumerate(WIDTH_ORDER):
                start = pl.multiple_of((index_ref[0] ^ bits) * run, run)
                out_ref[:, pl.ds(start, run)] = value[:, j * run : (j + 1) * run]

    shapes = [jax.ShapeDtypeStruct((rows, D), F32) for _ in tokens]
    return ranked_call(
        body,
        place_index,
        flat + list(tokens) + list(cots),
        shapes,
        "finish_grads",
        [(rows, D)] * (5 * count),
    )


def part_specs(rows, tile, width, parts):
    per_part = rows // tile

    def spec(k):
        return pl.BlockSpec((tile, width), lambda i: (jnp.clip(i - k * per_part, 0, per_part - 1), 0))

    return [spec(k) for k in range(parts)]


def norms_body(gain1, bias1, gain2, bias2, *refs):
    *parts, rows_ref, first_ref, second_ref, mean_ref, spread_ref = refs
    step = pl.program_id(0)
    per_part = pl.num_programs(0) // len(parts)
    for k, part in enumerate(parts):

        @pl.when(step // per_part == k)
        def _(part=part):
            rows_ref[...] = part[...]
            values = part[...].astype(F32)
            mean = jnp.mean(values, axis=1, keepdims=True)
            center = values - mean
            spread = lax.rsqrt(jnp.mean(center * center, axis=1, keepdims=True) + EPSILON)
            normed = center * spread
            first_ref[...] = (normed * gain1[...] + bias1[...]).astype(BF)
            second_ref[...] = (normed * gain2[...] + bias2[...]).astype(BF)
            mean_ref[...] = mean
            spread_ref[...] = spread


def both_low_norms(parts, gain1, bias1, gain2, bias2):
    tile = parts[0].shape[0]
    total = tile * len(parts)
    vector = pl.BlockSpec((1, D), lambda i: (0, 0))
    wide = pl.BlockSpec((tile, D), lambda i: (i, 0))
    thin = pl.BlockSpec((tile, 1), lambda i: (i, 0))
    return pl.pallas_call(
        norms_body,
        grid=(total // tile,),
        in_specs=[vector] * 4 + part_specs(tile, tile, D, len(parts)),
        out_specs=[wide, wide, wide, thin, thin],
        out_shape=[
            jax.ShapeDtypeStruct((total, D), BF),
            jax.ShapeDtypeStruct((total, D), BF),
            jax.ShapeDtypeStruct((total, D), BF),
            jax.ShapeDtypeStruct((total, 1), F32),
            jax.ShapeDtypeStruct((total, 1), F32),
        ],
        compiler_params=pltpu.CompilerParams(vmem_limit_bytes=56 << 20),
        cost_estimate=cost("norms"),
        name="norms",
    )(gain1, bias1, gain2, bias2, *parts)


def resident(array, block=None, at=(0, 0)):
    return pl.BlockSpec(block or array.shape, lambda i: at, pipeline_mode=pl.Buffered(1))


def times(rows, halves, columns):
    upper, lower = halves
    half = upper.shape[0]
    return matmul_nn(rows[:, :half], upper[:, columns]) + matmul_nn(rows[:, half:], lower[:, columns])


def runs_of(width, run):
    return [slice(at, at + run) for at in range(0, width, run)]


def kernel(body, steps, in_specs, out_specs, out_shape, name, scratch=()):
    return pl.pallas_call(
        body,
        grid=(steps,),
        in_specs=in_specs,
        out_specs=out_specs,
        out_shape=out_shape,
        scratch_shapes=scratch,
        compiler_params=pltpu.CompilerParams(vmem_limit_bytes=58 << 20),
        cost_estimate=cost(name),
        name=name,
    )


def stacked(parts):
    tile, width = parts[0].shape

    def body(*refs):
        *ins, out_ref = refs
        for k, part in enumerate(ins):

            @pl.when(pl.program_id(0) == k)
            def _(part=part):
                out_ref[...] = part[...]

    return kernel(
        body,
        len(parts),
        part_specs(tile, tile, width, len(parts)),
        by_rows(tile, width),
        jax.ShapeDtypeStruct((tile * len(parts), width), BF),
        "stacked",
    )(*parts)


def beside(entries):
    tile, width = entries[0][0].shape
    specs, arrays = [], []
    for entry in entries:
        if isinstance(entry, tuple):
            specs += [pl.BlockSpec((tile, width), lambda i: (0, 0))] * 2
            arrays += entry
        elif entry.shape[0] == tile:
            specs += [pl.BlockSpec((tile, width), lambda i, h=h: (0, h)) for h in range(2)]
            arrays += [entry, entry]
        else:
            specs += [pl.BlockSpec((tile, width), lambda i, h=h: (h, 0)) for h in range(2)]
            arrays += [entry, entry]

    def body(*refs):
        *ins, out_ref = refs
        for k in range(len(entries)):

            @pl.when(pl.program_id(0) == k)
            def _(k=k):
                out_ref[:, :width] = ins[2 * k][...]
                out_ref[:, width:] = ins[2 * k + 1][...]

    return kernel(
        body,
        len(entries),
        specs,
        by_rows(tile, 2 * width),
        jax.ShapeDtypeStruct((tile * len(entries), 2 * width), BF),
        "beside",
    )(*arrays)


def second_sum(left, right, part=None):
    rows, width = left.shape[0] // 2, left.shape[1] // (1 if part is None else 2)
    wide = 1024 if width % 1024 == 0 else 512
    first = (part or 0) * (width // wide)

    def body(left_ref, right_ref, out_ref):
        out_ref[...] = (left_ref[...].astype(F32) + right_ref[...].astype(F32)).astype(BF)

    lower = pl.BlockSpec((rows, wide), lambda i: (1, first + i))
    at = right.shape[0] // rows - 1
    return kernel(
        body,
        width // wide,
        [lower, pl.BlockSpec((rows, wide), lambda i: (at, first + i))],
        pl.BlockSpec((rows, wide), lambda i: (0, i)),
        jax.ShapeDtypeStruct((rows, width), BF),
        "second_sum",
    )(left, right)


def onward(far, over_y):
    rows, width = far.shape

    def body(far_ref, y_ref, out_ref):
        out_ref[0] = far_ref[...]
        out_ref[1] = y_ref[0]

    return kernel(
        body,
        1,
        [
            pl.BlockSpec((rows, width), lambda i: (0, 0)),
            pl.BlockSpec((1, rows, width), lambda i: (1, 0, 0)),
        ],
        pl.BlockSpec((2, rows, width), lambda i: (0, 0, 0)),
        jax.ShapeDtypeStruct((2, rows, width), BF),
        "onward",
    )(far, over_y)


def by_rows(tile, width, tiles=lambda i: i):
    return pl.BlockSpec((tile, width), lambda i: (tiles(i), 0))


def attention_grad(parts, halves, column_block):
    tile = parts[0].shape[0]
    total = tile * len(parts)

    def body(upper, lower, *refs):
        *ins, out_ref, rows_ref, held = refs
        for k, part in enumerate(ins):

            @pl.when(pl.program_id(0) == k)
            def _(part=part):
                held[...] = part[...]

        rows = held[...]
        rows_ref[...] = rows
        out_ref[...] = times(rows, (upper, lower), slice(0, HCOLS)).astype(BF)

    weight_spec = resident(halves[0], (D // 2, HCOLS), (0, column_block))
    return kernel(
        body,
        len(parts),
        [weight_spec, weight_spec] + part_specs(tile, tile, D, len(parts)),
        [by_rows(tile, HCOLS), by_rows(tile, D)],
        [jax.ShapeDtypeStruct((total, HCOLS), BF), jax.ShapeDtypeStruct((total, D), BF)],
        "attention_grad",
        [pltpu.VMEM((tile, D), BF)],
    )(*halves, *parts)


def feed_forward_up(rows, halves, bias):
    total, ff_here = rows.shape[0], bias.shape[1]
    tile, wide = total // 4, ff_here // 2
    half = D // 2

    def body(rows_ref, upper, lower, bias_ref, act_ref, slope_ref):
        values = rows_ref[...]
        for run in runs_of(wide, 256):
            pre = times(values, (upper, lower), run) + bias_ref[:, run]
            cdf = 0.5 * (1.0 + lax.erf(pre * math.sqrt(0.5)))
            density = jnp.exp(-0.5 * pre * pre) * (1.0 / math.sqrt(2.0 * math.pi))
            act_ref[:, run] = (pre * cdf).astype(BF)
            slope_ref[:, run] = (cdf + pre * density).astype(BF)

    weight_spec = pl.BlockSpec((half, wide), lambda i: (0, i // 4))
    out_spec = pl.BlockSpec((tile, wide), lambda i: (i % 4, i // 4))
    return kernel(
        body,
        8,
        [
            by_rows(tile, D, lambda i: i % 4),
            weight_spec,
            weight_spec,
            pl.BlockSpec((1, wide), lambda i: (0, i // 4)),
        ],
        [out_spec] * 2,
        [jax.ShapeDtypeStruct((total, ff_here), BF)] * 2,
        "feed_forward_up",
    )(rows, *halves, bias)


def feed_forward_back(cots, halves, slope):
    total, ff_here = slope.shape
    tile, wide = total // 2, ff_here // 2
    half = D // 2

    def body(cot_ref, upper, lower, slope_ref, out_ref, sum_ref):
        @pl.when(pl.program_id(0) % 2 == 0)
        def _():
            sum_ref[...] = jnp.zeros_like(sum_ref)

        values = cot_ref[...]
        for run in runs_of(wide, 512):
            grad = times(values, (upper, lower), run) * slope_ref[:, run].astype(F32)
            low = grad.astype(BF)
            out_ref[:, run] = low
            sum_ref[:, run] += low.astype(F32).sum(axis=0, keepdims=True)

    weight_spec = pl.BlockSpec((half, wide), lambda i: (0, i // 2))
    both = pl.BlockSpec((tile, wide), lambda i: (i % 2, i // 2))
    return kernel(
        body,
        4,
        [by_rows(tile, D, lambda i: i % 2), weight_spec, weight_spec, both],
        [both, pl.BlockSpec((1, wide), lambda i: (0, i // 2))],
        [jax.ShapeDtypeStruct((total, ff_here), BF), jax.ShapeDtypeStruct((1, ff_here), F32)],
        "feed_forward_back",
    )(cots, *halves, slope)


def weight_grad(left, rights, core_got=None):
    total = left.shape[0]
    width = sum(right.shape[1] for right in rights)
    half = D // 2
    wide = 512
    steps = width // wide if len(rights) == 1 else 1
    keep = core_got is not None

    def body(left_ref, *refs):
        ins, rest = refs[: len(rights)], refs[len(rights) :]
        values = left_ref[...]
        at = 0
        for right in ins:
            here = slice(at, at + right.shape[1])
            at += right.shape[1]
            product = contract_cols(values, right[...])
            if keep:
                got_ref, mine_ref, side_ref = rest
                product = product + got_ref[:, here].astype(F32)
                mine_ref[:, here] = product[: half // 2].astype(BF)
                side_ref[:, here] = product[half // 2 :].astype(BF)
            else:
                rest[0][:, here] = product.astype(BF)

    if len(rights) == 1:
        right_specs = [pl.BlockSpec((total, wide), lambda i: (0, i))]
    else:
        right_specs = [resident(right) for right in rights]
    rows = half // 2 if keep else half
    count = 2 if keep else 1
    outs = kernel(
        body,
        steps,
        [resident(left, (total, half), (0, 0 if keep else 1))]
        + right_specs
        + ([pl.BlockSpec((half, wide), lambda i: (0, i))] if keep else []),
        [pl.BlockSpec((rows, wide), lambda i: (0, i))] * count,
        [jax.ShapeDtypeStruct((rows, width), BF)] * count,
        "weight_grad",
    )(left, *rights, *([core_got] if keep else []))
    return outs if keep else outs[0]


def width_tile(halves, height, columns, block=0):
    per_half = halves[0].shape[0] // height
    return [
        pl.BlockSpec((height, columns), lambda i: (jnp.minimum(i, per_half - 1), block)),
        pl.BlockSpec((height, columns), lambda i: (jnp.maximum(i - per_half, 0), block)),
    ]


def chosen(upper, lower):
    in_upper = pl.program_id(0) < pl.num_programs(0) // 2
    return jnp.where(in_upper, upper[...], lower[...])


def quarter_rows(tile):
    return [tile, tile // 2, tile // 2] * 2


def quarter_specs(tile, wide):
    return [pl.BlockSpec((rows, wide), lambda i: (0, i)) for rows in quarter_rows(tile)]


def put_quarter(outs, k, value):
    at = 3 * (k // 2)
    if k % 2 == 0:
        outs[at][...] = value
    else:
        half = value.shape[0] // 2
        outs[at + 1][...] = value[:half]
        outs[at + 2][...] = value[half:]


def branch_outputs(heads_low, act_low, attn_halves, column_block, down_halves):
    total, ff_here = act_low.shape
    tile = total // 4
    wide = 512

    def body(*refs):
        heads = [refs[h * 4 : h * 4 + 4] for h in range(HEADS_HERE)]
        refs = refs[4 * HEADS_HERE :]
        acts, attn, down, outs = refs[:4], refs[4:6], refs[6:8], refs[8:]
        attn_tile, down_tile = chosen(*attn), chosen(*down)
        for k in range(4):
            value = contract_rows(acts[k][...], down_tile)
            for head in range(HEADS_HERE):
                cut = slice(head * HEAD, (head + 1) * HEAD)
                value = value + contract_rows(heads[head][k][...], attn_tile[:, cut])
            put_quarter(outs, k, value.astype(BF))

    return kernel(
        body,
        D // wide,
        [resident(h, (tile, HEAD), (k, 0)) for h in heads_low for k in range(4)]
        + [resident(act_low, (tile, ff_here), (k, 0)) for k in range(4)]
        + width_tile(attn_halves, wide, HCOLS, column_block)
        + width_tile(down_halves, wide, ff_here),
        quarter_specs(tile, wide),
        [jax.ShapeDtypeStruct((rows, D), BF) for rows in quarter_rows(tile)],
        "branch_outputs",
    )(*[h for h in heads_low for _ in range(4)], *([act_low] * 4), *attn_halves, *down_halves)


def norm_grad(grads, halves, gain, tokens, mean, spread, row_blocks, addends=(), cut=False):
    tile = grads.shape[0] // 4
    count = len(row_blocks)
    width = grads.shape[1]
    wide = 512

    def body(upper, lower, gain_ref, *refs):
        rows, means, spreads, token_refs = (refs[i * count : (i + 1) * count] for i in range(4))
        rest = refs[4 * count :]
        adds, outs, sum_ref = rest[: len(addends)], rest[len(addends) : -1], rest[-1]
        weight = chosen(upper, lower)
        dots = jnp.zeros((1, wide), F32)
        totals = jnp.zeros((1, wide), F32)
        for k in range(count):
            value = contract_rows(rows[k][...], weight)
            scaled = value * gain_ref[...]
            if adds:
                scaled = scaled + adds[k][...].astype(F32)
            low = scaled.astype(BF)
            if cut:
                outs[2 * k][...] = low[: tile // 2]
                outs[2 * k + 1][...] = low[tile // 2 :]
            else:
                outs[k][...] = low
            normed = (token_refs[k][...].astype(F32) - means[k][...]) * spreads[k][...]
            dots = dots + (value * normed).sum(axis=0, keepdims=True)
            totals = totals + value.sum(axis=0, keepdims=True)
        sum_ref[0:1, :] = dots
        sum_ref[1:2, :] = totals

    column = pl.BlockSpec((tile, wide), lambda i: (0, i))
    out_rows = [tile // 2] * (2 * count) if cut else [tile] * count
    outs = kernel(
        body,
        D // wide,
        [
            *width_tile(halves, wide, width),
            pl.BlockSpec((1, wide), lambda i: (0, i)),
            *[resident(grads, (tile, width), (k, 0)) for k in row_blocks],
            *[resident(mean, (tile, 1), (k, 0)) for k in row_blocks],
            *[resident(spread, (tile, 1), (k, 0)) for k in row_blocks],
            *[pl.BlockSpec((tile, wide), lambda i, k=k: (k, i)) for k in row_blocks],
            *([column] * len(addends)),
        ],
        [pl.BlockSpec((rows, wide), lambda i: (0, i)) for rows in out_rows]
        + [pl.BlockSpec((8, wide), lambda i: (0, i))],
        [jax.ShapeDtypeStruct((rows, D), BF) for rows in out_rows]
        + [jax.ShapeDtypeStruct((8, D), F32)],
        "norm_grad",
    )(
        *halves,
        gain,
        *([grads] * count),
        *([mean] * count),
        *([spread] * count),
        *([tokens] * count),
        *addends,
    )
    return outs[:-1], outs[-1]


def rotary_tables(positions):
    lane = jnp.arange(LANES, dtype=jnp.int32)
    half_rot = ROT // 2
    exponent = -(2.0 * (lane % half_rot).astype(F32)) / ROT
    angles = positions[:, None] * (ROPE_BASE**exponent)[None, :]
    turning = (lane < ROT)[None, :]
    cos_table = jnp.where(turning, jnp.cos(angles), 1.0)
    sin_part = jnp.sin(angles)
    sin_table = jnp.where((lane < half_rot)[None, :], -sin_part, sin_part)
    return cos_table, jnp.where(turning, sin_table, 0.0)


def swapped_halves(values):
    half_rot = ROT // 2
    lane = lax.broadcasted_iota(jnp.int32, values.shape, 1)
    return jnp.where(
        lane < half_rot,
        pltpu.roll(values, LANES - half_rot, 1),
        pltpu.roll(values, half_rot, 1),
    )


def turned(values, cos_table, sin_table):
    first = values[:, :LANES]
    return jnp.concatenate(
        [first * cos_table + swapped_halves(first) * sin_table, values[:, LANES:]], axis=1
    )


def project_qkv(head, rows, halves, bias, cos_table, sin_table):
    total = rows.shape[0]
    tile = total // 2
    half = D // 2

    def body(rows_ref, *refs):
        weights, biases = refs[:6], refs[6:9]
        cos_ref, sin_ref, q_ref, near_key_ref, near_value_ref, own_ref = refs[9:]
        values = rows_ref[...]
        cos_here, sin_here = cos_ref[...], sin_ref[...]

        def product(kind):
            whole_run = slice(0, HEAD)
            return times(values, weights[2 * kind : 2 * kind + 2], whole_run) + biases[kind][...]

        query = turned(product(0), cos_here, sin_here)
        q_ref[...] = (query * (1.0 / math.sqrt(HEAD))).astype(BF)
        key = turned(product(1), cos_here, sin_here).astype(BF)
        value = product(2).astype(BF)

        @pl.when(pl.program_id(0) == 0)
        def _():
            near_key_ref[...] = key
            near_value_ref[...] = value

        @pl.when(pl.program_id(0) == 1)
        def _():
            own_ref[:, :HEAD] = key
            own_ref[:, HEAD:] = value

    columns = [kind * HEADS_HERE + head for kind in range(3)]
    both = jax.ShapeDtypeStruct((tile, 2 * HEAD), BF)
    one = jax.ShapeDtypeStruct((tile, HEAD), BF)
    kept_both = pl.BlockSpec((tile, 2 * HEAD), lambda i: (0, 0))
    kept = pl.BlockSpec((tile, HEAD), lambda i: (0, 0))
    return kernel(
        body,
        2,
        [
            by_rows(tile, D),
            *[resident(h, (half, HEAD), (0, c)) for c in columns for h in halves],
            *[resident(bias, (1, HEAD), (0, c)) for c in columns],
            by_rows(tile, LANES),
            by_rows(tile, LANES),
        ],
        [by_rows(tile, HEAD), kept, kept, kept_both],
        [jax.ShapeDtypeStruct((total, HEAD), BF), one, one, both],
        "qkv_rotary",
    )(rows, *[h for _ in columns for h in halves], *([bias] * 3), cos_table, sin_table)


def attention_body(
    q_ref,
    do_ref,
    kl_ref,
    vl_ref,
    kr_ref,
    vr_ref,
    kc_ref,
    vc_ref,
    cos_ref,
    sin_ref,
    cosl_ref,
    sinl_ref,
    cosr_ref,
    sinr_ref,
    qmark_ref,
    kmark_ref,
    o_ref,
    dq_ref,
    down_ref,
    dnear_ref,
    dfar_key_ref,
    dfar_value_ref,
    akl,
    avl,
    akr,
    avr,
):
    step = pl.program_id(0)
    last = pl.num_programs(0) - 1
    near = kl_ref.shape[0]

    @pl.when(step == 0)
    def _():
        for acc in (akl, avl, akr, avr):
            acc[...] = jnp.zeros_like(acc)

    query, grad = q_ref[...], do_ref[...]

    def work(own):
        scores = [contract_rows(query, kl_ref[...]), contract_rows(query, kr_ref[...])]
        if own:
            mine = contract_rows(query, kc_ref[...])
            at_row = lax.broadcasted_iota(jnp.int32, mine.shape, 0)
            at_col = lax.broadcasted_iota(jnp.int32, mine.shape, 1)
            scores.append(jnp.where(at_col <= at_row, mine, NEG_FILL))
        else:
            marks = kmark_ref[...]
            own_mark = qmark_ref[...]
            scores[0] = jnp.where(marks[:, :near] <= own_mark, scores[0], NEG_FILL)
            scores[1] = jnp.where(marks[:, near:] <= own_mark, scores[1], NEG_FILL)
        top = scores[0].max(axis=1, keepdims=True)
        for part in scores[1:]:
            top = jnp.maximum(top, part.max(axis=1, keepdims=True))
        probs = [jnp.exp(part - top) for part in scores]
        total = probs[0].sum(axis=1, keepdims=True)
        for part in probs[1:]:
            total = total + part.sum(axis=1, keepdims=True)
        share = 1.0 / total
        probs = [part * share for part in probs]
        low = [part.astype(BF) for part in probs]
        values = [vl_ref, vr_ref] + ([vc_ref] if own else [])
        keys = [kl_ref, kr_ref] + ([kc_ref] if own else [])
        mixed = matmul_nn(low[0], values[0][...])
        for part, ref in zip(low[1:], values[1:]):
            mixed = mixed + matmul_nn(part, ref[...])
        o_ref[...] = mixed.astype(BF)
        prob_grad = [contract_rows(grad, ref[...]) for ref in values]
        delta = (probs[0] * prob_grad[0]).sum(axis=1, keepdims=True)
        for part, grad_part in zip(probs[1:], prob_grad[1:]):
            delta = delta + (part * grad_part).sum(axis=1, keepdims=True)
        slopes = [
            (part * (grad_part - delta)).astype(BF) for part, grad_part in zip(probs, prob_grad)
        ]
        query_grad = matmul_nn(slopes[0], keys[0][...])
        for part, ref in zip(slopes[1:], keys[1:]):
            query_grad = query_grad + matmul_nn(part, ref[...])
        query_grad = query_grad * (1.0 / math.sqrt(HEAD))
        dq_ref[...] = turned(query_grad, cos_ref[...], -sin_ref[...]).astype(BF)
        akl[...] += contract_cols(slopes[0], query)
        akr[...] += contract_cols(slopes[1], query)
        avl[...] += contract_cols(low[0], grad)
        avr[...] += contract_cols(low[1], grad)
        if own:
            key_grad = contract_cols(slopes[2], query)
            down_ref[:, :HEAD] = turned(key_grad, cos_ref[...], -sin_ref[...]).astype(BF)
            down_ref[:, HEAD:] = contract_cols(low[2], grad).astype(BF)

    @pl.when(step < TP)
    def _():
        work(False)

    @pl.when(step >= TP)
    def _():
        work(True)

    @pl.when(step == last)
    def _():
        dnear_ref[:, :HEAD] = turned(akl[...], cosl_ref[...], -sinl_ref[...])
        dnear_ref[:, HEAD:] = avl[...]
        dfar_key_ref[...] = turned(akr[...], cosr_ref[...], -sinr_ref[...]).astype(BF)
        dfar_value_ref[...] = avr[...].astype(BF)


def attend(
    head, queries, grads, near, far, own, tables, near_tables, far_tables, query_mark, key_mark
):
    total = queries.shape[0]
    tile = total // (2 * TP)
    keys = near[0].shape[0]

    def row_tile(j):
        return j

    def cont_tile(j):
        return jnp.maximum(j - TP, 0)

    query_spec = pl.BlockSpec((tile, HEAD), lambda j: (row_tile(j), 0))
    row_spec = pl.BlockSpec((tile, HEAD), lambda j: (row_tile(j), head))
    out_spec = pl.BlockSpec((tile, HEAD), lambda j: (row_tile(j), 0))
    key_spec = pl.BlockSpec((keys, HEAD), lambda j: (0, 0))
    own_key = pl.BlockSpec((tile, HEAD), lambda j: (cont_tile(j), 0))
    own_value = pl.BlockSpec((tile, HEAD), lambda j: (cont_tile(j), 1))
    own_both = pl.BlockSpec((tile, 2 * HEAD), lambda j: (cont_tile(j), 0))
    both = pl.BlockSpec((keys, 2 * HEAD), lambda j: (0, 0))
    table_spec = pl.BlockSpec((tile, LANES), lambda j: (row_tile(j), 0))
    key_table = pl.BlockSpec((keys, LANES), lambda j: (0, 0))
    mark_spec = pl.BlockSpec((tile, 1), lambda j: (row_tile(j), 0))
    key_mark_spec = pl.BlockSpec((1, 2 * keys), lambda j: (0, 0))
    wide = jax.ShapeDtypeStruct((total, HEAD), BF)
    return pl.pallas_call(
        attention_body,
        grid=(2 * TP,),
        in_specs=[
            query_spec,
            row_spec,
            key_spec,
            key_spec,
            key_spec,
            key_spec,
            own_key,
            own_value,
            table_spec,
            table_spec,
            key_table,
            key_table,
            key_table,
            key_table,
            mark_spec,
            key_mark_spec,
        ],
        out_specs=[out_spec, out_spec, own_both, both, key_spec, key_spec],
        out_shape=[
            wide,
            wide,
            jax.ShapeDtypeStruct((keys, 2 * HEAD), BF),
            jax.ShapeDtypeStruct((keys, 2 * HEAD), F32),
            jax.ShapeDtypeStruct((keys, HEAD), BF),
            jax.ShapeDtypeStruct((keys, HEAD), BF),
        ],
        scratch_shapes=[pltpu.VMEM((keys, HEAD), F32)] * 4,
        compiler_params=pltpu.CompilerParams(vmem_limit_bytes=56 << 20),
        cost_estimate=cost("attention_both_ways"),
        name="attention_both_ways",
    )(
        queries,
        grads,
        *near,
        *far,
        own,
        own,
        *tables,
        *near_tables,
        *far_tables,
        query_mark,
        key_mark,
    )


def join_grads(query_grads, own_grads, near_grads, far_keys, far_values):
    total = query_grads[0].shape[0]
    tile = total // 4

    def body(*refs):
        out_ref, sum_ref = refs[-2:]
        dq, down, dnear, dfar_key, dfar_value = (
            refs[i * HEADS_HERE : (i + 1) * HEADS_HERE] for i in range(5)
        )
        step = pl.program_id(0)

        @pl.when(step == 0)
        def _():
            sum_ref[...] = jnp.zeros_like(sum_ref)

        for head in range(HEADS_HERE):
            at = head * HEAD
            key_at, value_at = slice(HCOLS + at, HCOLS + at + HEAD), slice(
                2 * HCOLS + at, 2 * HCOLS + at + HEAD
            )
            out_ref[:, at : at + HEAD] = dq[head][...]

            @pl.when(step < 2)
            def _(head=head, key_at=key_at, value_at=value_at):
                near = dnear[head][...]
                out_ref[:, key_at] = (near[:, :HEAD] + dfar_key[head][...].astype(F32)).astype(BF)
                out_ref[:, value_at] = (near[:, HEAD:] + dfar_value[head][...].astype(F32)).astype(BF)

            @pl.when(step >= 2)
            def _(head=head, key_at=key_at, value_at=value_at):
                out_ref[:, key_at] = down[head][:, :HEAD]
                out_ref[:, value_at] = down[head][:, HEAD:]

        sum_ref[...] += out_ref[...].astype(F32).sum(axis=0, keepdims=True)

    prompt_spec, cont_spec = part_specs(total // 2, tile, 2 * HEAD, 2)
    far_spec, _ = part_specs(total // 2, tile, HEAD, 2)
    return pl.pallas_call(
        body,
        grid=(4,),
        in_specs=[
            *([pl.BlockSpec((tile, HEAD), lambda i: (i, 0))] * HEADS_HERE),
            *([cont_spec] * HEADS_HERE),
            *([prompt_spec] * HEADS_HERE),
            *([far_spec] * (2 * HEADS_HERE)),
        ],
        out_specs=[
            pl.BlockSpec((tile, 3 * HCOLS), lambda i: (i, 0)),
            pl.BlockSpec((1, 3 * HCOLS), lambda i: (0, 0)),
        ],
        out_shape=[
            jax.ShapeDtypeStruct((total, 3 * HCOLS), BF),
            jax.ShapeDtypeStruct((1, 3 * HCOLS), F32),
        ],
        compiler_params=pltpu.CompilerParams(vmem_limit_bytes=56 << 20),
        cost_estimate=cost("join_grads"),
        name="join_grads",
    )(*query_grads, *own_grads, *near_grads, *far_keys, *far_values)


class Values:
    pass


def square_plan(
    prompt,
    conts,
    assignment,
    offsets,
    ln1_gain,
    ln1_bias,
    ln2_gain,
    ln2_bias,
    qkv_weight,
    qkv_bias,
    out_weight,
    out_bias,
    up_weight,
    up_bias,
    down_weight,
    down_bias,
    prompt_cot,
    cont_cot,
):
    block, cont_rows = prompt.shape[1], conts.shape[2]
    shard = qkv_weight.shape[0]
    ff = up_weight.shape[1]
    ff_here = ff // TP
    half = D // 2
    grp_index, seq_index = lax.axis_index("grp"), lax.axis_index("seq")
    tp_rank, z_half = seq_index & 3, seq_index >> 2
    place_index = grp_index * 2 + z_half

    v = Values()


    branch_ids = jnp.arange(offsets.shape[1], dtype=jnp.int32)
    my_offset = jnp.sum(jnp.where(branch_ids == assignment[0, 0], offsets[0], 0)).reshape(1, 1)
    v.offsets = jnp.concatenate(
        [my_offset if bits == 0 else swap_seq(my_offset, bits) for bits in CONT_ORDER], axis=0
    )
    own1, v.side1, far1 = split_columns([qkv_weight, out_weight.T], [3, 1], tp_rank)
    v.got1_y = swap_seq(v.side1, 1)
    v.own_a, v.own_b = reorder_runs([prompt[0], conts[0, 0]], place_index)
    own2, v.side2, far2 = split_columns([up_weight], [1], tp_rank)
    v.got1_y, v.side2 = tie(v.got1_y, v.side2)
    v.got1_z = swap_seq(onward(far1, v.got1_y), 2)
    v.got2_y = swap_seq(v.side2, 1)
    own3, v.side3, far3 = split_columns([down_weight.T], [1], tp_rank)
    qkv_bias_here = pick(qkv_bias.reshape(3, TP, HCOLS), tp_rank, 1).reshape(1, 3 * HCOLS)
    up_bias_here = pick(up_bias.reshape(TP, ff_here), tp_rank, 0)[None]
    vectors = jnp.stack([ln1_gain, ln1_bias, ln2_gain, ln2_bias, out_bias + down_bias])
    vectors = jnp.concatenate([vectors, jnp.zeros((3, D), F32)], axis=0)
    (v.vectors,) = reorder_runs([vectors], place_index)
    prompt_ranks = (tp_rank ^ jnp.array(PROMPT_ORDER, dtype=jnp.int32))[:, None]
    prompt_iota = jnp.arange(block, dtype=jnp.int32)[None, :]
    cont_iota = jnp.arange(cont_rows, dtype=jnp.int32)[None, :]
    near_mark = ((z_half * TP + prompt_ranks) * block + prompt_iota).reshape(-1)
    far_mark = (((z_half ^ 1) * TP + prompt_ranks) * block + prompt_iota).reshape(-1)
    cont_positions = (PROMPT + cont_iota + v.offsets).reshape(-1)
    v.mark = jnp.concatenate([near_mark, cont_positions]).astype(F32)
    query_mark = jnp.concatenate([near_mark, near_mark]).reshape(-1, 1)
    key_mark = jnp.concatenate([near_mark, far_mark]).reshape(1, -1)
    (
        v.got1_z, v.got2_y, v.own_a, v.own_b, v.side3, v.offsets,
    ) = tie(
        v.got1_z, v.got2_y, v.own_a, v.own_b, v.side3, v.offsets,
    )
    v.base1a, v.base1b = stack_ranks(
        own1, v.got1_y, v.got1_z, (2 * HCOLS,) * 2, tp_rank
    )
    v.rows_az = swap_seq(v.own_a, 2)
    v.rows_ay = swap_seq(v.own_a, 1)
    v.z1a = swap_seq(v.base1a, 4)
    v.x1a = swap_grp(v.base1a, 2)
    v.send2 = onward(far2, v.got2_y)
    v.cot0, v.cot1 = prompt_cot[0], cont_cot[0, 0]
    v.cot0, v.cot1, v.base1b = tie(v.cot0, v.cot1, v.base1b)
    v.cot_a, v.cot_b, cot_sum = reorder_runs([v.cot0, v.cot1], place_index, sums=True)
    (
        v.rows_az, v.rows_ay, v.z1a, v.x1a, v.send2, v.base1b, v.own_b, v.cot_a, v.cot_b, v.mark,
    ) = tie(
        v.rows_az, v.rows_ay, v.z1a, v.x1a, v.send2, v.base1b, v.own_b, v.cot_a, v.cot_b, v.mark,
    )
    v.z1b = swap_seq(v.base1b, 4)
    v.got2_z = swap_seq(v.send2, 2)
    v.rows_by = swap_seq(v.own_b, 1)
    v.x1b = swap_grp(v.base1b, 2)
    v.zx1a = swap_grp(v.z1a, 2)
    v.base2a, v.base2b, v.base2 = stack_ranks(
        own2, v.got2_y, v.got2_z, (ff_here // 2,) * 2, tp_rank, True
    )
    tables = rotary_tables(v.mark)
    far_tables = rotary_tables(far_mark.astype(F32))
    v.tables0, v.tables1 = tables
    v.far0, v.far1 = far_tables
    (
        v.vectors, v.z1b, v.base2a, v.base2b, v.base2, v.rows_by, v.x1b, v.zx1a, v.rows_az,
        v.own_b, v.side3, v.tables0, v.tables1, v.far0, v.far1,
    ) = tie(
        v.vectors, v.z1b, v.base2a, v.base2b, v.base2, v.rows_by, v.x1b, v.zx1a, v.rows_az,
        v.own_b, v.side3, v.tables0, v.tables1, v.far0, v.far1,
    )
    tables, far_tables = (v.tables0, v.tables1), (v.far0, v.far1)
    shared = (tables, tables, far_tables, query_mark, key_mark)
    v.got3_y = swap_seq(v.side3, 1)
    v.rows_azy = swap_seq(v.rows_az, 1)
    v.rows_bz = swap_seq(v.own_b, 2)
    v.zx1b = swap_grp(v.z1b, 2)
    v.z2a = swap_seq(v.base2a, 4)
    (
        v.z2a, v.rows_azy, v.rows_bz, v.zx1b, v.got3_y, v.base2b, v.base2,
    ) = tie(
        v.z2a, v.rows_azy, v.rows_bz, v.zx1b, v.got3_y, v.base2b, v.base2,
    )
    v.rows_bzy = swap_seq(v.rows_bz, 1)
    v.z2b = swap_seq(v.base2b, 4)
    v.x2 = swap_grp(v.base2, 2)
    v.got3_z = swap_seq(onward(far3, v.got3_y), 2)
    v.base3a, v.base3b, v.base3 = stack_ranks(
        own3, v.got3_y, v.got3_z, (ff_here // 2,) * 2, tp_rank, True
    )
    v.core1 = beside(
        [(v.base1a, v.base1b), (v.z1a, v.z1b), (v.x1a, v.x1b), (v.zx1a, v.zx1b)]
    )
    gain1, bias1, gain2, bias2, bias_out = (v.vectors[i : i + 1] for i in range(5))
    (
        v.rows_bzy, v.z2a, v.z2b, v.x2, v.base3a, v.base3b, v.base3, v.core1, v.cot_a, v.cot_b,
    ) = tie(
        v.rows_bzy, v.z2a, v.z2b, v.x2, v.base3a, v.base3b, v.base3, v.core1, v.cot_a, v.cot_b,
    )

    v.swapped1 = swap_grp(v.core1, 1)
    v.cot_az = swap_seq(v.cot_a, 2)
    v.cot_ay = swap_seq(v.cot_a, 1)
    v.zx2 = swap_grp(stacked([v.z2a, v.z2b]), 2)
    v.z3a = swap_seq(v.base3a, 4)
    v.rows, v.first_low, v.second_low, mean, spread = both_low_norms(
        [v.own_a, v.rows_az, v.rows_ay, v.rows_azy, v.own_b, v.rows_by, v.rows_bz, v.rows_bzy],
        gain1,
        bias1,
        gain2,
        bias2,
    )
    v.core2 = beside(
        [(v.base2a, v.base2b), (v.z2a, v.z2b), v.x2, v.zx2]
    )
    (
        v.first_low, v.second_low, v.core2, v.swapped1, v.core1, v.base3, v.base3b, v.cot_az,
        v.cot_ay, v.z3a, v.cot_b,
    ) = tie(
        v.first_low, v.second_low, v.core2, v.swapped1, v.core1, v.base3, v.base3b, v.cot_az,
        v.cot_ay, v.z3a, v.cot_b,
    )
    v.cot_by = swap_seq(v.cot_b, 1)
    v.cot_bz = swap_seq(v.cot_b, 2)
    v.z3b = swap_seq(v.base3b, 4)
    v.x3 = swap_grp(v.base3, 2)
    v.swapped2 = swap_grp(v.core2, 1)
    weight1 = (v.core1, v.swapped1)
    v.query0, v.key0, v.value0, own0 = project_qkv(
        0, v.first_low, weight1, qkv_bias_here, *tables
    )
    v.query0, v.first_low = tie(v.query0, v.first_low)
    v.query1, v.key1, v.value1, own1_kv = project_qkv(
        1, v.first_low, weight1, qkv_bias_here, *tables
    )
    (
        v.query1, v.second_low, v.swapped2, v.core2, v.cot_az, v.x3, v.cot_by, v.cot_bz, v.z3b,
        v.key0, v.z3a,
    ) = tie(
        v.query1, v.second_low, v.swapped2, v.core2, v.cot_az, v.x3, v.cot_by, v.cot_bz, v.z3b,
        v.key0, v.z3a,
    )
    v.cot_azy = swap_seq(v.cot_az, 1)
    v.cot_bzy = swap_seq(v.cot_by, 2)
    v.far_key0 = swap_seq(v.key0, 4)
    v.zx3a = swap_grp(v.z3a, 2)
    v.zx3b = swap_grp(v.z3b, 2)
    weight2 = (v.core2, v.swapped2)
    v.act_low, v.slope = feed_forward_up(v.second_low, weight2, up_bias_here)
    (
        v.act_low, v.slope, v.cot_azy, v.cot_bzy, v.far_key0, v.zx3a, v.zx3b, v.value0,
    ) = tie(
        v.act_low, v.slope, v.cot_azy, v.cot_bzy, v.far_key0, v.zx3a, v.zx3b, v.value0,
    )
    v.far_value0 = swap_seq(v.value0, 4)
    v.core3 = beside(
        [(v.base3a, v.base3b), (v.z3a, v.z3b), v.x3, (v.zx3a, v.zx3b)]
    )
    v.swapped3 = swap_grp(v.core3, 1)
    v.attn_grad, v.cots = attention_grad(
        [v.cot_a, v.cot_az, v.cot_ay, v.cot_azy, v.cot_b, v.cot_by, v.cot_bz, v.cot_bzy],
        weight1,
        3,
    )
    v.attn_grad, v.cots, v.act_low = tie(v.attn_grad, v.cots, v.act_low)
    v.down_away = weight_grad(v.cots, [v.act_low])
    (
        v.down_away, v.far_value0, v.key1, v.value1, v.attn_grad, v.swapped3, v.core3,
    ) = tie(
        v.down_away, v.far_value0, v.key1, v.value1, v.attn_grad, v.swapped3, v.core3,
    )
    v.down_core = swap_grp(v.down_away, 1)
    v.far_key1 = swap_seq(v.key1, 4)
    v.attn0, dq0, down0, dnear0, v.dfar_key0, v.dfar_value0 = attend(
        0,
        v.query0,
        v.attn_grad,
        (v.key0, v.value0),
        (v.far_key0, v.far_value0),
        own0,
        *shared,
    )
    (
        v.attn0, v.down_core, v.cots, v.act_low, v.far_key1, v.value1,
    ) = tie(
        v.attn0, v.down_core, v.cots, v.act_low, v.far_key1, v.value1,
    )
    v.far_value1 = swap_seq(v.value1, 4)
    v.down_mine, v.down_send = weight_grad(v.cots, [v.act_low], v.down_core)
    (
        v.down_mine, v.down_send, v.cots, v.slope, v.core3, v.swapped3,
    ) = tie(
        v.down_mine, v.down_send, v.cots, v.slope, v.core3, v.swapped3,
    )
    v.down_side = swap_grp(v.down_send, 2)
    weight3 = (v.core3, v.swapped3)
    v.hidden_grad, up_bias_term = feed_forward_back(v.cots, weight3, v.slope)
    (
        v.hidden_grad, v.far_value1, v.dfar_key0, v.dfar_value0, v.attn_grad,
    ) = tie(
        v.hidden_grad, v.far_value1, v.dfar_key0, v.dfar_value0, v.attn_grad,
    )
    v.back_key0 = swap_seq(v.dfar_key0, 4)
    v.back_value0 = swap_seq(v.dfar_value0, 4)
    v.attn1, dq1, down1, v.dnear1, v.dfar_key1, v.dfar_value1 = attend(
        1,
        v.query1,
        v.attn_grad,
        (v.key1, v.value1),
        (v.far_key1, v.far_value1),
        own1_kv,
        *shared,
    )
    (
        v.attn1, v.second_low, v.hidden_grad, v.down_side, v.down_mine,
    ) = tie(
        v.attn1, v.second_low, v.hidden_grad, v.down_side, v.down_mine,
    )
    v.up_away = weight_grad(v.second_low, [v.hidden_grad])
    v.down_half_send = second_sum(v.down_mine, v.down_side)
    (
        v.up_away, v.back_key0, v.back_value0, v.dfar_key1, v.dfar_value1, v.act_low,
        v.down_half_send,
    ) = tie(
        v.up_away, v.back_key0, v.back_value0, v.dfar_key1, v.dfar_value1, v.act_low,
        v.down_half_send,
    )
    v.up_core = swap_grp(v.up_away, 1)
    v.back_key1 = swap_seq(v.dfar_key1, 4)
    branch = branch_outputs((v.attn0, v.attn1), v.act_low, weight1, 3, weight3)
    v.branch0, v.branch_y, v.branch_zy, v.branch2, v.branch_z, v.branch_yz = branch
    (
        v.branch0, v.branch_y, v.branch_zy, v.branch2, v.branch_z, v.branch_yz, v.up_core,
        v.second_low, v.hidden_grad, v.back_key1, v.dfar_value1,
    ) = tie(
        v.branch0, v.branch_y, v.branch_zy, v.branch2, v.branch_z, v.branch_yz, v.up_core,
        v.second_low, v.hidden_grad, v.back_key1, v.dfar_value1,
    )
    v.got_zy = swap_seq(v.branch_zy, 1)
    v.got_yz = swap_seq(v.branch_yz, 2)
    v.back_value1 = swap_seq(v.dfar_value1, 4)
    v.up_mine, v.up_send = weight_grad(v.second_low, [v.hidden_grad], v.up_core)
    v.up_mine, v.hidden_grad = tie(v.up_mine, v.hidden_grad)
    second_parts, second_sums = norm_grad(
        v.hidden_grad, weight2, gain2, v.rows, mean, spread, (0, 1, 2, 3)
    )
    v.second0, second1, second2, second3 = second_parts
    (
        v.second0, v.back_value1, v.dnear1, v.cots, v.down_half_send, v.up_send, v.got_zy,
        v.got_yz, v.branch0, v.branch2, v.branch_y, v.branch_z,
    ) = tie(
        v.second0, v.back_value1, v.dnear1, v.cots, v.down_half_send, v.up_send, v.got_zy,
        v.got_yz, v.branch0, v.branch2, v.branch_y, v.branch_z,
    )
    v.up_side = swap_grp(v.up_send, 2)
    v.down_half = swap_seq(v.down_half_send, 4)
    v.got_y = swap_seq(v.branch_y, 1)
    v.got_z = swap_seq(v.branch_z, 2)
    v.branch_a_far = second_sum(v.branch0, v.got_zy)
    v.branch_b_far = second_sum(v.branch2, v.got_yz)
    v.qkv_grad, qkv_bias_term = join_grads(
        (dq0, dq1),
        (down0, down1),
        (dnear0, v.dnear1),
        (v.back_key0, v.back_key1),
        (v.back_value0, v.back_value1),
    )
    v.qkv_grad, v.first_low, v.cots = tie(v.qkv_grad, v.first_low, v.cots)
    v.qkv_away = weight_grad(v.first_low, [v.qkv_grad])
    v.qkv_away, v.cots = tie(v.qkv_away, v.cots)
    v.out_away = weight_grad(v.cots, [v.attn0, v.attn1])
    (
        v.out_away, v.qkv_away, v.got_y, v.got_z, v.branch_a_far, v.branch_b_far, v.down_half,
        v.up_side, v.up_mine, v.qkv_grad,
    ) = tie(
        v.out_away, v.qkv_away, v.got_y, v.got_z, v.branch_a_far, v.branch_b_far, v.down_half,
        v.up_side, v.up_mine, v.qkv_grad,
    )
    v.qkv_core = swap_grp(v.qkv_away, 1)
    down_own, v.down_side2, v.down_far = split_rows(
        [(v.down_mine, v.down_side, (v.down_half,))], tp_rank
    )
    v.up_send_a = second_sum(v.up_mine, v.up_side, 0)
    v.up_half_a = swap_seq(v.up_send_a, 4)
    v.branch_far_a = swap_seq(v.branch_a_far, 2)
    v.branch_far_b = swap_seq(v.branch_b_far, 1)
    v.down_y = swap_seq(v.down_side2, 1)
    v.up_send_b = second_sum(v.up_mine, v.up_side, 1)
    (
        v.qkv_core, v.first_low, v.qkv_grad, v.up_send_b,
    ) = tie(
        v.qkv_core, v.first_low, v.qkv_grad, v.up_send_b,
    )
    v.qkv_mine, v.qkv_send = weight_grad(v.first_low, [v.qkv_grad], v.qkv_core)
    v.qkv_mine, v.qkv_send, v.qkv_grad = tie(v.qkv_mine, v.qkv_send, v.qkv_grad)
    v.qkv_side = swap_grp(v.qkv_send, 2)
    entry_far, v.far_sums = norm_grad(
        v.qkv_grad, weight1, gain1, v.rows, mean, spread, (1, 3), (second1, second3), True
    )
    v.entry_y, v.entry_zy, v.entry_z, v.entry_yz = entry_far
    (
        v.entry_y, v.entry_zy, v.entry_z, v.entry_yz, v.far_sums, v.out_away, v.branch_far_a,
        v.branch_far_b, v.down_y, v.down_far, v.up_half_a, v.up_send_b, v.qkv_grad, v.second0,
    ) = tie(
        v.entry_y, v.entry_zy, v.entry_z, v.entry_yz, v.far_sums, v.out_away, v.branch_far_a,
        v.branch_far_b, v.down_y, v.down_far, v.up_half_a, v.up_send_b, v.qkv_grad, v.second0,
    )
    v.entry_got_zy = swap_seq(v.entry_zy, 1)
    v.entry_got_yz = swap_seq(v.entry_yz, 2)
    v.out_core = swap_grp(v.out_away, 1)
    v.up_half_b = swap_seq(v.up_send_b, 4)
    (v.entry0, v.entry2), v.near_sums = norm_grad(
        v.qkv_grad, weight1, gain1, v.rows, mean, spread, (0, 2), (v.second0, second2)
    )
    (
        v.near_sums, v.out_core, v.cots, v.qkv_side, v.qkv_mine, v.up_half_b, v.branch0,
        v.entry_got_zy, v.entry_got_yz, v.entry_y, v.entry_z, v.entry0, v.entry2,
    ) = tie(
        v.near_sums, v.out_core, v.cots, v.qkv_side, v.qkv_mine, v.up_half_b, v.branch0,
        v.entry_got_zy, v.entry_got_yz, v.entry_y, v.entry_z, v.entry0, v.entry2,
    )
    v.entry_got_y = swap_seq(v.entry_y, 1)
    v.entry_got_z = swap_seq(v.entry_z, 2)
    v.qkv_half_send = second_sum(v.qkv_mine, v.qkv_side)
    v.qkv_half = swap_seq(v.qkv_half_send, 4)
    v.out_mine, v.out_send = weight_grad(
        v.cots, [v.attn0, v.attn1], v.out_core
    )
    v.out_side = swap_grp(v.out_send, 2)

    rank_ids = jnp.arange(TP, dtype=jnp.int32)
    first_sums = v.far_sums + v.near_sums
    wide_sums = jnp.concatenate(
        [first_sums[:2], second_sums[:2], cot_sum, jnp.zeros((3, D), F32)], axis=0
    )
    wide_sums = restore_runs(wide_sums, place_index)
    qkv_bias_term = qkv_bias_term.reshape(3, 1, HCOLS)
    v.sums = jnp.concatenate(
        [
            wide_sums[:5].reshape(-1),
            jnp.where((rank_ids == tp_rank)[None, :, None], qkv_bias_term, 0.0).reshape(-1),
            jnp.where((rank_ids == tp_rank)[:, None], up_bias_term, 0.0).reshape(-1),
        ]
    ).reshape(-1, LANES)
    v.sums_got = swap_grp(v.sums, 1)
    v.entry_a_far = second_sum(v.entry0, v.entry_got_zy)
    v.entry_b_far = second_sum(v.entry2, v.entry_got_yz)
    (
        v.sums, v.sums_got, v.out_send, v.out_mine, v.entry_got_y, v.entry_got_z, v.entry_a_far,
        v.entry_b_far, v.branch0, v.up_half_b,
    ) = tie(
        v.sums, v.sums_got, v.out_send, v.out_mine, v.entry_got_y, v.entry_got_z, v.entry_a_far,
        v.entry_b_far, v.branch0, v.up_half_b,
    )
    v.entry_far_a = swap_seq(v.entry_a_far, 2)
    v.entry_far_b = swap_seq(v.entry_b_far, 1)
    v.sums = v.sums + v.sums_got
    v.sums_got = swap_grp(v.sums, 2)
    v.layer_a, v.layer_b = finish_outputs(
        (
            (v.branch0, v.got_y, v.branch_far_a),
            (v.branch2, v.got_z, v.branch_far_b),
        ),
        (v.own_a, v.own_b),
        bias_out,
        place_index,
    )
    up_own, v.up_side2, v.up_far = split_rows(
        [(v.up_mine, v.up_side, (v.up_half_a, v.up_half_b))], tp_rank
    )
    (
        v.layer_a, v.sums, v.sums_got, v.up_side2, v.out_side, v.out_mine, v.qkv_half,
    ) = tie(
        v.layer_a, v.sums, v.sums_got, v.up_side2, v.out_side, v.out_mine, v.qkv_half,
    )
    v.out_half_send = second_sum(v.out_mine, v.out_side)
    v.out_half = swap_seq(v.out_half_send, 4)
    v.up_y = swap_seq(v.up_side2, 1)
    v.sums = v.sums + v.sums_got
    v.sums_got = swap_seq(v.sums, 4)
    v.down_on = onward(v.down_far, v.down_y)
    (
        v.entry_far_a, v.entry_far_b, v.out_half, v.up_y, v.up_far, v.down_on, v.sums,
        v.sums_got,
    ) = tie(
        v.entry_far_a, v.entry_far_b, v.out_half, v.up_y, v.up_far, v.down_on, v.sums,
        v.sums_got,
    )
    late_own, late_side, late_far = split_rows(
        [
            (v.qkv_mine, v.qkv_side, (v.qkv_half,)),
            (v.out_mine, v.out_side, (v.out_half,)),
        ],
        tp_rank,
    )
    v.late_y = swap_seq(late_side, 1)
    v.down_z = swap_seq(v.down_on, 2)
    v.up_z = swap_seq(onward(v.up_far, v.up_y), 2)
    v.sums = v.sums + v.sums_got
    v.sums_got = swap_seq(v.sums, 1)
    v.grad_a, grad_b = finish_grads(
        (
            (v.entry0, v.entry_got_y, v.entry_far_a),
            (v.entry2, v.entry_got_z, v.entry_far_b),
        ),
        (v.own_a, v.own_b),
        (v.cot_a, v.cot_b),
        place_index,
    )
    (
        v.grad_a, v.late_y, v.down_z, v.up_z, v.sums, v.sums_got,
    ) = tie(
        v.grad_a, v.late_y, v.down_z, v.up_z, v.sums, v.sums_got,
    )
    v.late_z = swap_seq(onward(late_far, v.late_y), 2)
    v.sums = v.sums + v.sums_got
    v.sums_got = swap_seq(v.sums, 2)
    (v.down_grad,) = join_columns(
        down_own, v.down_y, v.down_z, [(1, ff_here)], tp_rank
    )
    (v.up_grad,) = join_columns(up_own, v.up_y, v.up_z, [(1, ff_here)], tp_rank)
    grad_a, down_grad, up_weight_grad = v.grad_a, v.down_grad, v.up_grad
    qkv_weight_grad, out_grad = join_columns(
        late_own, v.late_y, v.late_z, [(3, HCOLS), (1, HCOLS)], tp_rank
    )
    down_weight_grad, out_weight_grad = down_grad.T, out_grad.T
    sums = (v.sums + v.sums_got).reshape(-1)
    cuts = np.cumsum([D, D, D, D, D, 3 * D])
    gain_one, shift_one, gain_two, shift_two, out_sum, qkv_sum, up_sum = jnp.split(sums, cuts)

    return (
        v.layer_a[None],
        v.layer_b[None, None],
        grad_a[None],
        grad_b[None, None],
        gain_one,
        shift_one,
        gain_two,
        shift_two,
        qkv_weight_grad,
        qkv_sum,
        out_weight_grad,
        out_sum,
        up_weight_grad,
        up_sum,
        down_weight_grad,
        out_sum,
    )


def solution(mesh):
    in_specs = (
        P("grp", "seq", None),
        P("grp", "seq", None, None),
        P("grp", "seq"),
        P("grp", None),
        P(),
        P(),
        P(),
        P(),
        P(("grp", "seq"), None),
        P(),
        P(None, ("grp", "seq")),
        P(),
        P(("grp", "seq"), None),
        P(),
        P(None, ("grp", "seq")),
        P(),
        P("grp", "seq", None),
        P("grp", "seq", None, None),
    )
    out_specs = (
        P("grp", "seq", None),
        P("grp", "seq", None, None),
        P("grp", "seq", None),
        P("grp", "seq", None, None),
        P(),
        P(),
        P(),
        P(),
        P(("grp", "seq"), None),
        P(),
        P(None, ("grp", "seq")),
        P(),
        P(("grp", "seq"), None),
        P(),
        P(None, ("grp", "seq")),
        P(),
    )
    plan = square_plan if (mesh.shape["grp"], mesh.shape["seq"]) == (4, 8) else local
    return jax.shard_map(plan, mesh=mesh, in_specs=in_specs, out_specs=out_specs, check_vma=False)
```
